32 devices in a mesh: rep: 4 (over x, core), shard: 8 (over z, y).
Axes of the slice: x: 2, y: 2, z: 4, core: 2. Of those that a mesh axis runs over, the one named last changes fastest.
Arguments:
- hidden: float32 [64, 1024, 768], P(('rep', 'shard')), may hold values from -6 to 6
- lengths: int32 [64], P(('rep', 'shard')), may hold values from 256 to 1024, as said below
- clusters: int32 [64, 12, 1024], P(('rep', 'shard')), may hold values from 0 to 1023, each once within a row
- input_weight: bfloat16 [768, 2304], P('shard'), may hold values from -0.3125 to 0.3125
- query_bias: bfloat16 [768], P('shard'), may hold values from -3 to 3
- value_bias: bfloat16 [768], P('shard'), may hold values from -1.1953125 to 1.1953125
- out_weight: bfloat16 [768, 768], P('shard'), may hold values from -0.875 to 0.875
- out_bias: bfloat16 [768], P('shard'), may hold values from -1.1953125 to 1.1953125
- norm1_gain: bfloat16 [768], P('shard'), may hold values from 0.5 to 1.5
- norm1_bias: bfloat16 [768], P('shard'), may hold values from -1.1953125 to 1.1953125
- up_weight: bfloat16 [768, 3072], P('shard'), may hold values from -0.21875 to 0.21875
- up_bias: bfloat16 [3072], P('shard'), may hold values from -1.796875 to 1.796875
- down_weight: bfloat16 [3072, 768], P('shard'), may hold values from -0.15625 to 0.15625
- down_bias: bfloat16 [768], P('shard'), may hold values from -1.1953125 to 1.1953125
- norm2_gain: bfloat16 [768], P('shard'), may hold values from 0.5 to 1.5
- norm2_bias: bfloat16 [768], P('shard'), may hold values from -1.1953125 to 1.1953125
- cotangent: float32 [64, 1024, 768], P(('rep', 'shard')), may hold values from -6 to 6
Outputs:
- output: float32 [64, 1024, 768], P(('rep', 'shard'))
- input_grad: float32 [64, 1024, 768], P(('rep', 'shard'))
- input_weight_grad: float32 [768, 2304], P('shard')
- query_bias_grad: float32 [768], P('shard')
- value_bias_grad: float32 [768], P('shard')
- out_weight_grad: float32 [768, 768], P('shard')
- out_bias_grad: float32 [768], P('shard')
- norm1_gain_grad: float32 [768], P('shard')
- norm1_bias_grad: float32 [768], P('shard')
- up_weight_grad: float32 [768, 3072], P('shard')
- up_bias_grad: float32 [3072], P('shard')
- down_weight_grad: float32 [3072, 768], P('shard')
- down_bias_grad: float32 [768], P('shard')
- norm2_gain_grad: float32 [768], P('shard')
- norm2_bias_grad: float32 [768], P('shard')
The draws below stay inside these ranges and needn't reach their ends.
Inputs may be any that keep to these rules, and one draw needn't show every extreme that they name: `lengths`: the longest sequence has 1024 valid tokens and the shortest 256, in every draw. `clusters`: each sequence's ordering for each head names every position once.
All inputs are finite; a program needn't handle non-finite values.
Results may differ from the reference program's by a relative error of at most 0.018.
The reference program's roundings to bfloat16 on the way count: a program that leaves them out, or rounds other values in their place, can miss the bound.
Values may be sent and summed in bfloat16 or wider, within the bound.
A program may use at most 256 MiB of HBM per device.

```python
import math
import jax
import jax.numpy as jnp
from jax import lax

D = 768
H = 12
DH = 64
FF = 3072
CLUSTER = 128
LEN = 1024
LMIN = 256
SEQS = 64


def draw_lengths(key, part):
    key_main, key_top, key_low = jax.random.split(key, 3)
    values = jax.random.randint(key_main, (SEQS,), LMIN, LEN + 1)
    top_at = jax.random.randint(key_top, (), 0, SEQS)
    low_at = (top_at + 1 + jax.random.randint(key_low, (), 0, SEQS - 1)) % SEQS
    values = values.at[top_at].set(LEN).at[low_at].set(LMIN)
    return values.astype(jnp.int32)


def steps_of(rng, extent, cuts, least, top_value):
    def one(dim, blocks):
        steps = jax.random.uniform(jax.random.fold_in(jax.random.fold_in(rng, 6), dim), (blocks,), jnp.float32, least / len(cuts), top_value / len(cuts))
        return jnp.repeat(jnp.exp(steps), extent[dim] // blocks).reshape((-1,) + (1,) * (len(extent) - dim - 1))

    level = one(*cuts[0])
    for cut in cuts[1:]:
        level = level * one(*cut)
    return level


def normal_values(key, shape, width, reach, cuts=(), kind=jnp.bfloat16):
    entries = width * jax.random.normal(key, shape, jnp.float32)
    if cuts:
        entries = entries * steps_of(key, shape, cuts, -0.22, 0.18)
    return jnp.clip(entries, -reach, reach).astype(kind)


def setup_inputs(seed: int = 0) -> dict:
    splits = jax.random.split(jax.random.key(seed), 18)
    return {
        "hidden": normal_values(splits[0], (SEQS, LEN, D), 1.0, 6.0, ((0, 32),), jnp.float32),
        "lengths": draw_lengths(jax.random.fold_in(splits[17], 71), 0),
        "clusters": jax.vmap(lambda own: jax.random.permutation(own, LEN))(jax.random.split(splits[2], SEQS * H)).reshape((SEQS, H, LEN)).astype(jnp.int32),
        "input_weight": normal_values(splits[3], (D, 3 * D), (D // 2) ** -0.5, 0.3125, ((0, 8),)),
        "query_bias": normal_values(splits[4], (D,), 0.5, 3.0, ((0, 8),)),
        "value_bias": normal_values(splits[5], (D,), 0.2, 1.1953125, ((0, 8),)),
        "out_weight": normal_values(splits[6], (D, D), (D // 16) ** -0.5, 0.875, ((0, 8),)),
        "out_bias": normal_values(splits[7], (D,), 0.2, 1.1953125, ((0, 8),)),
        "norm1_gain": jnp.clip(1.0 + 0.1 * jax.random.normal(splits[8], (D,), jnp.float32), 0.5, 1.5).astype(jnp.bfloat16),
        "norm1_bias": normal_values(splits[9], (D,), 0.2, 1.1953125, ((0, 8),)),
        "up_weight": normal_values(splits[10], (D, FF), D ** -0.5, 0.21875, ((0, 8),)),
        "up_bias": normal_values(splits[11], (FF,), 0.3, 1.796875, ((0, 8),)),
        "down_weight": normal_values(splits[12], (FF, D), (FF // 2) ** -0.5, 0.15625, ((0, 8),)),
        "down_bias": normal_values(splits[13], (D,), 0.2, 1.1953125, ((0, 8),)),
        "norm2_gain": jnp.clip(1.0 + 0.1 * jax.random.normal(splits[14], (D,), jnp.float32), 0.5, 1.5).astype(jnp.bfloat16),
        "norm2_bias": normal_values(splits[15], (D,), 0.2, 1.1953125, ((0, 8),)),
        "cotangent": normal_values(splits[16], (SEQS, LEN, D), 1.0, 6.0, ((0, 32),), jnp.float32),
    }


@jax.custom_vjp
def low(v):
    return lax.optimization_barrier(v.astype(jnp.bfloat16)).astype(jnp.float32)

@jax.custom_vjp
def low_back(v):
    return v

def low_keep(v):
    return (low(v), None)

def low_pass(kept, grad):
    return (grad,)

def back_keep(v):
    return (v, None)

def back_low(kept, grad):
    return (low(grad),)
low.defvjp(low_keep, low_pass)
low_back.defvjp(back_keep, back_low)
eps_norm = 1e-12

def dense(left, right):
    return jnp.dot(left, right, precision=lax.Precision.HIGHEST, preferred_element_type=jnp.float32)

def layer_norm(source, gain, shift):
    centre = lax.optimization_barrier(jnp.mean(source, axis=-1, keepdims=True))
    centred = source - centre
    variance = lax.optimization_barrier(jnp.mean(centred * centred, axis=-1, keepdims=True))
    return centred * lax.rsqrt(variance + eps_norm) * gain + shift

def cluster_attention(query_rows, key_rows, value_rows, order, valid):
    group = query_rows.shape[0]
    blocks_n = LEN // CLUSTER

    def to_blocks(source):
        shaped = source.reshape(group, LEN, H, DH).transpose(0, 2, 1, 3)
        picked = jnp.take_along_axis(shaped, order[..., None], axis=2)
        return picked.reshape(group, H, blocks_n, CLUSTER, DH)
    query_c = to_blocks(query_rows)
    key_c = to_blocks(key_rows)
    value_c = to_blocks(value_rows)
    key_valid = jnp.take_along_axis(jnp.broadcast_to(valid[:, None, :], order.shape), order, axis=2)
    key_bias = ((key_valid - 1.0) * 30000.0).reshape(group, H, blocks_n, 1, CLUSTER)
    product = jnp.einsum('ghcqd,ghckd->ghcqk', query_c, key_c, precision=lax.Precision.HIGHEST)
    scores = 0.125 * low_back(product) + key_bias
    probs = low(jax.nn.softmax(scores, axis=-1))
    mixed = jnp.einsum('ghcqk,ghckd->ghcqd', probs, value_c, precision=lax.Precision.HIGHEST)
    mixed = mixed.reshape(group, H, LEN, DH)
    inverse = jnp.argsort(order, axis=-1).astype(jnp.int32)
    placed = jnp.take_along_axis(mixed, inverse[..., None], axis=2)
    return placed.transpose(0, 2, 1, 3).reshape(group, LEN, D)

def layer_forward(weights, source, valid, order):
    input_weight, query_bias, value_bias, out_weight, out_bias, norm1_gain, norm1_bias, up_weight, up_bias, down_weight, down_bias, norm2_gain, norm2_bias = weights
    group = source.shape[0]
    flat = source.reshape(group * LEN, D)
    rounded = low(flat)
    bias_all = jnp.concatenate([query_bias, jnp.zeros((D,), jnp.float32), value_bias])
    projected = low(low_back(dense(rounded, input_weight)) + bias_all)
    query_rows = projected[:, :D].reshape(group, LEN, D)
    key_rows = projected[:, D:2 * D].reshape(group, LEN, D)
    value_rows = projected[:, 2 * D:].reshape(group, LEN, D)
    attended = low_back(low(cluster_attention(query_rows, key_rows, value_rows, order, valid)))
    attended = attended.reshape(group * LEN, D)
    branch = low_back(dense(attended, out_weight)) + out_bias
    first_out = layer_norm(flat + branch, norm1_gain, norm1_bias)
    pre_gelu = low_back(dense(low(first_out), up_weight)) + up_bias
    activated = low(jax.nn.gelu(pre_gelu, approximate=False))
    second_sum = first_out + low_back(dense(activated, down_weight)) + down_bias
    second_out = layer_norm(second_sum, norm2_gain, norm2_bias)
    return (second_out * valid.reshape(group * LEN, 1)).reshape(group, LEN, D)

def reference(hidden, lengths, clusters, input_weight, query_bias, value_bias, out_weight, out_bias, norm1_gain, norm1_bias, up_weight, up_bias, down_weight, down_bias, norm2_gain, norm2_bias, cotangent):
    params = tuple((weight_arg.astype(jnp.float32) for weight_arg in (input_weight, query_bias, value_bias, out_weight, out_bias, norm1_gain, norm1_bias, up_weight, up_bias, down_weight, down_bias, norm2_gain, norm2_bias)))
    group = math.gcd(SEQS, max(1, 4096 // LEN))
    steps_count = SEQS // group
    positions = jnp.arange(LEN, dtype=jnp.int32)
    valid_all = (positions[None, :] < lengths[:, None]).astype(jnp.float32)

    def one_group(totals, pieces):
        source, valid, order, upstream = pieces

        def apply_layer(weights, inputs):
            return layer_forward(weights, inputs, valid, order)
        result, pullback = jax.vjp(apply_layer, params, source)
        grads, back_input = pullback(upstream)
        return (jax.tree.map(jnp.add, totals, grads), (result, back_input))

    def regroup(source):
        return source.reshape((steps_count, group) + source.shape[1:])
    zeros_init = jax.tree.map(jnp.zeros_like, params)
    totals, (result, back_input) = lax.scan(one_group, zeros_init, (regroup(hidden.astype(jnp.float32)), regroup(valid_all), regroup(clusters), regroup(cotangent.astype(jnp.float32))))
    return (result.reshape(SEQS, LEN, D), back_input.reshape(SEQS, LEN, D), totals[0], totals[1], totals[2], totals[3], totals[4], totals[5], totals[6], totals[7], totals[8], totals[9], totals[10], totals[11], totals[12])
```

```python
from functools import partial

import jax
import jax.numpy as jnp
from jax import lax
from jax.experimental import pallas as pl
from jax.experimental.pallas import tpu as pltpu
from jax.sharding import PartitionSpec as P

D = 768
H = 12
DH = 64
FF = 3072
CLUSTER = 128
LEN = 1024
PAIRS = H // 2
SLICES = [slice(c * CLUSTER, (c + 1) * CLUSTER) for c in range(LEN // CLUSTER)]
bf = jnp.bfloat16
f32 = jnp.float32
eps_norm = 1e-12


def dot_nn(left, right):
    return lax.dot_general(left, right, (((1,), (0,)), ((), ())), preferred_element_type=f32)


def dot_nt(left, right):
    return lax.dot_general(left, right, (((1,), (1,)), ((), ())), preferred_element_type=f32)


def dot_tn(left, right):
    return lax.dot_general(left, right, (((0,), (0,)), ((), ())), preferred_element_type=f32)


def low_lanes():
    return lax.broadcasted_iota(jnp.int32, (LEN, CLUSTER), 1) < DH


def table_of(order_row):
    positions = lax.broadcasted_iota(jnp.int32, (LEN, LEN), 0)
    return jnp.where(jnp.broadcast_to(order_row, (LEN, LEN)) == positions, 1.0, 0.0).astype(bf)


def half_roll(source):
    return pltpu.roll(source.astype(f32), DH, 1).astype(bf)


def softmax_rows(scores):
    top = jnp.max(scores, axis=-1, keepdims=True)
    grown = jnp.exp(scores - top)
    return grown * (1.0 / jnp.sum(grown, axis=-1, keepdims=True))


def attention_forward_body(
    len_ref, x_ref, w_ref, b_ref, row_ref, att_ref, proj_ref, t0, t1, s0, s1, m0, m1
):
    count = len_ref[pl.program_id(0)]
    proj = (dot_nn(x_ref[...], w_ref[...]) + b_ref[0]).astype(bf)
    proj_ref[...] = proj
    low = low_lanes()
    tables, scores, mixed = (t0, t1), (s0, s1), (m0, m1)
    rows = [row_ref[0, 0, e : e + 1, :] for e in range(2)]
    for e in range(2):
        tables[e][...] = table_of(rows[e])
    picked = [
        dot_tn(tables[e][...], proj[:, 128 * e : 128 * e + 256]).astype(bf) for e in range(2)
    ]
    for e in range(2):
        qk = picked[e][:, 128 * e : 128 * e + 128]
        key_low = jnp.where(low, half_roll(qk), jnp.zeros((), bf))
        bias = jnp.where(rows[e] < count, 0.0, -30000.0)
        for sl in SLICES:
            scores[e][sl, :] = 0.125 * dot_nt(qk[sl], key_low[sl]) + bias[:, sl]
    for e in range(2):
        values = picked[e][:, 128 - 128 * e : 256 - 128 * e]
        for sl in SLICES:
            probs = softmax_rows(scores[e][sl, :]).astype(bf)
            mixed[e][sl, :] = dot_nn(probs, values[sl]).astype(bf)
    placed = [dot_nn(tables[e][...], mixed[e][...]) for e in range(2)]
    att_ref[...] = jnp.where(low, placed[0], placed[1]).astype(bf)


def attention_forward(lengths, rounded, weight, bias, rows):
    seqs = rows.shape[0]
    tokens = seqs * LEN
    return pl.pallas_call(
        attention_forward_body,
        grid_spec=pltpu.PrefetchScalarGridSpec(
            num_scalar_prefetch=1,
            grid=(seqs, PAIRS),
            in_specs=[
                pl.BlockSpec((LEN, D), lambda s, h, n: (s, 0)),
                pl.BlockSpec((D, 384), lambda s, h, n: (0, h)),
                pl.BlockSpec((1, 1, 384), lambda s, h, n: (h, 0, 0)),
                pl.BlockSpec((1, 1, 2, LEN), lambda s, h, n: (s, h, 0, 0)),
            ],
            out_specs=[
                pl.BlockSpec((LEN, 128), lambda s, h, n: (s, h)),
                pl.BlockSpec((LEN, 384), lambda s, h, n: (s, h)),
            ],
            scratch_shapes=[pltpu.VMEM((LEN, LEN), bf)] * 2
            + [pltpu.VMEM((LEN, 128), f32)] * 2
            + [pltpu.VMEM((LEN, 128), bf)] * 2,
        ),
        out_shape=[
            jax.ShapeDtypeStruct((tokens, D), bf),
            jax.ShapeDtypeStruct((tokens, 3 * D), bf),
        ],
        compiler_params=pltpu.CompilerParams(vmem_limit_bytes=50 << 20),
        cost_estimate=pl.CostEstimate(
            flops=44_000_000_000, bytes_accessed=24_000_000, transcendentals=0
        ),
        name="attention_forward",
    )(lengths, rounded, weight, bias, rows)


def attention_backward_body(
    len_ref,
    x_ref,
    proj_ref,
    datt_ref,
    row_ref,
    dproj_ref,
    dw_ref,
    db_ref,
    t0,
    t1,
    s0,
    s1,
    d0,
    d1,
    p0,
    p1,
    e0,
    e1,
    total,
):
    seq = pl.program_id(1)
    count = len_ref[seq]
    low = low_lanes()
    zero = jnp.zeros((), bf)
    tables, scores, back_probs, probs_low, backs = (t0, t1), (s0, s1), (d0, d1), (p0, p1), (e0, e1)
    rows = [row_ref[0, 0, e : e + 1, :] for e in range(2)]
    for e in range(2):
        tables[e][...] = table_of(rows[e])
    datt = datt_ref[...]
    swapped = half_roll(proj_ref[:, 128:256])
    middle = [jnp.where(low, datt, swapped), jnp.where(low, swapped, datt)]
    sources = [
        jnp.concatenate([proj_ref[:, 256 * e : 256 * e + 128], middle[e]], axis=1)
        for e in range(2)
    ]
    picked = [dot_tn(tables[e][...], sources[e]).astype(bf) for e in range(2)]
    for e in range(2):
        qk, dv = picked[e][:, 0:128], picked[e][:, 128:256]
        key_low = jnp.where(low, half_roll(qk), zero)
        turned = half_roll(dv)
        value_only = jnp.where(low, turned, zero) if e == 0 else jnp.where(low, zero, turned)
        bias = jnp.where(rows[e] < count, 0.0, -30000.0)
        for sl in SLICES:
            scores[e][sl, :] = 0.125 * dot_nt(qk[sl], key_low[sl]) + bias[:, sl]
            back_probs[e][sl, :] = dot_nt(dv[sl], value_only[sl])
    for e in range(2):
        for sl in SLICES:
            probs = softmax_rows(scores[e][sl, :])
            back = back_probs[e][sl, :]
            probs_low[e][sl, :] = probs.astype(bf)
            inner = jnp.sum(back * probs, axis=-1, keepdims=True)
            backs[e][sl, :] = (0.125 * (probs * (back - inner))).astype(bf)
    placed = []
    for e in range(2):
        qk, dv = picked[e][:, 0:128], picked[e][:, 128:256]
        queries, keys, values = [], [], []
        for sl in SLICES:
            back = backs[e][sl, :]
            queries.append(dot_nn(back, qk[sl]))
            keys.append(dot_tn(back, qk[sl]))
            values.append(dot_tn(probs_low[e][sl, :], dv[sl]))
        key_query = jnp.where(low, jnp.concatenate(keys, 0), jnp.concatenate(queries, 0))
        value = jnp.concatenate(values, 0)
        db_ref[0, 0, e : e + 1, :] = jnp.sum(key_query, axis=0, keepdims=True)
        db_ref[0, 0, 2 + e : 3 + e, :] = jnp.sum(value, axis=0, keepdims=True)
        parts = [half_roll(key_query), value.astype(bf)]
        placed.append(
            dot_nn(tables[e][...], jnp.concatenate(parts if e == 0 else parts[::-1], axis=1))
        )
    out = jnp.concatenate(
        [
            placed[0][:, 0:128],
            jnp.where(low, placed[0][:, 128:256], placed[1][:, 0:128]),
            placed[1][:, 128:256],
        ],
        axis=1,
    ).astype(bf)
    dproj_ref[...] = out
    part = dot_tn(x_ref[...], out)

    @pl.when(seq == 0)
    def _():
        total[...] = part

    @pl.when(seq != 0)
    def _():
        total[...] += part

    dw_ref[...] = total[...].astype(bf)


def attention_backward(lengths, rounded, proj, datt, rows):
    seqs = rows.shape[0]
    tokens = seqs * LEN
    return pl.pallas_call(
        attention_backward_body,
        grid_spec=pltpu.PrefetchScalarGridSpec(
            num_scalar_prefetch=1,
            grid=(PAIRS, seqs),
            in_specs=[
                pl.BlockSpec((LEN, D), lambda h, s, n: (s, 0)),
                pl.BlockSpec((LEN, 384), lambda h, s, n: (s, h)),
                pl.BlockSpec((LEN, 128), lambda h, s, n: (s, h)),
                pl.BlockSpec((1, 1, 2, LEN), lambda h, s, n: (s, h, 0, 0)),
            ],
            out_specs=[
                pl.BlockSpec((LEN, 384), lambda h, s, n: (s, h)),
                pl.BlockSpec((D, 384), lambda h, s, n: (0, h)),
                pl.BlockSpec((1, 1, 4, 128), lambda h, s, n: (s, h, 0, 0)),
            ],
            scratch_shapes=[pltpu.VMEM((LEN, LEN), bf)] * 2
            + [pltpu.VMEM((LEN, 128), f32)] * 4
            + [pltpu.VMEM((LEN, 128), bf)] * 4
            + [pltpu.VMEM((D, 384), f32)],
        ),
        out_shape=[
            jax.ShapeDtypeStruct((tokens, 3 * D), bf),
            jax.ShapeDtypeStruct((D, 3 * D), bf),
            jax.ShapeDtypeStruct((seqs, PAIRS, 4, 128), f32),
        ],
        compiler_params=pltpu.CompilerParams(vmem_limit_bytes=50 << 20),
        cost_estimate=pl.CostEstimate(
            flops=70_000_000_000, bytes_accessed=30_000_000, transcendentals=0
        ),
        name="attention_backward",
    )(lengths, rounded, proj, datt, rows)


def to_pairs(weight):
    parts = weight.reshape(weight.shape[:-1] + (3, PAIRS, 2, DH))
    query, key, value = parts[..., 0, :, :, :], parts[..., 1, :, :, :], parts[..., 2, :, :, :]
    a, b = 0, 1
    joined = jnp.concatenate(
        [
            query[..., a, :],
            key[..., a, :],
            value[..., a, :],
            value[..., b, :],
            query[..., b, :],
            key[..., b, :],
        ],
        axis=-1,
    )
    return joined.reshape(weight.shape)


def from_pairs(weight):
    parts = weight.reshape(weight.shape[:-1] + (PAIRS, 6, DH))
    query = jnp.stack([parts[..., 0, :], parts[..., 4, :]], axis=-2)
    key = jnp.stack([parts[..., 1, :], parts[..., 5, :]], axis=-2)
    value = jnp.stack([parts[..., 2, :], parts[..., 3, :]], axis=-2)
    lead = weight.shape[:-1]
    return jnp.concatenate([t.reshape(lead + (D,)) for t in (query, key, value)], axis=-1)


def norm_forward(source, gain, shift):
    centre = jnp.mean(source, axis=-1, keepdims=True)
    centred = source - centre
    variance = jnp.mean(centred * centred, axis=-1, keepdims=True)
    scale_inv = lax.rsqrt(variance + eps_norm)
    normed = centred * scale_inv
    return (normed * gain + shift, normed, scale_inv)


def norm_backward(upstream, normed, scale_inv, gain):
    scaled = upstream * gain
    mean_part = jnp.mean(scaled, axis=-1, keepdims=True)
    along_part = jnp.mean(scaled * normed, axis=-1, keepdims=True)
    back_rows = scale_inv * (scaled - mean_part - normed * along_part)
    return (back_rows, jnp.sum(upstream * normed, axis=0), jnp.sum(upstream, axis=0))


def local(
    hidden,
    lengths,
    clusters,
    input_weight,
    query_bias,
    value_bias,
    out_weight,
    out_bias,
    norm1_gain,
    norm1_bias,
    up_weight,
    up_bias,
    down_weight,
    down_bias,
    norm2_gain,
    norm2_bias,
    cotangent,
):
    seqs = hidden.shape[0]
    tokens = seqs * LEN
    gather = partial(lax.all_gather, axis_name="shard", axis=0, tiled=True)
    vectors = (
        query_bias,
        value_bias,
        out_bias,
        norm1_gain,
        norm1_bias,
        down_bias,
        norm2_gain,
        norm2_bias,
        up_bias,
    )
    widths = [v.shape[0] for v in vectors]
    marks = [sum(widths[:i]) for i in range(len(widths) + 1)]
    packed = lax.all_gather(jnp.concatenate(vectors)[None], "shard", axis=0, tiled=True)
    query_b, value_b, out_b, gain1, shift1, down_b, gain2, shift2, up_b = [
        packed[:, marks[i] : marks[i + 1]].reshape(-1).astype(f32) for i in range(len(widths))
    ]
    in_w = gather(to_pairs(input_weight))
    out_w = gather(out_weight)
    up_w = gather(up_weight)
    down_w = gather(down_weight)

    flat = hidden.reshape(tokens, D)
    rounded = flat.astype(bf)
    rows = clusters.reshape(seqs, PAIRS, 2, LEN)
    bias_pairs = to_pairs(jnp.concatenate([query_b, jnp.zeros_like(query_b), value_b]))
    attended, proj = attention_forward(
        lengths, rounded, in_w, bias_pairs.reshape(PAIRS, 1, 384), rows
    )
    positions = jnp.arange(LEN, dtype=jnp.int32)
    valid = (positions[None, :] < lengths[:, None]).astype(f32).reshape(tokens, 1)
    first_out, normed_one, scale_one = norm_forward(
        flat + dot_nn(attended, out_w) + out_b, gain1, shift1
    )
    first_low = first_out.astype(bf)
    pre_gelu = dot_nn(first_low, up_w) + up_b
    activated = jax.nn.gelu(pre_gelu, approximate=False).astype(bf)
    second_sum = first_out + dot_nn(activated, down_w) + down_b
    second_out, normed_two, scale_two = norm_forward(second_sum, gain2, shift2)
    result = (second_out * valid).reshape(seqs, LEN, D)

    back_out = cotangent.reshape(tokens, D) * valid
    back_second, gain2_grad, shift2_grad = norm_backward(back_out, normed_two, scale_two, gain2)
    down_b_grad = jnp.sum(back_second, axis=0)
    second_low = back_second.astype(bf)
    down_w_grad = dot_tn(activated, second_low).astype(bf)
    back_act = dot_nt(second_low, down_w)
    back_pre = jax.vjp(partial(jax.nn.gelu, approximate=False), pre_gelu)[1](back_act)[0]
    up_b_grad = jnp.sum(back_pre, axis=0)
    pre_low = back_pre.astype(bf)
    up_w_grad = dot_tn(first_low, pre_low).astype(bf)
    back_first = dot_nt(pre_low, up_w) + back_second
    back_sum, gain1_grad, shift1_grad = norm_backward(back_first, normed_one, scale_one, gain1)
    out_b_grad = jnp.sum(back_sum, axis=0)
    sum_low = back_sum.astype(bf)
    out_w_grad = dot_tn(attended, sum_low).astype(bf)
    back_attended = dot_nt(sum_low, out_w).astype(bf)
    dproj, in_w_grad, db = attention_backward(lengths, rounded, proj, back_attended, rows)
    db = jnp.sum(db, axis=0)
    query_b_grad = db[:, 0:2, DH:].reshape(D)
    value_b_grad = jnp.concatenate([db[:, 2, :DH], db[:, 3, DH:]], axis=1).reshape(D)
    back_input = (back_sum + dot_nt(dproj, in_w)).reshape(seqs, LEN, D)

    def scatter(grad):
        part = lax.psum_scatter(grad, "shard", scatter_dimension=0, tiled=True)
        return lax.psum(part.astype(f32), "rep")

    shards = packed.shape[0]
    small = jnp.concatenate(
        [
            g.reshape(shards, -1)
            for g in (
                query_b_grad,
                value_b_grad,
                out_b_grad,
                gain1_grad,
                shift1_grad,
                down_b_grad,
                gain2_grad,
                shift2_grad,
                up_b_grad,
            )
        ],
        axis=1,
    )
    small = lax.psum(small, ("rep", "shard"))
    mine = lax.dynamic_index_in_dim(small, lax.axis_index("shard"), 0, keepdims=False)
    small = [mine[marks[i] : marks[i + 1]] for i in range(len(widths))]
    return (
        result,
        back_input,
        from_pairs(scatter(in_w_grad)),
        small[0],
        small[1],
        scatter(out_w_grad),
        small[2],
        small[3],
        small[4],
        scatter(up_w_grad),
        small[8],
        scatter(down_w_grad),
        small[5],
        small[6],
        small[7],
    )


def solution(mesh):
    tokens = P(("rep", "shard"), None, None)
    matrix, vector = P("shard", None), P("shard")
    params = (
        matrix,
        vector,
        vector,
        matrix,
        vector,
        vector,
        vector,
        matrix,
        vector,
        matrix,
        vector,
        vector,
        vector,
    )
    return jax.shard_map(
        local,
        mesh=mesh,
        in_specs=(tokens, P(("rep", "shard")), tokens) + params + (tokens,),
        out_specs=(tokens, tokens) + params,
        check_vma=False,
    )
```

```python
from functools import partial

import jax
import jax.numpy as jnp
from jax import lax
from jax.experimental import pallas as pl
from jax.experimental.pallas import tpu as pltpu
from jax.sharding import PartitionSpec as P

D = 768
H = 12
DH = 64
FF = 3072
CLUSTER = 128
LEN = 1024
PAIRS = H // 2
SLICES = [slice(c * CLUSTER, (c + 1) * CLUSTER) for c in range(LEN // CLUSTER)]
bf = jnp.bfloat16
f32 = jnp.float32
eps_norm = 1e-12


def dot_nn(left, right):
    return lax.dot_general(left, right, (((1,), (0,)), ((), ())), preferred_element_type=f32)


def dot_nt(left, right):
    return lax.dot_general(left, right, (((1,), (1,)), ((), ())), preferred_element_type=f32)


def dot_tn(left, right):
    return lax.dot_general(left, right, (((0,), (0,)), ((), ())), preferred_element_type=f32)


def low_lanes():
    return lax.broadcasted_iota(jnp.int32, (LEN, CLUSTER), 1) < DH


def table_of(order_row):
    positions = lax.broadcasted_iota(jnp.int32, (LEN, LEN), 0)
    return jnp.where(jnp.broadcast_to(order_row, (LEN, LEN)) == positions, 1.0, 0.0).astype(bf)


def half_roll(source):
    return pltpu.roll(source.astype(f32), DH, 1).astype(bf)


def softmax_rows(scores):
    top = jnp.max(scores, axis=-1, keepdims=True)
    grown = jnp.exp(scores - top)
    return grown * (1.0 / jnp.sum(grown, axis=-1, keepdims=True))


def attention_forward_body(
    len_ref, x_ref, w_ref, b_ref, row_ref, att_ref, proj_ref, t0, t1, s0, s1, m0, m1
):
    count = len_ref[pl.program_id(0)]
    proj = (dot_nn(x_ref[...], w_ref[...]) + b_ref[0]).astype(bf)
    proj_ref[...] = proj
    low = low_lanes()
    tables, scores, mixed = (t0, t1), (s0, s1), (m0, m1)
    rows = [row_ref[0, 0, e : e + 1, :] for e in range(2)]
    for e in range(2):
        tables[e][...] = table_of(rows[e])
    picked = [
        dot_tn(tables[e][...], proj[:, 128 * e : 128 * e + 256]).astype(bf) for e in range(2)
    ]
    for e in range(2):
        qk = picked[e][:, 128 * e : 128 * e + 128]
        key_low = jnp.where(low, half_roll(qk), jnp.zeros((), bf))
        bias = jnp.where(rows[e] < count, 0.0, -30000.0)
        for sl in SLICES:
            scores[e][sl, :] = 0.125 * dot_nt(qk[sl], key_low[sl]) + bias[:, sl]
    for e in range(2):
        values = picked[e][:, 128 - 128 * e : 256 - 128 * e]
        for sl in SLICES:
            probs = softmax_rows(scores[e][sl, :]).astype(bf)
            mixed[e][sl, :] = dot_nn(probs, values[sl]).astype(bf)
    placed = [dot_nn(tables[e][...], mixed[e][...]) for e in range(2)]
    att_ref[...] = jnp.where(low, placed[0], placed[1]).astype(bf)


def attention_forward(lengths, rounded, weight, bias, rows):
    seqs = rows.shape[0]
    tokens = seqs * LEN
    return pl.pallas_call(
        attention_forward_body,
        grid_spec=pltpu.PrefetchScalarGridSpec(
            num_scalar_prefetch=1,
            grid=(seqs, PAIRS),
            in_specs=[
                pl.BlockSpec((LEN, D), lambda s, h, n: (s, 0)),
                pl.BlockSpec((D, 384), lambda s, h, n: (0, h)),
                pl.BlockSpec((1, 1, 384), lambda s, h, n: (h, 0, 0)),
                pl.BlockSpec((1, 1, 2, LEN), lambda s, h, n: (s, h, 0, 0)),
            ],
            out_specs=[
                pl.BlockSpec((LEN, 128), lambda s, h, n: (s, h)),
                pl.BlockSpec((LEN, 384), lambda s, h, n: (s, h)),
            ],
            scratch_shapes=[pltpu.VMEM((LEN, LEN), bf)] * 2
            + [pltpu.VMEM((LEN, 128), f32)] * 2
            + [pltpu.VMEM((LEN, 128), bf)] * 2,
        ),
        out_shape=[
            jax.ShapeDtypeStruct((tokens, D), bf),
            jax.ShapeDtypeStruct((tokens, 3 * D), bf),
        ],
        compiler_params=pltpu.CompilerParams(vmem_limit_bytes=50 << 20),
        cost_estimate=pl.CostEstimate(
            flops=44_000_000_000, bytes_accessed=24_000_000, transcendentals=0
        ),
        name="attention_forward",
    )(lengths, rounded, weight, bias, rows)


def attention_backward_body(
    len_ref,
    x_ref,
    proj_ref,
    datt_ref,
    row_ref,
    dproj_ref,
    dw_ref,
    db_ref,
    t0,
    t1,
    s0,
    s1,
    d0,
    d1,
    p0,
    p1,
    e0,
    e1,
    total,
):
    seq = pl.program_id(1)
    count = len_ref[seq]
    low = low_lanes()
    zero = jnp.zeros((), bf)
    tables, scores, back_probs, probs_low, backs = (t0, t1), (s0, s1), (d0, d1), (p0, p1), (e0, e1)
    rows = [row_ref[0, 0, e : e + 1, :] for e in range(2)]
    for e in range(2):
        tables[e][...] = table_of(rows[e])
    datt = datt_ref[...]
    swapped = half_roll(proj_ref[:, 128:256])
    middle = [jnp.where(low, datt, swapped), jnp.where(low, swapped, datt)]
    sources = [
        jnp.concatenate([proj_ref[:, 256 * e : 256 * e + 128], middle[e]], axis=1)
        for e in range(2)
    ]
    picked = [dot_tn(tables[e][...], sources[e]).astype(bf) for e in range(2)]
    for e in range(2):
        qk, dv = picked[e][:, 0:128], picked[e][:, 128:256]
        key_low = jnp.where(low, half_roll(qk), zero)
        turned = half_roll(dv)
        value_only = jnp.where(low, turned, zero) if e == 0 else jnp.where(low, zero, turned)
        bias = jnp.where(rows[e] < count, 0.0, -30000.0)
        for sl in SLICES:
            scores[e][sl, :] = 0.125 * dot_nt(qk[sl], key_low[sl]) + bias[:, sl]
            back_probs[e][sl, :] = dot_nt(dv[sl], value_only[sl])
    for e in range(2):
        for sl in SLICES:
            probs = softmax_rows(scores[e][sl, :])
            back = back_probs[e][sl, :]
            probs_low[e][sl, :] = probs.astype(bf)
            inner = jnp.sum(back * probs, axis=-1, keepdims=True)
            backs[e][sl, :] = (0.125 * (probs * (back - inner))).astype(bf)
    placed = []
    for e in range(2):
        qk, dv = picked[e][:, 0:128], picked[e][:, 128:256]
        queries, keys, values = [], [], []
        for sl in SLICES:
            back = backs[e][sl, :]
            queries.append(dot_nn(back, qk[sl]))
            keys.append(dot_tn(back, qk[sl]))
            values.append(dot_tn(probs_low[e][sl, :], dv[sl]))
        key_query = jnp.where(low, jnp.concatenate(keys, 0), jnp.concatenate(queries, 0))
        value = jnp.concatenate(values, 0)
        db_ref[0, 0, e : e + 1, :] = jnp.sum(key_query, axis=0, keepdims=True)
        db_ref[0, 0, 2 + e : 3 + e, :] = jnp.sum(value, axis=0, keepdims=True)
        parts = [half_roll(key_query), value.astype(bf)]
        placed.append(
            dot_nn(tables[e][...], jnp.concatenate(parts if e == 0 else parts[::-1], axis=1))
        )
    out = jnp.concatenate(
        [
            placed[0][:, 0:128],
            jnp.where(low, placed[0][:, 128:256], placed[1][:, 0:128]),
            placed[1][:, 128:256],
        ],
        axis=1,
    ).astype(bf)
    dproj_ref[...] = out
    part = dot_tn(x_ref[...], out)

    @pl.when(seq == 0)
    def _():
        total[...] = part

    @pl.when(seq != 0)
    def _():
        total[...] += part

    dw_ref[...] = total[...].astype(bf)


def attention_backward(lengths, rounded, proj, datt, rows):
    seqs = rows.shape[0]
    tokens = seqs * LEN
    return pl.pallas_call(
        attention_backward_body,
        grid_spec=pltpu.PrefetchScalarGridSpec(
            num_scalar_prefetch=1,
            grid=(PAIRS, seqs),
            in_specs=[
                pl.BlockSpec((LEN, D), lambda h, s, n: (s, 0)),
                pl.BlockSpec((LEN, 384), lambda h, s, n: (s, h)),
                pl.BlockSpec((LEN, 128), lambda h, s, n: (s, h)),
                pl.BlockSpec((1, 1, 2, LEN), lambda h, s, n: (s, h, 0, 0)),
            ],
            out_specs=[
                pl.BlockSpec((LEN, 384), lambda h, s, n: (s, h)),
                pl.BlockSpec((D, 384), lambda h, s, n: (0, h)),
                pl.BlockSpec((1, 1, 4, 128), lambda h, s, n: (s, h, 0, 0)),
            ],
            scratch_shapes=[pltpu.VMEM((LEN, LEN), bf)] * 2
            + [pltpu.VMEM((LEN, 128), f32)] * 4
            + [pltpu.VMEM((LEN, 128), bf)] * 4
            + [pltpu.VMEM((D, 384), f32)],
        ),
        out_shape=[
            jax.ShapeDtypeStruct((tokens, 3 * D), bf),
            jax.ShapeDtypeStruct((D, 3 * D), bf),
            jax.ShapeDtypeStruct((seqs, PAIRS, 4, 128), f32),
        ],
        compiler_params=pltpu.CompilerParams(vmem_limit_bytes=50 << 20),
        cost_estimate=pl.CostEstimate(
            flops=70_000_000_000, bytes_accessed=30_000_000, transcendentals=0
        ),
        name="attention_backward",
    )(lengths, rounded, proj, datt, rows)


def to_pairs(weight):
    parts = weight.reshape(weight.shape[:-1] + (3, PAIRS, 2, DH))
    query, key, value = parts[..., 0, :, :, :], parts[..., 1, :, :, :], parts[..., 2, :, :, :]
    a, b = 0, 1
    joined = jnp.concatenate(
        [
            query[..., a, :],
            key[..., a, :],
            value[..., a, :],
            value[..., b, :],
            query[..., b, :],
            key[..., b, :],
        ],
        axis=-1,
    )
    return joined.reshape(weight.shape)


def from_pairs(weight):
    parts = weight.reshape(weight.shape[:-1] + (PAIRS, 6, DH))
    query = jnp.stack([parts[..., 0, :], parts[..., 4, :]], axis=-2)
    key = jnp.stack([parts[..., 1, :], parts[..., 5, :]], axis=-2)
    value = jnp.stack([parts[..., 2, :], parts[..., 3, :]], axis=-2)
    lead = weight.shape[:-1]
    return jnp.concatenate([t.reshape(lead + (D,)) for t in (query, key, value)], axis=-1)


ROWS = 4
MESH=pl.DeviceIdType.MESH

def when(cond,do):
    if cond is None: do()
    else: pl.when(cond)(do)

class Place:
    def __init__(self,shards,reps):
        self.Y=shards//ROWS; self.S=shards; self.X=reps//2
        self.s=lax.axis_index("shard"); self.r=lax.axis_index("rep")
        self.z=self.s//self.Y; self.y=lax.rem(self.s,self.Y)
        self.core=lax.rem(self.r,2); self.x=self.r//2
    def near_z(self,step): return {"shard":self.s+step*self.Y}
    def other_y(self,k): return {"shard":self.z*self.Y+lax.rem(self.y+k,self.Y)}
    def other_core(self): return {"rep":self.r+1-2*self.core}
    def other_x(self,k): return {"rep":2*lax.rem(self.x+k,self.X)+self.core}

def meet(place,with_x):
    sem=pltpu.get_barrier_semaphore()
    def tell(dev): pl.semaphore_signal(sem,inc=1,device_id=dev,device_id_type=MESH)
    pl.when(place.z>0)(lambda: tell(place.near_z(-1)))
    pl.when(place.z<ROWS-1)(lambda: tell(place.near_z(1)))
    for k in range(1,place.Y): tell(place.other_y(k))
    tell(place.other_core())
    if with_x:
        for k in range(1,place.X): tell(place.other_x(k))
    others=place.Y+(place.X-1 if with_x else 0)
    inner=jnp.logical_and(place.z>0,place.z<ROWS-1)
    pl.when(inner)(lambda: pl.semaphore_wait(sem,others+2))
    pl.when(jnp.logical_not(inner))(lambda: pl.semaphore_wait(sem,others+1))

def gather_semaphores(count,shards):
    Y=shards//ROWS
    return [pltpu.SemaphoreType.DMA((count,2,ROWS)),pltpu.SemaphoreType.DMA((count,2,ROWS)),
            pltpu.SemaphoreType.DMA((count,ROWS,Y)),pltpu.SemaphoreType.DMA((count,ROWS,Y)),
            pltpu.SemaphoreType.DMA((count,shards)),pltpu.SemaphoreType.DMA((count,shards)),
            pltpu.SemaphoreType.DMA((count,))]

class Gather:
    def __init__(self,place,ins,outs,sems):
        self.p=place; self.ins=ins; self.outs=outs
        self.line_s,self.line_r,self.y_s,self.y_r,self.core_s,self.core_r,self.own=sems
        self.sent=[]
    def half(self,ref,shard=None):
        n=ref.shape[-1]//2
        cols=pl.ds(pl.multiple_of(self.p.core*n,128),n)
        return ref.at[:,cols] if shard is None else ref.at[shard,:,cols]
    def other_half(self,ref,shard):
        n=ref.shape[-1]//2
        return ref.at[shard,:,pl.ds(pl.multiple_of((1-self.p.core)*n,128),n)]
    def send(self,cond,desc):
        when(cond,desc.start); self.sent.append((cond,desc))
    def copy(self,src,dst,ss,rs,dev):
        return pltpu.make_async_remote_copy(src_ref=src,dst_ref=dst,send_sem=ss,recv_sem=rs,device_id=dev,device_id_type=MESH)
    def pass_on(self,cond,zz,own,direction):
        p=self.p; shard=zz*p.Y+p.y
        for a,(i,o) in enumerate(zip(self.ins,self.outs)):
            src=self.half(i) if own else self.half(o,shard); dst=self.half(o,shard)
            for d in direction:
                edge=(p.z<ROWS-1) if d==0 else (p.z>0)
                c=edge if cond is None else jnp.logical_and(cond,edge)
                self.send(c,self.copy(src,dst,self.line_s.at[a,d,zz],self.line_r.at[a,d,zz],p.near_z(1 if d==0 else -1)))
            for k in range(1,p.Y):
                self.send(cond,self.copy(src,dst,self.y_s.at[a,zz,k],self.y_r.at[a,zz,k],p.other_y(k)))
            if not own:
                self.send(cond,self.copy(src,dst,self.core_s.at[a,shard],self.core_r.at[a,shard],p.other_core()))
    def begin(self):
        for a,(i,o) in enumerate(zip(self.ins,self.outs)):
            pltpu.make_async_copy(i,o.at[self.p.s],self.own.at[a]).start()
        self.pass_on(None,self.p.z,True,(0,1))
    def wave(self,w):
        p=self.p
        for d in (0,1):
            zz=p.z-w if d==0 else p.z+w
            cond=p.z>=w if d==0 else p.z+w<ROWS
            for a,o in enumerate(self.outs):
                ref=self.half(o,jnp.clip(zz,0,ROWS-1)*p.Y+p.y);
                desc=self.copy(ref,ref,self.line_s.at[a,d,jnp.clip(zz,0,ROWS-1)],self.line_r.at[a,d,jnp.clip(zz,0,ROWS-1)],p.near_z(0))
                when(cond,desc.wait_recv)
            self.pass_on(cond,jnp.clip(zz,0,ROWS-1),False,(d,))
    def across(self,w):
        p=self.p
        for zz,cond in (((p.z,None),) if w==0 else ((p.z-w,p.z>=w),(p.z+w,p.z+w<ROWS))):
            zz=jnp.clip(zz,0,ROWS-1)
            for k in range(1,p.Y):
                shard=zz*p.Y+lax.rem(p.y-k+p.Y,p.Y)
                for a,o in enumerate(self.outs):
                    ref=self.half(o,shard)
                    desc=self.copy(ref,ref,self.y_s.at[a,zz,k],self.y_r.at[a,zz,k],p.other_y(k))
                    when(cond,desc.wait_recv)
                    self.send(cond,self.copy(ref,ref,self.core_s.at[a,shard],self.core_r.at[a,shard],p.other_core()))
    def finish(self):
        p=self.p
        for a,(i,o) in enumerate(zip(self.ins,self.outs)):
            for k in range(1,p.S):
                shard=lax.rem(p.s+k,p.S)
                ref=self.other_half(o,shard)
                self.copy(ref,ref,self.core_s.at[a,shard],self.core_r.at[a,shard],p.other_core()).wait_recv()
            pltpu.make_async_copy(i,o.at[p.s],self.own.at[a]).wait()
        for cond,desc in self.sent: when(cond,desc.wait_send)
    def steps(self):
        return [self.begin,lambda: self.wave(1),lambda: self.across(0),lambda: self.wave(2),lambda: self.across(1),lambda: self.wave(3),lambda: self.across(2),lambda: self.across(3),self.finish]

def gather_body(shards,reps,count,*refs):
    ins,outs,sems=refs[:count],refs[count:2*count],refs[2*count:]
    place=Place(shards,reps)
    meet(place,False)
    for step in Gather(place,ins,outs,sems).steps(): step()

def gather_now(arrays,shards,reps,collective_id):
    count=len(arrays)
    return pl.pallas_call(partial(gather_body,shards,reps,count),
        in_specs=[pl.BlockSpec(memory_space=pltpu.VMEM)]*count,
        out_specs=[pl.BlockSpec(memory_space=pl.ANY)]*count,
        out_shape=[jax.ShapeDtypeStruct((shards,)+a.shape,a.dtype) for a in arrays],
        scratch_shapes=gather_semaphores(count,shards),
        compiler_params=pltpu.CompilerParams(collective_id=collective_id,has_side_effects=True,vmem_limit_bytes=16<<20),
        name="gather_weights")(*arrays)

ORDER=(3,0,2,1)
def reduce_scratch(shapes,shards,reps,store=True):
    S=shards; Y=S//ROWS; X=reps//2; A=len(shapes)
    out=[]
    for r,c in shapes:
        n=c//2
        out+=[pltpu.VMEM((S,r,n),bf),pltpu.VMEM((S,r,n),bf),pltpu.VMEM((max(Y-1,1),ROWS,r,n),bf),
              pltpu.VMEM((2,ROWS,r,n),bf),pltpu.VMEM((X,r,n),bf)]
    dma=pltpu.SemaphoreType.DMA
    return out+[dma((A,S)),dma((A,S)),dma((A,S)),dma((A,Y,ROWS)),dma((A,Y,ROWS)),dma((A,2,ROWS)),dma((A,2,ROWS)),dma((A,X)),dma((A,X)),dma((A,)),dma((A,))]
class Reduce:
    def __init__(self,place,ins,outs,scratch):
        self.p=place; self.ins=ins; self.outs=outs; A=len(ins); self.A=range(A)
        self.bufs=[scratch[5*a:5*a+5] for a in range(A)]
        (self.own,self.core_s,self.core_r,self.y_s,self.y_r,self.line_s,self.line_r,self.x_s,self.x_r,self.end_s,self.end_r)=scratch[5*A:]
        self.sent=[]
    def copy(self,src,dst,ss,rs,dev):
        return pltpu.make_async_remote_copy(src_ref=src,dst_ref=dst,send_sem=ss,recv_sem=rs,device_id=dev,device_id_type=MESH)
    def send(self,cond,desc):
        when(cond,desc.start); self.sent.append((cond,desc))
    def half(self,a,shard,core):
        n=self.ins[a].shape[-1]//2
        return self.ins[a].at[shard,:,pl.ds(pl.multiple_of(core*n,128),n)]
    def add(self,dst,others):
        rows=dst.shape[0]; step=48 if rows%48==0 else 16
        def body(i,_):
            at=pl.ds(pl.multiple_of(i*step,16),step)
            value=dst[at,:].astype(f32)
            for o in others: value=value+o[at,:].astype(f32)
            dst[at,:]=value.astype(bf)
            return 0
        lax.fori_loop(0,rows//step,body,0)
    def begin(self):
        p=self.p
        for k in list(range(1,p.Y))+[0]:
            for d in ORDER:
                shard=d*p.Y+lax.rem(p.y+k,p.Y)
                for a in self.A:
                    H,Rc=self.bufs[a][0:2]
                    self.send(None,self.copy(self.half(a,shard,1-p.core),Rc.at[shard],self.core_s.at[a,shard],self.core_r.at[a,shard],p.other_core()))
                    pltpu.make_async_copy(self.half(a,shard,p.core),H.at[shard],self.own.at[a,shard]).start()
    def join_core(self,shard):
        p=self.p
        for a in self.A:
            H,Rc=self.bufs[a][0:2]
            pltpu.make_async_copy(self.half(a,shard,p.core),H.at[shard],self.own.at[a,shard]).wait()
            self.copy(Rc.at[shard],Rc.at[shard],self.core_s.at[a,shard],self.core_r.at[a,shard],p.other_core()).wait_recv()
            self.add(H.at[shard],[Rc.at[shard]])
    def to_y(self,d):
        p=self.p
        for k in range(1,p.Y):
            shard=d*p.Y+lax.rem(p.y+k,p.Y)
            self.join_core(shard)
            for a in self.A:
                H,_,Ry=self.bufs[a][0:3]
                self.send(None,self.copy(H.at[shard],Ry.at[k-1,d],self.y_s.at[a,k,d],self.y_r.at[a,k,d],p.other_y(k)))
    def own_y(self,d):
        self.join_core(d*self.p.Y+self.p.y)
    def line(self,d):
        p=self.p; shard=d*p.Y+p.y
        for a in self.A:
            H,_,Ry,Rl=self.bufs[a][0:4]
            for k in range(1,p.Y):
                self.copy(Ry.at[k-1,d],Ry.at[k-1,d],self.y_s.at[a,k,d],self.y_r.at[a,k,d],p.other_y(k)).wait_recv()
            self.add(H.at[shard],[Ry.at[k-1,d] for k in range(1,p.Y)])
        for up in (0,1):
            passes=(p.z<d) if up==0 else (p.z>d)
            inner=(p.z>0) if up==0 else (p.z<ROWS-1)
            def add_in(up=up):
                for a in self.A:
                    H,Rl=self.bufs[a][0],self.bufs[a][3]
                    self.copy(Rl.at[up,d],Rl.at[up,d],self.line_s.at[a,up,d],self.line_r.at[a,up,d],p.near_z(0)).wait_recv()
                    self.add(H.at[shard],[Rl.at[up,d]])
            pl.when(jnp.logical_and(passes,inner))(add_in)
            for a in self.A:
                H,Rl=self.bufs[a][0],self.bufs[a][3]
                self.send(passes,self.copy(H.at[shard],Rl.at[up,d],self.line_s.at[a,up,d],self.line_r.at[a,up,d],p.near_z(1 if up==0 else -1)))
    def to_x(self):
        p=self.p
        for up in (0,1):
            def add_in(up=up):
                for a in self.A:
                    H,Rl=self.bufs[a][0],self.bufs[a][3]
                    self.copy(Rl.at[up,p.z],Rl.at[up,p.z],self.line_s.at[a,up,p.z],self.line_r.at[a,up,p.z],p.near_z(0)).wait_recv()
                    self.add(H.at[p.s],[Rl.at[up,p.z]])
            pl.when((p.z>0) if up==0 else (p.z<ROWS-1))(add_in)
        for a in self.A:
            H,Rx=self.bufs[a][0],self.bufs[a][4]
            for k in range(1,p.X):
                self.send(None,self.copy(H.at[p.s],Rx.at[p.x],self.x_s.at[a,k],self.x_r.at[a,p.x],p.other_x(k)))
    def to_core(self):
        p=self.p
        for a in self.A:
            H,Rx=self.bufs[a][0],self.bufs[a][4]; out=self.outs[a]
            for k in range(1,p.X):
                src=lax.rem(p.x-k+p.X,p.X)
                self.copy(Rx.at[src],Rx.at[src],self.x_s.at[a,k],self.x_r.at[a,src],p.other_x(k)).wait_recv()
            rows=H.shape[1]; step=48 if rows%48==0 else 16
            def body(i,_):
                at=pl.ds(pl.multiple_of(i*step,16),step)
                own=H[p.s,at,:].astype(f32)
                value=jnp.zeros_like(own)
                for q in range(p.X):
                    value=value+jnp.where(p.x==q,own,Rx[q,at,:].astype(f32))
                out[p.core,at,:]=value
                return 0
            lax.fori_loop(0,rows//step,body,0)
        for a in self.A:
            out=self.outs[a]
            self.send(None,self.copy(out.at[p.core],out.at[p.core],self.end_s.at[a],self.end_r.at[a],p.other_core()))
    def finish(self):
        p=self.p
        for a in self.A:
            ref=self.outs[a].at[1-p.core]
            self.copy(ref,ref,self.end_s.at[a],self.end_r.at[a],p.other_core()).wait_recv()
        for cond,desc in self.sent: when(cond,desc.wait_send)
    def steps(self):
        part=lambda f,d: (lambda: f(d))
        return [self.begin]+[part(self.to_y,d) for d in ORDER]+[part(self.own_y,d) for d in ORDER]+[part(self.line,d) for d in ORDER]+[self.to_x,self.to_core,self.finish]
def reduce_body(shards,reps,count,*refs):
    ins,outs,scratch=refs[:count],refs[count:2*count],refs[2*count:]
    place=Place(shards,reps)
    meet(place,True)
    for step in Reduce(place,ins,outs,scratch).steps(): step()
def reduce_now(arrays,shards,reps,collective_id):
    count=len(arrays)
    return pl.pallas_call(partial(reduce_body,shards,reps,count),
        in_specs=[pl.BlockSpec(memory_space=pl.ANY)]*count,
        out_specs=[pl.BlockSpec(memory_space=pltpu.VMEM)]*count,
        out_shape=[jax.ShapeDtypeStruct((2,a.shape[1],a.shape[2]//2),f32) for a in arrays],
        scratch_shapes=reduce_scratch([a.shape[1:] for a in arrays],shards,reps),
        compiler_params=pltpu.CompilerParams(collective_id=collective_id,has_side_effects=True,vmem_limit_bytes=50<<20),
        name="reduce_grads")(*arrays)


def norm_stats(x):
    c=jnp.mean(x,axis=-1,keepdims=True)
    xc=x-c
    r=lax.rsqrt(jnp.mean(xc*xc,axis=-1,keepdims=True)+eps_norm)
    return xc*r,r

def norm_back(up,normed,r,gain):
    g=up*gain
    return r*(g-jnp.mean(g,axis=-1,keepdims=True)-normed*jnp.mean(g*normed,axis=-1,keepdims=True))

def colsum(x): return jnp.sum(x,axis=0,keepdims=True)

def gelu_parts(u):
    cdf=0.5+0.5*lax.erf(u*0.7071067811865476)
    pdf=jnp.exp(-0.5*u*u)*0.3989422804014327
    return u*cdf,cdf+u*pdf

def middle_body(len_ref,h_ref,a_ref,ct_ref,ow_ref,uw_ref,dw_ref,vec_ref,ub_ref,
               out_ref,bs_ref,ba_ref,act,pl_,low_ref,d2_ref,sl_ref,small_ref,ubg_ref,
               gp,n1_ref,*,T,sub_rows,chunk):
    i=pl.program_id(0)
    per=LEN//T
    count=len_ref[i//per]
    @pl.when(i==0)
    def _():
        small_ref[...]=jnp.zeros_like(small_ref); ubg_ref[...]=jnp.zeros_like(ubg_ref)
    out_b,g1,b1,down_b,g2,b2=[vec_ref[j:j+1,:] for j in range(6)]
    parts=[slice(k,k+sub_rows) for k in range(0,T,sub_rows)]
    r1s=[];sums=[]
    xs=[dot_nn(a_ref[p,:],ow_ref[...]) for p in parts]
    for p,x in zip(parts,xs):
        n1,r1=norm_stats(h_ref[p,:]+x+out_b)
        n1_ref[p,:]=n1; r1s.append(r1)
        low_ref[p,:]=(n1*g1+b1).astype(bf)
    for j in range(0,FF,chunk):
        sl=slice(j,j+chunk)
        for p in parts:
            u=dot_nn(low_ref[p,:],uw_ref[:,sl])+ub_ref[:,sl]
            a,g=gelu_parts(u)
            act[p,sl]=a.astype(bf); gp[p,sl]=g.astype(gp.dtype)
    ys=[dot_nn(act[p,:],dw_ref[...]) for p in parts]
    for p,y in zip(parts,ys):
        pos=lax.broadcasted_iota(jnp.int32,(sub_rows,1),0)+(i%per)*T+p.start
        valid=jnp.where(pos<count,1.0,0.0)
        second=n1_ref[p,:]*g1+b1+y+down_b
        n2,r2=norm_stats(second)
        out_ref[p,:]=valid*(n2*g2+b2)
        up=valid*ct_ref[p,:]
        b2nd=norm_back(up,n2,r2,g2)
        d2_ref[p,:]=b2nd.astype(bf)
        bs_ref[p,:]=b2nd
        sums.append(jnp.concatenate([colsum(b2nd),colsum(up*n2),colsum(up)],axis=0))
    small_ref[3:6,:]+=sum(sums[1:],sums[0])
    for j in range(0,FF,chunk):
        sl=slice(j,j+chunk)
        cs=[]
        for p in parts:
            bp=dot_nt(d2_ref[p,:],dw_ref[sl,:])*gp[p,sl].astype(f32)
            cs.append(colsum(bp))
            pl_[p,sl]=bp.astype(bf)
        ubg_ref[:,sl]+=sum(cs[1:],cs[0])
    zs=[dot_nt(pl_[p,:],uw_ref[...]) for p in parts]
    sums=[]
    for p,z,r1 in zip(parts,zs,r1s):
        bfirst=z+bs_ref[p,:]
        n1=n1_ref[p,:]
        bsum=norm_back(bfirst,n1,r1,g1)
        bs_ref[p,:]=bsum
        sl_ref[p,:]=bsum.astype(bf)
        sums.append(jnp.concatenate([colsum(bsum),colsum(bfirst*n1),colsum(bfirst)],axis=0))
    small_ref[0:3,:]+=sum(sums[1:],sums[0])
    for p in parts:
        ba_ref[p,:]=dot_nt(sl_ref[p,:],ow_ref[...]).astype(bf)

def middle(lengths,hidden,att,ct,ow,uw,dw,vec,ub,T=512,chunk=768,gpt=f32,sub_rows=256):
    tokens=hidden.shape[0]
    tile=lambda n=D: pl.BlockSpec((T,n),lambda i,l:(i,0))
    const=lambda shape: pl.BlockSpec(shape,lambda i,l:(0,0),pipeline_mode=pl.Buffered(1))
    whole=lambda shape: pl.BlockSpec(shape,lambda i,l:(0,0))
    sd=lambda n,dt: jax.ShapeDtypeStruct((tokens,n),dt)
    return pl.pallas_call(
        partial(middle_body,T=T,chunk=chunk,sub_rows=sub_rows),
        grid_spec=pltpu.PrefetchScalarGridSpec(num_scalar_prefetch=1,grid=(tokens//T,),
          in_specs=[tile(),tile(),tile(),const((D,D)),const((D,FF)),const((FF,D)),whole((8,D)),whole((1,FF))],
          out_specs=[tile(),tile(),tile(),tile(FF),tile(FF),tile(),tile(),tile(),whole((8,D)),whole((1,FF))],
          scratch_shapes=[pltpu.VMEM((T,FF),gpt),pltpu.VMEM((T,D),f32)]),
        out_shape=[sd(D,f32),sd(D,f32),sd(D,bf),sd(FF,bf),sd(FF,bf),sd(D,bf),sd(D,bf),sd(D,bf),jax.ShapeDtypeStruct((8,D),f32),jax.ShapeDtypeStruct((1,FF),f32)],
        compiler_params=pltpu.CompilerParams(vmem_limit_bytes=63<<20),
        name="middle")(lengths,hidden,att,ct,ow,uw,dw,vec,ub)


def weight_grad_body(l_ref,r_ref,out_ref):
    out_ref[...]=dot_tn(l_ref[...],r_ref[...]).astype(bf)
def weight_grad(left,right,block,name,columns=False):
    K,M=left.shape; N=right.shape[1]
    if columns:
        grid,lb,rb,ob,li,ri,oi=(N//block,),(K,M),(K,block),(M,block),(lambda i:(0,0)),(lambda i:(0,i)),(lambda i:(0,i))
    else:
        grid,lb,rb,ob,li,ri,oi=(M//block,),(K,block),(K,N),(block,N),(lambda i:(0,i)),(lambda i:(0,0)),(lambda i:(i,0))
    return pl.pallas_call(weight_grad_body,grid=grid,
        in_specs=[pl.BlockSpec(lb,li),pl.BlockSpec(rb,ri)],out_specs=pl.BlockSpec(ob,oi),
        out_shape=jax.ShapeDtypeStruct((M,N),bf),
        cost_estimate=pl.CostEstimate(flops=2*K*M*N,bytes_accessed=2*(K*M+K*N+M*N),transcendentals=0),
        compiler_params=pltpu.CompilerParams(vmem_limit_bytes=60<<20),name=name)(left,right)


WIDE = 4096


def shard_vectors(vectors):
    row = jnp.concatenate(vectors)
    return jnp.pad(row, (0, WIDE - row.shape[0])).reshape(16, 256)


def local(
    hidden,
    lengths,
    clusters,
    input_weight,
    query_bias,
    value_bias,
    out_weight,
    out_bias,
    norm1_gain,
    norm1_bias,
    up_weight,
    up_bias,
    down_weight,
    down_bias,
    norm2_gain,
    norm2_bias,
    cotangent,
    *,
    shards,
    reps,
):
    seqs = hidden.shape[0]
    tokens = seqs * LEN
    part = D // shards
    vectors = shard_vectors(
        (
            query_bias,
            value_bias,
            out_bias,
            norm1_gain,
            norm1_bias,
            down_bias,
            norm2_gain,
            norm2_bias,
            up_bias,
        )
    )
    in_w, vectors = gather_now((to_pairs(input_weight), vectors), shards, reps, 1)
    out_w, up_w, down_w = gather_now((out_weight, up_weight, down_weight), shards, reps, 2)
    in_w, out_w, up_w, down_w = [w.reshape(-1, w.shape[-1]) for w in (in_w, out_w, up_w, down_w)]
    vectors = vectors.reshape(shards, WIDE).astype(f32)
    table = vectors[:, : 8 * part].reshape(shards, 8, part).transpose(1, 0, 2).reshape(8, D)
    bias_pairs = to_pairs(
        jnp.concatenate([table[0], jnp.zeros((D,), f32), table[1]])
    ).reshape(PAIRS, 1, 384)
    norm_rows = jnp.concatenate([table[2:], table[:2]])
    up_b = vectors[:, 8 * part : 8 * part + FF // shards].reshape(1, FF)

    flat = hidden.reshape(tokens, D)
    rounded = flat.astype(bf)
    rows = clusters.reshape(seqs, PAIRS, 2, LEN)
    attended, proj = attention_forward(lengths, rounded, in_w, bias_pairs, rows)
    (
        result,
        back_sum,
        back_attended,
        activated,
        pre_low,
        first_low,
        second_low,
        sum_low,
        norm_sums,
        up_b_sum,
    ) = middle(
        lengths,
        flat,
        attended,
        cotangent.reshape(tokens, D),
        out_w,
        up_w,
        down_w,
        norm_rows,
        up_b,
    )
    down_g = weight_grad(activated, second_low, D, "down_weight_grad")
    up_g = weight_grad(first_low, pre_low, D, "up_weight_grad", True)
    out_g = weight_grad(attended, sum_low, D // 2, "out_weight_grad")
    dproj, in_g, bias_sums = attention_backward(lengths, rounded, proj, back_attended, rows)
    down_s, up_s, out_s = reduce_now(
        [g.reshape(shards, -1, g.shape[-1]) for g in (down_g, up_g, out_g)], shards, reps, 3
    )
    bias_sums = jnp.sum(bias_sums, axis=0)
    query_sum = bias_sums[:, 0:2, DH:].reshape(D)
    value_sum = jnp.concatenate([bias_sums[:, 2, :DH], bias_sums[:, 3, DH:]], axis=1).reshape(D)
    table = jnp.concatenate([query_sum[None], value_sum[None], norm_sums[:6]])
    small = jnp.concatenate(
        [
            table.reshape(8, shards, part).transpose(1, 0, 2).reshape(shards, 8 * part),
            up_b_sum.reshape(shards, FF // shards),
        ],
        axis=1,
    ).astype(bf)
    small = jnp.pad(small, ((0, 0), (0, WIDE - small.shape[1]))).reshape(shards, 16, 256)
    in_s, small_s = reduce_now(
        [in_g.reshape(shards, part, 3 * D), small], shards, reps, 4
    )
    back_input = (back_sum + dot_nt(dproj, in_w)).reshape(seqs, LEN, D)

    def whole(halves):
        return jnp.concatenate([halves[0], halves[1]], axis=1)

    small_s = whole(small_s).reshape(WIDE)
    vec = [small_s[i * part : (i + 1) * part] for i in range(8)]
    return (
        result.reshape(seqs, LEN, D),
        back_input,
        from_pairs(whole(in_s)),
        vec[0],
        vec[1],
        whole(out_s),
        vec[2],
        vec[3],
        vec[4],
        whole(up_s),
        small_s[8 * part : 8 * part + FF // shards],
        whole(down_s),
        vec[5],
        vec[6],
        vec[7],
    )


def solution(mesh):
    tokens = P(("rep", "shard"), None, None)
    matrix, vector = P("shard", None), P("shard")
    params = (
        matrix,
        vector,
        vector,
        matrix,
        vector,
        vector,
        vector,
        matrix,
        vector,
        matrix,
        vector,
        vector,
        vector,
    )
    return jax.shard_map(
        partial(local, shards=mesh.shape["shard"], reps=mesh.shape["rep"]),
        mesh=mesh,
        in_specs=(tokens, P(("rep", "shard")), tokens) + params + (tokens,),
        out_specs=(tokens, tokens) + params,
        check_vma=False,
    )
```

```python
from functools import partial

import jax
import jax.numpy as jnp
from jax import lax
from jax.experimental import pallas as pl
from jax.experimental.pallas import tpu as pltpu
from jax.sharding import PartitionSpec as P

D = 768
H = 12
DH = 64
FF = 3072
CLUSTER = 128
LEN = 1024
PAIRS = H // 2
SLICES = [slice(c * CLUSTER, (c + 1) * CLUSTER) for c in range(LEN // CLUSTER)]
bf = jnp.bfloat16
f32 = jnp.float32
eps_norm = 1e-12


def dot_nn(left, right):
    return lax.dot_general(left, right, (((1,), (0,)), ((), ())), preferred_element_type=f32)


def dot_nt(left, right):
    return lax.dot_general(left, right, (((1,), (1,)), ((), ())), preferred_element_type=f32)


def dot_tn(left, right):
    return lax.dot_general(left, right, (((0,), (0,)), ((), ())), preferred_element_type=f32)


ROWS = 4
MESH=pl.DeviceIdType.MESH

def when(cond,do):
    if cond is None: do()
    else: pl.when(cond)(do)

class Place:
    def __init__(self,shards,reps):
        self.Y=shards//ROWS; self.S=shards; self.X=reps//2
        self.s=lax.axis_index("shard"); self.r=lax.axis_index("rep")
        self.z=self.s//self.Y; self.y=lax.rem(self.s,self.Y)
        self.core=lax.rem(self.r,2); self.x=self.r//2
    def near_z(self,step): return {"shard":self.s+step*self.Y}
    def other_y(self,k): return {"shard":self.z*self.Y+lax.rem(self.y+k,self.Y)}
    def other_core(self): return {"rep":self.r+1-2*self.core}
    def other_x(self,k): return {"rep":2*lax.rem(self.x+k,self.X)+self.core}

def meet(place,with_x):
    sem=pltpu.get_barrier_semaphore()
    def tell(dev): pl.semaphore_signal(sem,inc=1,device_id=dev,device_id_type=MESH)
    pl.when(place.z>0)(lambda: tell(place.near_z(-1)))
    pl.when(place.z<ROWS-1)(lambda: tell(place.near_z(1)))
    for k in range(1,place.Y): tell(place.other_y(k))
    tell(place.other_core())
    if with_x:
        for k in range(1,place.X): tell(place.other_x(k))
    others=place.Y+(place.X-1 if with_x else 0)
    inner=jnp.logical_and(place.z>0,place.z<ROWS-1)
    pl.when(inner)(lambda: pl.semaphore_wait(sem,others+2))
    pl.when(jnp.logical_not(inner))(lambda: pl.semaphore_wait(sem,others+1))

def gather_semaphores(count,shards):
    Y=shards//ROWS
    return [pltpu.SemaphoreType.DMA((count,2,ROWS)),pltpu.SemaphoreType.DMA((count,2,ROWS)),
            pltpu.SemaphoreType.DMA((count,ROWS,Y)),pltpu.SemaphoreType.DMA((count,ROWS,Y)),
            pltpu.SemaphoreType.DMA((count,shards)),pltpu.SemaphoreType.DMA((count,shards)),
            pltpu.SemaphoreType.DMA((count,))]

class Gather:
    def __init__(self,place,ins,outs,sems):
        self.p=place; self.ins=ins; self.outs=outs
        self.line_s,self.line_r,self.y_s,self.y_r,self.core_s,self.core_r,self.own=sems
        self.sent=[]
    def half(self,ref,shard=None):
        n=ref.shape[-1]//2
        cols=pl.ds(pl.multiple_of(self.p.core*n,128),n)
        return ref.at[:,cols] if shard is None else ref.at[shard,:,cols]
    def other_half(self,ref,shard):
        n=ref.shape[-1]//2
        return ref.at[shard,:,pl.ds(pl.multiple_of((1-self.p.core)*n,128),n)]
    def send(self,make):
        cond,desc=make()
        when(cond,desc.start); self.sent.append(make)
    def copy(self,src,dst,ss,rs,dev):
        return pltpu.make_async_remote_copy(src_ref=src,dst_ref=dst,send_sem=ss,recv_sem=rs,device_id=dev,device_id_type=MESH)
    def at(self,places):
        zz=self.p.z+places
        if places==0: return None,zz
        return jnp.logical_and(zz>=0,zz<ROWS),jnp.clip(zz,0,ROWS-1)
    def to_line(self,a,places,d):
        p=self.p; i,o=self.ins[a],self.outs[a]
        def make():
            cond,zz=self.at(places); shard=zz*p.Y+p.y
            edge=(p.z<ROWS-1) if d==0 else (p.z>0)
            src=self.half(i) if places==0 else self.half(o,shard)
            return (edge if cond is None else jnp.logical_and(cond,edge)),self.copy(src,self.half(o,shard),self.line_s.at[a,d,zz],self.line_r.at[a,d,zz],p.near_z(1 if d==0 else -1))
        self.send(make)
    def to_y(self,a,places,k):
        p=self.p; i,o=self.ins[a],self.outs[a]
        def make():
            cond,zz=self.at(places); shard=zz*p.Y+p.y
            src=self.half(i) if places==0 else self.half(o,shard)
            return cond,self.copy(src,self.half(o,shard),self.y_s.at[a,zz,k],self.y_r.at[a,zz,k],p.other_y(k))
        self.send(make)
    def to_core(self,a,places,k):
        p=self.p; o=self.outs[a]
        def make():
            cond,zz=self.at(places); shard=zz*p.Y+lax.rem(p.y-k+p.Y,p.Y)
            ref=self.half(o,shard)
            return cond,self.copy(ref,ref,self.core_s.at[a,shard],self.core_r.at[a,shard],p.other_core())
        self.send(make)
    def begin(self):
        for a,(i,o) in enumerate(zip(self.ins,self.outs)):
            for d in (0,1): self.to_line(a,0,d)
            for k in range(1,self.p.Y): self.to_y(a,0,k)
            pltpu.make_async_copy(i,o.at[self.p.s],self.own.at[a]).start()
    def wave(self,w):
        p=self.p
        for d in (0,1):
            places=-w if d==0 else w
            for a,o in enumerate(self.outs):
                cond,zz=self.at(places); ref=self.half(o,zz*p.Y+p.y)
                when(cond,self.copy(ref,ref,self.line_s.at[a,d,zz],self.line_r.at[a,d,zz],p.near_z(0)).wait_recv)
                self.to_line(a,places,d)
                for k in range(1,p.Y): self.to_y(a,places,k)
                self.to_core(a,places,0)
    def across(self,w):
        p=self.p
        for places in ((0,) if w==0 else (-w,w)):
            for k in range(1,p.Y):
                for a,o in enumerate(self.outs):
                    cond,zz=self.at(places); shard=zz*p.Y+lax.rem(p.y-k+p.Y,p.Y)
                    ref=self.half(o,shard)
                    when(cond,self.copy(ref,ref,self.y_s.at[a,zz,k],self.y_r.at[a,zz,k],p.other_y(k)).wait_recv)
                    self.to_core(a,places,k)
    def finish(self):
        p=self.p
        for a,(i,o) in enumerate(zip(self.ins,self.outs)):
            for k in range(1,p.S):
                shard=lax.rem(p.s+k,p.S)
                ref=self.other_half(o,shard)
                self.copy(ref,ref,self.core_s.at[a,shard],self.core_r.at[a,shard],p.other_core()).wait_recv()
            pltpu.make_async_copy(i,o.at[p.s],self.own.at[a]).wait()
        for make in self.sent:
            cond,desc=make()
            when(cond,desc.wait_send)
    def steps(self):
        return [self.begin,lambda: self.wave(1),lambda: self.across(0),lambda: self.wave(2),lambda: self.across(1),lambda: self.wave(3),lambda: self.across(2),lambda: self.across(3),self.finish]

def gather_body(shards,reps,count,*refs):
    ins,outs,sems=refs[:count],refs[count:2*count],refs[2*count:]
    place=Place(shards,reps)
    meet(place,False)
    for step in Gather(place,ins,outs,sems).steps(): step()

def gather_now(arrays,shards,reps,collective_id):
    count=len(arrays)
    return pl.pallas_call(partial(gather_body,shards,reps,count),
        in_specs=[pl.BlockSpec(memory_space=pltpu.VMEM)]*count,
        out_specs=[pl.BlockSpec(memory_space=pl.ANY)]*count,
        out_shape=[jax.ShapeDtypeStruct((shards,)+a.shape,a.dtype) for a in arrays],
        scratch_shapes=gather_semaphores(count,shards),
        compiler_params=pltpu.CompilerParams(collective_id=collective_id,has_side_effects=True,vmem_limit_bytes=16<<20),
        name="gather_weights")(*arrays)

ORDER=(3,0,2,1)
def reduce_scratch(shapes,shards,reps,store=True):
    S=shards; Y=S//ROWS; X=reps//2; A=len(shapes)
    out=[]
    for r,c in shapes:
        n=c//2
        out+=[pltpu.VMEM((S,r,n),bf),pltpu.VMEM((S,r,n),bf),pltpu.VMEM((max(Y-1,1),ROWS,r,n),bf),
              pltpu.VMEM((2,ROWS,r,n),bf),pltpu.VMEM((X,r,n),bf)]
    dma=pltpu.SemaphoreType.DMA
    return out+[dma((A,S)),dma((A,S)),dma((A,S)),dma((A,Y,ROWS)),dma((A,Y,ROWS)),dma((A,2,ROWS)),dma((A,2,ROWS)),dma((A,X)),dma((A,X)),dma((A,)),dma((A,))]
class Reduce:
    def __init__(self,place,ins,outs,scratch):
        self.p=place; self.ins=ins; self.outs=outs; A=len(ins); self.A=range(A)
        self.bufs=[scratch[5*a:5*a+5] for a in range(A)]
        (self.own,self.core_s,self.core_r,self.y_s,self.y_r,self.line_s,self.line_r,self.x_s,self.x_r,self.end_s,self.end_r)=scratch[5*A:]
        self.sent=[]
    def copy(self,src,dst,ss,rs,dev):
        return pltpu.make_async_remote_copy(src_ref=src,dst_ref=dst,send_sem=ss,recv_sem=rs,device_id=dev,device_id_type=MESH)
    def send(self,make):
        cond,desc=make()
        when(cond,desc.start); self.sent.append(make)
    def half(self,a,shard,core):
        n=self.ins[a].shape[-1]//2
        return self.ins[a].at[shard,:,pl.ds(pl.multiple_of(core*n,128),n)]
    def add(self,dst,others):
        rows=dst.shape[0]; step=48 if rows%48==0 else 16
        def body(i,_):
            at=pl.ds(pl.multiple_of(i*step,16),step)
            value=dst[at,:].astype(f32)
            for o in others: value=value+o[at,:].astype(f32)
            dst[at,:]=value.astype(bf)
            return 0
        lax.fori_loop(0,rows//step,body,0)
    def begin(self):
        p=self.p
        for k in list(range(1,p.Y))+[0]:
            for d in ORDER:
                shard=d*p.Y+lax.rem(p.y+k,p.Y)
                for a in self.A:
                    H,Rc=self.bufs[a][0:2]
                    self.send(lambda a=a,Rc=Rc,shard=shard: (None,self.copy(self.half(a,shard,1-p.core),Rc.at[shard],self.core_s.at[a,shard],self.core_r.at[a,shard],p.other_core())))
                    pltpu.make_async_copy(self.half(a,shard,p.core),H.at[shard],self.own.at[a,shard]).start()
    def join_core(self,shard):
        p=self.p
        for a in self.A:
            H,Rc=self.bufs[a][0:2]
            pltpu.make_async_copy(self.half(a,shard,p.core),H.at[shard],self.own.at[a,shard]).wait()
            self.copy(Rc.at[shard],Rc.at[shard],self.core_s.at[a,shard],self.core_r.at[a,shard],p.other_core()).wait_recv()
            self.add(H.at[shard],[Rc.at[shard]])
    def to_y(self,d):
        p=self.p
        for k in range(1,p.Y):
            shard=d*p.Y+lax.rem(p.y+k,p.Y)
            self.join_core(shard)
            for a in self.A:
                H,_,Ry=self.bufs[a][0:3]
                self.send(lambda a=a,H=H,Ry=Ry,k=k,shard=shard: (None,self.copy(H.at[shard],Ry.at[k-1,d],self.y_s.at[a,k,d],self.y_r.at[a,k,d],p.other_y(k))))
    def own_y(self,d):
        self.join_core(d*self.p.Y+self.p.y)
    def line(self,d):
        p=self.p; shard=d*p.Y+p.y
        for a in self.A:
            H,_,Ry,Rl=self.bufs[a][0:4]
            for k in range(1,p.Y):
                self.copy(Ry.at[k-1,d],Ry.at[k-1,d],self.y_s.at[a,k,d],self.y_r.at[a,k,d],p.other_y(k)).wait_recv()
            self.add(H.at[shard],[Ry.at[k-1,d] for k in range(1,p.Y)])
        for up in (0,1):
            passes=(p.z<d) if up==0 else (p.z>d)
            inner=(p.z>0) if up==0 else (p.z<ROWS-1)
            def add_in(up=up):
                for a in self.A:
                    H,Rl=self.bufs[a][0],self.bufs[a][3]
                    self.copy(Rl.at[up,d],Rl.at[up,d],self.line_s.at[a,up,d],self.line_r.at[a,up,d],p.near_z(0)).wait_recv()
                    self.add(H.at[shard],[Rl.at[up,d]])
            pl.when(jnp.logical_and(passes,inner))(add_in)
            for a in self.A:
                H,Rl=self.bufs[a][0],self.bufs[a][3]
                self.send(lambda a=a,H=H,Rl=Rl,up=up,passes=passes: (passes,self.copy(H.at[shard],Rl.at[up,d],self.line_s.at[a,up,d],self.line_r.at[a,up,d],p.near_z(1 if up==0 else -1))))
    def to_x(self):
        p=self.p
        for up in (0,1):
            def add_in(up=up):
                for a in self.A:
                    H,Rl=self.bufs[a][0],self.bufs[a][3]
                    self.copy(Rl.at[up,p.z],Rl.at[up,p.z],self.line_s.at[a,up,p.z],self.line_r.at[a,up,p.z],p.near_z(0)).wait_recv()
                    self.add(H.at[p.s],[Rl.at[up,p.z]])
            pl.when((p.z>0) if up==0 else (p.z<ROWS-1))(add_in)
        for a in self.A:
            H,Rx=self.bufs[a][0],self.bufs[a][4]
            for k in range(1,p.X):
                self.send(lambda a=a,H=H,Rx=Rx,k=k: (None,self.copy(H.at[p.s],Rx.at[p.x],self.x_s.at[a,k],self.x_r.at[a,p.x],p.other_x(k))))
    def to_core(self):
        p=self.p
        for a in self.A:
            H,Rx=self.bufs[a][0],self.bufs[a][4]; out=self.outs[a]
            for k in range(1,p.X):
                src=lax.rem(p.x-k+p.X,p.X)
                self.copy(Rx.at[src],Rx.at[src],self.x_s.at[a,k],self.x_r.at[a,src],p.other_x(k)).wait_recv()
            rows=H.shape[1]; step=48 if rows%48==0 else 16
            def body(i,_):
                at=pl.ds(pl.multiple_of(i*step,16),step)
                own=H[p.s,at,:].astype(f32)
                value=jnp.zeros_like(own)
                for q in range(p.X):
                    value=value+jnp.where(p.x==q,own,Rx[q,at,:].astype(f32))
                out[p.core,at,:]=value
                return 0
            lax.fori_loop(0,rows//step,body,0)
        for a in self.A:
            out=self.outs[a]
            self.send(lambda a=a,out=out: (None,self.copy(out.at[p.core],out.at[p.core],self.end_s.at[a],self.end_r.at[a],p.other_core())))
    def finish(self):
        p=self.p
        for a in self.A:
            ref=self.outs[a].at[1-p.core]
            self.copy(ref,ref,self.end_s.at[a],self.end_r.at[a],p.other_core()).wait_recv()
        for make in self.sent:
            cond,desc=make()
            when(cond,desc.wait_send)
    def steps(self):
        part=lambda f,d: (lambda: f(d))
        return [self.begin]+[part(self.to_y,d) for d in ORDER]+[part(self.own_y,d) for d in ORDER]+[part(self.line,d) for d in ORDER]+[self.to_x,self.to_core,self.finish]
def reduce_body(shards,reps,count,*refs):
    ins,outs,scratch=refs[:count],refs[count:2*count],refs[2*count:]
    place=Place(shards,reps)
    meet(place,True)
    for step in Reduce(place,ins,outs,scratch).steps(): step()
def reduce_now(arrays,shards,reps,collective_id):
    count=len(arrays)
    return pl.pallas_call(partial(reduce_body,shards,reps,count),
        in_specs=[pl.BlockSpec(memory_space=pl.ANY)]*count,
        out_specs=[pl.BlockSpec(memory_space=pltpu.VMEM)]*count,
        out_shape=[jax.ShapeDtypeStruct((2,a.shape[1],a.shape[2]//2),f32) for a in arrays],
        scratch_shapes=reduce_scratch([a.shape[1:] for a in arrays],shards,reps),
        compiler_params=pltpu.CompilerParams(collective_id=collective_id,has_side_effects=True,vmem_limit_bytes=50<<20),
        name="reduce_grads")(*arrays)

GATHER_PLAN = {
    0: (("u", 0), ("d", 0)),
    2: (("u", 1),),
    3: (("d", 1), ("u", 2)),
    4: (("d", 2),),
    5: (("u", 3), ("u", 4)),
    6: (("d", 3), ("d", 4)),
    8: (("u", 5), ("u", 6)),
    9: (("d", 5), ("d", 6)),
    11: (("u", 7),),
    100: (("d", 7), ("u", 8), ("d", 8)),
}


def low_lanes():
    return lax.broadcasted_iota(jnp.int32, (LEN, CLUSTER), 1) < DH


def table_of(order_row):
    positions = lax.broadcasted_iota(jnp.int32, (LEN, LEN), 0)
    return jnp.where(jnp.broadcast_to(order_row, (LEN, LEN)) == positions, 1.0, 0.0).astype(bf)


def half_roll(source):
    return pltpu.roll(source.astype(f32), DH, 1).astype(bf)


def softmax_rows(scores):
    top = jnp.max(scores, axis=-1, keepdims=True)
    grown = jnp.exp(scores - top)
    return grown * (1.0 / jnp.sum(grown, axis=-1, keepdims=True))


def attention_forward_body(
    shards, reps, len_ref, x_ref, wq_ref, wk_ref, wv_ref, bq_ref, bk_ref, bv_ref, row_ref, *rest
):
    ins, (att_ref, proj_ref), outs = rest[:3], rest[3:5], rest[5:8]
    tables, scores, mixed = rest[8:10], rest[10:12], rest[12:14]
    sems = rest[14:]
    step = pl.program_id(0) * PAIRS + pl.program_id(1)
    place = Place(shards, reps)
    up, down = [
        Gather(place, [ins[a] for a in which], [outs[a] for a in which], sems[7 * k : 7 * k + 7])
        for k, which in enumerate(((0,), (1, 2)))
    ]
    u, d = up.steps(), down.steps()
    plan = GATHER_PLAN

    def run(at):
        for name, k in plan.get(at, ()):
            (u if name == "u" else d)[k]()

    def first():
        meet(place, False)
        run(0)

    pl.when(step == 0)(first)
    for at in sorted(plan):
        if 0 < at < 100:
            pl.when(step == at)(partial(run, at))

    count = len_ref[pl.program_id(0)]
    weight = jnp.concatenate([wq_ref[...], wk_ref[...], wv_ref[...]], axis=1)
    bias = jnp.concatenate([bq_ref[...], bk_ref[...], bv_ref[...]], axis=1)
    proj = (dot_nn(x_ref[...], weight) + bias).astype(bf)
    low = low_lanes()
    query, key, value = proj[:, 0:128], proj[:, 128:256], proj[:, 256:384]
    pairs = [jnp.where(low, query, half_roll(key)), jnp.where(low, half_roll(query), key)]
    proj_ref[...] = jnp.concatenate([pairs[0], value, pairs[1]], axis=1)
    rows = [row_ref[0, 0, e : e + 1, :] for e in range(2)]
    for e in range(2):
        tables[e][...] = table_of(rows[e])
    picked = [
        dot_tn(tables[e][...], jnp.concatenate([pairs[e], value], axis=1)).astype(bf)
        for e in range(2)
    ]
    for e in range(2):
        qk = picked[e][:, 0:128]
        key_low = jnp.where(low, half_roll(qk), jnp.zeros((), bf))
        bias = jnp.where(rows[e] < count, 0.0, -30000.0)
        for sl in SLICES:
            scores[e][sl, :] = 0.125 * dot_nt(qk[sl], key_low[sl]) + bias[:, sl]
    for e in range(2):
        values = picked[e][:, 128:256]
        for sl in SLICES:
            probs = softmax_rows(scores[e][sl, :]).astype(bf)
            mixed[e][sl, :] = dot_nn(probs, values[sl]).astype(bf)
    placed = [dot_nn(tables[e][...], mixed[e][...]) for e in range(2)]
    att_ref[...] = jnp.where(low, placed[0], placed[1]).astype(bf)
    pl.when(step == pl.num_programs(0) * PAIRS - 1)(partial(run, 100))


def attention_forward(lengths, rounded, weight, bias, rows, arrays, shards, reps, collective_id):
    seqs = rows.shape[0]
    tokens = seqs * LEN
    column = lambda part: pl.BlockSpec((D, 128), lambda s, h, n: (0, part * PAIRS + h))
    column_b = lambda part: pl.BlockSpec((1, 128), lambda s, h, n: (0, part * PAIRS + h))
    return pl.pallas_call(
        partial(attention_forward_body, shards, reps),
        grid_spec=pltpu.PrefetchScalarGridSpec(
            num_scalar_prefetch=1,
            grid=(seqs, PAIRS),
            in_specs=[pl.BlockSpec((LEN, D), lambda s, h, n: (s, 0))]
            + [column(part) for part in range(3)]
            + [column_b(part) for part in range(3)]
            + [pl.BlockSpec((1, 1, 2, LEN), lambda s, h, n: (s, h, 0, 0))]
            + [pl.BlockSpec(memory_space=pltpu.VMEM)] * 3,
            out_specs=[
                pl.BlockSpec((LEN, 128), lambda s, h, n: (s, h)),
                pl.BlockSpec((LEN, 384), lambda s, h, n: (s, h)),
            ]
            + [pl.BlockSpec(memory_space=pl.ANY)] * 3,
            scratch_shapes=[pltpu.VMEM((LEN, LEN), bf)] * 2
            + [pltpu.VMEM((LEN, 128), f32)] * 2
            + [pltpu.VMEM((LEN, 128), bf)] * 2
            + gather_semaphores(1, shards)
            + gather_semaphores(2, shards),
        ),
        out_shape=[
            jax.ShapeDtypeStruct((tokens, D), bf),
            jax.ShapeDtypeStruct((tokens, 3 * D), bf),
        ]
        + [jax.ShapeDtypeStruct((shards,) + a.shape, bf) for a in arrays],
        compiler_params=pltpu.CompilerParams(
            vmem_limit_bytes=50 << 20, collective_id=collective_id, has_side_effects=True
        ),
        name="attention_forward",
    )(lengths, rounded, weight, weight, weight, bias, bias, bias, rows, *arrays)


def attention_backward_body(
    len_ref,
    x_ref,
    proj_ref,
    datt_ref,
    row_ref,
    dq_ref,
    dk_ref,
    dv_ref,
    dw_ref,
    db_ref,
    t0,
    t1,
    s0,
    s1,
    d0,
    d1,
    p0,
    p1,
    e0,
    e1,
    total,
):
    seq = pl.program_id(1)
    count = len_ref[seq]
    low = low_lanes()
    zero = jnp.zeros((), bf)
    tables, scores, back_probs, probs_low, backs = (t0, t1), (s0, s1), (d0, d1), (p0, p1), (e0, e1)
    rows = [row_ref[0, 0, e : e + 1, :] for e in range(2)]
    for e in range(2):
        tables[e][...] = table_of(rows[e])
    datt = datt_ref[...]
    swapped = half_roll(proj_ref[:, 128:256])
    middle = [jnp.where(low, datt, swapped), jnp.where(low, swapped, datt)]
    sources = [
        jnp.concatenate([proj_ref[:, 256 * e : 256 * e + 128], middle[e]], axis=1)
        for e in range(2)
    ]
    picked = [dot_tn(tables[e][...], sources[e]).astype(bf) for e in range(2)]
    for e in range(2):
        qk, dv = picked[e][:, 0:128], picked[e][:, 128:256]
        key_low = jnp.where(low, half_roll(qk), zero)
        turned = half_roll(dv)
        value_only = jnp.where(low, turned, zero) if e == 0 else jnp.where(low, zero, turned)
        bias = jnp.where(rows[e] < count, 0.0, -30000.0)
        for sl in SLICES:
            scores[e][sl, :] = 0.125 * dot_nt(qk[sl], key_low[sl]) + bias[:, sl]
            back_probs[e][sl, :] = dot_nt(dv[sl], value_only[sl])
    for e in range(2):
        for sl in SLICES:
            probs = softmax_rows(scores[e][sl, :])
            back = back_probs[e][sl, :]
            probs_low[e][sl, :] = probs.astype(bf)
            inner = jnp.sum(back * probs, axis=-1, keepdims=True)
            backs[e][sl, :] = (0.125 * (probs * (back - inner))).astype(bf)
    placed = []
    for e in range(2):
        qk, dv = picked[e][:, 0:128], picked[e][:, 128:256]
        queries, keys, values = [], [], []
        for sl in SLICES:
            back = backs[e][sl, :]
            queries.append(dot_nn(back, qk[sl]))
            keys.append(dot_tn(back, qk[sl]))
            values.append(dot_tn(probs_low[e][sl, :], dv[sl]))
        key_query = jnp.where(low, jnp.concatenate(keys, 0), jnp.concatenate(queries, 0))
        value = jnp.concatenate(values, 0)
        db_ref[0, 0, e : e + 1, :] = jnp.sum(key_query, axis=0, keepdims=True)
        db_ref[0, 0, 2 + e : 3 + e, :] = jnp.sum(value, axis=0, keepdims=True)
        parts = [key_query.astype(bf), value.astype(bf)]
        placed.append(
            dot_nn(tables[e][...], jnp.concatenate(parts, axis=1))
        )
    key_queries = [placed[e][:, 0:128] for e in range(2)]
    turned = [pltpu.roll(t, DH, 1) for t in key_queries]
    query = jnp.where(low, turned[0], key_queries[1]).astype(bf)
    key = jnp.where(low, key_queries[0], turned[1]).astype(bf)
    value = jnp.where(low, placed[0][:, 128:256], placed[1][:, 128:256]).astype(bf)
    dq_ref[...] = query
    dk_ref[...] = key
    dv_ref[...] = value
    out = jnp.concatenate([query, key, value], axis=1)
    part = dot_tn(x_ref[...], out)

    @pl.when(seq == 0)
    def _():
        total[...] = part

    @pl.when(seq != 0)
    def _():
        total[...] += part

    dw_ref[0] = total[...].astype(bf)


def pair_at(i):
    return (i % 2) * (PAIRS // 2) + i // 2


def attention_backward(lengths, rounded, proj, datt, rows):
    seqs = rows.shape[0]
    tokens = seqs * LEN
    own = lambda width: pl.BlockSpec((LEN, width), lambda i, s, n: (s, pair_at(i)))
    return pl.pallas_call(
        attention_backward_body,
        grid_spec=pltpu.PrefetchScalarGridSpec(
            num_scalar_prefetch=1,
            grid=(PAIRS, seqs),
            in_specs=[
                pl.BlockSpec((LEN, D), lambda i, s, n: (s, 0)),
                own(384),
                own(128),
                pl.BlockSpec((1, 1, 2, LEN), lambda i, s, n: (s, pair_at(i), 0, 0)),
            ],
            out_specs=[own(128)] * 3
            + [
                pl.BlockSpec((1, D, 384), lambda i, s, n: (i // 2, 0, i % 2)),
                pl.BlockSpec((1, 1, 4, 128), lambda i, s, n: (s, pair_at(i), 0, 0)),
            ],
            scratch_shapes=[pltpu.VMEM((LEN, LEN), bf)] * 2
            + [pltpu.VMEM((LEN, 128), f32)] * 4
            + [pltpu.VMEM((LEN, 128), bf)] * 4
            + [pltpu.VMEM((D, 384), f32)],
        ),
        out_shape=[jax.ShapeDtypeStruct((tokens, D), bf)] * 3
        + [
            jax.ShapeDtypeStruct((PAIRS // 2, D, D), bf),
            jax.ShapeDtypeStruct((seqs, PAIRS, 4, 128), f32),
        ],
        compiler_params=pltpu.CompilerParams(vmem_limit_bytes=50 << 20),
        cost_estimate=pl.CostEstimate(
            flops=70_000_000_000, bytes_accessed=30_000_000, transcendentals=0
        ),
        name="attention_backward",
    )(lengths, rounded, proj, datt, rows)


def norm_stats(x):
    c=jnp.mean(x,axis=-1,keepdims=True)
    xc=x-c
    r=lax.rsqrt(jnp.mean(xc*xc,axis=-1,keepdims=True)+eps_norm)
    return xc*r,r

def norm_back(up,normed,r,gain):
    g=up*gain
    return r*(g-jnp.mean(g,axis=-1,keepdims=True)-normed*jnp.mean(g*normed,axis=-1,keepdims=True))

def colsum(x): return jnp.sum(x,axis=0,keepdims=True)

def gelu_parts(u):
    cdf=0.5+0.5*lax.erf(u*0.7071067811865476)
    pdf=jnp.exp(-0.5*u*u)*0.3989422804014327
    return u*cdf,cdf+u*pdf

def middle_body(len_ref,h_ref,a_ref,ct_ref,ow_ref,uw_ref,dw_ref,vec_ref,ub_ref,
               out_ref,bs_ref,ba_ref,act,pl_,low_ref,d2_ref,sl_ref,small_ref,ubg_ref,
               gp,n1_ref,*,T,sub_rows,chunk):
    i=pl.program_id(0)
    per=LEN//T
    count=len_ref[i//per]
    @pl.when(i==0)
    def _():
        small_ref[...]=jnp.zeros_like(small_ref); ubg_ref[...]=jnp.zeros_like(ubg_ref)
    out_b,g1,b1,down_b,g2,b2=[vec_ref[j:j+1,:] for j in range(6)]
    parts=[slice(k,k+sub_rows) for k in range(0,T,sub_rows)]
    r1s=[];sums=[]
    xs=[dot_nn(a_ref[p,:],ow_ref[...]) for p in parts]
    for p,x in zip(parts,xs):
        n1,r1=norm_stats(h_ref[p,:]+x+out_b)
        n1_ref[p,:]=n1; r1s.append(r1)
        low_ref[p,:]=(n1*g1+b1).astype(bf)
    for j in range(0,FF,chunk):
        sl=slice(j,j+chunk)
        for p in parts:
            u=dot_nn(low_ref[p,:],uw_ref[:,sl])+ub_ref[:,sl]
            a,g=gelu_parts(u)
            act[p,sl]=a.astype(bf); gp[p,sl]=g.astype(gp.dtype)
    ys=[dot_nn(act[p,:],dw_ref[...]) for p in parts]
    for p,y in zip(parts,ys):
        pos=lax.broadcasted_iota(jnp.int32,(sub_rows,1),0)+(i%per)*T+p.start
        valid=jnp.where(pos<count,1.0,0.0)
        second=n1_ref[p,:]*g1+b1+y+down_b
        n2,r2=norm_stats(second)
        out_ref[p,:]=valid*(n2*g2+b2)
        up=valid*ct_ref[p,:]
        b2nd=norm_back(up,n2,r2,g2)
        d2_ref[p,:]=b2nd.astype(bf)
        bs_ref[p,:]=b2nd
        sums.append(jnp.concatenate([colsum(b2nd),colsum(up*n2),colsum(up)],axis=0))
    small_ref[3:6,:]+=sum(sums[1:],sums[0])
    for j in range(0,FF,chunk):
        sl=slice(j,j+chunk)
        cs=[]
        for p in parts:
            bp=dot_nt(d2_ref[p,:],dw_ref[sl,:])*gp[p,sl].astype(f32)
            cs.append(colsum(bp))
            pl_[p,sl]=bp.astype(bf)
        ubg_ref[:,sl]+=sum(cs[1:],cs[0])
    zs=[dot_nt(pl_[p,:],uw_ref[...]) for p in parts]
    sums=[]
    for p,z,r1 in zip(parts,zs,r1s):
        bfirst=z+bs_ref[p,:]
        n1=n1_ref[p,:]
        bsum=norm_back(bfirst,n1,r1,g1)
        bs_ref[p,:]=bsum
        sl_ref[p,:]=bsum.astype(bf)
        sums.append(jnp.concatenate([colsum(bsum),colsum(bfirst*n1),colsum(bfirst)],axis=0))
    small_ref[0:3,:]+=sum(sums[1:],sums[0])
    for p in parts:
        ba_ref[p,:]=dot_nt(sl_ref[p,:],ow_ref[...]).astype(bf)

def middle(lengths,hidden,att,ct,ow,uw,dw,vec,ub,T=512,chunk=768,gpt=f32,sub_rows=256):
    tokens=hidden.shape[0]
    tile=lambda n=D: pl.BlockSpec((T,n),lambda i,l:(i,0))
    const=lambda shape: pl.BlockSpec(shape,lambda i,l:(0,0),pipeline_mode=pl.Buffered(1))
    whole=lambda shape: pl.BlockSpec(shape,lambda i,l:(0,0))
    sd=lambda n,dt: jax.ShapeDtypeStruct((tokens,n),dt)
    return pl.pallas_call(
        partial(middle_body,T=T,chunk=chunk,sub_rows=sub_rows),
        grid_spec=pltpu.PrefetchScalarGridSpec(num_scalar_prefetch=1,grid=(tokens//T,),
          in_specs=[tile(),tile(),tile(),const((D,D)),const((D,FF)),const((FF,D)),whole((8,D)),whole((1,FF))],
          out_specs=[tile(),tile(),tile(),tile(FF),tile(FF),tile(),tile(),tile(),whole((8,D)),whole((1,FF))],
          scratch_shapes=[pltpu.VMEM((T,FF),gpt),pltpu.VMEM((T,D),f32)]),
        out_shape=[sd(D,f32),sd(D,f32),sd(D,bf),sd(FF,bf),sd(FF,bf),sd(D,bf),sd(D,bf),sd(D,bf),jax.ShapeDtypeStruct((8,D),f32),jax.ShapeDtypeStruct((1,FF),f32)],
        compiler_params=pltpu.CompilerParams(vmem_limit_bytes=63<<20),
        name="middle")(lengths,hidden,att,ct,ow,uw,dw,vec,ub)


def weight_grad_body(l_ref,r_ref,out_ref):
    out_ref[...]=dot_tn(l_ref[...],r_ref[...]).astype(bf)
def weight_grad(left,right,block,name,columns=False):
    K,M=left.shape; N=right.shape[1]
    if columns:
        grid,lb,rb,ob,li,ri,oi=(N//block,),(K,M),(K,block),(M,block),(lambda i:(0,0)),(lambda i:(0,i)),(lambda i:(0,i))
    else:
        grid,lb,rb,ob,li,ri,oi=(M//block,),(K,block),(K,N),(block,N),(lambda i:(0,i)),(lambda i:(0,0)),(lambda i:(i,0))
    return pl.pallas_call(weight_grad_body,grid=grid,
        in_specs=[pl.BlockSpec(lb,li),pl.BlockSpec(rb,ri)],out_specs=pl.BlockSpec(ob,oi),
        out_shape=jax.ShapeDtypeStruct((M,N),bf),
        cost_estimate=pl.CostEstimate(flops=2*K*M*N,bytes_accessed=2*(K*M+K*N+M*N),transcendentals=0),
        compiler_params=pltpu.CompilerParams(vmem_limit_bytes=60<<20),name=name)(left,right)


def input_grad_body(bs_ref,dq_ref,dk_ref,dv_ref,w_ref,out_ref):
    out_ref[...]=bs_ref[...]+dot_nt(dq_ref[...],w_ref[:,0:D])+dot_nt(dk_ref[...],w_ref[:,D:2*D])+dot_nt(dv_ref[...],w_ref[:,2*D:3*D])
def input_grad(back_sum,dq,dk,dv,weight,rows=512):
    tile=pl.BlockSpec((rows,D),lambda i:(i,0))
    return pl.pallas_call(input_grad_body,grid=(back_sum.shape[0]//rows,),
        in_specs=[tile]*4+[pl.BlockSpec((D,3*D),lambda i:(0,0),pipeline_mode=pl.Buffered(1))],out_specs=tile,
        out_shape=jax.ShapeDtypeStruct(back_sum.shape,f32),
        compiler_params=pltpu.CompilerParams(vmem_limit_bytes=50<<20),name="input_grad")(back_sum,dq,dk,dv,weight)


WIDE = 4096


def shard_vectors(vectors):
    row = jnp.concatenate(vectors)
    return jnp.pad(row, (0, WIDE - row.shape[0])).reshape(16, 256)


def local(
    hidden,
    lengths,
    clusters,
    input_weight,
    query_bias,
    value_bias,
    out_weight,
    out_bias,
    norm1_gain,
    norm1_bias,
    up_weight,
    up_bias,
    down_weight,
    down_bias,
    norm2_gain,
    norm2_bias,
    cotangent,
    *,
    shards,
    reps,
):
    seqs = hidden.shape[0]
    tokens = seqs * LEN
    part = D // shards
    vectors = shard_vectors(
        (
            query_bias,
            value_bias,
            out_bias,
            norm1_gain,
            norm1_bias,
            down_bias,
            norm2_gain,
            norm2_bias,
            up_bias,
        )
    )
    in_w, vectors = gather_now((input_weight, vectors), shards, reps, 1)
    in_w = in_w.reshape(D, 3 * D)
    vectors = vectors.reshape(shards, WIDE).astype(f32)
    table = vectors[:, : 8 * part].reshape(shards, 8, part).transpose(1, 0, 2).reshape(8, D)
    bias_all = jnp.concatenate([table[0], jnp.zeros((D,), f32), table[1]])[None]
    norm_rows = jnp.concatenate([table[2:], table[:2]])
    up_b = vectors[:, 8 * part : 8 * part + FF // shards].reshape(1, FF)

    flat = hidden.reshape(tokens, D)
    rounded = flat.astype(bf)
    rows = clusters.reshape(seqs, PAIRS, 2, LEN)
    attended, proj, up_w, down_w, out_w = attention_forward(
        lengths,
        rounded,
        in_w,
        bias_all,
        rows,
        (up_weight, down_weight, out_weight),
        shards,
        reps,
        2,
    )
    out_w, up_w, down_w = [w.reshape(-1, w.shape[-1]) for w in (out_w, up_w, down_w)]
    (
        result,
        back_sum,
        back_attended,
        activated,
        pre_low,
        first_low,
        second_low,
        sum_low,
        norm_sums,
        up_b_sum,
    ) = middle(
        lengths,
        flat,
        attended,
        cotangent.reshape(tokens, D),
        out_w,
        up_w,
        down_w,
        norm_rows,
        up_b,
    )
    down_g = weight_grad(activated, second_low, D, "down_weight_grad")
    up_g = weight_grad(first_low, pre_low, D, "up_weight_grad", True)
    out_g = weight_grad(attended, sum_low, D // 2, "out_weight_grad")
    dq, dk, dv, in_g, bias_sums = attention_backward(lengths, rounded, proj, back_attended, rows)
    down_s, up_s, out_s = reduce_now(
        [g.reshape(shards, -1, g.shape[-1]) for g in (down_g, up_g, out_g)], shards, reps, 3
    )
    bias_sums = jnp.sum(bias_sums, axis=0)
    query_sum = bias_sums[:, 0:2, DH:].reshape(D)
    value_sum = jnp.concatenate([bias_sums[:, 2, :DH], bias_sums[:, 3, DH:]], axis=1).reshape(D)
    table = jnp.concatenate([query_sum[None], value_sum[None], norm_sums[:6]])
    small = jnp.concatenate(
        [
            table.reshape(8, shards, part).transpose(1, 0, 2).reshape(shards, 8 * part),
            up_b_sum.reshape(shards, FF // shards),
        ],
        axis=1,
    ).astype(bf)
    small = jnp.pad(small, ((0, 0), (0, WIDE - small.shape[1]))).reshape(shards, 16, 256)
    *in_s, small_s = reduce_now(
        [in_g[g].reshape(shards, part, D) for g in range(PAIRS // 2)] + [small], shards, reps, 4
    )
    back_input = input_grad(back_sum, dq, dk, dv, in_w).reshape(seqs, LEN, D)
    in_s = jnp.concatenate(
        [
            in_s[g][c, :, 128 * t : 128 * t + 128]
            for t in range(3)
            for c in range(2)
            for g in range(PAIRS // 2)
        ],
        axis=1,
    )

    def whole(halves):
        return jnp.concatenate([halves[0], halves[1]], axis=1)

    small_s = whole(small_s).reshape(WIDE)
    vec = [small_s[i * part : (i + 1) * part] for i in range(8)]
    return (
        result.reshape(seqs, LEN, D),
        back_input,
        in_s,
        vec[0],
        vec[1],
        whole(out_s),
        vec[2],
        vec[3],
        vec[4],
        whole(up_s),
        small_s[8 * part : 8 * part + FF // shards],
        whole(down_s),
        vec[5],
        vec[6],
        vec[7],
    )


def solution(mesh):
    tokens = P(("rep", "shard"), None, None)
    matrix, vector = P("shard", None), P("shard")
    params = (
        matrix,
        vector,
        vector,
        matrix,
        vector,
        vector,
        vector,
        matrix,
        vector,
        matrix,
        vector,
        vector,
        vector,
    )
    return jax.shard_map(
        partial(local, shards=mesh.shape["shard"], reps=mesh.shape["rep"]),
        mesh=mesh,
        in_specs=(tokens, P(("rep", "shard")), tokens) + params + (tokens,),
        out_specs=(tokens, tokens) + params,
        check_vma=False,
    )
```

```python
from functools import partial

import jax
import jax.numpy as jnp
from jax import lax
from jax.experimental import pallas as pl
from jax.experimental.pallas import tpu as pltpu
from jax.sharding import PartitionSpec as P

D = 768
H = 12
DH = 64
FF = 3072
CLUSTER = 128
LEN = 1024
PAIRS = H // 2
SLICES = [slice(c * CLUSTER, (c + 1) * CLUSTER) for c in range(LEN // CLUSTER)]
bf = jnp.bfloat16
f32 = jnp.float32
eps_norm = 1e-12


def dot_nn(left, right):
    return lax.dot_general(left, right, (((1,), (0,)), ((), ())), preferred_element_type=f32)


def dot_nt(left, right):
    return lax.dot_general(left, right, (((1,), (1,)), ((), ())), preferred_element_type=f32)


def dot_tn(left, right):
    return lax.dot_general(left, right, (((0,), (0,)), ((), ())), preferred_element_type=f32)


ROWS = 4
MESH=pl.DeviceIdType.MESH

def when(cond,do):
    if cond is None: do()
    else: pl.when(cond)(do)

class Place:
    def __init__(self,shards,reps):
        self.Y=shards//ROWS; self.S=shards; self.X=reps//2
        self.s=lax.axis_index("shard"); self.r=lax.axis_index("rep")
        self.z=self.s//self.Y; self.y=lax.rem(self.s,self.Y)
        self.core=lax.rem(self.r,2); self.x=self.r//2
    def near_z(self,step): return {"shard":self.s+step*self.Y}
    def other_y(self,k): return {"shard":self.z*self.Y+lax.rem(self.y+k,self.Y)}
    def other_core(self): return {"rep":self.r+1-2*self.core}
    def other_x(self,k): return {"rep":2*lax.rem(self.x+k,self.X)+self.core}

def meet(place,with_x):
    sem=pltpu.get_barrier_semaphore()
    def tell(dev): pl.semaphore_signal(sem,inc=1,device_id=dev,device_id_type=MESH)
    pl.when(place.z>0)(lambda: tell(place.near_z(-1)))
    pl.when(place.z<ROWS-1)(lambda: tell(place.near_z(1)))
    for k in range(1,place.Y): tell(place.other_y(k))
    tell(place.other_core())
    if with_x:
        for k in range(1,place.X): tell(place.other_x(k))
    others=place.Y+(place.X-1 if with_x else 0)
    inner=jnp.logical_and(place.z>0,place.z<ROWS-1)
    pl.when(inner)(lambda: pl.semaphore_wait(sem,others+2))
    pl.when(jnp.logical_not(inner))(lambda: pl.semaphore_wait(sem,others+1))

def gather_semaphores(count,shards):
    Y=shards//ROWS
    return [pltpu.SemaphoreType.DMA((count,2,ROWS)),pltpu.SemaphoreType.DMA((count,2,ROWS)),
            pltpu.SemaphoreType.DMA((count,ROWS,Y)),pltpu.SemaphoreType.DMA((count,ROWS,Y)),
            pltpu.SemaphoreType.DMA((count,shards)),pltpu.SemaphoreType.DMA((count,shards)),
            pltpu.SemaphoreType.DMA((count,))]

class Gather:
    def __init__(self,place,ins,outs,sems):
        self.p=place; self.ins=ins; self.outs=outs
        self.line_s,self.line_r,self.y_s,self.y_r,self.core_s,self.core_r,self.own=sems
        self.sent=[]
    def half(self,ref,shard=None):
        n=ref.shape[-1]//2
        cols=pl.ds(pl.multiple_of(self.p.core*n,128),n)
        return ref.at[:,cols] if shard is None else ref.at[shard,:,cols]
    def other_half(self,ref,shard):
        n=ref.shape[-1]//2
        return ref.at[shard,:,pl.ds(pl.multiple_of((1-self.p.core)*n,128),n)]
    def send(self,make):
        cond,desc=make()
        when(cond,desc.start); self.sent.append(make)
    def copy(self,src,dst,ss,rs,dev):
        return pltpu.make_async_remote_copy(src_ref=src,dst_ref=dst,send_sem=ss,recv_sem=rs,device_id=dev,device_id_type=MESH)
    def at(self,places):
        zz=self.p.z+places
        if places==0: return None,zz
        return jnp.logical_and(zz>=0,zz<ROWS),jnp.clip(zz,0,ROWS-1)
    def to_line(self,a,places,d):
        p=self.p; i,o=self.ins[a],self.outs[a]
        def make():
            cond,zz=self.at(places); shard=zz*p.Y+p.y
            edge=(p.z<ROWS-1) if d==0 else (p.z>0)
            src=self.half(i) if places==0 else self.half(o,shard)
            return (edge if cond is None else jnp.logical_and(cond,edge)),self.copy(src,self.half(o,shard),self.line_s.at[a,d,zz],self.line_r.at[a,d,zz],p.near_z(1 if d==0 else -1))
        self.send(make)
    def to_y(self,a,places,k):
        p=self.p; i,o=self.ins[a],self.outs[a]
        def make():
            cond,zz=self.at(places); shard=zz*p.Y+p.y
            src=self.half(i) if places==0 else self.half(o,shard)
            return cond,self.copy(src,self.half(o,shard),self.y_s.at[a,zz,k],self.y_r.at[a,zz,k],p.other_y(k))
        self.send(make)
    def to_core(self,a,places,k):
        p=self.p; o=self.outs[a]
        def make():
            cond,zz=self.at(places); shard=zz*p.Y+lax.rem(p.y-k+p.Y,p.Y)
            ref=self.half(o,shard)
            return cond,self.copy(ref,ref,self.core_s.at[a,shard],self.core_r.at[a,shard],p.other_core())
        self.send(make)
    def begin(self):
        for a,(i,o) in enumerate(zip(self.ins,self.outs)):
            for d in (0,1): self.to_line(a,0,d)
            for k in range(1,self.p.Y): self.to_y(a,0,k)
            pltpu.make_async_copy(i,o.at[self.p.s],self.own.at[a]).start()
    def wave(self,w):
        p=self.p
        for d in (0,1):
            places=-w if d==0 else w
            for a,o in enumerate(self.outs):
                cond,zz=self.at(places); ref=self.half(o,zz*p.Y+p.y)
                when(cond,self.copy(ref,ref,self.line_s.at[a,d,zz],self.line_r.at[a,d,zz],p.near_z(0)).wait_recv)
                self.to_line(a,places,d)
                for k in range(1,p.Y): self.to_y(a,places,k)
                self.to_core(a,places,0)
    def across(self,w):
        p=self.p
        for places in ((0,) if w==0 else (-w,w)):
            for k in range(1,p.Y):
                for a,o in enumerate(self.outs):
                    cond,zz=self.at(places); shard=zz*p.Y+lax.rem(p.y-k+p.Y,p.Y)
                    ref=self.half(o,shard)
                    when(cond,self.copy(ref,ref,self.y_s.at[a,zz,k],self.y_r.at[a,zz,k],p.other_y(k)).wait_recv)
                    self.to_core(a,places,k)
    def finish(self):
        p=self.p
        for a,(i,o) in enumerate(zip(self.ins,self.outs)):
            for k in range(1,p.S):
                shard=lax.rem(p.s+k,p.S)
                ref=self.other_half(o,shard)
                self.copy(ref,ref,self.core_s.at[a,shard],self.core_r.at[a,shard],p.other_core()).wait_recv()
            pltpu.make_async_copy(i,o.at[p.s],self.own.at[a]).wait()
        for make in self.sent:
            cond,desc=make()
            when(cond,desc.wait_send)
def gather_body(shards,reps,count,*refs):
    ins,outs,sems=refs[:count],refs[count:2*count],refs[2*count:]
    place=Place(shards,reps)
    meet(place,False)
    G=Gather(place,ins,outs,sems)
    G.begin(); G.wave(1); G.across(0); G.wave(2); G.across(1); G.wave(3); G.across(2); G.across(3); G.finish()

def gather_now(arrays,shards,reps,collective_id):
    count=len(arrays)
    return pl.pallas_call(partial(gather_body,shards,reps,count),
        in_specs=[pl.BlockSpec(memory_space=pltpu.VMEM)]*count,
        out_specs=[pl.BlockSpec(memory_space=pl.ANY)]*count,
        out_shape=[jax.ShapeDtypeStruct((shards,)+a.shape,a.dtype) for a in arrays],
        scratch_shapes=gather_semaphores(count,shards),
        compiler_params=pltpu.CompilerParams(collective_id=collective_id,has_side_effects=True,vmem_limit_bytes=16<<20),
        name="gather_weights")(*arrays)

ORDER=(3,0,2,1)
def reduce_scratch(shapes,shards,reps):
    S=shards; Y=S//ROWS; X=reps//2; A=len(shapes)
    out=[]
    for r,c in shapes:
        n=c//2
        out+=[pltpu.VMEM((S,r,n),bf),pltpu.VMEM((S,r,n),bf),pltpu.VMEM((max(Y-1,1),ROWS,r,n),bf),
              pltpu.VMEM((ROWS+1,r,n),bf),pltpu.VMEM((X,r,n),bf),pltpu.VMEM((2,r,n),f32)]
    dma=pltpu.SemaphoreType.DMA
    return out+[dma((A,S)),dma((A,S)),dma((A,S)),dma((A,Y,ROWS)),dma((A,Y,ROWS)),dma((A,ROWS+1)),dma((A,ROWS+1)),dma((A,X)),dma((A,X)),dma((A,)),dma((A,)),dma((A,))]
class Reduce:
    def __init__(self,place,ins,outs,scratch):
        self.p=place; self.ins=ins; self.outs=outs; A=len(ins); self.A=range(A)
        self.bufs=[scratch[6*a:6*a+6] for a in range(A)]
        (self.own,self.core_s,self.core_r,self.y_s,self.y_r,self.line_s,self.line_r,self.x_s,self.x_r,self.end_s,self.end_r,self.out_s)=scratch[6*A:]
        self.sent=[]
    def copy(self,src,dst,ss,rs,dev):
        return pltpu.make_async_remote_copy(src_ref=src,dst_ref=dst,send_sem=ss,recv_sem=rs,device_id=dev,device_id_type=MESH)
    def send(self,make):
        cond,desc=make()
        when(cond,desc.start); self.sent.append(make)
    def half(self,a,shard,core):
        n=self.ins[a].shape[-1]//2
        return self.ins[a].at[shard,:,pl.ds(pl.multiple_of(core*n,128),n)]
    def add(self,dst,others):
        rows,n=dst.shape; step=next(s for s in (96,48,16) if rows%s==0 and (s==16 or s*n<=96*512))
        def block(at):
            value=dst[at,:].astype(f32)
            for o in others: value=value+o[at,:].astype(f32)
            dst[at,:]=value.astype(bf)
        if rows==step: block(slice(0,rows)); return
        def body(i,_):
            block(pl.ds(pl.multiple_of(i*step,16),step))
            return 0
        lax.fori_loop(0,rows//step,body,0)
    def begin(self):
        p=self.p
        for k in list(range(1,p.Y))+[0]:
            for d in ORDER:
                for a in self.A:
                    H,Rc=self.bufs[a][0:2]
                    def make(a=a,d=d,k=k,Rc=Rc):
                        shard=d*p.Y+lax.rem(p.y+k,p.Y)
                        return None,self.copy(self.half(a,shard,1-p.core),Rc.at[shard],self.core_s.at[a,shard],self.core_r.at[a,shard],p.other_core())
                    self.send(make)
                    shard=d*p.Y+lax.rem(p.y+k,p.Y)
                    pltpu.make_async_copy(self.half(a,shard,p.core),H.at[shard],self.own.at[a,shard]).start()
    def join_core(self,shard):
        p=self.p
        for a in self.A:
            H,Rc=self.bufs[a][0:2]
            pltpu.make_async_copy(self.half(a,shard,p.core),H.at[shard],self.own.at[a,shard]).wait()
            self.copy(Rc.at[shard],Rc.at[shard],self.core_s.at[a,shard],self.core_r.at[a,shard],p.other_core()).wait_recv()
            self.add(H.at[shard],[Rc.at[shard]])
    def to_y(self,d):
        p=self.p
        for k in range(1,p.Y):
            self.join_core(d*p.Y+lax.rem(p.y+k,p.Y))
            for a in self.A:
                H,_,Ry=self.bufs[a][0:3]
                def make(a=a,H=H,Ry=Ry,k=k):
                    shard=d*p.Y+lax.rem(p.y+k,p.Y)
                    return None,self.copy(H.at[shard],Ry.at[k-1,d],self.y_s.at[a,k,d],self.y_r.at[a,k,d],p.other_y(k))
                self.send(make)
    def own_y(self,d):
        self.join_core(d*self.p.Y+self.p.y)
    def along(self,d,up,j):
        p=self.p
        if (j>=d) if up else (ROWS-1-j<=d): return
        here=p.z==(j if up else ROWS-1-j)
        shard=d*p.Y+p.y
        if j>0:
            def add_in():
                for a in self.A:
                    H,Rl=self.bufs[a][0],self.bufs[a][3]
                    self.copy(Rl.at[d],Rl.at[d],self.line_s.at[a,d],self.line_r.at[a,d],p.near_z(0)).wait_recv()
                    self.add(H.at[shard],[Rl.at[d]])
            pl.when(here)(add_in)
        last=(j==d-1) if up else (ROWS-1-j==d+1)
        slot=ROWS if last and not up else d
        for a in self.A:
            def make(a=a):
                H,Rl=self.bufs[a][0],self.bufs[a][3]
                return p.z==(j if up else ROWS-1-j),self.copy(H.at[d*p.Y+p.y],Rl.at[slot],self.line_s.at[a,slot],self.line_r.at[a,slot],p.near_z(1 if up else -1))
            self.send(make)
    def line(self,d):
        p=self.p; shard=d*p.Y+p.y
        for a in self.A:
            H,_,Ry=self.bufs[a][0:3]
            for k in range(1,p.Y):
                self.copy(Ry.at[k-1,d],Ry.at[k-1,d],self.y_s.at[a,k,d],self.y_r.at[a,k,d],p.other_y(k)).wait_recv()
            self.add(H.at[shard],[Ry.at[k-1,d] for k in range(1,p.Y)])
        self.along(d,True,0); self.along(d,False,0)
    def relay(self,d,j):
        self.along(d,True,j); self.along(d,False,j)
    def to_x(self):
        p=self.p
        for slot,cond in ((p.z,p.z>0),(ROWS,p.z<ROWS-1)):
            def add_in(slot=slot):
                for a in self.A:
                    H,Rl=self.bufs[a][0],self.bufs[a][3]
                    self.copy(Rl.at[slot],Rl.at[slot],self.line_s.at[a,slot],self.line_r.at[a,slot],p.near_z(0)).wait_recv()
                    self.add(H.at[p.s],[Rl.at[slot]])
            pl.when(cond)(add_in)
        for a in self.A:
            H,Rx=self.bufs[a][0],self.bufs[a][4]
            for k in range(1,p.X):
                self.send(lambda a=a,H=H,Rx=Rx,k=k: (None,self.copy(H.at[p.s],Rx.at[p.x],self.x_s.at[a,k],self.x_r.at[a,p.x],p.other_x(k))))
    def to_core(self):
        p=self.p
        for a in self.A:
            H,Rx,F=self.bufs[a][0],self.bufs[a][4],self.bufs[a][5]
            for k in range(1,p.X):
                src=lax.rem(p.x-k+p.X,p.X)
                self.copy(Rx.at[src],Rx.at[src],self.x_s.at[a,k],self.x_r.at[a,src],p.other_x(k)).wait_recv()
            rows=H.shape[1]; step=48 if rows%48==0 else 16
            def body(i,_):
                at=pl.ds(pl.multiple_of(i*step,16),step)
                own=H[p.s,at,:].astype(f32)
                value=jnp.zeros_like(own)
                for q in range(p.X):
                    value=value+jnp.where(p.x==q,own,Rx[q,at,:].astype(f32))
                F[p.core,at,:]=value
                return 0
            lax.fori_loop(0,rows//step,body,0)
        for a in self.A:
            F=self.bufs[a][5]
            self.send(lambda a=a,F=F: (None,self.copy(F.at[p.core],F.at[p.core],self.end_s.at[a],self.end_r.at[a],p.other_core())))
    def finish(self):
        p=self.p
        for a in self.A:
            F=self.bufs[a][5]; ref=F.at[1-p.core]
            self.copy(ref,ref,self.end_s.at[a],self.end_r.at[a],p.other_core()).wait_recv()
            pltpu.make_async_copy(F,self.outs[a],self.out_s.at[a]).start()
        for make in self.sent:
            cond,desc=make()
            when(cond,desc.wait_send)
        for a in self.A: pltpu.make_async_copy(self.bufs[a][5],self.outs[a],self.out_s.at[a]).wait()
    def run(self,what,*args): getattr(self,what)(*args)
def result_shapes(shapes):
    return [jax.ShapeDtypeStruct((2,r,c//2),f32) for r,c in shapes]

GATHER_PLAN = {
    0: (("u", "begin"), ("d", "begin")),
    2: (("u", "wave", 1),),
    3: (("d", "wave", 1),),
    4: (("u", "across", 0), ("d", "across", 0)),
    5: (("u", "wave", 2),),
    6: (("d", "wave", 2), ("u", "across", 1)),
    8: (("u", "wave", 3),),
    9: (("d", "wave", 3), ("d", "across", 1)),
    11: (("u", "across", 2),),
    100: (("d", "across", 2), ("u", "across", 3), ("d", "across", 3), ("u", "finish"), ("d", "finish")),
}


def each(name, what, *more):
    return tuple((name, what, d) + more for d in ORDER)


REDUCE_PLAN = {
    0: (("d", "begin"), ("u", "begin")),
    1: each("d", "to_y") + each("d", "own_y"),
    2: each("u", "to_y") + (("d", "line", 3),) + each("u", "own_y"),
    3: (("d", "line", 0), ("d", "relay", 3, 1)),
    4: (("g", "begin"), ("d", "line", 2), ("d", "relay", 0, 1), ("d", "relay", 3, 2)),
    5: each("g", "to_y")
    + each("g", "own_y")
    + (("d", "line", 1), ("d", "relay", 2, 1), ("d", "relay", 0, 2)),
    6: (("d", "relay", 1, 1), ("u", "line", 3)),
    7: (("d", "to_x"), ("u", "line", 0), ("u", "relay", 3, 1)),
    8: (("d", "to_core"), ("u", "line", 2), ("u", "relay", 0, 1), ("u", "relay", 3, 2)),
    9: (("u", "line", 1), ("u", "relay", 2, 1), ("u", "relay", 0, 2)) + each("g", "line"),
    10: (("u", "relay", 1, 1),) + each("g", "relay", 1),
    11: each("g", "relay", 2) + (("u", "to_x"),),
    100: (
        ("g", "to_x"),
        ("u", "to_core"),
        ("g", "to_core"),
        ("d", "finish"),
        ("u", "finish"),
        ("g", "finish"),
    ),
}
LAST_PLAN = {
    0: (("r", "begin"),),
    1: each("r", "to_y") + each("r", "own_y"),
    2: each("r", "line"),
    3: each("r", "relay", 1),
    100: each("r", "relay", 2) + (("r", "to_x"), ("r", "to_core"), ("r", "finish")),
}


def follow(plan, jobs, step, last, ready):
    def run(at):
        for name, what, *more in plan.get(at, ()):
            getattr(jobs[name], what)(*more)

    def first():
        ready()
        run(0)

    pl.when(step == 0)(first)
    for at in sorted(plan):
        if 0 < at < 100:
            pl.when(step == at)(partial(run, at))
    return lambda: pl.when(step == last)(partial(run, 100))


def low_lanes():
    return lax.broadcasted_iota(jnp.int32, (LEN, CLUSTER), 1) < DH


def table_of(order_row):
    positions = lax.broadcasted_iota(jnp.int32, (LEN, LEN), 0)
    return jnp.where(jnp.broadcast_to(order_row, (LEN, LEN)) == positions, 1.0, 0.0).astype(bf)


def half_roll(source):
    return pltpu.roll(source.astype(f32), DH, 1).astype(bf)


def softmax_rows(scores):
    top = jnp.max(scores, axis=-1, keepdims=True)
    grown = jnp.exp(scores - top)
    return grown * (1.0 / jnp.sum(grown, axis=-1, keepdims=True))


def attention_forward_body(
    shards, reps, len_ref, x_ref, wq_ref, wk_ref, wv_ref, bq_ref, bk_ref, bv_ref, row_ref, *rest
):
    ins, (att_ref, proj_ref), outs = rest[:3], rest[3:5], rest[5:8]
    tables, scores, mixed = rest[8:10], rest[10:12], rest[12:14]
    sems = rest[14:]
    step = pl.program_id(0) * PAIRS + pl.program_id(1)
    place = Place(shards, reps)
    jobs = {
        "u": Gather(place, ins[:1], outs[:1], sems[:7]),
        "d": Gather(place, ins[1:], outs[1:], sems[7:]),
    }
    end = follow(
        GATHER_PLAN, jobs, step, pl.num_programs(0) * PAIRS - 1, lambda: meet(place, False)
    )

    count = len_ref[pl.program_id(0)]
    weight = jnp.concatenate([wq_ref[...], wk_ref[...], wv_ref[...]], axis=1)
    bias = jnp.concatenate([bq_ref[...], bk_ref[...], bv_ref[...]], axis=1)
    proj = (dot_nn(x_ref[...], weight) + bias).astype(bf)
    low = low_lanes()
    query, key, value = proj[:, 0:128], proj[:, 128:256], proj[:, 256:384]
    pairs = [jnp.where(low, query, half_roll(key)), jnp.where(low, half_roll(query), key)]
    proj_ref[...] = jnp.concatenate([pairs[0], value, pairs[1]], axis=1)
    rows = [row_ref[0, 0, e : e + 1, :] for e in range(2)]
    for e in range(2):
        tables[e][...] = table_of(rows[e])
    picked = [
        dot_tn(tables[e][...], jnp.concatenate([pairs[e], value], axis=1)).astype(bf)
        for e in range(2)
    ]
    for e in range(2):
        qk = picked[e][:, 0:128]
        key_low = jnp.where(low, half_roll(qk), jnp.zeros((), bf))
        bias = jnp.where(rows[e] < count, 0.0, -30000.0)
        for sl in SLICES:
            scores[e][sl, :] = 0.125 * dot_nt(qk[sl], key_low[sl]) + bias[:, sl]
    for e in range(2):
        values = picked[e][:, 128:256]
        for sl in SLICES:
            probs = softmax_rows(scores[e][sl, :]).astype(bf)
            mixed[e][sl, :] = dot_nn(probs, values[sl]).astype(bf)
    placed = [dot_nn(tables[e][...], mixed[e][...]) for e in range(2)]
    att_ref[...] = jnp.where(low, placed[0], placed[1]).astype(bf)
    end()


def attention_forward(lengths, rounded, weight, bias, rows, arrays, shards, reps, collective_id):
    seqs = rows.shape[0]
    tokens = seqs * LEN
    column = lambda part: pl.BlockSpec((D, 128), lambda s, h, n: (0, part * PAIRS + h))
    column_b = lambda part: pl.BlockSpec((1, 128), lambda s, h, n: (0, part * PAIRS + h))
    return pl.pallas_call(
        partial(attention_forward_body, shards, reps),
        grid_spec=pltpu.PrefetchScalarGridSpec(
            num_scalar_prefetch=1,
            grid=(seqs, PAIRS),
            in_specs=[pl.BlockSpec((LEN, D), lambda s, h, n: (s, 0))]
            + [column(part) for part in range(3)]
            + [column_b(part) for part in range(3)]
            + [pl.BlockSpec((1, 1, 2, LEN), lambda s, h, n: (s, h, 0, 0))]
            + [pl.BlockSpec(memory_space=pltpu.VMEM)] * 3,
            out_specs=[
                pl.BlockSpec((LEN, 128), lambda s, h, n: (s, h)),
                pl.BlockSpec((LEN, 384), lambda s, h, n: (s, h)),
            ]
            + [pl.BlockSpec(memory_space=pl.ANY)] * 3,
            scratch_shapes=[pltpu.VMEM((LEN, LEN), bf)] * 2
            + [pltpu.VMEM((LEN, 128), f32)] * 2
            + [pltpu.VMEM((LEN, 128), bf)] * 2
            + gather_semaphores(1, shards)
            + gather_semaphores(2, shards),
        ),
        out_shape=[
            jax.ShapeDtypeStruct((tokens, D), bf),
            jax.ShapeDtypeStruct((tokens, 3 * D), bf),
        ]
        + [jax.ShapeDtypeStruct((shards,) + a.shape, bf) for a in arrays],
        compiler_params=pltpu.CompilerParams(
            vmem_limit_bytes=50 << 20, collective_id=collective_id, has_side_effects=True
        ),
        name="attention_forward",
    )(lengths, rounded, weight, weight, weight, bias, bias, bias, rows, *arrays)


def attention_backward_body(shards, reps, shapes, *refs):
    len_ref, x_ref, proj_ref, datt_ref, row_ref = refs[:5]
    grads, refs = refs[5:8], refs[8:]
    (dq_ref, dk_ref, dv_ref, dw_ref, db_ref), sums, refs = refs[:5], refs[5:9], refs[9:]
    t0, t1, s0, s1, d0, d1, p0, p1, e0, e1, total, group = refs[:12]
    refs = refs[12:]
    turn = pl.program_id(0)
    step = turn * pl.num_programs(1) + pl.program_id(1)
    place = Place(shards, reps)
    sizes = [len(reduce_scratch(shapes[k], shards, reps)) for k in "dug"]
    parts = [refs[sum(sizes[:k]) : sum(sizes[: k + 1])] for k in range(3)]
    jobs = {
        "d": Reduce(place, grads[:1], sums[:1], parts[0]),
        "u": Reduce(place, grads[1:], sums[1:3], parts[1]),
        "g": Reduce(place, [group], sums[3:], parts[2]),
    }
    end = follow(
        REDUCE_PLAN,
        jobs,
        step,
        pl.num_programs(0) * pl.num_programs(1) - 1,
        lambda: meet(place, True),
    )
    seq = pl.program_id(1)
    count = len_ref[seq]
    low = low_lanes()
    zero = jnp.zeros((), bf)
    tables, scores, back_probs, probs_low, backs = (t0, t1), (s0, s1), (d0, d1), (p0, p1), (e0, e1)
    rows = [row_ref[0, 0, e : e + 1, :] for e in range(2)]
    for e in range(2):
        tables[e][...] = table_of(rows[e])
    datt = datt_ref[...]
    swapped = half_roll(proj_ref[:, 128:256])
    middle = [jnp.where(low, datt, swapped), jnp.where(low, swapped, datt)]
    sources = [
        jnp.concatenate([proj_ref[:, 256 * e : 256 * e + 128], middle[e]], axis=1)
        for e in range(2)
    ]
    picked = [dot_tn(tables[e][...], sources[e]).astype(bf) for e in range(2)]
    for e in range(2):
        qk, dv = picked[e][:, 0:128], picked[e][:, 128:256]
        key_low = jnp.where(low, half_roll(qk), zero)
        turned = half_roll(dv)
        value_only = jnp.where(low, turned, zero) if e == 0 else jnp.where(low, zero, turned)
        bias = jnp.where(rows[e] < count, 0.0, -30000.0)
        for sl in SLICES:
            scores[e][sl, :] = 0.125 * dot_nt(qk[sl], key_low[sl]) + bias[:, sl]
            back_probs[e][sl, :] = dot_nt(dv[sl], value_only[sl])
    for e in range(2):
        for sl in SLICES:
            probs = softmax_rows(scores[e][sl, :])
            back = back_probs[e][sl, :]
            probs_low[e][sl, :] = probs.astype(bf)
            inner = jnp.sum(back * probs, axis=-1, keepdims=True)
            backs[e][sl, :] = (0.125 * (probs * (back - inner))).astype(bf)
    placed = []
    for e in range(2):
        qk, dv = picked[e][:, 0:128], picked[e][:, 128:256]
        queries, keys, values = [], [], []
        for sl in SLICES:
            back = backs[e][sl, :]
            queries.append(dot_nn(back, qk[sl]))
            keys.append(dot_tn(back, qk[sl]))
            values.append(dot_tn(probs_low[e][sl, :], dv[sl]))
        key_query = jnp.where(low, jnp.concatenate(keys, 0), jnp.concatenate(queries, 0))
        value = jnp.concatenate(values, 0)
        db_ref[0, 0, e : e + 1, :] = jnp.sum(key_query, axis=0, keepdims=True)
        db_ref[0, 0, 2 + e : 3 + e, :] = jnp.sum(value, axis=0, keepdims=True)
        parts = [key_query.astype(bf), value.astype(bf)]
        placed.append(
            dot_nn(tables[e][...], jnp.concatenate(parts, axis=1))
        )
    key_queries = [placed[e][:, 0:128] for e in range(2)]
    turned = [pltpu.roll(t, DH, 1) for t in key_queries]
    query = jnp.where(low, turned[0], key_queries[1]).astype(bf)
    key = jnp.where(low, key_queries[0], turned[1]).astype(bf)
    value = jnp.where(low, placed[0][:, 128:256], placed[1][:, 128:256]).astype(bf)
    dq_ref[...] = query
    dk_ref[...] = key
    dv_ref[...] = value
    out = jnp.concatenate([query, key, value], axis=1)
    part = dot_tn(x_ref[...], out)

    @pl.when(seq == 0)
    def _():
        total[...] = part

    @pl.when(seq != 0)
    def _():
        total[...] += part

    dw_ref[0] = total[...].astype(bf)

    @pl.when(turn < 2)
    def _():
        rows = D // shards
        columns = pl.ds(pl.multiple_of(turn * 384, 128), 384)
        for k in range(shards):
            group[k, :, columns] = total[k * rows : (k + 1) * rows, :].astype(bf)

    end()


def pair_at(i):
    return (i % 2) * (PAIRS // 2) + i // 2


def pair_at(i):
    return (i % 2) * (PAIRS // 2) + i // 2


def attention_backward(lengths, rounded, proj, datt, rows, grads, shards, reps, collective_id):
    seqs = rows.shape[0]
    tokens = seqs * LEN
    own = lambda width: pl.BlockSpec((LEN, width), lambda i, s, n: (s, pair_at(i)))
    part = (D // shards, D)
    shapes = {
        "d": [grads[0].shape[1:]],
        "u": [g.shape[1:] for g in grads[1:]],
        "g": [part],
    }
    every = shapes["d"] + shapes["u"] + shapes["g"]
    return pl.pallas_call(
        partial(attention_backward_body, shards, reps, shapes),
        grid_spec=pltpu.PrefetchScalarGridSpec(
            num_scalar_prefetch=1,
            grid=(PAIRS, seqs),
            in_specs=[
                pl.BlockSpec((LEN, D), lambda i, s, n: (s, 0)),
                own(384),
                own(128),
                pl.BlockSpec((1, 1, 2, LEN), lambda i, s, n: (s, pair_at(i), 0, 0)),
            ]
            + [pl.BlockSpec(memory_space=pl.ANY)] * 3,
            out_specs=[own(128)] * 3
            + [
                pl.BlockSpec((1, D, 384), lambda i, s, n: (i // 2, 0, i % 2)),
                pl.BlockSpec((1, 1, 4, 128), lambda i, s, n: (s, pair_at(i), 0, 0)),
            ]
            + [pl.BlockSpec(memory_space=pl.ANY)] * 4,
            scratch_shapes=[pltpu.VMEM((LEN, LEN), bf)] * 2
            + [pltpu.VMEM((LEN, 128), f32)] * 4
            + [pltpu.VMEM((LEN, 128), bf)] * 4
            + [pltpu.VMEM((D, 384), f32), pltpu.VMEM((shards,) + part, bf)]
            + sum([reduce_scratch(shapes[k], shards, reps) for k in "dug"], []),
        ),
        out_shape=[jax.ShapeDtypeStruct((tokens, D), bf)] * 3
        + [
            jax.ShapeDtypeStruct((PAIRS // 2, D, D), bf),
            jax.ShapeDtypeStruct((seqs, PAIRS, 4, 128), f32),
        ]
        + result_shapes(every),
        compiler_params=pltpu.CompilerParams(
            vmem_limit_bytes=62 << 20, collective_id=collective_id, has_side_effects=True
        ),
        name="attention_backward",
    )(lengths, rounded, proj, datt, rows, *grads)


def norm_stats(x):
    c=jnp.mean(x,axis=-1,keepdims=True)
    xc=x-c
    r=lax.rsqrt(jnp.mean(xc*xc,axis=-1,keepdims=True)+eps_norm)
    return xc*r,r

def norm_back(up,normed,r,gain):
    g=up*gain
    return r*(g-jnp.mean(g,axis=-1,keepdims=True)-normed*jnp.mean(g*normed,axis=-1,keepdims=True))

def colsum(x): return jnp.sum(x,axis=0,keepdims=True)

def gelu_parts(u):
    cdf=0.5+0.5*lax.erf(u*0.7071067811865476)
    pdf=jnp.exp(-0.5*u*u)*0.3989422804014327
    return u*cdf,cdf+u*pdf

def middle_body(len_ref,h_ref,a_ref,ct_ref,ow_ref,uw_ref,dw_ref,vec_ref,ub_ref,
               out_ref,bs_ref,ba_ref,act,pl_,low_ref,d2_ref,sl_ref,small_ref,ubg_ref,
               gp,n1_ref,*,T,sub_rows,chunk):
    i=pl.program_id(0)
    per=LEN//T
    count=len_ref[i//per]
    @pl.when(i==0)
    def _():
        small_ref[...]=jnp.zeros_like(small_ref); ubg_ref[...]=jnp.zeros_like(ubg_ref)
    out_b,g1,b1,down_b,g2,b2=[vec_ref[j:j+1,:] for j in range(6)]
    parts=[slice(k,k+sub_rows) for k in range(0,T,sub_rows)]
    r1s=[];sums=[]
    xs=[dot_nn(a_ref[p,:],ow_ref[...]) for p in parts]
    for p,x in zip(parts,xs):
        n1,r1=norm_stats(h_ref[p,:]+x+out_b)
        n1_ref[p,:]=n1; r1s.append(r1)
        low_ref[p,:]=(n1*g1+b1).astype(bf)
    for j in range(0,FF,chunk):
        sl=slice(j,j+chunk)
        for p in parts:
            u=dot_nn(low_ref[p,:],uw_ref[:,sl])+ub_ref[:,sl]
            a,g=gelu_parts(u)
            act[p,sl]=a.astype(bf); gp[p,sl]=g.astype(gp.dtype)
    ys=[dot_nn(act[p,:],dw_ref[...]) for p in parts]
    for p,y in zip(parts,ys):
        pos=lax.broadcasted_iota(jnp.int32,(sub_rows,1),0)+(i%per)*T+p.start
        valid=jnp.where(pos<count,1.0,0.0)
        second=n1_ref[p,:]*g1+b1+y+down_b
        n2,r2=norm_stats(second)
        out_ref[p,:]=valid*(n2*g2+b2)
        up=valid*ct_ref[p,:]
        b2nd=norm_back(up,n2,r2,g2)
        d2_ref[p,:]=b2nd.astype(bf)
        bs_ref[p,:]=b2nd
        sums.append(jnp.concatenate([colsum(b2nd),colsum(up*n2),colsum(up)],axis=0))
    small_ref[3:6,:]+=sum(sums[1:],sums[0])
    for j in range(0,FF,chunk):
        sl=slice(j,j+chunk)
        cs=[]
        for p in parts:
            bp=dot_nt(d2_ref[p,:],dw_ref[sl,:])*gp[p,sl].astype(f32)
            cs.append(colsum(bp))
            pl_[p,sl]=bp.astype(bf)
        ubg_ref[:,sl]+=sum(cs[1:],cs[0])
    zs=[dot_nt(pl_[p,:],uw_ref[...]) for p in parts]
    sums=[]
    for p,z,r1 in zip(parts,zs,r1s):
        bfirst=z+bs_ref[p,:]
        n1=n1_ref[p,:]
        bsum=norm_back(bfirst,n1,r1,g1)
        bs_ref[p,:]=bsum
        sl_ref[p,:]=bsum.astype(bf)
        sums.append(jnp.concatenate([colsum(bsum),colsum(bfirst*n1),colsum(bfirst)],axis=0))
    small_ref[0:3,:]+=sum(sums[1:],sums[0])
    for p in parts:
        ba_ref[p,:]=dot_nt(sl_ref[p,:],ow_ref[...]).astype(bf)

def middle(lengths,hidden,att,ct,ow,uw,dw,vec,ub,T=512,chunk=768,gpt=f32,sub_rows=256):
    tokens=hidden.shape[0]
    tile=lambda n=D: pl.BlockSpec((T,n),lambda i,l:(i,0))
    const=lambda shape: pl.BlockSpec(shape,lambda i,l:(0,0),pipeline_mode=pl.Buffered(1))
    whole=lambda shape: pl.BlockSpec(shape,lambda i,l:(0,0))
    sd=lambda n,dt: jax.ShapeDtypeStruct((tokens,n),dt)
    return pl.pallas_call(
        partial(middle_body,T=T,chunk=chunk,sub_rows=sub_rows),
        grid_spec=pltpu.PrefetchScalarGridSpec(num_scalar_prefetch=1,grid=(tokens//T,),
          in_specs=[tile(),tile(),tile(),const((D,D)),const((D,FF)),const((FF,D)),whole((8,D)),whole((1,FF))],
          out_specs=[tile(),tile(),tile(),tile(FF),tile(FF),tile(),tile(),tile(),whole((8,D)),whole((1,FF))],
          scratch_shapes=[pltpu.VMEM((T,FF),gpt),pltpu.VMEM((T,D),f32)]),
        out_shape=[sd(D,f32),sd(D,f32),sd(D,bf),sd(FF,bf),sd(FF,bf),sd(D,bf),sd(D,bf),sd(D,bf),jax.ShapeDtypeStruct((8,D),f32),jax.ShapeDtypeStruct((1,FF),f32)],
        compiler_params=pltpu.CompilerParams(vmem_limit_bytes=63<<20),
        name="middle")(lengths,hidden,att,ct,ow,uw,dw,vec,ub)


def weight_grad_body(l_ref,r_ref,out_ref):
    out_ref[...]=dot_tn(l_ref[...],r_ref[...]).astype(bf)
def weight_grad(left,right,block,name,columns=False):
    K,M=left.shape; N=right.shape[1]
    if columns:
        grid,lb,rb,ob,li,ri,oi=(N//block,),(K,M),(K,block),(M,block),(lambda i:(0,0)),(lambda i:(0,i)),(lambda i:(0,i))
    else:
        grid,lb,rb,ob,li,ri,oi=(M//block,),(K,block),(K,N),(block,N),(lambda i:(0,i)),(lambda i:(0,0)),(lambda i:(i,0))
    return pl.pallas_call(weight_grad_body,grid=grid,
        in_specs=[pl.BlockSpec(lb,li),pl.BlockSpec(rb,ri)],out_specs=pl.BlockSpec(ob,oi),
        out_shape=jax.ShapeDtypeStruct((M,N),bf),
        cost_estimate=pl.CostEstimate(flops=2*K*M*N,bytes_accessed=2*(K*M+K*N+M*N),transcendentals=0),
        compiler_params=pltpu.CompilerParams(vmem_limit_bytes=60<<20),name=name)(left,right)


def input_grad_body(shards,reps,shapes,bs_ref,dq_ref,dk_ref,dv_ref,w_ref,*refs):
    n=len(shapes)
    grads,out_ref,sums,scratch=refs[:n],refs[n],refs[n+1:2*n+1],refs[2*n+1:]
    place=Place(shards,reps); step=pl.program_id(0)
    end=follow(LAST_PLAN,{"r":Reduce(place,grads,sums,scratch)},step,pl.num_programs(0)-1,lambda: meet(place,True))
    out_ref[...]=bs_ref[...]+dot_nt(dq_ref[...],w_ref[:,0:D])+dot_nt(dk_ref[...],w_ref[:,D:2*D])+dot_nt(dv_ref[...],w_ref[:,2*D:3*D])
    end()
def input_grad(back_sum,dq,dk,dv,weight,grads,shards,reps,collective_id):
    rows=back_sum.shape[0]//4
    tile=pl.BlockSpec((rows,D),lambda i:(i,0))
    anywhere=[pl.BlockSpec(memory_space=pl.ANY)]*len(grads)
    shapes=[g.shape[1:] for g in grads]
    return pl.pallas_call(partial(input_grad_body,shards,reps,shapes),grid=(4,),
        in_specs=[tile]*4+[pl.BlockSpec((D,3*D),lambda i:(0,0),pipeline_mode=pl.Buffered(1))]+anywhere,
        out_specs=[tile]+anywhere,
        out_shape=[jax.ShapeDtypeStruct(back_sum.shape,f32)]+result_shapes(shapes),
        scratch_shapes=reduce_scratch(shapes,shards,reps),
        compiler_params=pltpu.CompilerParams(vmem_limit_bytes=50<<20,collective_id=collective_id,has_side_effects=True),name="input_grad")(back_sum,dq,dk,dv,weight,*grads)


WIDE = 4096


def shard_vectors(vectors):
    row = jnp.concatenate(vectors)
    return jnp.pad(row, (0, WIDE - row.shape[0])).reshape(16, 256)


def local(
    hidden,
    lengths,
    clusters,
    input_weight,
    query_bias,
    value_bias,
    out_weight,
    out_bias,
    norm1_gain,
    norm1_bias,
    up_weight,
    up_bias,
    down_weight,
    down_bias,
    norm2_gain,
    norm2_bias,
    cotangent,
    *,
    shards,
    reps,
):
    seqs = hidden.shape[0]
    tokens = seqs * LEN
    part = D // shards
    vectors = shard_vectors(
        (
            query_bias,
            value_bias,
            out_bias,
            norm1_gain,
            norm1_bias,
            down_bias,
            norm2_gain,
            norm2_bias,
            up_bias,
        )
    )
    in_w, vectors = gather_now((input_weight, vectors), shards, reps, 1)
    in_w = in_w.reshape(D, 3 * D)
    vectors = vectors.reshape(shards, WIDE).astype(f32)
    table = vectors[:, : 8 * part].reshape(shards, 8, part).transpose(1, 0, 2).reshape(8, D)
    bias_all = jnp.concatenate([table[0], jnp.zeros((D,), f32), table[1]])[None]
    norm_rows = jnp.concatenate([table[2:], table[:2]])
    up_b = vectors[:, 8 * part : 8 * part + FF // shards].reshape(1, FF)

    flat = hidden.reshape(tokens, D)
    rounded = flat.astype(bf)
    rows = clusters.reshape(seqs, PAIRS, 2, LEN)
    attended, proj, up_w, down_w, out_w = attention_forward(
        lengths,
        rounded,
        in_w,
        bias_all,
        rows,
        (up_weight, down_weight, out_weight),
        shards,
        reps,
        2,
    )
    out_w, up_w, down_w = [w.reshape(-1, w.shape[-1]) for w in (out_w, up_w, down_w)]
    (
        result,
        back_sum,
        back_attended,
        activated,
        pre_low,
        first_low,
        second_low,
        sum_low,
        norm_sums,
        up_b_sum,
    ) = middle(
        lengths,
        flat,
        attended,
        cotangent.reshape(tokens, D),
        out_w,
        up_w,
        down_w,
        norm_rows,
        up_b,
    )
    down_g = weight_grad(activated, second_low, D, "down_weight_grad")
    up_g = weight_grad(first_low, pre_low, D, "up_weight_grad", True)
    out_g = weight_grad(attended, sum_low, D // 2, "out_weight_grad")
    dq, dk, dv, in_g, bias_sums, down_s, up_s, out_s, in_first = attention_backward(
        lengths,
        rounded,
        proj,
        back_attended,
        rows,
        [g.reshape(shards, -1, g.shape[-1]) for g in (down_g, up_g, out_g)],
        shards,
        reps,
        3,
    )
    bias_sums = jnp.sum(bias_sums, axis=0)
    query_sum = bias_sums[:, 0:2, DH:].reshape(D)
    value_sum = jnp.concatenate([bias_sums[:, 2, :DH], bias_sums[:, 3, DH:]], axis=1).reshape(D)
    table = jnp.concatenate([query_sum[None], value_sum[None], norm_sums[:6]])
    small = jnp.concatenate(
        [
            table.reshape(8, shards, part).transpose(1, 0, 2).reshape(shards, 8 * part),
            up_b_sum.reshape(shards, FF // shards),
        ],
        axis=1,
    ).astype(bf)
    small = jnp.pad(small, ((0, 0), (0, WIDE - small.shape[1]))).reshape(shards, 16, 256)
    back_input, *in_s, small_s = input_grad(
        back_sum,
        dq,
        dk,
        dv,
        in_w,
        [in_g[g].reshape(shards, part, D) for g in range(1, PAIRS // 2)] + [small],
        shards,
        reps,
        4,
    )
    back_input = back_input.reshape(seqs, LEN, D)
    in_s = [in_first] + in_s
    in_s = jnp.concatenate(
        [
            in_s[g][c, :, 128 * t : 128 * t + 128]
            for t in range(3)
            for c in range(2)
            for g in range(PAIRS // 2)
        ],
        axis=1,
    )

    def whole(halves):
        return jnp.concatenate([halves[0], halves[1]], axis=1)

    small_s = whole(small_s).reshape(WIDE)
    vec = [small_s[i * part : (i + 1) * part] for i in range(8)]
    return (
        result.reshape(seqs, LEN, D),
        back_input,
        in_s,
        vec[0],
        vec[1],
        whole(out_s),
        vec[2],
        vec[3],
        vec[4],
        whole(up_s),
        small_s[8 * part : 8 * part + FF // shards],
        whole(down_s),
        vec[5],
        vec[6],
        vec[7],
    )


def solution(mesh):
    tokens = P(("rep", "shard"), None, None)
    matrix, vector = P("shard", None), P("shard")
    params = (
        matrix,
        vector,
        vector,
        matrix,
        vector,
        vector,
        vector,
        matrix,
        vector,
        matrix,
        vector,
        vector,
        vector,
    )
    return jax.shard_map(
        partial(local, shards=mesh.shape["shard"], reps=mesh.shape["rep"]),
        mesh=mesh,
        in_specs=(tokens, P(("rep", "shard")), tokens) + params + (tokens,),
        out_specs=(tokens, tokens) + params,
        check_vma=False,
    )
```

```python
from functools import partial

import jax
import jax.numpy as jnp
from jax import lax
from jax.experimental import pallas as pl
from jax.experimental.pallas import tpu as pltpu
from jax.sharding import PartitionSpec as P

D = 768
H = 12
DH = 64
FF = 3072
CLUSTER = 128
LEN = 1024
PAIRS = H // 2
SLICES = [slice(c * CLUSTER, (c + 1) * CLUSTER) for c in range(LEN // CLUSTER)]
bf = jnp.bfloat16
f32 = jnp.float32
eps_norm = 1e-12


def dot_nn(left, right):
    return lax.dot_general(left, right, (((1,), (0,)), ((), ())), preferred_element_type=f32)


def dot_nt(left, right):
    return lax.dot_general(left, right, (((1,), (1,)), ((), ())), preferred_element_type=f32)


def dot_tn(left, right):
    return lax.dot_general(left, right, (((0,), (0,)), ((), ())), preferred_element_type=f32)


ROWS = 4
MESH=pl.DeviceIdType.MESH

def when(cond,do):
    if cond is None: do()
    else: pl.when(cond)(do)

class Place:
    def __init__(self,shards,reps):
        self.Y=shards//ROWS; self.S=shards; self.X=reps//2
        self.s=lax.axis_index("shard"); self.r=lax.axis_index("rep")
        self.z=self.s//self.Y; self.y=lax.rem(self.s,self.Y)
        self.core=lax.rem(self.r,2); self.x=self.r//2
    def near_z(self,step): return {"shard":self.s+step*self.Y}
    def other_y(self,k): return {"shard":self.z*self.Y+lax.rem(self.y+k,self.Y)}
    def other_core(self): return {"rep":self.r+1-2*self.core}
    def other_x(self,k): return {"rep":2*lax.rem(self.x+k,self.X)+self.core}

def meet(place,with_x):
    sem=pltpu.get_barrier_semaphore()
    def tell(dev): pl.semaphore_signal(sem,inc=1,device_id=dev,device_id_type=MESH)
    pl.when(place.z>0)(lambda: tell(place.near_z(-1)))
    pl.when(place.z<ROWS-1)(lambda: tell(place.near_z(1)))
    for k in range(1,place.Y): tell(place.other_y(k))
    tell(place.other_core())
    if with_x:
        for k in range(1,place.X): tell(place.other_x(k))
    others=place.Y+(place.X-1 if with_x else 0)
    inner=jnp.logical_and(place.z>0,place.z<ROWS-1)
    pl.when(inner)(lambda: pl.semaphore_wait(sem,others+2))
    pl.when(jnp.logical_not(inner))(lambda: pl.semaphore_wait(sem,others+1))

def gather_semaphores(count,shards):
    Y=shards//ROWS; dma=pltpu.SemaphoreType.DMA
    return [dma((count,2,ROWS)),dma((count,2,ROWS)),dma((count,ROWS,Y)),dma((count,ROWS,Y)),
            dma((count,2,shards)),dma((count,2,shards)),dma((count,shards)),dma((count,shards)),dma((count,))]

class Gather:
    def __init__(self,place,ins,outs,sems,share=False):
        self.p=place; self.ins=ins; self.outs=outs; self.share=share and place.X==2
        self.line_s,self.line_r,self.y_s,self.y_r,self.core_s,self.core_r,self.x_s,self.x_r,self.own=sems
        self.sent=[]
    def piece(self,ref,shard=None,core=None,x=None):
        p=self.p; n=ref.shape[-1]//2; r=ref.shape[-2]
        cols=pl.ds(pl.multiple_of((p.core if core is None else core)*n,128),n)
        rows=slice(None)
        if self.share:
            rows=pl.ds(pl.multiple_of((p.x if x is None else x)*(r//2),16),r//2)
        return ref.at[rows,cols] if shard is None else ref.at[shard,rows,cols]
    def send(self,make):
        cond,desc=make()
        when(cond,desc.start); self.sent.append(make)
    def copy(self,src,dst,ss,rs,dev):
        return pltpu.make_async_remote_copy(src_ref=src,dst_ref=dst,send_sem=ss,recv_sem=rs,device_id=dev,device_id_type=MESH)
    def at(self,places):
        zz=self.p.z+places
        if places==0: return None,zz
        return jnp.logical_and(zz>=0,zz<ROWS),jnp.clip(zz,0,ROWS-1)
    def shard_at(self,zz,k):
        p=self.p
        return zz*p.Y+(lax.rem(p.y-k+p.Y,p.Y) if k else p.y)
    def to_line(self,a,places,d):
        p=self.p; i,o=self.ins[a],self.outs[a]
        def make():
            cond,zz=self.at(places); shard=zz*p.Y+p.y
            edge=(p.z<ROWS-1) if d==0 else (p.z>0)
            src=self.piece(i) if places==0 else self.piece(o,shard)
            return (edge if cond is None else jnp.logical_and(cond,edge)),self.copy(src,self.piece(o,shard),self.line_s.at[a,d,zz],self.line_r.at[a,d,zz],p.near_z(1 if d==0 else -1))
        self.send(make)
    def to_y(self,a,places,k):
        p=self.p; i,o=self.ins[a],self.outs[a]
        def make():
            cond,zz=self.at(places); shard=zz*p.Y+p.y
            src=self.piece(i) if places==0 else self.piece(o,shard)
            return cond,self.copy(src,self.piece(o,shard),self.y_s.at[a,zz,k],self.y_r.at[a,zz,k],p.other_y(k))
        self.send(make)
    def to_core(self,a,places,k,other=False):
        p=self.p; o=self.outs[a]; slot=1 if other else 0
        def make():
            cond,zz=self.at(places); shard=self.shard_at(zz,k)
            ref=self.piece(o,shard,x=1-p.x if other else p.x)
            return cond,self.copy(ref,ref,self.core_s.at[a,slot,shard],self.core_r.at[a,slot,shard],p.other_core())
        self.send(make)
    def to_x(self,a,places,k):
        p=self.p; o=self.outs[a]
        if not self.share: return
        def make():
            cond,zz=self.at(places); shard=self.shard_at(zz,k)
            ref=self.piece(o,shard)
            return cond,self.copy(ref,ref,self.x_s.at[a,shard],self.x_r.at[a,shard],p.other_x(1))
        self.send(make)
    def begin(self):
        for a,(i,o) in enumerate(zip(self.ins,self.outs)):
            for d in (0,1): self.to_line(a,0,d)
            for k in range(1,self.p.Y): self.to_y(a,0,k)
            pltpu.make_async_copy(i,o.at[self.p.s],self.own.at[a]).start()
    def wave(self,w):
        p=self.p
        for d in (0,1):
            places=-w if d==0 else w
            for a,o in enumerate(self.outs):
                cond,zz=self.at(places); ref=self.piece(o,zz*p.Y+p.y)
                when(cond,self.copy(ref,ref,self.line_s.at[a,d,zz],self.line_r.at[a,d,zz],p.near_z(0)).wait_recv)
                self.to_line(a,places,d)
                for k in range(1,p.Y): self.to_y(a,places,k)
                self.to_x(a,places,0); self.to_core(a,places,0)
    def across(self,w):
        p=self.p
        for places in ((0,) if w==0 else (-w,w)):
            for k in range(1,p.Y):
                for a,o in enumerate(self.outs):
                    cond,zz=self.at(places); ref=self.piece(o,self.shard_at(zz,k))
                    when(cond,self.copy(ref,ref,self.y_s.at[a,zz,k],self.y_r.at[a,zz,k],p.other_y(k)).wait_recv)
                    self.to_x(a,places,k); self.to_core(a,places,k)
    def over(self,w):
        p=self.p
        if not self.share: return
        for places in ((0,) if w==0 else (-w,w)):
            for k in range(1 if w==0 else 0,p.Y):
                for a,o in enumerate(self.outs):
                    cond,zz=self.at(places); shard=self.shard_at(zz,k); ref=self.piece(o,shard,x=1-p.x)
                    when(cond,self.copy(ref,ref,self.x_s.at[a,shard],self.x_r.at[a,shard],p.other_x(1)).wait_recv)
                    self.to_core(a,places,k,True)
    def finish(self):
        p=self.p
        for a,(i,o) in enumerate(zip(self.ins,self.outs)):
            for k in range(1,p.S):
                shard=lax.rem(p.s+k,p.S)
                for slot in range(2 if self.share else 1):
                    ref=self.piece(o,shard,core=1-p.core,x=1-p.x if slot else p.x)
                    self.copy(ref,ref,self.core_s.at[a,slot,shard],self.core_r.at[a,slot,shard],p.other_core()).wait_recv()
            pltpu.make_async_copy(i,o.at[p.s],self.own.at[a]).wait()
        for make in self.sent:
            cond,desc=make()
            when(cond,desc.wait_send)
def gather_body(shards,reps,count,*refs):
    ins,outs,sems=refs[:count],refs[count:2*count],refs[2*count:]
    place=Place(shards,reps)
    meet(place,False)
    G=Gather(place,ins,outs,sems)
    G.begin(); G.wave(1); G.across(0); G.wave(2); G.across(1); G.wave(3); G.across(2); G.across(3); G.finish()

def gather_now(arrays,shards,reps,collective_id):
    count=len(arrays)
    return pl.pallas_call(partial(gather_body,shards,reps,count),
        in_specs=[pl.BlockSpec(memory_space=pltpu.VMEM)]*count,
        out_specs=[pl.BlockSpec(memory_space=pl.ANY)]*count,
        out_shape=[jax.ShapeDtypeStruct((shards,)+a.shape,a.dtype) for a in arrays],
        scratch_shapes=gather_semaphores(count,shards),
        compiler_params=pltpu.CompilerParams(collective_id=collective_id,has_side_effects=True,vmem_limit_bytes=16<<20),
        name="gather_weights")(*arrays)

ORDER=(3,0,2,1)
def reduce_scratch(shapes,shards,reps,x_first=False):
    x_first=x_first and reps==4
    S=shards; Y=S//ROWS; X=reps//2; A=len(shapes)
    out=[]
    for r,c in shapes:
        n=c//2; m=r//2 if x_first else r
        out+=[pltpu.VMEM((S,r,n),bf),pltpu.VMEM((S,r,n),bf),pltpu.VMEM((max(Y-1,1),ROWS,m,n),bf),
              pltpu.VMEM((ROWS+1,m,n),bf),pltpu.VMEM((S+1,m,n) if x_first else (X,r,n),bf),pltpu.VMEM((2,r,n),f32)]
    dma=pltpu.SemaphoreType.DMA
    return out+[dma((A,S)),dma((A,S)),dma((A,S)),dma((A,Y,ROWS)),dma((A,Y,ROWS)),dma((A,ROWS+1)),dma((A,ROWS+1)),dma((A,S+X)),dma((A,S+X)),dma((A,)),dma((A,)),dma((A,))]
class Reduce:
    def __init__(self,place,ins,outs,scratch,x_first=False):
        self.p=place; self.ins=ins; self.outs=outs; A=len(ins); self.A=range(A)
        self.bufs=[scratch[6*a:6*a+6] for a in range(A)]
        (self.own,self.core_s,self.core_r,self.y_s,self.y_r,self.line_s,self.line_r,self.x_s,self.x_r,self.end_s,self.end_r,self.out_s)=scratch[6*A:]
        self.sent=[]; self.x_first=x_first and place.X==2
    def copy(self,src,dst,ss,rs,dev):
        return pltpu.make_async_remote_copy(src_ref=src,dst_ref=dst,send_sem=ss,recv_sem=rs,device_id=dev,device_id_type=MESH)
    def send(self,make):
        cond,desc=make()
        when(cond,desc.start); self.sent.append(make)
    def half(self,a,shard,core):
        n=self.ins[a].shape[-1]//2
        return self.ins[a].at[shard,:,pl.ds(pl.multiple_of(core*n,128),n)]
    def mine(self,a,shard,x=None):
        H=self.bufs[a][0]
        if not self.x_first: return H.at[shard]
        m=H.shape[1]//2
        return H.at[shard,pl.ds(pl.multiple_of((self.p.x if x is None else x)*m,16),m)]
    def add(self,dst,others):
        rows,n=dst.shape; step=next(s for s in (192,96,48,16) if rows%s==0 and (s==16 or s*n<=96*768))
        def block(at):
            value=dst[at,:]
            for o in others: value=value+o[at,:]
            dst[at,:]=value
        if rows==step: block(slice(0,rows)); return
        def body(i,_):
            block(pl.ds(pl.multiple_of(i*step,16),step))
            return 0
        lax.fori_loop(0,rows//step,body,0)
    def begin(self):
        p=self.p
        for k in list(range(1,p.Y))+[0]:
            for d in ORDER:
                for a in self.A:
                    H,Rc=self.bufs[a][0:2]
                    def make(a=a,d=d,k=k,Rc=Rc):
                        shard=d*p.Y+lax.rem(p.y+k,p.Y)
                        return None,self.copy(self.half(a,shard,1-p.core),Rc.at[shard],self.core_s.at[a,shard],self.core_r.at[a,shard],p.other_core())
                    self.send(make)
                    shard=d*p.Y+lax.rem(p.y+k,p.Y)
                    pltpu.make_async_copy(self.half(a,shard,p.core),H.at[shard],self.own.at[a,shard]).start()
    def join_core(self,shard):
        p=self.p
        for a in self.A:
            H,Rc=self.bufs[a][0:2]
            pltpu.make_async_copy(self.half(a,shard,p.core),H.at[shard],self.own.at[a,shard]).wait()
            self.copy(Rc.at[shard],Rc.at[shard],self.core_s.at[a,shard],self.core_r.at[a,shard],p.other_core()).wait_recv()
            self.add(H.at[shard],[Rc.at[shard]])
    def to_pair(self,k,d):
        p=self.p; shard=d*p.Y+lax.rem(p.y+k,p.Y)
        if not self.x_first: return
        self.join_core(shard)
        for a in self.A:
            def make(a=a):
                shard=d*p.Y+lax.rem(p.y+k,p.Y)
                return None,self.copy(self.mine(a,shard,1-p.x),self.bufs[a][4].at[shard],self.x_s.at[a,shard],self.x_r.at[a,shard],p.other_x(1))
            self.send(make)
    def ready(self,shard):
        p=self.p
        if not self.x_first: self.join_core(shard); return
        for a in self.A:
            got=self.bufs[a][4].at[shard]
            self.copy(got,got,self.x_s.at[a,shard],self.x_r.at[a,shard],p.other_x(1)).wait_recv()
            self.add(self.mine(a,shard),[got])
    def to_y(self,d):
        p=self.p
        for k in range(1,p.Y):
            self.ready(d*p.Y+lax.rem(p.y+k,p.Y))
            for a in self.A:
                H,_,Ry=self.bufs[a][0:3]
                def make(a=a,H=H,Ry=Ry,k=k):
                    shard=d*p.Y+lax.rem(p.y+k,p.Y)
                    return None,self.copy(self.mine(a,shard),Ry.at[k-1,d],self.y_s.at[a,k,d],self.y_r.at[a,k,d],p.other_y(k))
                self.send(make)
    def own_y(self,d):
        self.ready(d*self.p.Y+self.p.y)
    def along(self,d,up,j):
        p=self.p
        if (j>=d) if up else (ROWS-1-j<=d): return
        here=p.z==(j if up else ROWS-1-j)
        shard=d*p.Y+p.y
        if j>0:
            def add_in():
                for a in self.A:
                    H,Rl=self.bufs[a][0],self.bufs[a][3]
                    self.copy(Rl.at[d],Rl.at[d],self.line_s.at[a,d],self.line_r.at[a,d],p.near_z(0)).wait_recv()
                    self.add(self.mine(a,shard),[Rl.at[d]])
            pl.when(here)(add_in)
        last=(j==d-1) if up else (ROWS-1-j==d+1)
        slot=ROWS if last and not up else d
        for a in self.A:
            def make(a=a):
                H,Rl=self.bufs[a][0],self.bufs[a][3]
                return p.z==(j if up else ROWS-1-j),self.copy(self.mine(a,d*p.Y+p.y),Rl.at[slot],self.line_s.at[a,slot],self.line_r.at[a,slot],p.near_z(1 if up else -1))
            self.send(make)
    def line(self,d):
        p=self.p; shard=d*p.Y+p.y
        for a in self.A:
            H,_,Ry=self.bufs[a][0:3]
            for k in range(1,p.Y):
                self.copy(Ry.at[k-1,d],Ry.at[k-1,d],self.y_s.at[a,k,d],self.y_r.at[a,k,d],p.other_y(k)).wait_recv()
            self.add(self.mine(a,shard),[Ry.at[k-1,d] for k in range(1,p.Y)])
        self.along(d,True,0); self.along(d,False,0)
    def relay(self,d,j):
        self.along(d,True,j); self.along(d,False,j)
    def to_x(self):
        p=self.p
        for slot,cond in ((p.z,p.z>0),(ROWS,p.z<ROWS-1)):
            def add_in(slot=slot):
                for a in self.A:
                    H,Rl=self.bufs[a][0],self.bufs[a][3]
                    self.copy(Rl.at[slot],Rl.at[slot],self.line_s.at[a,slot],self.line_r.at[a,slot],p.near_z(0)).wait_recv()
                    self.add(self.mine(a,p.s),[Rl.at[slot]])
            pl.when(cond)(add_in)
        for a in self.A:
            H,Rx=self.bufs[a][0],self.bufs[a][4]
            if self.x_first:
                self.send(lambda a=a,Rx=Rx: (None,self.copy(self.mine(a,p.s),Rx.at[p.S],self.x_s.at[a,p.S],self.x_r.at[a,p.S],p.other_x(1))))
                continue
            for k in range(1,p.X):
                self.send(lambda a=a,H=H,Rx=Rx,k=k: (None,self.copy(H.at[p.s],Rx.at[p.x],self.x_s.at[a,k],self.x_r.at[a,p.x],p.other_x(k))))
    def to_core(self):
        p=self.p
        for a in self.A:
            H,Rx,F=self.bufs[a][0],self.bufs[a][4],self.bufs[a][5]
            if self.x_first:
                got=Rx.at[p.S]; m=H.shape[1]//2
                self.copy(got,got,self.x_s.at[a,p.S],self.x_r.at[a,p.S],p.other_x(1)).wait_recv()
                for x in range(2):
                    own=H[p.s,x*m:(x+1)*m,:]
                    F[p.core,x*m:(x+1)*m,:]=jnp.where(p.x==x,own,Rx[p.S]).astype(f32)
                continue
            for k in range(1,p.X):
                src=lax.rem(p.x-k+p.X,p.X)
                self.copy(Rx.at[src],Rx.at[src],self.x_s.at[a,k],self.x_r.at[a,src],p.other_x(k)).wait_recv()
            rows=H.shape[1]; step=48 if rows%48==0 else 16
            def body(i,_):
                at=pl.ds(pl.multiple_of(i*step,16),step)
                own=H[p.s,at,:].astype(f32)
                value=jnp.zeros_like(own)
                for q in range(p.X):
                    value=value+jnp.where(p.x==q,own,Rx[q,at,:].astype(f32))
                F[p.core,at,:]=value
                return 0
            lax.fori_loop(0,rows//step,body,0)
        for a in self.A:
            F=self.bufs[a][5]
            self.send(lambda a=a,F=F: (None,self.copy(F.at[p.core],F.at[p.core],self.end_s.at[a],self.end_r.at[a],p.other_core())))
    def finish(self):
        p=self.p
        for a in self.A:
            F=self.bufs[a][5]; ref=F.at[1-p.core]
            self.copy(ref,ref,self.end_s.at[a],self.end_r.at[a],p.other_core()).wait_recv()
            pltpu.make_async_copy(F,self.outs[a],self.out_s.at[a]).start()
        for make in self.sent:
            cond,desc=make()
            when(cond,desc.wait_send)
        for a in self.A: pltpu.make_async_copy(self.bufs[a][5],self.outs[a],self.out_s.at[a]).wait()
    def run(self,what,*args): getattr(self,what)(*args)
def result_shapes(shapes):
    return [jax.ShapeDtypeStruct((2,r,c//2),f32) for r,c in shapes]

GATHER_PLAN = {
    0: (("u", "begin"), ("d", "begin")),
    2: (("u", "wave", 1),),
    3: (("d", "wave", 1), ("u", "across", 0), ("d", "across", 0)),
    4: (("u", "wave", 2),),
    5: (("d", "wave", 2),),
    6: (("u", "across", 1), ("d", "over", 0)),
    7: (("u", "wave", 3),),
    8: (("d", "wave", 3), ("d", "across", 1)),
    9: (("u", "across", 2), ("u", "across", 3)),
    10: (("d", "across", 2), ("d", "across", 3), ("d", "over", 1)),
    100: (("d", "over", 2), ("d", "over", 3), ("u", "finish"), ("d", "finish")),
}


def each(name, what, *more):
    return tuple((name, what, d) + more for d in ORDER)


REDUCE_PLAN = {
    0: (("d", "begin"), ("u", "begin")),
    1: each("d", "to_y"),
    2: tuple(("u", "to_pair", 1, d) for d in ORDER) + each("d", "own_y"),
    3: tuple(("u", "to_pair", 0, d) for d in ORDER) + (("d", "line", 3),),
    4: (("g", "begin"), ("d", "line", 0)),
    5: each("u", "to_y") + (("d", "line", 2), ("d", "relay", 3, 1)),
    6: each("g", "to_y") + each("g", "own_y") + (("d", "line", 1), ("d", "relay", 0, 1)),
    7: (("d", "relay", 3, 2), ("d", "relay", 2, 1), ("u", "own_y", 3), ("u", "own_y", 0)),
    8: (("d", "relay", 0, 2), ("d", "relay", 1, 1), ("u", "own_y", 2), ("u", "own_y", 1))
    + (("u", "line", 3), ("u", "line", 0)),
    9: (("d", "to_x"), ("u", "line", 2), ("u", "line", 1), ("u", "relay", 3, 1), ("u", "relay", 0, 1)),
    10: (("d", "to_core"), ("u", "relay", 2, 1), ("u", "relay", 3, 2), ("u", "relay", 0, 2))
    + each("g", "line"),
    11: (("u", "relay", 1, 1),) + each("g", "relay", 1),
    100: each("g", "relay", 2)
    + (
        ("u", "to_x"),
        ("g", "to_x"),
        ("u", "to_core"),
        ("g", "to_core"),
        ("d", "finish"),
        ("u", "finish"),
        ("g", "finish"),
    ),
}
LAST_PLAN = {
    0: (("a", "begin"), ("b", "begin")),
    1: each("a", "to_y"),
    2: tuple(("b", "to_pair", k, d) for k in (1, 0) for d in ORDER) + each("a", "own_y"),
    4: (("a", "line", 3), ("a", "line", 0)),
    5: (("a", "line", 2), ("a", "line", 1)) + each("b", "to_y"),
    6: each("b", "own_y") + each("a", "relay", 1),
    7: (("a", "relay", 3, 2), ("a", "relay", 0, 2)) + each("b", "line"),
    100: (("a", "to_x"),)
    + each("b", "relay", 1)
    + (("a", "to_core"),)
    + each("b", "relay", 2)
    + (("b", "to_x"), ("b", "to_core"), ("a", "finish"), ("b", "finish")),
}


def follow(plan, jobs, step, last, ready):
    def run(at):
        for name, what, *more in plan.get(at, ()):
            getattr(jobs[name], what)(*more)

    def first():
        ready()
        run(0)

    pl.when(step == 0)(first)
    for at in sorted(plan):
        if 0 < at < 100:
            pl.when(step == at)(partial(run, at))
    return lambda: pl.when(step == last)(partial(run, 100))


def low_lanes():
    return lax.broadcasted_iota(jnp.int32, (LEN, CLUSTER), 1) < DH


def table_of(order_row):
    held = jnp.broadcast_to(order_row.astype(jnp.int16), (LEN, LEN))
    positions = lax.broadcasted_iota(jnp.int16, (LEN, LEN), 0)
    return jnp.where(held == positions, jnp.ones((), bf), jnp.zeros((), bf))


def turned_table_of(order_row):
    held = jnp.transpose(jnp.broadcast_to(order_row, (128, LEN))).astype(jnp.int16)
    lanes = lax.broadcasted_iota(jnp.int16, (LEN, 128), 1)
    return jnp.concatenate(
        [
            jnp.where(held == lanes + jnp.int16(128 * b), jnp.ones((), bf), jnp.zeros((), bf))
            for b in range(LEN // 128)
        ],
        axis=1,
    )


def half_roll(source):
    return pltpu.roll(source, DH, 1)


def softmax_rows(scores):
    top = jnp.max(scores, axis=-1, keepdims=True)
    grown = jnp.exp(scores - top)
    return grown * (1.0 / jnp.sum(grown, axis=-1, keepdims=True))


def attention_forward_body(
    shards, reps, len_ref, h_ref, wq_ref, wk_ref, wv_ref, bq_ref, bk_ref, bv_ref, row_ref, *rest
):
    ins, (att_ref, proj_ref, x_ref), outs = rest[:3], rest[3:6], rest[6:9]
    tables, scores, mixed = rest[9:11], rest[11:13], rest[13:15]
    sems = rest[15:]
    step = pl.program_id(0) * PAIRS + pl.program_id(1)
    place = Place(shards, reps)
    jobs = {
        "u": Gather(place, ins[:1], outs[:1], sems[:9]),
        "d": Gather(place, ins[1:], outs[1:], sems[9:], True),
    }
    end = follow(
        GATHER_PLAN, jobs, step, pl.num_programs(0) * PAIRS - 1, lambda: meet(place, True)
    )

    @pl.when(pl.program_id(1) == 0)
    def _():
        x_ref[...] = h_ref[...].astype(bf)

    count = len_ref[pl.program_id(0)]
    weight = jnp.concatenate([wq_ref[...], wk_ref[...], wv_ref[...]], axis=1)
    bias = jnp.concatenate([bq_ref[...], bk_ref[...], bv_ref[...]], axis=1)
    proj = (dot_nn(x_ref[...], weight) + bias).astype(bf)
    low = low_lanes()
    query, key, value = proj[:, 0:128], proj[:, 128:256], proj[:, 256:384]
    pairs = [jnp.where(low, query, half_roll(key)), jnp.where(low, half_roll(query), key)]
    proj_ref[...] = jnp.concatenate([pairs[0], value, pairs[1]], axis=1)
    rows = [row_ref[0, pl.ds(2 * pl.program_id(1) + e, 1), :] for e in range(2)]
    for e in range(2):
        tables[e][...] = table_of(rows[e])
    picked = [
        dot_nn(turned_table_of(rows[e]), jnp.concatenate([pairs[e], value], axis=1)).astype(bf)
        for e in range(2)
    ]
    for e in range(2):
        qk = picked[e][:, 0:128]
        key_low = jnp.where(low, half_roll(qk), jnp.zeros((), bf))
        bias = jnp.where(rows[e] < count, 0.0, -30000.0)
        for sl in SLICES:
            scores[e][sl, :] = 0.125 * dot_nt(qk[sl], key_low[sl]) + bias[:, sl]
    for e in range(2):
        values = picked[e][:, 128:256]
        for sl in SLICES:
            probs = softmax_rows(scores[e][sl, :]).astype(bf)
            mixed[e][sl, :] = dot_nn(probs, values[sl]).astype(bf)
    placed = [dot_nn(tables[e][...], mixed[e][...]) for e in range(2)]
    att_ref[...] = jnp.where(low, placed[0], placed[1]).astype(bf)
    end()


def attention_forward(lengths, hidden, weight, bias, rows, arrays, shards, reps, collective_id):
    seqs = rows.shape[0]
    tokens = seqs * LEN
    column = lambda part: pl.BlockSpec((D, 128), lambda s, h, n: (0, part * PAIRS + h))
    column_b = lambda part: pl.BlockSpec((1, 128), lambda s, h, n: (0, part * PAIRS + h))
    return pl.pallas_call(
        partial(attention_forward_body, shards, reps),
        grid_spec=pltpu.PrefetchScalarGridSpec(
            num_scalar_prefetch=1,
            grid=(seqs, PAIRS),
            in_specs=[pl.BlockSpec((LEN, D), lambda s, h, n: (s, 0))]
            + [column(part) for part in range(3)]
            + [column_b(part) for part in range(3)]
            + [pl.BlockSpec((1, H, LEN), lambda s, h, n: (s, 0, 0))]
            + [pl.BlockSpec(memory_space=pltpu.VMEM)] * 3,
            out_specs=[
                pl.BlockSpec((LEN, 128), lambda s, h, n: (s, h)),
                pl.BlockSpec((LEN, 384), lambda s, h, n: (s, h)),
                pl.BlockSpec((LEN, D), lambda s, h, n: (s, 0)),
            ]
            + [pl.BlockSpec(memory_space=pl.ANY)] * 3,
            scratch_shapes=[pltpu.VMEM((LEN, LEN), bf)] * 2
            + [pltpu.VMEM((LEN, 128), f32)] * 2
            + [pltpu.VMEM((LEN, 128), bf)] * 2
            + gather_semaphores(1, shards)
            + gather_semaphores(2, shards),
        ),
        out_shape=[
            jax.ShapeDtypeStruct((tokens, D), bf),
            jax.ShapeDtypeStruct((tokens, 3 * D), bf),
            jax.ShapeDtypeStruct((tokens, D), bf),
        ]
        + [jax.ShapeDtypeStruct((shards,) + a.shape, bf) for a in arrays],
        compiler_params=pltpu.CompilerParams(
            vmem_limit_bytes=50 << 20, collective_id=collective_id, has_side_effects=True
        ),
        name="attention_forward",
    )(lengths, hidden, weight, weight, weight, bias, bias, bias, rows, *arrays)


def attention_backward_body(shards, reps, shapes, *refs):
    len_ref, x_ref, proj_ref, datt_ref, row_ref = refs[:5]
    grads, refs = refs[5:8], refs[8:]
    (dq_ref, dk_ref, dv_ref, dw_ref, db_ref), sums, refs = refs[:5], refs[5:9], refs[9:]
    t0, t1, s0, s1, d0, d1, p0, p1, e0, e1, total, group = refs[:12]
    refs = refs[12:]
    turn = pl.program_id(0)
    step = turn * pl.num_programs(1) + pl.program_id(1)
    place = Place(shards, reps)
    sizes = [len(reduce_scratch(shapes[k], shards, reps, k == "u")) for k in "dug"]
    parts = [refs[sum(sizes[:k]) : sum(sizes[: k + 1])] for k in range(3)]
    jobs = {
        "d": Reduce(place, grads[:1], sums[:1], parts[0]),
        "u": Reduce(place, grads[1:], sums[1:3], parts[1], True),
        "g": Reduce(place, [group], sums[3:], parts[2]),
    }
    end = follow(
        REDUCE_PLAN,
        jobs,
        step,
        pl.num_programs(0) * pl.num_programs(1) - 1,
        lambda: meet(place, True),
    )
    seq = pl.program_id(1)
    count = len_ref[seq]
    low = low_lanes()
    zero = jnp.zeros((), bf)
    tables, scores, back_probs, probs_low, backs = (t0, t1), (s0, s1), (d0, d1), (p0, p1), (e0, e1)
    rows = [row_ref[0, pl.ds(2 * pair_at(turn) + e, 1), :] for e in range(2)]
    for e in range(2):
        tables[e][...] = table_of(rows[e])
    datt = datt_ref[...]
    swapped = half_roll(proj_ref[:, 128:256])
    middle = [jnp.where(low, datt, swapped), jnp.where(low, swapped, datt)]
    sources = [
        jnp.concatenate([proj_ref[:, 256 * e : 256 * e + 128], middle[e]], axis=1)
        for e in range(2)
    ]
    picked = [dot_nn(turned_table_of(rows[e]), sources[e]).astype(bf) for e in range(2)]
    for e in range(2):
        qk, dv = picked[e][:, 0:128], picked[e][:, 128:256]
        key_low = jnp.where(low, half_roll(qk), zero)
        turned = half_roll(dv)
        value_only = jnp.where(low, turned, zero) if e == 0 else jnp.where(low, zero, turned)
        bias = jnp.where(rows[e] < count, 0.0, -30000.0)
        for sl in SLICES:
            scores[e][sl, :] = 0.125 * dot_nt(qk[sl], key_low[sl]) + bias[:, sl]
            back_probs[e][sl, :] = dot_nt(dv[sl], value_only[sl])
    for e in range(2):
        for sl in SLICES:
            probs = softmax_rows(scores[e][sl, :])
            back = back_probs[e][sl, :]
            probs_low[e][sl, :] = probs.astype(bf)
            inner = jnp.sum(back * probs, axis=-1, keepdims=True)
            backs[e][sl, :] = (0.125 * (probs * (back - inner))).astype(bf)
    moved = []
    for e in range(2):
        qk, dv = picked[e][:, 0:128], picked[e][:, 128:256]
        queries, keys, values = [], [], []
        for sl in SLICES:
            back = backs[e][sl, :]
            queries.append(dot_nn(back, qk[sl]))
            keys.append(dot_tn(back, qk[sl]))
            values.append(dot_tn(probs_low[e][sl, :], dv[sl]))
        key_query = jnp.where(low, jnp.concatenate(keys, 0), jnp.concatenate(queries, 0))
        value = jnp.concatenate(values, 0)
        db_ref[0, 0, e : e + 1, :] = jnp.sum(key_query, axis=0, keepdims=True)
        db_ref[0, 0, 2 + e : 3 + e, :] = jnp.sum(value, axis=0, keepdims=True)
        moved.append(jnp.concatenate([key_query.astype(bf), value.astype(bf)], axis=1))
    placed = [dot_nn(tables[e][...], moved[e]) for e in range(2)]
    key_queries = [placed[e][:, 0:128] for e in range(2)]
    turned = [pltpu.roll(t, DH, 1) for t in key_queries]
    query = jnp.where(low, turned[0], key_queries[1]).astype(bf)
    key = jnp.where(low, key_queries[0], turned[1]).astype(bf)
    value = jnp.where(low, placed[0][:, 128:256], placed[1][:, 128:256]).astype(bf)
    dq_ref[...] = query
    dk_ref[...] = key
    dv_ref[...] = value
    out = jnp.concatenate([query, key, value], axis=1)
    part = dot_tn(x_ref[...], out)

    @pl.when(seq == 0)
    def _():
        total[...] = part

    @pl.when(seq != 0)
    def _():
        total[...] += part

    dw_ref[0] = total[...].astype(bf)

    @pl.when(turn < 2)
    def _():
        rows = D // shards
        columns = pl.ds(pl.multiple_of(turn * 384, 128), 384)
        for k in range(shards):
            group[k, :, columns] = total[k * rows : (k + 1) * rows, :].astype(bf)

    end()


def pair_at(i):
    return (i % 2) * (PAIRS // 2) + i // 2


def pair_at(i):
    return (i % 2) * (PAIRS // 2) + i // 2


def attention_backward(lengths, rounded, proj, datt, rows, grads, shards, reps, collective_id):
    seqs = rows.shape[0]
    tokens = seqs * LEN
    own = lambda width: pl.BlockSpec((LEN, width), lambda i, s, n: (s, pair_at(i)))
    part = (D // shards, D)
    shapes = {
        "d": [grads[0].shape[1:]],
        "u": [g.shape[1:] for g in grads[1:]],
        "g": [part],
    }
    every = shapes["d"] + shapes["u"] + shapes["g"]
    return pl.pallas_call(
        partial(attention_backward_body, shards, reps, shapes),
        grid_spec=pltpu.PrefetchScalarGridSpec(
            num_scalar_prefetch=1,
            grid=(PAIRS, seqs),
            in_specs=[
                pl.BlockSpec((LEN, D), lambda i, s, n: (s, 0)),
                own(384),
                own(128),
                pl.BlockSpec((1, H, LEN), lambda i, s, n: (s, 0, 0)),
            ]
            + [pl.BlockSpec(memory_space=pl.ANY)] * 3,
            out_specs=[own(128)] * 3
            + [
                pl.BlockSpec((1, D, 384), lambda i, s, n: (i // 2, 0, i % 2)),
                pl.BlockSpec((1, 1, 4, 128), lambda i, s, n: (s, pair_at(i), 0, 0)),
            ]
            + [pl.BlockSpec(memory_space=pl.ANY)] * 4,
            scratch_shapes=[pltpu.VMEM((LEN, LEN), bf)] * 2
            + [pltpu.VMEM((LEN, 128), f32)] * 4
            + [pltpu.VMEM((LEN, 128), bf)] * 4
            + [pltpu.VMEM((D, 384), f32), pltpu.VMEM((shards,) + part, bf)]
            + sum([reduce_scratch(shapes[k], shards, reps, k == "u") for k in "dug"], []),
        ),
        out_shape=[jax.ShapeDtypeStruct((tokens, D), bf)] * 3
        + [
            jax.ShapeDtypeStruct((PAIRS // 2, D, D), bf),
            jax.ShapeDtypeStruct((seqs, PAIRS, 4, 128), f32),
        ]
        + result_shapes(every),
        compiler_params=pltpu.CompilerParams(
            vmem_limit_bytes=62 << 20, collective_id=collective_id, has_side_effects=True
        ),
        name="attention_backward",
    )(lengths, rounded, proj, datt, rows, *grads)


def norm_stats(x):
    c=jnp.mean(x,axis=-1,keepdims=True)
    xc=x-c
    r=lax.rsqrt(jnp.mean(xc*xc,axis=-1,keepdims=True)+eps_norm)
    return xc*r,r

def norm_back(up,normed,r,gain):
    g=up*gain
    return r*(g-jnp.mean(g,axis=-1,keepdims=True)-normed*jnp.mean(g*normed,axis=-1,keepdims=True))

def colsum(x): return jnp.sum(x,axis=0,keepdims=True)

def gelu_parts(u):
    cdf=0.5+0.5*lax.erf(u*0.7071067811865476)
    pdf=jnp.exp(-0.5*u*u)*0.3989422804014327
    return u*cdf,cdf+u*pdf

def middle_body(len_ref,h_ref,a_ref,ct_ref,ow_ref,uw_ref,dw_ref,vec_ref,ub_ref,
               out_ref,bs_ref,ba_ref,act,pl_,low_ref,d2_ref,sl_ref,small_ref,ubg_ref,
               gp,n1_ref,*,T,sub_rows,chunk):
    i=pl.program_id(0)
    per=LEN//T
    count=len_ref[i//per]
    @pl.when(i==0)
    def _():
        small_ref[...]=jnp.zeros_like(small_ref); ubg_ref[...]=jnp.zeros_like(ubg_ref)
    out_b,g1,b1,down_b,g2,b2=[vec_ref[j:j+1,:] for j in range(6)]
    parts=[slice(k,k+sub_rows) for k in range(0,T,sub_rows)]
    r1s=[];sums=[]
    xs=[dot_nn(a_ref[p,:],ow_ref[...]) for p in parts]
    for p,x in zip(parts,xs):
        n1,r1=norm_stats(h_ref[p,:]+x+out_b)
        n1_ref[p,:]=n1; r1s.append(r1)
        low_ref[p,:]=(n1*g1+b1).astype(bf)
    for j in range(0,FF,chunk):
        sl=slice(j,j+chunk)
        for p in parts:
            u=dot_nn(low_ref[p,:],uw_ref[:,sl])+ub_ref[:,sl]
            a,g=gelu_parts(u)
            act[p,sl]=a.astype(bf); gp[p,sl]=g.astype(gp.dtype)
    ys=[dot_nn(act[p,:],dw_ref[...]) for p in parts]
    for p,y in zip(parts,ys):
        pos=lax.broadcasted_iota(jnp.int32,(sub_rows,1),0)+(i%per)*T+p.start
        valid=jnp.where(pos<count,1.0,0.0)
        second=n1_ref[p,:]*g1+b1+y+down_b
        n2,r2=norm_stats(second)
        out_ref[p,:]=valid*(n2*g2+b2)
        up=valid*ct_ref[p,:]
        b2nd=norm_back(up,n2,r2,g2)
        d2_ref[p,:]=b2nd.astype(bf)
        bs_ref[p,:]=b2nd
        sums.append(jnp.concatenate([colsum(b2nd),colsum(up*n2),colsum(up)],axis=0))
    small_ref[3:6,:]+=sum(sums[1:],sums[0])
    for j in range(0,FF,chunk):
        sl=slice(j,j+chunk)
        cs=[]
        for p in parts:
            bp=dot_nt(d2_ref[p,:],dw_ref[sl,:])*gp[p,sl].astype(f32)
            cs.append(colsum(bp))
            pl_[p,sl]=bp.astype(bf)
        ubg_ref[:,sl]+=sum(cs[1:],cs[0])
    zs=[dot_nt(pl_[p,:],uw_ref[...]) for p in parts]
    sums=[]
    for p,z,r1 in zip(parts,zs,r1s):
        bfirst=z+bs_ref[p,:]
        n1=n1_ref[p,:]
        bsum=norm_back(bfirst,n1,r1,g1)
        bs_ref[p,:]=bsum
        sl_ref[p,:]=bsum.astype(bf)
        sums.append(jnp.concatenate([colsum(bsum),colsum(bfirst*n1),colsum(bfirst)],axis=0))
    small_ref[0:3,:]+=sum(sums[1:],sums[0])
    for p in parts:
        ba_ref[p,:]=dot_nt(sl_ref[p,:],ow_ref[...]).astype(bf)

def middle(lengths,hidden,att,ct,ow,uw,dw,vec,ub,T=512,chunk=768,gpt=f32,sub_rows=256):
    tokens=hidden.shape[0]
    tile=lambda n=D: pl.BlockSpec((T,n),lambda i,l:(i,0))
    const=lambda shape: pl.BlockSpec(shape,lambda i,l:(0,0),pipeline_mode=pl.Buffered(1))
    whole=lambda shape: pl.BlockSpec(shape,lambda i,l:(0,0))
    sd=lambda n,dt: jax.ShapeDtypeStruct((tokens,n),dt)
    return pl.pallas_call(
        partial(middle_body,T=T,chunk=chunk,sub_rows=sub_rows),
        grid_spec=pltpu.PrefetchScalarGridSpec(num_scalar_prefetch=1,grid=(tokens//T,),
          in_specs=[tile(),tile(),tile(),const((D,D)),const((D,FF)),const((FF,D)),whole((8,D)),whole((1,FF))],
          out_specs=[tile(),tile(),tile(),tile(FF),tile(FF),tile(),tile(),tile(),whole((8,D)),whole((1,FF))],
          scratch_shapes=[pltpu.VMEM((T,FF),gpt),pltpu.VMEM((T,D),f32)]),
        out_shape=[sd(D,f32),sd(D,f32),sd(D,bf),sd(FF,bf),sd(FF,bf),sd(D,bf),sd(D,bf),sd(D,bf),jax.ShapeDtypeStruct((8,D),f32),jax.ShapeDtypeStruct((1,FF),f32)],
        compiler_params=pltpu.CompilerParams(vmem_limit_bytes=63<<20),
        name="middle")(lengths,hidden,att,ct,ow,uw,dw,vec,ub)


def weight_grad_body(l_ref,r_ref,out_ref):
    out_ref[...]=dot_tn(l_ref[...],r_ref[...]).astype(bf)
def weight_grad(left,right,block,name,columns=False):
    K,M=left.shape; N=right.shape[1]
    if columns:
        grid,lb,rb,ob,li,ri,oi=(N//block,),(K,M),(K,block),(M,block),(lambda i:(0,0)),(lambda i:(0,i)),(lambda i:(0,i))
    else:
        grid,lb,rb,ob,li,ri,oi=(M//block,),(K,block),(K,N),(block,N),(lambda i:(0,i)),(lambda i:(0,0)),(lambda i:(i,0))
    return pl.pallas_call(weight_grad_body,grid=grid,
        in_specs=[pl.BlockSpec(lb,li),pl.BlockSpec(rb,ri)],out_specs=pl.BlockSpec(ob,oi),
        out_shape=jax.ShapeDtypeStruct((M,N),bf),
        cost_estimate=pl.CostEstimate(flops=2*K*M*N,bytes_accessed=2*(K*M+K*N+M*N),transcendentals=0),
        compiler_params=pltpu.CompilerParams(vmem_limit_bytes=60<<20),name=name)(left,right)


def input_grad_body(shards,reps,shapes,bs_ref,dq_ref,dk_ref,dv_ref,w_ref,*refs):
    n=len(shapes)
    grads,out_ref,sums,scratch=refs[:n],refs[n],refs[n+1:2*n+1],refs[2*n+1:]
    place=Place(shards,reps); step=pl.program_id(0)
    size=len(reduce_scratch(shapes[1:],shards,reps))
    jobs={"a":Reduce(place,grads[1:],sums[1:],scratch[:size]),"b":Reduce(place,grads[:1],sums[:1],scratch[size:],True)}
    end=follow(LAST_PLAN,jobs,step,pl.num_programs(0)-1,lambda: meet(place,True))
    out_ref[...]=bs_ref[...]+dot_nt(dq_ref[...],w_ref[:,0:D])+dot_nt(dk_ref[...],w_ref[:,D:2*D])+dot_nt(dv_ref[...],w_ref[:,2*D:3*D])
    end()
def input_grad(back_sum,dq,dk,dv,weight,grads,shards,reps,collective_id):
    rows=back_sum.shape[0]//8
    tile=pl.BlockSpec((rows,D),lambda i:(i,0))
    anywhere=[pl.BlockSpec(memory_space=pl.ANY)]*len(grads)
    shapes=[g.shape[1:] for g in grads]
    return pl.pallas_call(partial(input_grad_body,shards,reps,shapes),grid=(8,),
        in_specs=[tile]*4+[pl.BlockSpec((D,3*D),lambda i:(0,0),pipeline_mode=pl.Buffered(1))]+anywhere,
        out_specs=[tile]+anywhere,
        out_shape=[jax.ShapeDtypeStruct(back_sum.shape,f32)]+result_shapes(shapes),
        scratch_shapes=reduce_scratch(shapes[1:],shards,reps)+reduce_scratch(shapes[:1],shards,reps,True),
        compiler_params=pltpu.CompilerParams(vmem_limit_bytes=50<<20,collective_id=collective_id,has_side_effects=True),name="input_grad")(back_sum,dq,dk,dv,weight,*grads)


def as_rows(row):
    filled = -(-row.shape[-1] // 128)
    row = jnp.pad(row, ((0, 0), (0, filled * 128 - row.shape[-1])))
    return jnp.pad(row.reshape(-1, filled, 128), ((0, 0), (0, 0), (0, 128)))


def pack_vectors(vectors):
    rows = jnp.concatenate([as_rows(v) for v in vectors], axis=1)
    return jnp.pad(rows, ((0, 0), (0, 16 - rows.shape[1]), (0, 0)))


def local(
    hidden,
    lengths,
    clusters,
    input_weight,
    query_bias,
    value_bias,
    out_weight,
    out_bias,
    norm1_gain,
    norm1_bias,
    up_weight,
    up_bias,
    down_weight,
    down_bias,
    norm2_gain,
    norm2_bias,
    cotangent,
    *,
    shards,
    reps,
):
    seqs = hidden.shape[0]
    tokens = seqs * LEN
    part = D // shards
    vectors = pack_vectors(
        [
            v[None]
            for v in (
            query_bias,
            value_bias,
            out_bias,
            norm1_gain,
            norm1_bias,
            down_bias,
            norm2_gain,
            norm2_bias,
            up_bias,
            )
        ]
    )[0]
    in_w, vectors = gather_now((input_weight, vectors), shards, reps, 1)
    in_w = in_w.reshape(D, 3 * D)
    vectors = vectors.astype(f32)
    table = vectors[:, :8, :part].transpose(1, 0, 2).reshape(8, D)
    bias_all = jnp.concatenate([table[0], jnp.zeros((D,), f32), table[1]])[None]
    norm_rows = jnp.concatenate([table[2:], table[:2]])
    up_b = vectors[:, 8:, :128].reshape(shards, -1)[:, : FF // shards].reshape(1, FF)

    flat = hidden.reshape(tokens, D)
    attended, proj, rounded, up_w, down_w, out_w = attention_forward(
        lengths,
        flat,
        in_w,
        bias_all,
        clusters,
        (up_weight, down_weight, out_weight),
        shards,
        reps,
        2,
    )
    out_w, up_w, down_w = [w.reshape(-1, w.shape[-1]) for w in (out_w, up_w, down_w)]
    (
        result,
        back_sum,
        back_attended,
        activated,
        pre_low,
        first_low,
        second_low,
        sum_low,
        norm_sums,
        up_b_sum,
    ) = middle(
        lengths,
        flat,
        attended,
        cotangent.reshape(tokens, D),
        out_w,
        up_w,
        down_w,
        norm_rows,
        up_b,
    )
    down_g = weight_grad(activated, second_low, D, "down_weight_grad")
    up_g = weight_grad(first_low, pre_low, D, "up_weight_grad", True)
    out_g = weight_grad(attended, sum_low, D // 2, "out_weight_grad")
    dq, dk, dv, in_g, bias_sums, down_s, up_s, out_s, in_first = attention_backward(
        lengths,
        rounded,
        proj,
        back_attended,
        clusters,
        [g.reshape(shards, -1, g.shape[-1]) for g in (down_g, up_g, out_g)],
        shards,
        reps,
        3,
    )
    bias_sums = jnp.sum(bias_sums, axis=0)
    query_sum = bias_sums[:, 0:2, DH:].reshape(D)
    value_sum = jnp.concatenate([bias_sums[:, 2, :DH], bias_sums[:, 3, DH:]], axis=1).reshape(D)
    table = jnp.concatenate([query_sum[None], value_sum[None], norm_sums[:6]])
    table = table.reshape(8, shards, part)
    small = pack_vectors(
        [table[i].astype(bf) for i in range(8)] + [up_b_sum.reshape(shards, -1).astype(bf)]
    )
    back_input, *in_s, small_s = input_grad(
        back_sum,
        dq,
        dk,
        dv,
        in_w,
        [in_g[2].reshape(shards, part, D), in_g[1].reshape(shards, part, D), small],
        shards,
        reps,
        4,
    )
    back_input = back_input.reshape(seqs, LEN, D)
    in_s = [in_first, in_s[1], in_s[0]]
    in_s = jnp.concatenate(
        [
            in_s[g][c, :, 128 * t : 128 * t + 128]
            for t in range(3)
            for c in range(2)
            for g in range(PAIRS // 2)
        ],
        axis=1,
    )

    def whole(halves):
        return jnp.concatenate([halves[0], halves[1]], axis=1)

    small_s = small_s[0]
    vec = [small_s[i, :part] for i in range(8)]
    return (
        result.reshape(seqs, LEN, D),
        back_input,
        in_s,
        vec[0],
        vec[1],
        whole(out_s),
        vec[2],
        vec[3],
        vec[4],
        whole(up_s),
        small_s[8:].reshape(-1)[: FF // shards],
        whole(down_s),
        vec[5],
        vec[6],
        vec[7],
    )


def solution(mesh):
    tokens = P(("rep", "shard"), None, None)
    matrix, vector = P("shard", None), P("shard")
    params = (
        matrix,
        vector,
        vector,
        matrix,
        vector,
        vector,
        vector,
        matrix,
        vector,
        matrix,
        vector,
        vector,
        vector,
    )
    return jax.shard_map(
        partial(local, shards=mesh.shape["shard"], reps=mesh.shape["rep"]),
        mesh=mesh,
        in_specs=(tokens, P(("rep", "shard")), tokens) + params + (tokens,),
        out_specs=(tokens, tokens) + params,
        check_vma=False,
    )
```

```python
from functools import partial

import jax
import jax.numpy as jnp
from jax import lax
from jax.experimental import pallas as pl
from jax.experimental.pallas import tpu as pltpu
from jax.sharding import PartitionSpec as P

D = 768
H = 12
DH = 64
FF = 3072
CLUSTER = 128
LEN = 1024
PAIRS = H // 2
SLICES = [slice(c * CLUSTER, (c + 1) * CLUSTER) for c in range(LEN // CLUSTER)]
bf = jnp.bfloat16
f32 = jnp.float32
eps_norm = 1e-12


def dot_nn(left, right):
    return lax.dot_general(left, right, (((1,), (0,)), ((), ())), preferred_element_type=f32)


def dot_nt(left, right):
    return lax.dot_general(left, right, (((1,), (1,)), ((), ())), preferred_element_type=f32)


def dot_tn(left, right):
    return lax.dot_general(left, right, (((0,), (0,)), ((), ())), preferred_element_type=f32)


ROWS = 4
MESH=pl.DeviceIdType.MESH

def when(cond,do):
    if cond is None: do()
    else: pl.when(cond)(do)

class Place:
    def __init__(self,shards,reps):
        self.Y=shards//ROWS; self.S=shards; self.X=reps//2
        self.s=lax.axis_index("shard"); self.r=lax.axis_index("rep")
        self.z=self.s//self.Y; self.y=lax.rem(self.s,self.Y)
        self.core=lax.rem(self.r,2); self.x=self.r//2
    def near_z(self,step): return {"shard":self.s+step*self.Y}
    def other_y(self,k): return {"shard":self.z*self.Y+lax.rem(self.y+k,self.Y)}
    def other_core(self): return {"rep":self.r+1-2*self.core}
    def other_x(self,k): return {"rep":2*lax.rem(self.x+k,self.X)+self.core}

def meet(place,with_x):
    sem=pltpu.get_barrier_semaphore()
    def tell(dev): pl.semaphore_signal(sem,inc=1,device_id=dev,device_id_type=MESH)
    pl.when(place.z>0)(lambda: tell(place.near_z(-1)))
    pl.when(place.z<ROWS-1)(lambda: tell(place.near_z(1)))
    for k in range(1,place.Y): tell(place.other_y(k))
    tell(place.other_core())
    if with_x:
        for k in range(1,place.X): tell(place.other_x(k))
    others=place.Y+(place.X-1 if with_x else 0)
    inner=jnp.logical_and(place.z>0,place.z<ROWS-1)
    pl.when(inner)(lambda: pl.semaphore_wait(sem,others+2))
    pl.when(jnp.logical_not(inner))(lambda: pl.semaphore_wait(sem,others+1))

def gather_semaphores(count,shards):
    Y=shards//ROWS; dma=pltpu.SemaphoreType.DMA
    return [dma((count,2,ROWS)),dma((count,2,ROWS)),dma((count,ROWS,Y)),dma((count,ROWS,Y)),
            dma((count,2,shards)),dma((count,2,shards)),dma((count,shards)),dma((count,shards)),dma((count,))]

class Gather:
    def __init__(self,place,ins,outs,sems,share=False):
        self.p=place; self.ins=ins; self.outs=outs; self.share=share and place.X==2
        self.line_s,self.line_r,self.y_s,self.y_r,self.core_s,self.core_r,self.x_s,self.x_r,self.own=sems
        self.sent=[]
    def piece(self,ref,shard=None,core=None,x=None):
        p=self.p; n=ref.shape[-1]//2; r=ref.shape[-2]
        cols=pl.ds(pl.multiple_of((p.core if core is None else core)*n,128),n)
        rows=slice(None)
        if self.share:
            rows=pl.ds(pl.multiple_of((p.x if x is None else x)*(r//2),16),r//2)
        return ref.at[rows,cols] if shard is None else ref.at[shard,rows,cols]
    def send(self,make):
        cond,desc=make()
        when(cond,desc.start); self.sent.append(make)
    def copy(self,src,dst,ss,rs,dev):
        return pltpu.make_async_remote_copy(src_ref=src,dst_ref=dst,send_sem=ss,recv_sem=rs,device_id=dev,device_id_type=MESH)
    def at(self,places):
        zz=self.p.z+places
        if places==0: return None,zz
        return jnp.logical_and(zz>=0,zz<ROWS),jnp.clip(zz,0,ROWS-1)
    def shard_at(self,zz,k):
        p=self.p
        return zz*p.Y+(lax.rem(p.y-k+p.Y,p.Y) if k else p.y)
    def to_line(self,a,places,d):
        p=self.p; i,o=self.ins[a],self.outs[a]
        def make():
            cond,zz=self.at(places); shard=zz*p.Y+p.y
            edge=(p.z<ROWS-1) if d==0 else (p.z>0)
            src=self.piece(i) if places==0 else self.piece(o,shard)
            return (edge if cond is None else jnp.logical_and(cond,edge)),self.copy(src,self.piece(o,shard),self.line_s.at[a,d,zz],self.line_r.at[a,d,zz],p.near_z(1 if d==0 else -1))
        self.send(make)
    def to_y(self,a,places,k):
        p=self.p; i,o=self.ins[a],self.outs[a]
        def make():
            cond,zz=self.at(places); shard=zz*p.Y+p.y
            src=self.piece(i) if places==0 else self.piece(o,shard)
            return cond,self.copy(src,self.piece(o,shard),self.y_s.at[a,zz,k],self.y_r.at[a,zz,k],p.other_y(k))
        self.send(make)
    def to_core(self,a,places,k,other=False):
        p=self.p; o=self.outs[a]; slot=1 if other else 0
        def make():
            cond,zz=self.at(places); shard=self.shard_at(zz,k)
            ref=self.piece(o,shard,x=1-p.x if other else p.x)
            return cond,self.copy(ref,ref,self.core_s.at[a,slot,shard],self.core_r.at[a,slot,shard],p.other_core())
        self.send(make)
    def to_x(self,a,places,k):
        p=self.p; o=self.outs[a]
        if not self.share: return
        def make():
            cond,zz=self.at(places); shard=self.shard_at(zz,k)
            ref=self.piece(o,shard)
            return cond,self.copy(ref,ref,self.x_s.at[a,shard],self.x_r.at[a,shard],p.other_x(1))
        self.send(make)
    def begin(self):
        for a,(i,o) in enumerate(zip(self.ins,self.outs)):
            for d in (0,1): self.to_line(a,0,d)
            for k in range(1,self.p.Y): self.to_y(a,0,k)
            pltpu.make_async_copy(i,o.at[self.p.s],self.own.at[a]).start()
    def wave(self,w):
        p=self.p
        for d in (0,1):
            places=-w if d==0 else w
            for a,o in enumerate(self.outs):
                cond,zz=self.at(places); ref=self.piece(o,zz*p.Y+p.y)
                when(cond,self.copy(ref,ref,self.line_s.at[a,d,zz],self.line_r.at[a,d,zz],p.near_z(0)).wait_recv)
                self.to_line(a,places,d)
                for k in range(1,p.Y): self.to_y(a,places,k)
                self.to_x(a,places,0); self.to_core(a,places,0)
    def across(self,w):
        p=self.p
        for places in ((0,) if w==0 else (-w,w)):
            for k in range(1,p.Y):
                for a,o in enumerate(self.outs):
                    cond,zz=self.at(places); ref=self.piece(o,self.shard_at(zz,k))
                    when(cond,self.copy(ref,ref,self.y_s.at[a,zz,k],self.y_r.at[a,zz,k],p.other_y(k)).wait_recv)
                    self.to_x(a,places,k); self.to_core(a,places,k)
    def over(self,w):
        p=self.p
        if not self.share: return
        for places in ((0,) if w==0 else (-w,w)):
            for k in range(1 if w==0 else 0,p.Y):
                for a,o in enumerate(self.outs):
                    cond,zz=self.at(places); shard=self.shard_at(zz,k); ref=self.piece(o,shard,x=1-p.x)
                    when(cond,self.copy(ref,ref,self.x_s.at[a,shard],self.x_r.at[a,shard],p.other_x(1)).wait_recv)
                    self.to_core(a,places,k,True)
    def finish(self):
        p=self.p
        for a,(i,o) in enumerate(zip(self.ins,self.outs)):
            for k in range(1,p.S):
                shard=lax.rem(p.s+k,p.S)
                for slot in range(2 if self.share else 1):
                    ref=self.piece(o,shard,core=1-p.core,x=1-p.x if slot else p.x)
                    self.copy(ref,ref,self.core_s.at[a,slot,shard],self.core_r.at[a,slot,shard],p.other_core()).wait_recv()
            pltpu.make_async_copy(i,o.at[p.s],self.own.at[a]).wait()
        for make in self.sent:
            cond,desc=make()
            when(cond,desc.wait_send)
def gather_body(shards,reps,count,*refs):
    ins,outs,sems=refs[:count],refs[count:2*count],refs[2*count:]
    place=Place(shards,reps)
    meet(place,False)
    G=Gather(place,ins,outs,sems)
    G.begin(); G.wave(1); G.across(0); G.wave(2); G.across(1); G.wave(3); G.across(2); G.across(3); G.finish()

def gather_now(arrays,shards,reps,collective_id):
    count=len(arrays)
    return pl.pallas_call(partial(gather_body,shards,reps,count),
        in_specs=[pl.BlockSpec(memory_space=pltpu.VMEM)]*count,
        out_specs=[pl.BlockSpec(memory_space=pl.ANY)]*count,
        out_shape=[jax.ShapeDtypeStruct((shards,)+a.shape,a.dtype) for a in arrays],
        scratch_shapes=gather_semaphores(count,shards),
        compiler_params=pltpu.CompilerParams(collective_id=collective_id,has_side_effects=True,vmem_limit_bytes=16<<20),
        name="gather_weights")(*arrays)

ORDER=(3,0,2,1)
def reduce_scratch(shapes,shards,reps,x_first=False):
    x_first=x_first and reps==4
    S=shards; Y=S//ROWS; X=reps//2; A=len(shapes)
    out=[]
    for r,c in shapes:
        n=c//2; m=r//2 if x_first else r
        out+=[pltpu.VMEM((S,r,n),bf),pltpu.VMEM((S,r,n),bf),pltpu.VMEM((max(Y-1,1),ROWS,m,n),bf),
              pltpu.VMEM((ROWS+1,m,n),bf),pltpu.VMEM((S+1,m,n) if x_first else (X,r,n),bf),pltpu.VMEM((2,r,n),f32)]
    dma=pltpu.SemaphoreType.DMA
    return out+[dma((A,S)),dma((A,S)),dma((A,S)),dma((A,Y,ROWS)),dma((A,Y,ROWS)),dma((A,ROWS+1)),dma((A,ROWS+1)),dma((A,S+X)),dma((A,S+X)),dma((A,)),dma((A,)),dma((A,))]
class Reduce:
    def __init__(self,place,ins,outs,scratch,x_first=False):
        self.p=place; self.ins=ins; self.outs=outs; A=len(ins); self.A=range(A)
        self.bufs=[scratch[6*a:6*a+6] for a in range(A)]
        (self.own,self.core_s,self.core_r,self.y_s,self.y_r,self.line_s,self.line_r,self.x_s,self.x_r,self.end_s,self.end_r,self.out_s)=scratch[6*A:]
        self.sent=[]; self.x_first=x_first and place.X==2
    def copy(self,src,dst,ss,rs,dev):
        return pltpu.make_async_remote_copy(src_ref=src,dst_ref=dst,send_sem=ss,recv_sem=rs,device_id=dev,device_id_type=MESH)
    def send(self,make):
        cond,desc=make()
        when(cond,desc.start); self.sent.append(make)
    def half(self,a,shard,core):
        n=self.ins[a].shape[-1]//2
        return self.ins[a].at[shard,:,pl.ds(pl.multiple_of(core*n,128),n)]
    def mine(self,a,shard,x=None):
        H=self.bufs[a][0]
        if not self.x_first: return H.at[shard]
        m=H.shape[1]//2
        return H.at[shard,pl.ds(pl.multiple_of((self.p.x if x is None else x)*m,16),m)]
    def add(self,dst,others):
        rows,n=dst.shape; step=next(s for s in (192,96,48,16) if rows%s==0 and (s==16 or s*n<=96*768))
        def block(at):
            value=dst[at,:]
            for o in others: value=value+o[at,:]
            dst[at,:]=value
        if rows==step: block(slice(0,rows)); return
        def body(i,_):
            block(pl.ds(pl.multiple_of(i*step,16),step))
            return 0
        lax.fori_loop(0,rows//step,body,0)
    def begin(self):
        p=self.p
        for k in list(range(1,p.Y))+[0]:
            for d in ORDER:
                for a in self.A:
                    H,Rc=self.bufs[a][0:2]
                    def make(a=a,d=d,k=k,Rc=Rc):
                        shard=d*p.Y+lax.rem(p.y+k,p.Y)
                        return None,self.copy(self.half(a,shard,1-p.core),Rc.at[shard],self.core_s.at[a,shard],self.core_r.at[a,shard],p.other_core())
                    self.send(make)
                    shard=d*p.Y+lax.rem(p.y+k,p.Y)
                    pltpu.make_async_copy(self.half(a,shard,p.core),H.at[shard],self.own.at[a,shard]).start()
    def join_core(self,shard):
        p=self.p
        for a in self.A:
            H,Rc=self.bufs[a][0:2]
            pltpu.make_async_copy(self.half(a,shard,p.core),H.at[shard],self.own.at[a,shard]).wait()
            self.copy(Rc.at[shard],Rc.at[shard],self.core_s.at[a,shard],self.core_r.at[a,shard],p.other_core()).wait_recv()
            self.add(H.at[shard],[Rc.at[shard]])
    def to_pair(self,k,d):
        p=self.p; shard=d*p.Y+lax.rem(p.y+k,p.Y)
        if not self.x_first: return
        self.join_core(shard)
        for a in self.A:
            def make(a=a):
                shard=d*p.Y+lax.rem(p.y+k,p.Y)
                return None,self.copy(self.mine(a,shard,1-p.x),self.bufs[a][4].at[shard],self.x_s.at[a,shard],self.x_r.at[a,shard],p.other_x(1))
            self.send(make)
    def ready(self,shard):
        p=self.p
        if not self.x_first: self.join_core(shard); return
        for a in self.A:
            got=self.bufs[a][4].at[shard]
            self.copy(got,got,self.x_s.at[a,shard],self.x_r.at[a,shard],p.other_x(1)).wait_recv()
            self.add(self.mine(a,shard),[got])
    def to_y(self,d):
        p=self.p
        for k in range(1,p.Y):
            self.ready(d*p.Y+lax.rem(p.y+k,p.Y))
            for a in self.A:
                H,_,Ry=self.bufs[a][0:3]
                def make(a=a,H=H,Ry=Ry,k=k):
                    shard=d*p.Y+lax.rem(p.y+k,p.Y)
                    return None,self.copy(self.mine(a,shard),Ry.at[k-1,d],self.y_s.at[a,k,d],self.y_r.at[a,k,d],p.other_y(k))
                self.send(make)
    def own_y(self,d):
        self.ready(d*self.p.Y+self.p.y)
    def along(self,d,up,j):
        p=self.p
        if (j>=d) if up else (ROWS-1-j<=d): return
        here=p.z==(j if up else ROWS-1-j)
        shard=d*p.Y+p.y
        if j>0:
            def add_in():
                for a in self.A:
                    H,Rl=self.bufs[a][0],self.bufs[a][3]
                    self.copy(Rl.at[d],Rl.at[d],self.line_s.at[a,d],self.line_r.at[a,d],p.near_z(0)).wait_recv()
                    self.add(self.mine(a,shard),[Rl.at[d]])
            pl.when(here)(add_in)
        last=(j==d-1) if up else (ROWS-1-j==d+1)
        slot=ROWS if last and not up else d
        for a in self.A:
            def make(a=a):
                H,Rl=self.bufs[a][0],self.bufs[a][3]
                return p.z==(j if up else ROWS-1-j),self.copy(self.mine(a,d*p.Y+p.y),Rl.at[slot],self.line_s.at[a,slot],self.line_r.at[a,slot],p.near_z(1 if up else -1))
            self.send(make)
    def line(self,d):
        p=self.p; shard=d*p.Y+p.y
        for a in self.A:
            H,_,Ry=self.bufs[a][0:3]
            for k in range(1,p.Y):
                self.copy(Ry.at[k-1,d],Ry.at[k-1,d],self.y_s.at[a,k,d],self.y_r.at[a,k,d],p.other_y(k)).wait_recv()
            self.add(self.mine(a,shard),[Ry.at[k-1,d] for k in range(1,p.Y)])
        self.along(d,True,0); self.along(d,False,0)
    def relay(self,d,j):
        self.along(d,True,j); self.along(d,False,j)
    def to_x(self):
        p=self.p
        for slot,cond in ((p.z,p.z>0),(ROWS,p.z<ROWS-1)):
            def add_in(slot=slot):
                for a in self.A:
                    H,Rl=self.bufs[a][0],self.bufs[a][3]
                    self.copy(Rl.at[slot],Rl.at[slot],self.line_s.at[a,slot],self.line_r.at[a,slot],p.near_z(0)).wait_recv()
                    self.add(self.mine(a,p.s),[Rl.at[slot]])
            pl.when(cond)(add_in)
        for a in self.A:
            H,Rx=self.bufs[a][0],self.bufs[a][4]
            if self.x_first:
                self.send(lambda a=a,Rx=Rx: (None,self.copy(self.mine(a,p.s),Rx.at[p.S],self.x_s.at[a,p.S],self.x_r.at[a,p.S],p.other_x(1))))
                continue
            for k in range(1,p.X):
                self.send(lambda a=a,H=H,Rx=Rx,k=k: (None,self.copy(H.at[p.s],Rx.at[p.x],self.x_s.at[a,k],self.x_r.at[a,p.x],p.other_x(k))))
    def to_core(self):
        p=self.p
        for a in self.A:
            H,Rx,F=self.bufs[a][0],self.bufs[a][4],self.bufs[a][5]
            if self.x_first:
                got=Rx.at[p.S]; m=H.shape[1]//2
                self.copy(got,got,self.x_s.at[a,p.S],self.x_r.at[a,p.S],p.other_x(1)).wait_recv()
                for x in range(2):
                    own=H[p.s,x*m:(x+1)*m,:]
                    F[p.core,x*m:(x+1)*m,:]=jnp.where(p.x==x,own,Rx[p.S]).astype(f32)
                continue
            for k in range(1,p.X):
                src=lax.rem(p.x-k+p.X,p.X)
                self.copy(Rx.at[src],Rx.at[src],self.x_s.at[a,k],self.x_r.at[a,src],p.other_x(k)).wait_recv()
            rows=H.shape[1]; step=48 if rows%48==0 else 16
            def body(i,_):
                at=pl.ds(pl.multiple_of(i*step,16),step)
                own=H[p.s,at,:].astype(f32)
                value=jnp.zeros_like(own)
                for q in range(p.X):
                    value=value+jnp.where(p.x==q,own,Rx[q,at,:].astype(f32))
                F[p.core,at,:]=value
                return 0
            lax.fori_loop(0,rows//step,body,0)
        for a in self.A:
            F=self.bufs[a][5]
            self.send(lambda a=a,F=F: (None,self.copy(F.at[p.core],F.at[p.core],self.end_s.at[a],self.end_r.at[a],p.other_core())))
    def finish(self):
        p=self.p
        for a in self.A:
            F=self.bufs[a][5]; ref=F.at[1-p.core]
            self.copy(ref,ref,self.end_s.at[a],self.end_r.at[a],p.other_core()).wait_recv()
            pltpu.make_async_copy(F,self.outs[a],self.out_s.at[a]).start()
        for make in self.sent:
            cond,desc=make()
            when(cond,desc.wait_send)
        for a in self.A: pltpu.make_async_copy(self.bufs[a][5],self.outs[a],self.out_s.at[a]).wait()
    def run(self,what,*args): getattr(self,what)(*args)
def result_shapes(shapes):
    return [jax.ShapeDtypeStruct((2,r,c//2),f32) for r,c in shapes]

GATHER_PLAN = {
    0: (("u", "begin"), ("d", "begin")),
    2: (("u", "wave", 1),),
    3: (("d", "wave", 1), ("u", "across", 0), ("d", "across", 0)),
    4: (("u", "wave", 2),),
    5: (("d", "wave", 2),),
    6: (("u", "across", 1), ("d", "over", 0)),
    7: (("u", "wave", 3),),
    8: (("d", "wave", 3), ("d", "across", 1)),
    9: (("u", "across", 2), ("u", "across", 3)),
    10: (("d", "across", 2), ("d", "across", 3), ("d", "over", 1)),
    100: (("d", "over", 2), ("d", "over", 3), ("u", "finish"), ("d", "finish")),
}


def each(name, what, *more):
    return tuple((name, what, d) + more for d in ORDER)


REDUCE_PLAN = {
    0: (("d", "begin"), ("u", "begin")),
    1: each("d", "to_y"),
    2: tuple(("u", "to_pair", 1, d) for d in ORDER) + each("d", "own_y"),
    3: tuple(("u", "to_pair", 0, d) for d in ORDER) + (("d", "line", 3),),
    4: (("g", "begin"), ("d", "line", 0)),
    5: each("u", "to_y") + (("d", "line", 2), ("d", "relay", 3, 1)),
    6: each("g", "to_y") + each("g", "own_y") + (("d", "line", 1), ("d", "relay", 0, 1)),
    7: (("d", "relay", 3, 2), ("d", "relay", 2, 1), ("u", "own_y", 3), ("u", "own_y", 0)),
    8: (("d", "relay", 0, 2), ("d", "relay", 1, 1), ("u", "own_y", 2), ("u", "own_y", 1))
    + (("u", "line", 3), ("u", "line", 0)),
    9: (("d", "to_x"), ("u", "line", 2), ("u", "line", 1), ("u", "relay", 3, 1), ("u", "relay", 0, 1)),
    10: (("d", "to_core"), ("u", "relay", 2, 1), ("u", "relay", 3, 2), ("u", "relay", 0, 2))
    + each("g", "line"),
    11: (("u", "relay", 1, 1),) + each("g", "relay", 1),
    100: each("g", "relay", 2)
    + (
        ("u", "to_x"),
        ("g", "to_x"),
        ("u", "to_core"),
        ("g", "to_core"),
        ("d", "finish"),
        ("u", "finish"),
        ("g", "finish"),
    ),
}
LAST_PLAN = {
    0: (("a", "begin"), ("b", "begin")),
    1: each("a", "to_y"),
    2: tuple(("b", "to_pair", k, d) for k in (1, 0) for d in ORDER) + each("a", "own_y"),
    4: (("a", "line", 3), ("a", "line", 0)),
    5: (("a", "line", 2), ("a", "line", 1)) + each("b", "to_y"),
    6: each("b", "own_y") + each("a", "relay", 1),
    7: (("a", "relay", 3, 2), ("a", "relay", 0, 2)) + each("b", "line"),
    100: (("a", "to_x"),)
    + each("b", "relay", 1)
    + (("a", "to_core"),)
    + each("b", "relay", 2)
    + (("b", "to_x"), ("b", "to_core"), ("a", "finish"), ("b", "finish")),
}


def follow(plan, jobs, step, last, ready):
    def run(at):
        for name, what, *more in plan.get(at, ()):
            getattr(jobs[name], what)(*more)

    def first():
        ready()
        run(0)

    pl.when(step == 0)(first)
    for at in sorted(plan):
        if 0 < at < 100:
            pl.when(step == at)(partial(run, at))
    return lambda: pl.when(step == last)(partial(run, 100))


def low_lanes():
    return lax.broadcasted_iota(jnp.int32, (LEN, CLUSTER), 1) < DH


def table_of(order_row):
    held = jnp.broadcast_to(order_row.astype(jnp.int16), (LEN, LEN))
    positions = lax.broadcasted_iota(jnp.int16, (LEN, LEN), 0)
    return jnp.where(held == positions, jnp.ones((), bf), jnp.zeros((), bf))


def turned_table_of(order_row):
    held = jnp.transpose(jnp.broadcast_to(order_row, (128, LEN))).astype(jnp.int16)
    lanes = lax.broadcasted_iota(jnp.int16, (LEN, 128), 1)
    return jnp.concatenate(
        [
            jnp.where(held == lanes + jnp.int16(128 * b), jnp.ones((), bf), jnp.zeros((), bf))
            for b in range(LEN // 128)
        ],
        axis=1,
    )


def half_roll(source):
    return pltpu.roll(source, DH, 1)


def softmax_rows(scores):
    top = jnp.max(scores, axis=-1, keepdims=True)
    grown = jnp.exp(scores - top)
    return grown * (1.0 / jnp.sum(grown, axis=-1, keepdims=True))


def attention_forward_body(
    shards, reps, len_ref, h_ref, wq_ref, wk_ref, wv_ref, bq_ref, bk_ref, bv_ref, row_ref, *rest
):
    ins, (att_ref, proj_ref, x_ref), outs = rest[:3], rest[3:6], rest[6:9]
    tables, scores, mixed = rest[9:11], rest[11:13], rest[13:15]
    sems = rest[15:]
    step = pl.program_id(0) * PAIRS + pl.program_id(1)
    place = Place(shards, reps)
    jobs = {
        "u": Gather(place, ins[:1], outs[:1], sems[:9]),
        "d": Gather(place, ins[1:], outs[1:], sems[9:], True),
    }
    end = follow(
        GATHER_PLAN, jobs, step, pl.num_programs(0) * PAIRS - 1, lambda: meet(place, True)
    )

    @pl.when(pl.program_id(1) == 0)
    def _():
        x_ref[...] = h_ref[...].astype(bf)

    count = len_ref[pl.program_id(0)]
    weight = jnp.concatenate([wq_ref[...], wk_ref[...], wv_ref[...]], axis=1)
    bias = jnp.concatenate([bq_ref[...], bk_ref[...], bv_ref[...]], axis=1)
    proj = (dot_nn(x_ref[...], weight) + bias).astype(bf)
    low = low_lanes()
    query, key, value = proj[:, 0:128], proj[:, 128:256], proj[:, 256:384]
    pairs = [jnp.where(low, query, half_roll(key)), jnp.where(low, half_roll(query), key)]
    proj_ref[...] = jnp.concatenate([pairs[0], value, pairs[1]], axis=1)
    rows = [row_ref[0, pl.ds(2 * pl.program_id(1) + e, 1), :] for e in range(2)]
    for e in range(2):
        tables[e][...] = table_of(rows[e])
    picked = [
        dot_nn(turned_table_of(rows[e]), jnp.concatenate([pairs[e], value], axis=1)).astype(bf)
        for e in range(2)
    ]
    for e in range(2):
        qk = picked[e][:, 0:128]
        key_low = jnp.where(low, half_roll(qk), jnp.zeros((), bf))
        bias = jnp.where(rows[e] < count, 0.0, -30000.0)
        for sl in SLICES:
            scores[e][sl, :] = 0.125 * dot_nt(qk[sl], key_low[sl]) + bias[:, sl]
    for e in range(2):
        values = picked[e][:, 128:256]
        for sl in SLICES:
            probs = softmax_rows(scores[e][sl, :]).astype(bf)
            mixed[e][sl, :] = dot_nn(probs, values[sl]).astype(bf)
    placed = [dot_nn(tables[e][...], mixed[e][...]) for e in range(2)]
    att_ref[...] = jnp.where(low, placed[0], placed[1]).astype(bf)
    end()


def attention_forward(lengths, hidden, weight, bias, rows, arrays, shards, reps, collective_id):
    seqs = rows.shape[0]
    tokens = seqs * LEN
    column = lambda part: pl.BlockSpec((D, 128), lambda s, h, n: (0, part * PAIRS + h))
    column_b = lambda part: pl.BlockSpec((1, 128), lambda s, h, n: (0, part * PAIRS + h))
    return pl.pallas_call(
        partial(attention_forward_body, shards, reps),
        grid_spec=pltpu.PrefetchScalarGridSpec(
            num_scalar_prefetch=1,
            grid=(seqs, PAIRS),
            in_specs=[pl.BlockSpec((LEN, D), lambda s, h, n: (s, 0))]
            + [column(part) for part in range(3)]
            + [column_b(part) for part in range(3)]
            + [pl.BlockSpec((1, H, LEN), lambda s, h, n: (s, 0, 0))]
            + [pl.BlockSpec(memory_space=pl.ANY)] * 3,
            out_specs=[
                pl.BlockSpec((LEN, 128), lambda s, h, n: (s, h)),
                pl.BlockSpec((LEN, 384), lambda s, h, n: (s, h)),
                pl.BlockSpec((LEN, D), lambda s, h, n: (s, 0)),
            ]
            + [pl.BlockSpec(memory_space=pl.ANY)] * 3,
            scratch_shapes=[pltpu.VMEM((LEN, LEN), bf)] * 2
            + [pltpu.VMEM((LEN, 128), f32)] * 2
            + [pltpu.VMEM((LEN, 128), bf)] * 2
            + gather_semaphores(1, shards)
            + gather_semaphores(2, shards),
        ),
        out_shape=[
            jax.ShapeDtypeStruct((tokens, D), bf),
            jax.ShapeDtypeStruct((tokens, 3 * D), bf),
            jax.ShapeDtypeStruct((tokens, D), bf),
        ]
        + [jax.ShapeDtypeStruct((shards,) + a.shape, bf) for a in arrays],
        compiler_params=pltpu.CompilerParams(
            vmem_limit_bytes=50 << 20, collective_id=collective_id, has_side_effects=True
        ),
        name="attention_forward",
    )(lengths, hidden, weight, weight, weight, bias, bias, bias, rows, *arrays)


def attention_backward_body(shards, reps, shapes, *refs):
    len_ref, x_ref, proj_ref, datt_ref, row_ref = refs[:5]
    grads, refs = refs[5:8], refs[8:]
    (dq_ref, dk_ref, dv_ref, dw_ref, db_ref), sums, refs = refs[:5], refs[5:9], refs[9:]
    t0, t1, s0, s1, d0, d1, p0, p1, e0, e1, total, group = refs[:12]
    refs = refs[12:]
    turn = pl.program_id(0)
    step = turn * pl.num_programs(1) + pl.program_id(1)
    place = Place(shards, reps)
    sizes = [len(reduce_scratch(shapes[k], shards, reps, k == "u")) for k in "dug"]
    parts = [refs[sum(sizes[:k]) : sum(sizes[: k + 1])] for k in range(3)]
    jobs = {
        "d": Reduce(place, grads[:1], sums[:1], parts[0]),
        "u": Reduce(place, grads[1:], sums[1:3], parts[1], True),
        "g": Reduce(place, [group], sums[3:], parts[2]),
    }
    end = follow(
        REDUCE_PLAN,
        jobs,
        step,
        pl.num_programs(0) * pl.num_programs(1) - 1,
        lambda: meet(place, True),
    )
    seq = pl.program_id(1)
    count = len_ref[seq]
    low = low_lanes()
    zero = jnp.zeros((), bf)
    tables, scores, back_probs, probs_low, backs = (t0, t1), (s0, s1), (d0, d1), (p0, p1), (e0, e1)
    rows = [row_ref[0, pl.ds(2 * pair_at(turn) + e, 1), :] for e in range(2)]
    for e in range(2):
        tables[e][...] = table_of(rows[e])
    datt = datt_ref[...]
    swapped = half_roll(proj_ref[:, 128:256])
    middle = [jnp.where(low, datt, swapped), jnp.where(low, swapped, datt)]
    sources = [
        jnp.concatenate([proj_ref[:, 256 * e : 256 * e + 128], middle[e]], axis=1)
        for e in range(2)
    ]
    picked = [dot_nn(turned_table_of(rows[e]), sources[e]).astype(bf) for e in range(2)]
    for e in range(2):
        qk, dv = picked[e][:, 0:128], picked[e][:, 128:256]
        key_low = jnp.where(low, half_roll(qk), zero)
        turned = half_roll(dv)
        value_only = jnp.where(low, turned, zero) if e == 0 else jnp.where(low, zero, turned)
        bias = jnp.where(rows[e] < count, 0.0, -30000.0)
        for sl in SLICES:
            scores[e][sl, :] = 0.125 * dot_nt(qk[sl], key_low[sl]) + bias[:, sl]
            back_probs[e][sl, :] = dot_nt(dv[sl], value_only[sl])
    for e in range(2):
        for sl in SLICES:
            probs = softmax_rows(scores[e][sl, :])
            back = back_probs[e][sl, :]
            probs_low[e][sl, :] = probs.astype(bf)
            inner = jnp.sum(back * probs, axis=-1, keepdims=True)
            backs[e][sl, :] = (0.125 * (probs * (back - inner))).astype(bf)
    moved = []
    for e in range(2):
        qk, dv = picked[e][:, 0:128], picked[e][:, 128:256]
        queries, keys, values = [], [], []
        for sl in SLICES:
            back = backs[e][sl, :]
            queries.append(dot_nn(back, qk[sl]))
            keys.append(dot_tn(back, qk[sl]))
            values.append(dot_tn(probs_low[e][sl, :], dv[sl]))
        key_query = jnp.where(low, jnp.concatenate(keys, 0), jnp.concatenate(queries, 0))
        value = jnp.concatenate(values, 0)
        db_ref[0, 0, e : e + 1, :] = jnp.sum(key_query, axis=0, keepdims=True)
        db_ref[0, 0, 2 + e : 3 + e, :] = jnp.sum(value, axis=0, keepdims=True)
        moved.append(jnp.concatenate([key_query.astype(bf), value.astype(bf)], axis=1))
    placed = [dot_nn(tables[e][...], moved[e]) for e in range(2)]
    key_queries = [placed[e][:, 0:128] for e in range(2)]
    turned = [pltpu.roll(t, DH, 1) for t in key_queries]
    query = jnp.where(low, turned[0], key_queries[1]).astype(bf)
    key = jnp.where(low, key_queries[0], turned[1]).astype(bf)
    value = jnp.where(low, placed[0][:, 128:256], placed[1][:, 128:256]).astype(bf)
    dq_ref[...] = query
    dk_ref[...] = key
    dv_ref[...] = value
    out = jnp.concatenate([query, key, value], axis=1)
    part = dot_tn(x_ref[...], out)

    @pl.when(seq == 0)
    def _():
        total[...] = part

    @pl.when(seq != 0)
    def _():
        total[...] += part

    dw_ref[0] = total[...].astype(bf)

    @pl.when(turn < 2)
    def _():
        rows = D // shards
        columns = pl.ds(pl.multiple_of(turn * 384, 128), 384)
        for k in range(shards):
            group[k, :, columns] = total[k * rows : (k + 1) * rows, :].astype(bf)

    end()


def pair_at(i):
    return (i % 2) * (PAIRS // 2) + i // 2


def pair_at(i):
    return (i % 2) * (PAIRS // 2) + i // 2


def attention_backward(lengths, rounded, proj, datt, rows, grads, shards, reps, collective_id):
    seqs = rows.shape[0]
    tokens = seqs * LEN
    own = lambda width: pl.BlockSpec((LEN, width), lambda i, s, n: (s, pair_at(i)))
    part = (D // shards, D)
    shapes = {
        "d": [grads[0].shape[1:]],
        "u": [g.shape[1:] for g in grads[1:]],
        "g": [part],
    }
    every = shapes["d"] + shapes["u"] + shapes["g"]
    return pl.pallas_call(
        partial(attention_backward_body, shards, reps, shapes),
        grid_spec=pltpu.PrefetchScalarGridSpec(
            num_scalar_prefetch=1,
            grid=(PAIRS, seqs),
            in_specs=[
                pl.BlockSpec((LEN, D), lambda i, s, n: (s, 0)),
                own(384),
                own(128),
                pl.BlockSpec((1, H, LEN), lambda i, s, n: (s, 0, 0)),
            ]
            + [pl.BlockSpec(memory_space=pl.ANY)] * 3,
            out_specs=[own(128)] * 3
            + [
                pl.BlockSpec((1, D, 384), lambda i, s, n: (i // 2, 0, i % 2)),
                pl.BlockSpec((1, 1, 4, 128), lambda i, s, n: (s, pair_at(i), 0, 0)),
            ]
            + [pl.BlockSpec(memory_space=pl.ANY)] * 4,
            scratch_shapes=[pltpu.VMEM((LEN, LEN), bf)] * 2
            + [pltpu.VMEM((LEN, 128), f32)] * 4
            + [pltpu.VMEM((LEN, 128), bf)] * 4
            + [pltpu.VMEM((D, 384), f32), pltpu.VMEM((shards,) + part, bf)]
            + sum([reduce_scratch(shapes[k], shards, reps, k == "u") for k in "dug"], []),
        ),
        out_shape=[jax.ShapeDtypeStruct((tokens, D), bf)] * 3
        + [
            jax.ShapeDtypeStruct((PAIRS // 2, D, D), bf),
            jax.ShapeDtypeStruct((seqs, PAIRS, 4, 128), f32),
        ]
        + result_shapes(every),
        compiler_params=pltpu.CompilerParams(
            vmem_limit_bytes=62 << 20, collective_id=collective_id, has_side_effects=True
        ),
        name="attention_backward",
    )(lengths, rounded, proj, datt, rows, *grads)


def norm_stats(x):
    c=jnp.mean(x,axis=-1,keepdims=True)
    xc=x-c
    r=lax.rsqrt(jnp.mean(xc*xc,axis=-1,keepdims=True)+eps_norm)
    return xc*r,r

def norm_back(up,normed,r,gain):
    g=up*gain
    return r*(g-jnp.mean(g,axis=-1,keepdims=True)-normed*jnp.mean(g*normed,axis=-1,keepdims=True))

def colsum(x): return jnp.sum(x,axis=0,keepdims=True)

def gelu_parts(u):
    cdf=0.5+0.5*lax.erf(u*0.7071067811865476)
    pdf=jnp.exp(-0.5*u*u)*0.3989422804014327
    return u*cdf,cdf+u*pdf

def middle_body(len_ref,h_ref,a_ref,ct_ref,ow_ref,uw_ref,dw_ref,vec_ref,ub_ref,
               out_ref,bs_ref,ba_ref,act,pl_,low_ref,d2_ref,sl_ref,small_ref,ubg_ref,
               gp,n1_ref,*,T,sub_rows,chunk):
    i=pl.program_id(0)
    per=LEN//T
    count=len_ref[i//per]
    @pl.when(i==0)
    def _():
        small_ref[...]=jnp.zeros_like(small_ref); ubg_ref[...]=jnp.zeros_like(ubg_ref)
    out_b,g1,b1,down_b,g2,b2=[vec_ref[j:j+1,:] for j in range(6)]
    parts=[slice(k,k+sub_rows) for k in range(0,T,sub_rows)]
    r1s=[];sums=[]
    xs=[dot_nn(a_ref[p,:],ow_ref[...]) for p in parts]
    for p,x in zip(parts,xs):
        n1,r1=norm_stats(h_ref[p,:]+x+out_b)
        n1_ref[p,:]=n1; r1s.append(r1)
        low_ref[p,:]=(n1*g1+b1).astype(bf)
    for j in range(0,FF,chunk):
        sl=slice(j,j+chunk)
        for p in parts:
            u=dot_nn(low_ref[p,:],uw_ref[:,sl])+ub_ref[:,sl]
            a,g=gelu_parts(u)
            act[p,sl]=a.astype(bf); gp[p,sl]=g.astype(gp.dtype)
    ys=[dot_nn(act[p,:],dw_ref[...]) for p in parts]
    for p,y in zip(parts,ys):
        pos=lax.broadcasted_iota(jnp.int32,(sub_rows,1),0)+(i%per)*T+p.start
        valid=jnp.where(pos<count,1.0,0.0)
        second=n1_ref[p,:]*g1+b1+y+down_b
        n2,r2=norm_stats(second)
        out_ref[p,:]=valid*(n2*g2+b2)
        up=valid*ct_ref[p,:]
        b2nd=norm_back(up,n2,r2,g2)
        d2_ref[p,:]=b2nd.astype(bf)
        bs_ref[p,:]=b2nd
        sums.append(jnp.concatenate([colsum(b2nd),colsum(up*n2),colsum(up)],axis=0))
    small_ref[3:6,:]+=sum(sums[1:],sums[0])
    for j in range(0,FF,chunk):
        sl=slice(j,j+chunk)
        cs=[]
        for p in parts:
            bp=dot_nt(d2_ref[p,:],dw_ref[sl,:])*gp[p,sl].astype(f32)
            cs.append(colsum(bp))
            pl_[p,sl]=bp.astype(bf)
        ubg_ref[:,sl]+=sum(cs[1:],cs[0])
    zs=[dot_nt(pl_[p,:],uw_ref[...]) for p in parts]
    sums=[]
    for p,z,r1 in zip(parts,zs,r1s):
        bfirst=z+bs_ref[p,:]
        n1=n1_ref[p,:]
        bsum=norm_back(bfirst,n1,r1,g1)
        bs_ref[p,:]=bsum
        sl_ref[p,:]=bsum.astype(bf)
        sums.append(jnp.concatenate([colsum(bsum),colsum(bfirst*n1),colsum(bfirst)],axis=0))
    small_ref[0:3,:]+=sum(sums[1:],sums[0])
    for p in parts:
        ba_ref[p,:]=dot_nt(sl_ref[p,:],ow_ref[...]).astype(bf)

def middle(lengths,hidden,att,ct,ow,uw,dw,vec,ub,T=512,chunk=768,gpt=f32,sub_rows=256):
    tokens=hidden.shape[0]
    tile=lambda n=D: pl.BlockSpec((T,n),lambda i,l:(i,0))
    const=lambda shape: pl.BlockSpec(shape,lambda i,l:(0,0),pipeline_mode=pl.Buffered(1))
    whole=lambda shape: pl.BlockSpec(shape,lambda i,l:(0,0))
    sd=lambda n,dt: jax.ShapeDtypeStruct((tokens,n),dt)
    return pl.pallas_call(
        partial(middle_body,T=T,chunk=chunk,sub_rows=sub_rows),
        grid_spec=pltpu.PrefetchScalarGridSpec(num_scalar_prefetch=1,grid=(tokens//T,),
          in_specs=[tile(),tile(),tile(),const((D,D)),const((D,FF)),const((FF,D)),whole((8,D)),whole((1,FF))],
          out_specs=[tile(),tile(),tile(),tile(FF),tile(FF),tile(),tile(),tile(),whole((8,D)),whole((1,FF))],
          scratch_shapes=[pltpu.VMEM((T,FF),gpt),pltpu.VMEM((T,D),f32)]),
        out_shape=[sd(D,f32),sd(D,f32),sd(D,bf),sd(FF,bf),sd(FF,bf),sd(D,bf),sd(D,bf),sd(D,bf),jax.ShapeDtypeStruct((8,D),f32),jax.ShapeDtypeStruct((1,FF),f32)],
        compiler_params=pltpu.CompilerParams(vmem_limit_bytes=63<<20),
        name="middle")(lengths,hidden,att,ct,ow,uw,dw,vec,ub)


def weight_grads_body(act,d2,low,pre,att,sl,down_ref,up_ref,out_ref,left,right,left_sem,right_sem):
    i=pl.program_id(0)
    def block(ref,j):
        return ref if ref.shape[1]==D else ref.at[:,j*D:(j+1)*D]
    def fetch(ref,j,slot,to_left):
        return pltpu.make_async_copy(block(ref,j),(left if to_left else right).at[slot],(left_sem if to_left else right_sem).at[slot])
    loads={0:((act,0,0,True),(d2,0,0,False),(act,1,1,True)),1:((act,2,0,True),(pre,0,1,False)),2:((act,3,1,True),),
           3:((low,0,0,True),),4:((pre,1,0,False),(att,0,1,True)),5:((pre,2,1,False),),6:((pre,3,0,False),),7:((sl,0,1,False),)}
    needs={0:((act,0,0,True),(d2,0,0,False)),1:((act,1,1,True),),2:((act,2,0,True),),3:((act,3,1,True),),4:((low,0,0,True),(pre,0,1,False)),
           5:((pre,1,0,False),),6:((pre,2,1,False),),7:((pre,3,0,False),),8:((att,0,1,True),(sl,0,1,False))}
    for k in range(9):
        def move(k=k):
            for one in loads.get(k,()): fetch(*one).start()
            for one in needs[k]: fetch(*one).wait()
        pl.when(i==k)(move)
    l=jnp.where(i<4,lax.rem(i,2),jnp.where(i<8,0,1))
    r=jnp.where(i<4,0,jnp.where(i<8,lax.rem(i+1,2),1))
    grad=dot_tn(left[l],right[r]).astype(bf)
    @pl.when(i<4)
    def _(): down_ref[...]=grad
    @pl.when(jnp.logical_and(i>=4,i<8))
    def _(): up_ref[...]=grad
    @pl.when(i==8)
    def _(): out_ref[...]=grad
def weight_grads(act,d2,low,pre,att,sl):
    tokens=act.shape[0]
    return pl.pallas_call(weight_grads_body,grid=(9,),
        in_specs=[pl.BlockSpec(memory_space=pl.ANY)]*6,
        out_specs=[pl.BlockSpec((D,D),lambda i:(jnp.minimum(i,3),0)),pl.BlockSpec((D,D),lambda i:(0,jnp.clip(i-4,0,3))),pl.BlockSpec((D,D),lambda i:(0,0))],
        out_shape=[jax.ShapeDtypeStruct((FF,D),bf),jax.ShapeDtypeStruct((D,FF),bf),jax.ShapeDtypeStruct((D,D),bf)],
        scratch_shapes=[pltpu.VMEM((2,tokens,D),bf),pltpu.VMEM((2,tokens,D),bf),pltpu.SemaphoreType.DMA((2,)),pltpu.SemaphoreType.DMA((2,))],
        compiler_params=pltpu.CompilerParams(vmem_limit_bytes=60<<20),name="weight_grads")(act,d2,low,pre,att,sl)


def input_grad_body(shards,reps,shapes,bs_ref,dq_ref,dk_ref,dv_ref,w_ref,*refs):
    n=len(shapes)
    grads,out_ref,sums,scratch=refs[:n],refs[n],refs[n+1:2*n+1],refs[2*n+1:]
    place=Place(shards,reps); step=pl.program_id(0)
    size=len(reduce_scratch(shapes[1:],shards,reps))
    jobs={"a":Reduce(place,grads[1:],sums[1:],scratch[:size]),"b":Reduce(place,grads[:1],sums[:1],scratch[size:],True)}
    end=follow(LAST_PLAN,jobs,step,pl.num_programs(0)-1,lambda: meet(place,True))
    out_ref[...]=bs_ref[...]+dot_nt(dq_ref[...],w_ref[:,0:D])+dot_nt(dk_ref[...],w_ref[:,D:2*D])+dot_nt(dv_ref[...],w_ref[:,2*D:3*D])
    end()
def input_grad(back_sum,dq,dk,dv,weight,grads,shards,reps,collective_id):
    rows=back_sum.shape[0]//8
    tile=pl.BlockSpec((rows,D),lambda i:(i,0))
    anywhere=[pl.BlockSpec(memory_space=pl.ANY)]*len(grads)
    shapes=[g.shape[1:] for g in grads]
    return pl.pallas_call(partial(input_grad_body,shards,reps,shapes),grid=(8,),
        in_specs=[tile]*4+[pl.BlockSpec((D,3*D),lambda i:(0,0),pipeline_mode=pl.Buffered(1))]+anywhere,
        out_specs=[tile]+anywhere,
        out_shape=[jax.ShapeDtypeStruct(back_sum.shape,f32)]+result_shapes(shapes),
        scratch_shapes=reduce_scratch(shapes[1:],shards,reps)+reduce_scratch(shapes[:1],shards,reps,True),
        compiler_params=pltpu.CompilerParams(vmem_limit_bytes=50<<20,collective_id=collective_id,has_side_effects=True),name="input_grad")(back_sum,dq,dk,dv,weight,*grads)


def as_rows(row):
    filled = -(-row.shape[-1] // 128)
    row = jnp.pad(row, ((0, 0), (0, filled * 128 - row.shape[-1])))
    return jnp.pad(row.reshape(-1, filled, 128), ((0, 0), (0, 0), (0, 128)))


def pack_body(*refs):
    *ins, out = refs
    rows = []
    for ref in ins:
        value = ref[...].astype(f32)
        for at in range(0, value.shape[0], 128):
            part = value[at : at + 128].reshape(1, -1)
            rows.append(jnp.pad(part, ((0, 0), (0, 256 - part.shape[1]))))
    rows.append(jnp.zeros((16 - len(rows), 256), f32))
    out[...] = jnp.concatenate(rows, axis=0).astype(bf)


def pack_shards(vectors):
    return pl.pallas_call(
        pack_body, out_shape=jax.ShapeDtypeStruct((16, 256), bf), name="pack_vectors"
    )(*vectors)


def pack_vectors(vectors):
    rows = jnp.concatenate([as_rows(v) for v in vectors], axis=1)
    return jnp.pad(rows, ((0, 0), (0, 16 - rows.shape[1]), (0, 0)))


def local(
    hidden,
    lengths,
    clusters,
    input_weight,
    query_bias,
    value_bias,
    out_weight,
    out_bias,
    norm1_gain,
    norm1_bias,
    up_weight,
    up_bias,
    down_weight,
    down_bias,
    norm2_gain,
    norm2_bias,
    cotangent,
    *,
    shards,
    reps,
):
    seqs = hidden.shape[0]
    tokens = seqs * LEN
    part = D // shards
    vectors = pack_shards(
        (
            query_bias,
            value_bias,
            out_bias,
            norm1_gain,
            norm1_bias,
            down_bias,
            norm2_gain,
            norm2_bias,
            up_bias,
        )
    )
    in_w, vectors = gather_now((input_weight, vectors), shards, reps, 1)
    in_w = in_w.reshape(D, 3 * D)
    vectors = vectors.astype(f32)
    table = vectors[:, :8, :part].transpose(1, 0, 2).reshape(8, D)
    bias_all = jnp.concatenate([table[0], jnp.zeros((D,), f32), table[1]])[None]
    norm_rows = jnp.concatenate([table[2:], table[:2]])
    up_b = vectors[:, 8:, :128].reshape(shards, -1)[:, : FF // shards].reshape(1, FF)

    flat = hidden.reshape(tokens, D)
    attended, proj, rounded, up_w, down_w, out_w = attention_forward(
        lengths,
        flat,
        in_w,
        bias_all,
        clusters,
        (up_weight, down_weight, out_weight),
        shards,
        reps,
        2,
    )
    out_w, up_w, down_w = [w.reshape(-1, w.shape[-1]) for w in (out_w, up_w, down_w)]
    (
        result,
        back_sum,
        back_attended,
        activated,
        pre_low,
        first_low,
        second_low,
        sum_low,
        norm_sums,
        up_b_sum,
    ) = middle(
        lengths,
        flat,
        attended,
        cotangent.reshape(tokens, D),
        out_w,
        up_w,
        down_w,
        norm_rows,
        up_b,
    )
    down_g, up_g, out_g = weight_grads(
        activated, second_low, first_low, pre_low, attended, sum_low
    )
    dq, dk, dv, in_g, bias_sums, down_s, up_s, out_s, in_first = attention_backward(
        lengths,
        rounded,
        proj,
        back_attended,
        clusters,
        [g.reshape(shards, -1, g.shape[-1]) for g in (down_g, up_g, out_g)],
        shards,
        reps,
        3,
    )
    bias_sums = jnp.sum(bias_sums, axis=0)
    query_sum = bias_sums[:, 0:2, DH:].reshape(D)
    value_sum = jnp.concatenate([bias_sums[:, 2, :DH], bias_sums[:, 3, DH:]], axis=1).reshape(D)
    table = jnp.concatenate([query_sum[None], value_sum[None], norm_sums[:6]])
    table = table.reshape(8, shards, part)
    small = pack_vectors(
        [table[i].astype(bf) for i in range(8)] + [up_b_sum.reshape(shards, -1).astype(bf)]
    )
    back_input, *in_s, small_s = input_grad(
        back_sum,
        dq,
        dk,
        dv,
        in_w,
        [in_g[2].reshape(shards, part, D), in_g[1].reshape(shards, part, D), small],
        shards,
        reps,
        4,
    )
    back_input = back_input.reshape(seqs, LEN, D)
    in_s = [in_first, in_s[1], in_s[0]]
    in_s = jnp.concatenate(
        [
            in_s[g][c, :, 128 * t : 128 * t + 128]
            for t in range(3)
            for c in range(2)
            for g in range(PAIRS // 2)
        ],
        axis=1,
    )

    def whole(halves):
        return jnp.concatenate([halves[0], halves[1]], axis=1)

    small_s = small_s[0]
    vec = [small_s[i, :part] for i in range(8)]
    return (
        result.reshape(seqs, LEN, D),
        back_input,
        in_s,
        vec[0],
        vec[1],
        whole(out_s),
        vec[2],
        vec[3],
        vec[4],
        whole(up_s),
        small_s[8:].reshape(-1)[: FF // shards],
        whole(down_s),
        vec[5],
        vec[6],
        vec[7],
    )


def solution(mesh):
    tokens = P(("rep", "shard"), None, None)
    matrix, vector = P("shard", None), P("shard")
    params = (
        matrix,
        vector,
        vector,
        matrix,
        vector,
        vector,
        vector,
        matrix,
        vector,
        matrix,
        vector,
        vector,
        vector,
    )
    return jax.shard_map(
        partial(local, shards=mesh.shape["shard"], reps=mesh.shape["rep"]),
        mesh=mesh,
        in_specs=(tokens, P(("rep", "shard")), tokens) + params + (tokens,),
        out_specs=(tokens, tokens) + params,
        check_vma=False,
    )
```

```python
from functools import partial

import jax
import jax.numpy as jnp
from jax import lax
from jax.experimental import pallas as pl
from jax.experimental.pallas import tpu as pltpu
from jax.sharding import PartitionSpec as P

D = 768
H = 12
DH = 64
FF = 3072
CLUSTER = 128
LEN = 1024
PAIRS = H // 2
SLICES = [slice(c * CLUSTER, (c + 1) * CLUSTER) for c in range(LEN // CLUSTER)]
bf = jnp.bfloat16
f32 = jnp.float32
eps_norm = 1e-12


def dot_nn(left, right):
    return lax.dot_general(left, right, (((1,), (0,)), ((), ())), preferred_element_type=f32)


def dot_nt(left, right):
    return lax.dot_general(left, right, (((1,), (1,)), ((), ())), preferred_element_type=f32)


def dot_tn(left, right):
    return lax.dot_general(left, right, (((0,), (0,)), ((), ())), preferred_element_type=f32)


ROWS = 4
MESH=pl.DeviceIdType.MESH

def when(cond,do):
    if cond is None: do()
    else: pl.when(cond)(do)

class Place:
    def __init__(self,shards,reps):
        self.Y=shards//ROWS; self.S=shards; self.X=reps//2
        self.s=lax.axis_index("shard"); self.r=lax.axis_index("rep")
        self.z=self.s//self.Y; self.y=lax.rem(self.s,self.Y)
        self.core=lax.rem(self.r,2); self.x=self.r//2
    def near_z(self,step): return {"shard":self.s+step*self.Y}
    def other_y(self,k): return {"shard":self.z*self.Y+lax.rem(self.y+k,self.Y)}
    def other_core(self): return {"rep":self.r+1-2*self.core}
    def other_x(self,k): return {"rep":2*lax.rem(self.x+k,self.X)+self.core}

def meet(place,with_x):
    sem=pltpu.get_barrier_semaphore()
    def tell(dev): pl.semaphore_signal(sem,inc=1,device_id=dev,device_id_type=MESH)
    pl.when(place.z>0)(lambda: tell(place.near_z(-1)))
    pl.when(place.z<ROWS-1)(lambda: tell(place.near_z(1)))
    for k in range(1,place.Y): tell(place.other_y(k))
    tell(place.other_core())
    if with_x:
        for k in range(1,place.X): tell(place.other_x(k))
    others=place.Y+(place.X-1 if with_x else 0)
    inner=jnp.logical_and(place.z>0,place.z<ROWS-1)
    pl.when(inner)(lambda: pl.semaphore_wait(sem,others+2))
    pl.when(jnp.logical_not(inner))(lambda: pl.semaphore_wait(sem,others+1))

def gather_semaphores(count,shards):
    Y=shards//ROWS; dma=pltpu.SemaphoreType.DMA
    return [dma((count,2,ROWS)),dma((count,2,ROWS)),dma((count,ROWS,Y)),dma((count,ROWS,Y)),
            dma((count,2,shards)),dma((count,2,shards)),dma((count,shards)),dma((count,shards)),dma((count,))]

class Gather:
    def __init__(self,place,ins,outs,sems,share=False):
        self.p=place; self.ins=ins; self.outs=outs; self.share=share and place.X==2
        self.line_s,self.line_r,self.y_s,self.y_r,self.core_s,self.core_r,self.x_s,self.x_r,self.own=sems
        self.sent=[]
    def piece(self,ref,shard=None,core=None,x=None):
        p=self.p; n=ref.shape[-1]//2; r=ref.shape[-2]
        cols=pl.ds(pl.multiple_of((p.core if core is None else core)*n,128),n)
        rows=slice(None)
        if self.share:
            rows=pl.ds(pl.multiple_of((p.x if x is None else x)*(r//2),16),r//2)
        return ref.at[rows,cols] if shard is None else ref.at[shard,rows,cols]
    def send(self,make):
        cond,desc=make()
        when(cond,desc.start); self.sent.append(make)
    def copy(self,src,dst,ss,rs,dev):
        return pltpu.make_async_remote_copy(src_ref=src,dst_ref=dst,send_sem=ss,recv_sem=rs,device_id=dev,device_id_type=MESH)
    def at(self,places):
        zz=self.p.z+places
        if places==0: return None,zz
        return jnp.logical_and(zz>=0,zz<ROWS),jnp.clip(zz,0,ROWS-1)
    def shard_at(self,zz,k):
        p=self.p
        return zz*p.Y+(lax.rem(p.y-k+p.Y,p.Y) if k else p.y)
    def to_line(self,a,places,d):
        p=self.p; i,o=self.ins[a],self.outs[a]
        def make():
            cond,zz=self.at(places); shard=zz*p.Y+p.y
            edge=(p.z<ROWS-1) if d==0 else (p.z>0)
            src=self.piece(i) if places==0 else self.piece(o,shard)
            return (edge if cond is None else jnp.logical_and(cond,edge)),self.copy(src,self.piece(o,shard),self.line_s.at[a,d,zz],self.line_r.at[a,d,zz],p.near_z(1 if d==0 else -1))
        self.send(make)
    def to_y(self,a,places,k):
        p=self.p; i,o=self.ins[a],self.outs[a]
        def make():
            cond,zz=self.at(places); shard=zz*p.Y+p.y
            src=self.piece(i) if places==0 else self.piece(o,shard)
            return cond,self.copy(src,self.piece(o,shard),self.y_s.at[a,zz,k],self.y_r.at[a,zz,k],p.other_y(k))
        self.send(make)
    def to_core(self,a,places,k,other=False):
        p=self.p; o=self.outs[a]; slot=1 if other else 0
        def make():
            cond,zz=self.at(places); shard=self.shard_at(zz,k)
            ref=self.piece(o,shard,x=1-p.x if other else p.x)
            return cond,self.copy(ref,ref,self.core_s.at[a,slot,shard],self.core_r.at[a,slot,shard],p.other_core())
        self.send(make)
    def to_x(self,a,places,k):
        p=self.p; o=self.outs[a]
        if not self.share: return
        def make():
            cond,zz=self.at(places); shard=self.shard_at(zz,k)
            ref=self.piece(o,shard)
            return cond,self.copy(ref,ref,self.x_s.at[a,shard],self.x_r.at[a,shard],p.other_x(1))
        self.send(make)
    def begin(self):
        for a,(i,o) in enumerate(zip(self.ins,self.outs)):
            for d in (0,1): self.to_line(a,0,d)
            for k in range(1,self.p.Y): self.to_y(a,0,k)
            pltpu.make_async_copy(i,o.at[self.p.s],self.own.at[a]).start()
    def wave(self,w):
        p=self.p
        for d in (0,1):
            places=-w if d==0 else w
            for a,o in enumerate(self.outs):
                cond,zz=self.at(places); ref=self.piece(o,zz*p.Y+p.y)
                when(cond,self.copy(ref,ref,self.line_s.at[a,d,zz],self.line_r.at[a,d,zz],p.near_z(0)).wait_recv)
                self.to_line(a,places,d)
                for k in range(1,p.Y): self.to_y(a,places,k)
                self.to_x(a,places,0); self.to_core(a,places,0)
    def across(self,w):
        p=self.p
        for places in ((0,) if w==0 else (-w,w)):
            for k in range(1,p.Y):
                for a,o in enumerate(self.outs):
                    cond,zz=self.at(places); ref=self.piece(o,self.shard_at(zz,k))
                    when(cond,self.copy(ref,ref,self.y_s.at[a,zz,k],self.y_r.at[a,zz,k],p.other_y(k)).wait_recv)
                    self.to_x(a,places,k); self.to_core(a,places,k)
    def over(self,w):
        p=self.p
        if not self.share: return
        for places in ((0,) if w==0 else (-w,w)):
            for k in range(1 if w==0 else 0,p.Y):
                for a,o in enumerate(self.outs):
                    cond,zz=self.at(places); shard=self.shard_at(zz,k); ref=self.piece(o,shard,x=1-p.x)
                    when(cond,self.copy(ref,ref,self.x_s.at[a,shard],self.x_r.at[a,shard],p.other_x(1)).wait_recv)
                    self.to_core(a,places,k,True)
    def finish(self):
        p=self.p
        for a,(i,o) in enumerate(zip(self.ins,self.outs)):
            for k in range(1,p.S):
                shard=lax.rem(p.s+k,p.S)
                for slot in range(2 if self.share else 1):
                    ref=self.piece(o,shard,core=1-p.core,x=1-p.x if slot else p.x)
                    self.copy(ref,ref,self.core_s.at[a,slot,shard],self.core_r.at[a,slot,shard],p.other_core()).wait_recv()
            pltpu.make_async_copy(i,o.at[p.s],self.own.at[a]).wait()
        for make in self.sent:
            cond,desc=make()
            when(cond,desc.wait_send)
def gather_body(shards,reps,count,*refs):
    ins,outs,sems=refs[:count],refs[count:2*count],refs[2*count:]
    place=Place(shards,reps)
    meet(place,False)
    G=Gather(place,ins,outs,sems)
    G.begin(); G.wave(1); G.across(0); G.wave(2); G.across(1); G.wave(3); G.across(2); G.across(3); G.finish()

def gather_now(arrays,shards,reps,collective_id):
    count=len(arrays)
    return pl.pallas_call(partial(gather_body,shards,reps,count),
        in_specs=[pl.BlockSpec(memory_space=pltpu.VMEM)]*count,
        out_specs=[pl.BlockSpec(memory_space=pl.ANY)]*count,
        out_shape=[jax.ShapeDtypeStruct((shards,)+a.shape,a.dtype) for a in arrays],
        scratch_shapes=gather_semaphores(count,shards),
        compiler_params=pltpu.CompilerParams(collective_id=collective_id,has_side_effects=True,vmem_limit_bytes=16<<20),
        name="gather_weights")(*arrays)

ORDER=(3,0,2,1)
def reduce_scratch(shapes,shards,reps,x_first=False):
    x_first=x_first and reps==4
    S=shards; Y=S//ROWS; X=reps//2; A=len(shapes)
    out=[]
    for r,c in shapes:
        n=c//2; m=r//2 if x_first else r
        out+=[pltpu.VMEM((S,r,n),bf),pltpu.VMEM((S,r,n),bf),pltpu.VMEM((max(Y-1,1),ROWS,m,n),bf),
              pltpu.VMEM((ROWS+1,m,n),bf),pltpu.VMEM((S+1,m,n) if x_first else (X,r,n),bf),pltpu.VMEM((2,r,n),f32)]
    dma=pltpu.SemaphoreType.DMA
    return out+[dma((A,S)),dma((A,S)),dma((A,S)),dma((A,Y,ROWS)),dma((A,Y,ROWS)),dma((A,ROWS+1)),dma((A,ROWS+1)),dma((A,S+X)),dma((A,S+X)),dma((A,)),dma((A,)),dma((A,2))]
class Reduce:
    def __init__(self,place,ins,outs,scratch,x_first=False):
        self.p=place; self.ins=ins; self.outs=outs; A=len(ins); self.A=range(A)
        self.bufs=[scratch[6*a:6*a+6] for a in range(A)]
        (self.own,self.core_s,self.core_r,self.y_s,self.y_r,self.line_s,self.line_r,self.x_s,self.x_r,self.end_s,self.end_r,self.out_s)=scratch[6*A:]
        self.sent=[]; self.x_first=x_first and place.X==2
    def copy(self,src,dst,ss,rs,dev):
        return pltpu.make_async_remote_copy(src_ref=src,dst_ref=dst,send_sem=ss,recv_sem=rs,device_id=dev,device_id_type=MESH)
    def send(self,make):
        cond,desc=make()
        when(cond,desc.start); self.sent.append(make)
    def half(self,a,shard,core):
        n=self.ins[a].shape[-1]//2
        return self.ins[a].at[shard,:,pl.ds(pl.multiple_of(core*n,128),n)]
    def mine(self,a,shard,x=None):
        H=self.bufs[a][0]
        if not self.x_first: return H.at[shard]
        m=H.shape[1]//2
        return H.at[shard,pl.ds(pl.multiple_of((self.p.x if x is None else x)*m,16),m)]
    def add(self,dst,others):
        rows,n=dst.shape; step=next(s for s in (192,96,48,16) if rows%s==0 and (s==16 or s*n<=96*768))
        def block(at):
            value=dst[at,:]
            for o in others: value=value+o[at,:]
            dst[at,:]=value
        if rows==step: block(slice(0,rows)); return
        def body(i,_):
            block(pl.ds(pl.multiple_of(i*step,16),step))
            return 0
        lax.fori_loop(0,rows//step,body,0)
    def begin(self,ks=None):
        p=self.p
        for k in (list(range(1,p.Y)) if ks is None else ks):
            for d in ORDER:
                for a in self.A:
                    H,Rc=self.bufs[a][0:2]
                    def make(a=a,d=d,k=k,Rc=Rc):
                        shard=d*p.Y+lax.rem(p.y+k,p.Y)
                        return None,self.copy(self.half(a,shard,1-p.core),Rc.at[shard],self.core_s.at[a,shard],self.core_r.at[a,shard],p.other_core())
                    self.send(make)
                    shard=d*p.Y+lax.rem(p.y+k,p.Y)
                    pltpu.make_async_copy(self.half(a,shard,p.core),H.at[shard],self.own.at[a,shard]).start()
    def join_core(self,shard):
        p=self.p
        for a in self.A:
            H,Rc=self.bufs[a][0:2]
            pltpu.make_async_copy(self.half(a,shard,p.core),H.at[shard],self.own.at[a,shard]).wait()
            self.copy(Rc.at[shard],Rc.at[shard],self.core_s.at[a,shard],self.core_r.at[a,shard],p.other_core()).wait_recv()
            self.add(H.at[shard],[Rc.at[shard]])
    def to_pair(self,k,d):
        p=self.p; shard=d*p.Y+lax.rem(p.y+k,p.Y)
        if not self.x_first: return
        self.join_core(shard)
        for a in self.A:
            def make(a=a):
                shard=d*p.Y+lax.rem(p.y+k,p.Y)
                return None,self.copy(self.mine(a,shard,1-p.x),self.bufs[a][4].at[shard],self.x_s.at[a,shard],self.x_r.at[a,shard],p.other_x(1))
            self.send(make)
    def ready(self,shard):
        p=self.p
        if not self.x_first: self.join_core(shard); return
        for a in self.A:
            got=self.bufs[a][4].at[shard]
            self.copy(got,got,self.x_s.at[a,shard],self.x_r.at[a,shard],p.other_x(1)).wait_recv()
            self.add(self.mine(a,shard),[got])
    def to_y(self,d):
        p=self.p
        for k in range(1,p.Y):
            self.ready(d*p.Y+lax.rem(p.y+k,p.Y))
            for a in self.A:
                H,_,Ry=self.bufs[a][0:3]
                def make(a=a,H=H,Ry=Ry,k=k):
                    shard=d*p.Y+lax.rem(p.y+k,p.Y)
                    return None,self.copy(self.mine(a,shard),Ry.at[k-1,d],self.y_s.at[a,k,d],self.y_r.at[a,k,d],p.other_y(k))
                self.send(make)
    def own_y(self,d):
        self.ready(d*self.p.Y+self.p.y)
    def along(self,d,up,j):
        p=self.p
        if (j>=d) if up else (ROWS-1-j<=d): return
        here=p.z==(j if up else ROWS-1-j)
        shard=d*p.Y+p.y
        if j>0:
            def add_in():
                for a in self.A:
                    H,Rl=self.bufs[a][0],self.bufs[a][3]
                    self.copy(Rl.at[d],Rl.at[d],self.line_s.at[a,d],self.line_r.at[a,d],p.near_z(0)).wait_recv()
                    self.add(self.mine(a,shard),[Rl.at[d]])
            pl.when(here)(add_in)
        last=(j==d-1) if up else (ROWS-1-j==d+1)
        slot=ROWS if last and not up else d
        for a in self.A:
            def make(a=a):
                H,Rl=self.bufs[a][0],self.bufs[a][3]
                return p.z==(j if up else ROWS-1-j),self.copy(self.mine(a,d*p.Y+p.y),Rl.at[slot],self.line_s.at[a,slot],self.line_r.at[a,slot],p.near_z(1 if up else -1))
            self.send(make)
    def line(self,d):
        p=self.p; shard=d*p.Y+p.y
        for a in self.A:
            H,_,Ry=self.bufs[a][0:3]
            for k in range(1,p.Y):
                self.copy(Ry.at[k-1,d],Ry.at[k-1,d],self.y_s.at[a,k,d],self.y_r.at[a,k,d],p.other_y(k)).wait_recv()
            self.add(self.mine(a,shard),[Ry.at[k-1,d] for k in range(1,p.Y)])
        self.along(d,True,0); self.along(d,False,0)
    def relay(self,d,j):
        self.along(d,True,j); self.along(d,False,j)
    def to_x(self):
        p=self.p
        for slot,cond in ((p.z,p.z>0),(ROWS,p.z<ROWS-1)):
            def add_in(slot=slot):
                for a in self.A:
                    H,Rl=self.bufs[a][0],self.bufs[a][3]
                    self.copy(Rl.at[slot],Rl.at[slot],self.line_s.at[a,slot],self.line_r.at[a,slot],p.near_z(0)).wait_recv()
                    self.add(self.mine(a,p.s),[Rl.at[slot]])
            pl.when(cond)(add_in)
        for a in self.A:
            H,Rx=self.bufs[a][0],self.bufs[a][4]
            if self.x_first:
                self.send(lambda a=a,Rx=Rx: (None,self.copy(self.mine(a,p.s),Rx.at[p.S],self.x_s.at[a,p.S],self.x_r.at[a,p.S],p.other_x(1))))
                continue
            for k in range(1,p.X):
                self.send(lambda a=a,H=H,Rx=Rx,k=k: (None,self.copy(H.at[p.s],Rx.at[p.x],self.x_s.at[a,k],self.x_r.at[a,p.x],p.other_x(k))))
    def to_core(self):
        p=self.p
        for a in self.A:
            H,Rx,F=self.bufs[a][0],self.bufs[a][4],self.bufs[a][5]
            if self.x_first:
                got=Rx.at[p.S]; m=H.shape[1]//2
                self.copy(got,got,self.x_s.at[a,p.S],self.x_r.at[a,p.S],p.other_x(1)).wait_recv()
                for x in range(2):
                    own=H[p.s,x*m:(x+1)*m,:]
                    F[p.core,x*m:(x+1)*m,:]=jnp.where(p.x==x,own,Rx[p.S]).astype(f32)
                continue
            for k in range(1,p.X):
                src=lax.rem(p.x-k+p.X,p.X)
                self.copy(Rx.at[src],Rx.at[src],self.x_s.at[a,k],self.x_r.at[a,src],p.other_x(k)).wait_recv()
            rows=H.shape[1]; step=48 if rows%48==0 else 16
            def body(i,_):
                at=pl.ds(pl.multiple_of(i*step,16),step)
                own=H[p.s,at,:].astype(f32)
                value=jnp.zeros_like(own)
                for q in range(p.X):
                    value=value+jnp.where(p.x==q,own,Rx[q,at,:].astype(f32))
                F[p.core,at,:]=value
                return 0
            lax.fori_loop(0,rows//step,body,0)
        for a in self.A:
            F=self.bufs[a][5]
            self.send(lambda a=a,F=F: (None,self.copy(F.at[p.core],F.at[p.core],self.end_s.at[a],self.end_r.at[a],p.other_core())))
    def result(self,a,core):
        F=self.bufs[a][5]; n=F.shape[2]
        return pltpu.make_async_copy(F.at[core],self.outs[a].at[:,core*n:(core+1)*n],self.out_s.at[a,core])
    def finish(self):
        p=self.p
        for a in self.A:
            ref=self.bufs[a][5].at[1-p.core]
            self.copy(ref,ref,self.end_s.at[a],self.end_r.at[a],p.other_core()).wait_recv()
            for core in range(2): self.result(a,core).start()
        for make in self.sent:
            cond,desc=make()
            when(cond,desc.wait_send)
        for a in self.A:
            for core in range(2): self.result(a,core).wait()
def result_shapes(shapes):
    return [jax.ShapeDtypeStruct((r,c),f32) for r,c in shapes]

GATHER_PLAN = {
    0: (("u", "begin"), ("d", "begin")),
    2: (("u", "wave", 1),),
    3: (("d", "wave", 1), ("u", "across", 0)),
    4: (("u", "wave", 2), ("d", "across", 0)),
    6: (("d", "wave", 2),),
    7: (("u", "wave", 3), ("u", "across", 1)),
    8: (("d", "wave", 3), ("d", "across", 1), ("d", "over", 0)),
    10: (("u", "across", 2), ("u", "across", 3), ("d", "across", 2), ("d", "across", 3)),
    11: (("d", "over", 1),),
    100: (("d", "over", 2), ("d", "over", 3), ("u", "finish"), ("d", "finish")),
}


def each(name, what, *more):
    return tuple((name, what, d) + more for d in ORDER)


REDUCE_PLAN = {
    0: (("d", "begin"), ("u", "begin"), ("d", "begin", (0,)), ("u", "begin", (0,))),
    1: each("d", "to_y") + tuple(("u", "to_pair", 1, d) for d in ORDER),
    2: tuple(("u", "to_pair", 0, d) for d in ORDER) + each("d", "own_y") + (("d", "line", 3),),
    3: (("d", "line", 0), ("d", "relay", 3, 1)),
    4: (("g", "begin"), ("g", "begin", (0,)))
    + (("d", "line", 2), ("d", "relay", 0, 1), ("d", "relay", 3, 2))
    + each("u", "to_y"),
    5: (("d", "line", 1), ("d", "relay", 2, 1), ("d", "relay", 0, 2))
    + each("g", "to_y")
    + each("g", "own_y")
    + (("u", "own_y", 3), ("u", "own_y", 0)),
    6: (("d", "relay", 1, 1), ("u", "line", 3), ("u", "line", 0), ("u", "own_y", 2), ("u", "own_y", 1)),
    7: (("d", "to_x"), ("u", "relay", 3, 1), ("u", "relay", 0, 1), ("u", "line", 2), ("u", "line", 1)),
    8: (("d", "to_core"), ("u", "relay", 3, 2), ("u", "relay", 0, 2)) + each("g", "line"),
    9: (("u", "relay", 2, 1), ("u", "relay", 1, 1)) + each("g", "relay", 1),
    10: (("u", "to_x"),) + each("g", "relay", 2),
    11: (("g", "to_x"), ("u", "to_core")),
    100: (("g", "to_core"), ("d", "finish"), ("u", "finish"), ("g", "finish")),
}
LAST_PLAN = {
    0: (("a", "begin"), ("b", "begin"), ("a", "begin", (0,)), ("b", "begin", (0,))),
    1: each("a", "to_y"),
    2: tuple(("b", "to_pair", k, d) for k in (1, 0) for d in ORDER) + each("a", "own_y"),
    4: (("a", "line", 3), ("a", "line", 0)),
    5: (("a", "line", 2), ("a", "line", 1)) + each("b", "to_y"),
    6: each("b", "own_y") + each("a", "relay", 1),
    7: (("a", "relay", 3, 2), ("a", "relay", 0, 2)) + each("b", "line"),
    100: (("a", "to_x"),)
    + each("b", "relay", 1)
    + (("a", "to_core"),)
    + each("b", "relay", 2)
    + (("b", "to_x"), ("b", "to_core"), ("a", "finish"), ("b", "finish")),
}


def follow(plan, jobs, step, last, ready):
    def run(at):
        for name, what, *more in plan.get(at, ()):
            getattr(jobs[name], what)(*more)

    def first():
        ready()
        run(0)

    pl.when(step == 0)(first)
    for at in sorted(plan):
        if 0 < at < 100:
            pl.when(step == at)(partial(run, at))
    return lambda: pl.when(step == last)(partial(run, 100))


def low_lanes():
    return lax.broadcasted_iota(jnp.int32, (LEN, CLUSTER), 1) < DH


def table_of(order_row):
    held = jnp.broadcast_to(order_row.astype(jnp.int16), (LEN, LEN))
    positions = lax.broadcasted_iota(jnp.int16, (LEN, LEN), 0)
    return jnp.where(held == positions, jnp.ones((), bf), jnp.zeros((), bf))


def turned_table_of(order_row):
    held = jnp.transpose(jnp.broadcast_to(order_row, (128, LEN))).astype(jnp.int16)
    lanes = lax.broadcasted_iota(jnp.int16, (LEN, 128), 1)
    return jnp.concatenate(
        [
            jnp.where(held == lanes + jnp.int16(128 * b), jnp.ones((), bf), jnp.zeros((), bf))
            for b in range(LEN // 128)
        ],
        axis=1,
    )


def half_roll(source):
    return pltpu.roll(source, DH, 1)


def softmax_rows(scores):
    top = jnp.max(scores, axis=-1, keepdims=True)
    grown = jnp.exp(scores - top)
    return grown * (1.0 / jnp.sum(grown, axis=-1, keepdims=True))


def attention_forward_body(
    shards, reps, len_ref, h_ref, wq_ref, wk_ref, wv_ref, bq_ref, bk_ref, bv_ref, row_ref, *rest
):
    ins, (att_ref, proj_ref, x_ref), outs = rest[:3], rest[3:6], rest[6:9]
    tables, scores, mixed = rest[9:11], rest[11:13], rest[13:15]
    sems = rest[15:]
    step = pl.program_id(0) * PAIRS + pl.program_id(1)
    place = Place(shards, reps)
    jobs = {
        "u": Gather(place, ins[:1], outs[:1], sems[:9]),
        "d": Gather(place, ins[1:], outs[1:], sems[9:], True),
    }
    end = follow(
        GATHER_PLAN, jobs, step, pl.num_programs(0) * PAIRS - 1, lambda: meet(place, True)
    )

    @pl.when(pl.program_id(1) == 0)
    def _():
        x_ref[...] = h_ref[...].astype(bf)

    count = len_ref[pl.program_id(0)]
    weight = jnp.concatenate([wq_ref[...], wk_ref[...], wv_ref[...]], axis=1)
    bias = jnp.concatenate([bq_ref[...], bk_ref[...], bv_ref[...]], axis=1)
    proj = (dot_nn(x_ref[...], weight) + bias).astype(bf)
    low = low_lanes()
    query, key, value = proj[:, 0:128], proj[:, 128:256], proj[:, 256:384]
    pairs = [jnp.where(low, query, half_roll(key)), jnp.where(low, half_roll(query), key)]
    proj_ref[...] = jnp.concatenate([pairs[0], value, pairs[1]], axis=1)
    rows = [row_ref[0, pl.ds(2 * pl.program_id(1) + e, 1), :] for e in range(2)]
    for e in range(2):
        tables[e][...] = table_of(rows[e])
    picked = [
        dot_nn(turned_table_of(rows[e]), jnp.concatenate([pairs[e], value], axis=1)).astype(bf)
        for e in range(2)
    ]
    for e in range(2):
        qk = picked[e][:, 0:128]
        key_low = jnp.where(low, half_roll(qk), jnp.zeros((), bf))
        bias = jnp.where(rows[e] < count, 0.0, -30000.0)
        for sl in SLICES:
            scores[e][sl, :] = 0.125 * dot_nt(qk[sl], key_low[sl]) + bias[:, sl]
    for e in range(2):
        values = picked[e][:, 128:256]
        for sl in SLICES:
            probs = softmax_rows(scores[e][sl, :]).astype(bf)
            mixed[e][sl, :] = dot_nn(probs, values[sl]).astype(bf)
    placed = [dot_nn(tables[e][...], mixed[e][...]) for e in range(2)]
    att_ref[...] = jnp.where(low, placed[0], placed[1]).astype(bf)
    end()


def attention_forward(lengths, hidden, weight, bias, rows, arrays, shards, reps, collective_id):
    seqs = rows.shape[0]
    tokens = seqs * LEN
    column = lambda part: pl.BlockSpec((D, 128), lambda s, h, n: (0, part * PAIRS + h))
    column_b = lambda part: pl.BlockSpec((1, 128), lambda s, h, n: (0, part * PAIRS + h))
    return pl.pallas_call(
        partial(attention_forward_body, shards, reps),
        grid_spec=pltpu.PrefetchScalarGridSpec(
            num_scalar_prefetch=1,
            grid=(seqs, PAIRS),
            in_specs=[pl.BlockSpec((LEN, D), lambda s, h, n: (s, 0))]
            + [column(part) for part in range(3)]
            + [column_b(part) for part in range(3)]
            + [pl.BlockSpec((1, H, LEN), lambda s, h, n: (s, 0, 0))]
            + [pl.BlockSpec(memory_space=pl.ANY)] * 3,
            out_specs=[
                pl.BlockSpec((LEN, 128), lambda s, h, n: (s, h)),
                pl.BlockSpec((LEN, 384), lambda s, h, n: (s, h)),
                pl.BlockSpec((LEN, D), lambda s, h, n: (s, 0)),
            ]
            + [pl.BlockSpec(memory_space=pl.ANY)] * 3,
            scratch_shapes=[pltpu.VMEM((LEN, LEN), bf)] * 2
            + [pltpu.VMEM((LEN, 128), f32)] * 2
            + [pltpu.VMEM((LEN, 128), bf)] * 2
            + gather_semaphores(1, shards)
            + gather_semaphores(2, shards),
        ),
        out_shape=[
            jax.ShapeDtypeStruct((tokens, D), bf),
            jax.ShapeDtypeStruct((tokens, 3 * D), bf),
            jax.ShapeDtypeStruct((tokens, D), bf),
        ]
        + [jax.ShapeDtypeStruct((shards,) + a.shape, bf) for a in arrays],
        compiler_params=pltpu.CompilerParams(
            vmem_limit_bytes=63 << 20, collective_id=collective_id, has_side_effects=True
        ),
        name="attention_forward",
    )(lengths, hidden, weight, weight, weight, bias, bias, bias, rows, *arrays)


def attention_backward_body(shards, reps, shapes, *refs):
    len_ref, x_ref, proj_ref, datt_ref, row_ref = refs[:5]
    grads, refs = refs[5:8], refs[8:]
    (dq_ref, dk_ref, dv_ref, dw_ref, db_ref), sums, refs = refs[:5], refs[5:9], refs[9:]
    t0, t1, s0, s1, d0, d1, p0, p1, e0, e1, total, group = refs[:12]
    refs = refs[12:]
    turn = pl.program_id(0)
    step = turn * pl.num_programs(1) + pl.program_id(1)
    place = Place(shards, reps)
    sizes = [len(reduce_scratch(shapes[k], shards, reps, k == "u")) for k in "dug"]
    parts = [refs[sum(sizes[:k]) : sum(sizes[: k + 1])] for k in range(3)]
    jobs = {
        "d": Reduce(place, grads[:1], sums[:1], parts[0]),
        "u": Reduce(place, grads[1:], sums[1:3], parts[1], True),
        "g": Reduce(place, [group], sums[3:], parts[2]),
    }
    end = follow(
        REDUCE_PLAN,
        jobs,
        step,
        pl.num_programs(0) * pl.num_programs(1) - 1,
        lambda: meet(place, True),
    )
    seq = pl.program_id(1)
    count = len_ref[seq]
    low = low_lanes()
    zero = jnp.zeros((), bf)
    tables, scores, back_probs, probs_low, backs = (t0, t1), (s0, s1), (d0, d1), (p0, p1), (e0, e1)
    rows = [row_ref[0, pl.ds(2 * pair_at(turn) + e, 1), :] for e in range(2)]
    for e in range(2):
        tables[e][...] = table_of(rows[e])
    datt = datt_ref[...]
    swapped = half_roll(proj_ref[:, 128:256])
    middle = [jnp.where(low, datt, swapped), jnp.where(low, swapped, datt)]
    sources = [
        jnp.concatenate([proj_ref[:, 256 * e : 256 * e + 128], middle[e]], axis=1)
        for e in range(2)
    ]
    picked = [dot_nn(turned_table_of(rows[e]), sources[e]).astype(bf) for e in range(2)]
    for e in range(2):
        qk, dv = picked[e][:, 0:128], picked[e][:, 128:256]
        key_low = jnp.where(low, half_roll(qk), zero)
        turned = half_roll(dv)
        value_only = jnp.where(low, turned, zero) if e == 0 else jnp.where(low, zero, turned)
        bias = jnp.where(rows[e] < count, 0.0, -30000.0)
        for sl in SLICES:
            scores[e][sl, :] = 0.125 * dot_nt(qk[sl], key_low[sl]) + bias[:, sl]
            back_probs[e][sl, :] = dot_nt(dv[sl], value_only[sl])
    for e in range(2):
        for sl in SLICES:
            probs = softmax_rows(scores[e][sl, :])
            back = back_probs[e][sl, :]
            probs_low[e][sl, :] = probs.astype(bf)
            inner = jnp.sum(back * probs, axis=-1, keepdims=True)
            backs[e][sl, :] = (0.125 * (probs * (back - inner))).astype(bf)
    moved = []
    for e in range(2):
        qk, dv = picked[e][:, 0:128], picked[e][:, 128:256]
        queries, keys, values = [], [], []
        for sl in SLICES:
            back = backs[e][sl, :]
            queries.append(dot_nn(back, qk[sl]))
            keys.append(dot_tn(back, qk[sl]))
            values.append(dot_tn(probs_low[e][sl, :], dv[sl]))
        key_query = jnp.where(low, jnp.concatenate(keys, 0), jnp.concatenate(queries, 0))
        value = jnp.concatenate(values, 0)
        db_ref[0, 0, e : e + 1, :] = jnp.sum(key_query, axis=0, keepdims=True)
        db_ref[0, 0, 2 + e : 3 + e, :] = jnp.sum(value, axis=0, keepdims=True)
        moved.append(jnp.concatenate([key_query.astype(bf), value.astype(bf)], axis=1))
    placed = [dot_nn(tables[e][...], moved[e]) for e in range(2)]
    key_queries = [placed[e][:, 0:128] for e in range(2)]
    turned = [pltpu.roll(t, DH, 1) for t in key_queries]
    query = jnp.where(low, turned[0], key_queries[1]).astype(bf)
    key = jnp.where(low, key_queries[0], turned[1]).astype(bf)
    value = jnp.where(low, placed[0][:, 128:256], placed[1][:, 128:256]).astype(bf)
    dq_ref[...] = query
    dk_ref[...] = key
    dv_ref[...] = value
    out = jnp.concatenate([query, key, value], axis=1)
    part = dot_tn(x_ref[...], out)

    @pl.when(seq == 0)
    def _():
        total[...] = part

    @pl.when(seq != 0)
    def _():
        total[...] += part

    dw_ref[0] = total[...].astype(bf)

    @pl.when(turn < 2)
    def _():
        rows = D // shards
        columns = pl.ds(pl.multiple_of(turn * 384, 128), 384)
        for k in range(shards):
            group[k, :, columns] = total[k * rows : (k + 1) * rows, :].astype(bf)

    end()


def pair_at(i):
    return (i % 2) * (PAIRS // 2) + i // 2


def pair_at(i):
    return (i % 2) * (PAIRS // 2) + i // 2


def attention_backward(lengths, rounded, proj, datt, rows, grads, shards, reps, collective_id):
    seqs = rows.shape[0]
    tokens = seqs * LEN
    own = lambda width: pl.BlockSpec((LEN, width), lambda i, s, n: (s, pair_at(i)))
    part = (D // shards, D)
    shapes = {
        "d": [grads[0].shape[1:]],
        "u": [g.shape[1:] for g in grads[1:]],
        "g": [part],
    }
    every = shapes["d"] + shapes["u"] + shapes["g"]
    return pl.pallas_call(
        partial(attention_backward_body, shards, reps, shapes),
        grid_spec=pltpu.PrefetchScalarGridSpec(
            num_scalar_prefetch=1,
            grid=(PAIRS, seqs),
            in_specs=[
                pl.BlockSpec((LEN, D), lambda i, s, n: (s, 0)),
                own(384),
                own(128),
                pl.BlockSpec((1, H, LEN), lambda i, s, n: (s, 0, 0)),
            ]
            + [pl.BlockSpec(memory_space=pl.ANY)] * 3,
            out_specs=[own(128)] * 3
            + [
                pl.BlockSpec((1, D, 384), lambda i, s, n: (i // 2, 0, i % 2)),
                pl.BlockSpec((1, 1, 4, 128), lambda i, s, n: (s, pair_at(i), 0, 0)),
            ]
            + [pl.BlockSpec(memory_space=pl.ANY)] * 4,
            scratch_shapes=[pltpu.VMEM((LEN, LEN), bf)] * 2
            + [pltpu.VMEM((LEN, 128), f32)] * 4
            + [pltpu.VMEM((LEN, 128), bf)] * 4
            + [pltpu.VMEM((D, 384), f32), pltpu.VMEM((shards,) + part, bf)]
            + sum([reduce_scratch(shapes[k], shards, reps, k == "u") for k in "dug"], []),
        ),
        out_shape=[jax.ShapeDtypeStruct((tokens, D), bf)] * 3
        + [
            jax.ShapeDtypeStruct((PAIRS // 2, D, D), bf),
            jax.ShapeDtypeStruct((seqs, PAIRS, 4, 128), f32),
        ]
        + result_shapes(every),
        compiler_params=pltpu.CompilerParams(
            vmem_limit_bytes=62 << 20, collective_id=collective_id, has_side_effects=True
        ),
        name="attention_backward",
    )(lengths, rounded, proj, datt, rows, *grads)


def norm_stats(x):
    c=jnp.mean(x,axis=-1,keepdims=True)
    xc=x-c
    r=lax.rsqrt(jnp.mean(xc*xc,axis=-1,keepdims=True)+eps_norm)
    return xc*r,r

def norm_back(up,normed,r,gain):
    g=up*gain
    return r*(g-jnp.mean(g,axis=-1,keepdims=True)-normed*jnp.mean(g*normed,axis=-1,keepdims=True))

def colsum(x): return jnp.sum(x,axis=0,keepdims=True)

def gelu_parts(u):
    cdf=0.5+0.5*lax.erf(u*0.7071067811865476)
    pdf=jnp.exp(-0.5*u*u)*0.3989422804014327
    return u*cdf,cdf+u*pdf

def middle_body(len_ref,h_ref,a_ref,ct_ref,ow_ref,uw_ref,dw_ref,vec_ref,ub_ref,
               out_ref,bs_ref,ba_ref,act,pl_,low_ref,d2_ref,sl_ref,small_ref,ubg_ref,
               gp,n1_ref,*,T,sub_rows,chunk):
    i=pl.program_id(0)
    per=LEN//T
    count=len_ref[i//per]
    @pl.when(i==0)
    def _():
        small_ref[...]=jnp.zeros_like(small_ref); ubg_ref[...]=jnp.zeros_like(ubg_ref)
    out_b,g1,b1,down_b,g2,b2=[vec_ref[j:j+1,:] for j in range(6)]
    parts=[slice(k,k+sub_rows) for k in range(0,T,sub_rows)]
    r1s=[];sums=[]
    xs=[dot_nn(a_ref[p,:],ow_ref[...]) for p in parts]
    for p,x in zip(parts,xs):
        n1,r1=norm_stats(h_ref[p,:]+x+out_b)
        n1_ref[p,:]=n1; r1s.append(r1)
        low_ref[p,:]=(n1*g1+b1).astype(bf)
    for j in range(0,FF,chunk):
        sl=slice(j,j+chunk)
        for p in parts:
            u=dot_nn(low_ref[p,:],uw_ref[:,sl])+ub_ref[:,sl]
            a,g=gelu_parts(u)
            act[p,sl]=a.astype(bf); gp[p,sl]=g.astype(gp.dtype)
    ys=[dot_nn(act[p,:],dw_ref[...]) for p in parts]
    for p,y in zip(parts,ys):
        pos=lax.broadcasted_iota(jnp.int32,(sub_rows,1),0)+(i%per)*T+p.start
        valid=jnp.where(pos<count,1.0,0.0)
        second=n1_ref[p,:]*g1+b1+y+down_b
        n2,r2=norm_stats(second)
        out_ref[p,:]=valid*(n2*g2+b2)
        up=valid*ct_ref[p,:]
        b2nd=norm_back(up,n2,r2,g2)
        d2_ref[p,:]=b2nd.astype(bf)
        bs_ref[p,:]=b2nd
        sums.append(jnp.concatenate([colsum(b2nd),colsum(up*n2),colsum(up)],axis=0))
    small_ref[3:6,:]+=sum(sums[1:],sums[0])
    for j in range(0,FF,chunk):
        sl=slice(j,j+chunk)
        cs=[]
        for p in parts:
            bp=dot_nt(d2_ref[p,:],dw_ref[sl,:])*gp[p,sl].astype(f32)
            cs.append(colsum(bp))
            pl_[p,sl]=bp.astype(bf)
        ubg_ref[:,sl]+=sum(cs[1:],cs[0])
    zs=[dot_nt(pl_[p,:],uw_ref[...]) for p in parts]
    sums=[]
    for p,z,r1 in zip(parts,zs,r1s):
        bfirst=z+bs_ref[p,:]
        n1=n1_ref[p,:]
        bsum=norm_back(bfirst,n1,r1,g1)
        bs_ref[p,:]=bsum
        sl_ref[p,:]=bsum.astype(bf)
        sums.append(jnp.concatenate([colsum(bsum),colsum(bfirst*n1),colsum(bfirst)],axis=0))
    small_ref[0:3,:]+=sum(sums[1:],sums[0])
    for p in parts:
        ba_ref[p,:]=dot_nt(sl_ref[p,:],ow_ref[...]).astype(bf)

def middle(lengths,hidden,att,ct,ow,uw,dw,vec,ub,T=512,chunk=768,gpt=f32,sub_rows=256):
    tokens=hidden.shape[0]
    tile=lambda n=D: pl.BlockSpec((T,n),lambda i,l:(i,0))
    const=lambda shape: pl.BlockSpec(shape,lambda i,l:(0,0),pipeline_mode=pl.Buffered(1))
    whole=lambda shape: pl.BlockSpec(shape,lambda i,l:(0,0))
    sd=lambda n,dt: jax.ShapeDtypeStruct((tokens,n),dt)
    return pl.pallas_call(
        partial(middle_body,T=T,chunk=chunk,sub_rows=sub_rows),
        grid_spec=pltpu.PrefetchScalarGridSpec(num_scalar_prefetch=1,grid=(tokens//T,),
          in_specs=[tile(),tile(),tile(),const((D,D)),const((D,FF)),const((FF,D)),whole((8,D)),whole((1,FF))],
          out_specs=[tile(),tile(),tile(),tile(FF),tile(FF),tile(),tile(),tile(),whole((8,D)),whole((1,FF))],
          scratch_shapes=[pltpu.VMEM((T,FF),gpt),pltpu.VMEM((T,D),f32)]),
        out_shape=[sd(D,f32),sd(D,f32),sd(D,bf),sd(FF,bf),sd(FF,bf),sd(D,bf),sd(D,bf),sd(D,bf),jax.ShapeDtypeStruct((8,D),f32),jax.ShapeDtypeStruct((1,FF),f32)],
        compiler_params=pltpu.CompilerParams(vmem_limit_bytes=63<<20),
        name="middle")(lengths,hidden,att,ct,ow,uw,dw,vec,ub)


def weight_grads_body(act,d2,low,pre,att,sl,down_ref,up_ref,out_ref,left,right,left_sem,right_sem):
    i=pl.program_id(0)
    def block(ref,j):
        return ref if ref.shape[1]==D else ref.at[:,j*D:(j+1)*D]
    def fetch(ref,j,slot,to_left):
        return pltpu.make_async_copy(block(ref,j),(left if to_left else right).at[slot],(left_sem if to_left else right_sem).at[slot])
    loads={0:((act,0,0,True),(d2,0,0,False),(act,1,1,True)),1:((act,2,0,True),(pre,0,1,False)),2:((act,3,1,True),),
           3:((low,0,0,True),),4:((pre,1,0,False),(att,0,1,True)),5:((pre,2,1,False),),6:((pre,3,0,False),),7:((sl,0,1,False),)}
    needs={0:((act,0,0,True),(d2,0,0,False)),1:((act,1,1,True),),2:((act,2,0,True),),3:((act,3,1,True),),4:((low,0,0,True),(pre,0,1,False)),
           5:((pre,1,0,False),),6:((pre,2,1,False),),7:((pre,3,0,False),),8:((att,0,1,True),(sl,0,1,False))}
    for k in range(9):
        def move(k=k):
            for one in loads.get(k,()): fetch(*one).start()
            for one in needs[k]: fetch(*one).wait()
        pl.when(i==k)(move)
    l=jnp.where(i<4,lax.rem(i,2),jnp.where(i<8,0,1))
    r=jnp.where(i<4,0,jnp.where(i<8,lax.rem(i+1,2),1))
    grad=dot_tn(left[l],right[r]).astype(bf)
    @pl.when(i<4)
    def _(): down_ref[...]=grad
    @pl.when(jnp.logical_and(i>=4,i<8))
    def _(): up_ref[...]=grad
    @pl.when(i==8)
    def _(): out_ref[...]=grad
def weight_grads(act,d2,low,pre,att,sl):
    tokens=act.shape[0]
    return pl.pallas_call(weight_grads_body,grid=(9,),
        in_specs=[pl.BlockSpec(memory_space=pl.ANY)]*6,
        out_specs=[pl.BlockSpec((D,D),lambda i:(jnp.minimum(i,3),0)),pl.BlockSpec((D,D),lambda i:(0,jnp.clip(i-4,0,3))),pl.BlockSpec((D,D),lambda i:(0,0))],
        out_shape=[jax.ShapeDtypeStruct((FF,D),bf),jax.ShapeDtypeStruct((D,FF),bf),jax.ShapeDtypeStruct((D,D),bf)],
        scratch_shapes=[pltpu.VMEM((2,tokens,D),bf),pltpu.VMEM((2,tokens,D),bf),pltpu.SemaphoreType.DMA((2,)),pltpu.SemaphoreType.DMA((2,))],
        compiler_params=pltpu.CompilerParams(vmem_limit_bytes=60<<20),name="weight_grads")(act,d2,low,pre,att,sl)


def input_grad_body(shards,reps,shapes,bs_ref,dq_ref,dk_ref,dv_ref,w_ref,*refs):
    n=len(shapes)
    grads,out_ref,sums,scratch=refs[:n],refs[n],refs[n+1:2*n+1],refs[2*n+1:]
    place=Place(shards,reps); step=pl.program_id(0)
    size=len(reduce_scratch(shapes[1:],shards,reps))
    jobs={"a":Reduce(place,grads[1:],sums[1:],scratch[:size]),"b":Reduce(place,grads[:1],sums[:1],scratch[size:],True)}
    end=follow(LAST_PLAN,jobs,step,pl.num_programs(0)-1,lambda: meet(place,True))
    out_ref[...]=bs_ref[...]+dot_nt(dq_ref[...],w_ref[:,0:D])+dot_nt(dk_ref[...],w_ref[:,D:2*D])+dot_nt(dv_ref[...],w_ref[:,2*D:3*D])
    end()
def input_grad(back_sum,dq,dk,dv,weight,grads,shards,reps,collective_id):
    rows=back_sum.shape[0]//8
    tile=pl.BlockSpec((rows,D),lambda i:(i,0))
    anywhere=[pl.BlockSpec(memory_space=pl.ANY)]*len(grads)
    shapes=[g.shape[1:] for g in grads]
    return pl.pallas_call(partial(input_grad_body,shards,reps,shapes),grid=(8,),
        in_specs=[tile]*4+[pl.BlockSpec((D,3*D),lambda i:(0,0),pipeline_mode=pl.Buffered(1))]+anywhere,
        out_specs=[tile]+anywhere,
        out_shape=[jax.ShapeDtypeStruct(back_sum.shape,f32)]+result_shapes(shapes),
        scratch_shapes=reduce_scratch(shapes[1:],shards,reps)+reduce_scratch(shapes[:1],shards,reps,True),
        compiler_params=pltpu.CompilerParams(vmem_limit_bytes=50<<20,collective_id=collective_id,has_side_effects=True),name="input_grad")(back_sum,dq,dk,dv,weight,*grads)


def as_rows(row):
    filled = -(-row.shape[-1] // 128)
    row = jnp.pad(row, ((0, 0), (0, filled * 128 - row.shape[-1])))
    return jnp.pad(row.reshape(-1, filled, 128), ((0, 0), (0, 0), (0, 128)))


def pack_body(*refs):
    *ins, out = refs
    rows = []
    for ref in ins:
        value = ref[...].astype(f32)
        for at in range(0, value.shape[0], 128):
            part = value[at : at + 128].reshape(1, -1)
            rows.append(jnp.pad(part, ((0, 0), (0, 256 - part.shape[1]))))
    rows.append(jnp.zeros((16 - len(rows), 256), f32))
    out[...] = jnp.concatenate(rows, axis=0).astype(bf)


def pack_shards(vectors):
    return pl.pallas_call(
        pack_body, out_shape=jax.ShapeDtypeStruct((16, 256), bf), name="pack_vectors"
    )(*vectors)


def pack_vectors(vectors):
    rows = jnp.concatenate([as_rows(v) for v in vectors], axis=1)
    return jnp.pad(rows, ((0, 0), (0, 16 - rows.shape[1]), (0, 0)))


def local(
    hidden,
    lengths,
    clusters,
    input_weight,
    query_bias,
    value_bias,
    out_weight,
    out_bias,
    norm1_gain,
    norm1_bias,
    up_weight,
    up_bias,
    down_weight,
    down_bias,
    norm2_gain,
    norm2_bias,
    cotangent,
    *,
    shards,
    reps,
):
    seqs = hidden.shape[0]
    tokens = seqs * LEN
    part = D // shards
    vectors = pack_shards(
        (
            query_bias,
            value_bias,
            out_bias,
            norm1_gain,
            norm1_bias,
            down_bias,
            norm2_gain,
            norm2_bias,
            up_bias,
        )
    )
    in_w, vectors = gather_now((input_weight, vectors), shards, reps, 1)
    in_w = in_w.reshape(D, 3 * D)
    vectors = vectors.astype(f32)
    table = vectors[:, :8, :part].transpose(1, 0, 2).reshape(8, D)
    bias_all = jnp.concatenate([table[0], jnp.zeros((D,), f32), table[1]])[None]
    norm_rows = jnp.concatenate([table[2:], table[:2]])
    up_b = vectors[:, 8:, :128].reshape(shards, -1)[:, : FF // shards].reshape(1, FF)

    flat = hidden.reshape(tokens, D)
    attended, proj, rounded, up_w, down_w, out_w = attention_forward(
        lengths,
        flat,
        in_w,
        bias_all,
        clusters,
        (up_weight, down_weight, out_weight),
        shards,
        reps,
        2,
    )
    out_w, up_w, down_w = [w.reshape(-1, w.shape[-1]) for w in (out_w, up_w, down_w)]
    (
        result,
        back_sum,
        back_attended,
        activated,
        pre_low,
        first_low,
        second_low,
        sum_low,
        norm_sums,
        up_b_sum,
    ) = middle(
        lengths,
        flat,
        attended,
        cotangent.reshape(tokens, D),
        out_w,
        up_w,
        down_w,
        norm_rows,
        up_b,
    )
    down_g, up_g, out_g = weight_grads(
        activated, second_low, first_low, pre_low, attended, sum_low
    )
    dq, dk, dv, in_g, bias_sums, down_s, up_s, out_s, in_first = attention_backward(
        lengths,
        rounded,
        proj,
        back_attended,
        clusters,
        [g.reshape(shards, -1, g.shape[-1]) for g in (down_g, up_g, out_g)],
        shards,
        reps,
        3,
    )
    bias_sums = jnp.sum(bias_sums, axis=0)
    query_sum = bias_sums[:, 0:2, DH:].reshape(D)
    value_sum = jnp.concatenate([bias_sums[:, 2, :DH], bias_sums[:, 3, DH:]], axis=1).reshape(D)
    table = jnp.concatenate([query_sum[None], value_sum[None], norm_sums[:6]])
    table = table.reshape(8, shards, part)
    small = pack_vectors(
        [table[i].astype(bf) for i in range(8)] + [up_b_sum.reshape(shards, -1).astype(bf)]
    )
    back_input, *in_s, small_s = input_grad(
        back_sum,
        dq,
        dk,
        dv,
        in_w,
        [in_g[2].reshape(shards, part, D), in_g[1].reshape(shards, part, D), small],
        shards,
        reps,
        4,
    )
    back_input = back_input.reshape(seqs, LEN, D)
    in_s = [in_first, in_s[1], in_s[0]]
    in_s = jnp.concatenate(
        [
            in_s[g][:, 384 * c + 128 * t : 384 * c + 128 * t + 128]
            for t in range(3)
            for c in range(2)
            for g in range(PAIRS // 2)
        ],
        axis=1,
    )

    small_s = small_s[:, :128]
    vec = [small_s[i, :part] for i in range(8)]
    return (
        result.reshape(seqs, LEN, D),
        back_input,
        in_s,
        vec[0],
        vec[1],
        out_s,
        vec[2],
        vec[3],
        vec[4],
        up_s,
        small_s[8:].reshape(-1)[: FF // shards],
        down_s,
        vec[5],
        vec[6],
        vec[7],
    )


def solution(mesh):
    tokens = P(("rep", "shard"), None, None)
    matrix, vector = P("shard", None), P("shard")
    params = (
        matrix,
        vector,
        vector,
        matrix,
        vector,
        vector,
        vector,
        matrix,
        vector,
        matrix,
        vector,
        vector,
        vector,
    )
    return jax.shard_map(
        partial(local, shards=mesh.shape["shard"], reps=mesh.shape["rep"]),
        mesh=mesh,
        in_specs=(tokens, P(("rep", "shard")), tokens) + params + (tokens,),
        out_specs=(tokens, tokens) + params,
        check_vma=False,
    )
```

```python
from functools import partial

import jax
import jax.numpy as jnp
from jax import lax
from jax.experimental import pallas as pl
from jax.experimental.pallas import tpu as pltpu
from jax.sharding import PartitionSpec as P

D = 768
H = 12
DH = 64
FF = 3072
CLUSTER = 128
LEN = 1024
PAIRS = H // 2
SLICES = [slice(c * CLUSTER, (c + 1) * CLUSTER) for c in range(LEN // CLUSTER)]
bf = jnp.bfloat16
f32 = jnp.float32
eps_norm = 1e-12


def dot_nn(left, right):
    return lax.dot_general(left, right, (((1,), (0,)), ((), ())), preferred_element_type=f32)


def dot_nt(left, right):
    return lax.dot_general(left, right, (((1,), (1,)), ((), ())), preferred_element_type=f32)


def dot_tn(left, right):
    return lax.dot_general(left, right, (((0,), (0,)), ((), ())), preferred_element_type=f32)


ROWS = 4
MESH=pl.DeviceIdType.MESH

def when(cond,do):
    if cond is None: do()
    else: pl.when(cond)(do)

class Place:
    def __init__(self,shards,reps):
        self.Y=shards//ROWS; self.S=shards; self.X=reps//2
        self.s=lax.axis_index("shard"); self.r=lax.axis_index("rep")
        self.z=self.s//self.Y; self.y=lax.rem(self.s,self.Y)
        self.core=lax.rem(self.r,2); self.x=self.r//2
    def near_z(self,step): return {"shard":self.s+step*self.Y}
    def other_y(self,k): return {"shard":self.z*self.Y+lax.rem(self.y+k,self.Y)}
    def other_core(self): return {"rep":self.r+1-2*self.core}
    def other_x(self,k): return {"rep":2*lax.rem(self.x+k,self.X)+self.core}

def meet(place,with_x):
    sem=pltpu.get_barrier_semaphore()
    def tell(dev): pl.semaphore_signal(sem,inc=1,device_id=dev,device_id_type=MESH)
    pl.when(place.z>0)(lambda: tell(place.near_z(-1)))
    pl.when(place.z<ROWS-1)(lambda: tell(place.near_z(1)))
    for k in range(1,place.Y): tell(place.other_y(k))
    tell(place.other_core())
    if with_x:
        for k in range(1,place.X): tell(place.other_x(k))
    others=place.Y+(place.X-1 if with_x else 0)
    inner=jnp.logical_and(place.z>0,place.z<ROWS-1)
    pl.when(inner)(lambda: pl.semaphore_wait(sem,others+2))
    pl.when(jnp.logical_not(inner))(lambda: pl.semaphore_wait(sem,others+1))

def gather_semaphores(count,shards):
    Y=shards//ROWS; dma=pltpu.SemaphoreType.DMA
    return [dma((count,2,ROWS)),dma((count,2,ROWS)),dma((count,ROWS,Y)),dma((count,ROWS,Y)),
            dma((count,2,shards)),dma((count,2,shards)),dma((count,shards)),dma((count,shards)),dma((count,))]

class Gather:
    def __init__(self,place,ins,outs,sems,share=False):
        self.p=place; self.ins=ins; self.outs=outs; self.share=share and place.X==2
        self.line_s,self.line_r,self.y_s,self.y_r,self.core_s,self.core_r,self.x_s,self.x_r,self.own=sems
        self.sent=[]
    def piece(self,ref,shard=None,core=None,x=None):
        p=self.p; n=ref.shape[-1]//2; r=ref.shape[-2]
        cols=pl.ds(pl.multiple_of((p.core if core is None else core)*n,128),n)
        rows=slice(None)
        if self.share:
            rows=pl.ds(pl.multiple_of((p.x if x is None else x)*(r//2),16),r//2)
        return ref.at[rows,cols] if shard is None else ref.at[shard,rows,cols]
    def send(self,make):
        cond,desc=make()
        when(cond,desc.start); self.sent.append(make)
    def copy(self,src,dst,ss,rs,dev):
        return pltpu.make_async_remote_copy(src_ref=src,dst_ref=dst,send_sem=ss,recv_sem=rs,device_id=dev,device_id_type=MESH)
    def at(self,places):
        zz=self.p.z+places
        if places==0: return None,zz
        return jnp.logical_and(zz>=0,zz<ROWS),jnp.clip(zz,0,ROWS-1)
    def shard_at(self,zz,k):
        p=self.p
        return zz*p.Y+(lax.rem(p.y-k+p.Y,p.Y) if k else p.y)
    def to_line(self,a,places,d):
        p=self.p; i,o=self.ins[a],self.outs[a]
        def make():
            cond,zz=self.at(places); shard=zz*p.Y+p.y
            edge=(p.z<ROWS-1) if d==0 else (p.z>0)
            src=self.piece(i) if places==0 else self.piece(o,shard)
            return (edge if cond is None else jnp.logical_and(cond,edge)),self.copy(src,self.piece(o,shard),self.line_s.at[a,d,zz],self.line_r.at[a,d,zz],p.near_z(1 if d==0 else -1))
        self.send(make)
    def to_y(self,a,places,k):
        p=self.p; i,o=self.ins[a],self.outs[a]
        def make():
            cond,zz=self.at(places); shard=zz*p.Y+p.y
            src=self.piece(i) if places==0 else self.piece(o,shard)
            return cond,self.copy(src,self.piece(o,shard),self.y_s.at[a,zz,k],self.y_r.at[a,zz,k],p.other_y(k))
        self.send(make)
    def to_core(self,a,places,k,other=False):
        p=self.p; o=self.outs[a]; slot=1 if other else 0
        def make():
            cond,zz=self.at(places); shard=self.shard_at(zz,k)
            ref=self.piece(o,shard,x=1-p.x if other else p.x)
            return cond,self.copy(ref,ref,self.core_s.at[a,slot,shard],self.core_r.at[a,slot,shard],p.other_core())
        self.send(make)
    def to_x(self,a,places,k):
        p=self.p; o=self.outs[a]
        if not self.share: return
        def make():
            cond,zz=self.at(places); shard=self.shard_at(zz,k)
            ref=self.piece(o,shard)
            return cond,self.copy(ref,ref,self.x_s.at[a,shard],self.x_r.at[a,shard],p.other_x(1))
        self.send(make)
    def begin(self):
        for a,(i,o) in enumerate(zip(self.ins,self.outs)):
            for d in (0,1): self.to_line(a,0,d)
            for k in range(1,self.p.Y): self.to_y(a,0,k)
            pltpu.make_async_copy(i,o.at[self.p.s],self.own.at[a]).start()
    def wave(self,w):
        p=self.p
        for d in (0,1):
            places=-w if d==0 else w
            for a,o in enumerate(self.outs):
                cond,zz=self.at(places); ref=self.piece(o,zz*p.Y+p.y)
                when(cond,self.copy(ref,ref,self.line_s.at[a,d,zz],self.line_r.at[a,d,zz],p.near_z(0)).wait_recv)
                self.to_line(a,places,d)
                for k in range(1,p.Y): self.to_y(a,places,k)
                self.to_x(a,places,0); self.to_core(a,places,0)
    def across(self,w):
        p=self.p
        for places in ((0,) if w==0 else (-w,w)):
            for k in range(1,p.Y):
                for a,o in enumerate(self.outs):
                    cond,zz=self.at(places); ref=self.piece(o,self.shard_at(zz,k))
                    when(cond,self.copy(ref,ref,self.y_s.at[a,zz,k],self.y_r.at[a,zz,k],p.other_y(k)).wait_recv)
                    self.to_x(a,places,k); self.to_core(a,places,k)
    def over(self,w):
        p=self.p
        if not self.share: return
        for places in ((0,) if w==0 else (-w,w)):
            for k in range(1 if w==0 else 0,p.Y):
                for a,o in enumerate(self.outs):
                    cond,zz=self.at(places); shard=self.shard_at(zz,k); ref=self.piece(o,shard,x=1-p.x)
                    when(cond,self.copy(ref,ref,self.x_s.at[a,shard],self.x_r.at[a,shard],p.other_x(1)).wait_recv)
                    self.to_core(a,places,k,True)
    def finish(self):
        p=self.p
        for a,(i,o) in enumerate(zip(self.ins,self.outs)):
            for k in range(1,p.S):
                shard=lax.rem(p.s+k,p.S)
                for slot in range(2 if self.share else 1):
                    ref=self.piece(o,shard,core=1-p.core,x=1-p.x if slot else p.x)
                    self.copy(ref,ref,self.core_s.at[a,slot,shard],self.core_r.at[a,slot,shard],p.other_core()).wait_recv()
            pltpu.make_async_copy(i,o.at[p.s],self.own.at[a]).wait()
        for make in self.sent:
            cond,desc=make()
            when(cond,desc.wait_send)
def gather_body(shards,reps,count,*refs):
    ins,outs,sems=refs[:count],refs[count:2*count],refs[2*count:]
    place=Place(shards,reps)
    meet(place,False)
    G=Gather(place,ins,outs,sems)
    G.begin(); G.wave(1); G.across(0); G.wave(2); G.across(1); G.wave(3); G.across(2); G.across(3); G.finish()

def gather_now(arrays,shards,reps,collective_id):
    count=len(arrays)
    return pl.pallas_call(partial(gather_body,shards,reps,count),
        in_specs=[pl.BlockSpec(memory_space=pltpu.VMEM)]*count,
        out_specs=[pl.BlockSpec(memory_space=pl.ANY)]*count,
        out_shape=[jax.ShapeDtypeStruct((shards,)+a.shape,a.dtype) for a in arrays],
        scratch_shapes=gather_semaphores(count,shards),
        compiler_params=pltpu.CompilerParams(collective_id=collective_id,has_side_effects=True,vmem_limit_bytes=16<<20),
        name="gather_weights")(*arrays)

ORDER=(3,0,2,1)
def reduce_scratch(shapes,shards,reps,x_first=False):
    x_first=x_first and reps==4
    S=shards; Y=S//ROWS; X=reps//2; A=len(shapes)
    out=[]
    for r,c in shapes:
        n=c//2; m=r//2 if x_first else r
        out+=[pltpu.VMEM((S,r,n),bf),pltpu.VMEM((S,r,n),bf),pltpu.VMEM((max(Y-1,1),ROWS,m,n),bf),
              pltpu.VMEM((ROWS+1,m,n),bf),pltpu.VMEM((S+1,m,n) if x_first else (X,r,n),bf),pltpu.VMEM((2,r,n),f32)]
    dma=pltpu.SemaphoreType.DMA
    return out+[dma((A,S)),dma((A,S)),dma((A,S)),dma((A,Y,ROWS)),dma((A,Y,ROWS)),dma((A,ROWS+1)),dma((A,ROWS+1)),dma((A,S+X)),dma((A,S+X)),dma((A,)),dma((A,)),dma((A,2))]
class Reduce:
    def __init__(self,place,ins,outs,scratch,x_first=False):
        self.p=place; self.ins=ins; self.outs=outs; A=len(ins); self.A=range(A)
        self.bufs=[scratch[6*a:6*a+6] for a in range(A)]
        (self.own,self.core_s,self.core_r,self.y_s,self.y_r,self.line_s,self.line_r,self.x_s,self.x_r,self.end_s,self.end_r,self.out_s)=scratch[6*A:]
        self.sent=[]; self.x_first=x_first and place.X==2
    def copy(self,src,dst,ss,rs,dev):
        return pltpu.make_async_remote_copy(src_ref=src,dst_ref=dst,send_sem=ss,recv_sem=rs,device_id=dev,device_id_type=MESH)
    def send(self,make):
        cond,desc=make()
        when(cond,desc.start); self.sent.append(make)
    def half(self,a,shard,core):
        n=self.ins[a].shape[-1]//2
        return self.ins[a].at[shard,:,pl.ds(pl.multiple_of(core*n,128),n)]
    def mine(self,a,shard,x=None):
        H=self.bufs[a][0]
        if not self.x_first: return H.at[shard]
        m=H.shape[1]//2
        return H.at[shard,pl.ds(pl.multiple_of((self.p.x if x is None else x)*m,16),m)]
    def add(self,dst,others):
        rows,n=dst.shape; step=next(s for s in (192,96,48,16) if rows%s==0 and (s==16 or s*n<=96*768))
        def block(at):
            value=dst[at,:]
            for o in others: value=value+o[at,:]
            dst[at,:]=value
        if rows==step: block(slice(0,rows)); return
        def body(i,_):
            block(pl.ds(pl.multiple_of(i*step,16),step))
            return 0
        lax.fori_loop(0,rows//step,body,0)
    def begin(self,ks=None):
        p=self.p
        for k in (list(range(1,p.Y)) if ks is None else ks):
            for d in ORDER:
                for a in self.A:
                    H,Rc=self.bufs[a][0:2]
                    def make(a=a,d=d,k=k,Rc=Rc):
                        shard=d*p.Y+lax.rem(p.y+k,p.Y)
                        return None,self.copy(self.half(a,shard,1-p.core),Rc.at[shard],self.core_s.at[a,shard],self.core_r.at[a,shard],p.other_core())
                    self.send(make)
                    shard=d*p.Y+lax.rem(p.y+k,p.Y)
                    pltpu.make_async_copy(self.half(a,shard,p.core),H.at[shard],self.own.at[a,shard]).start()
    def join_core(self,shard):
        p=self.p
        for a in self.A:
            H,Rc=self.bufs[a][0:2]
            pltpu.make_async_copy(self.half(a,shard,p.core),H.at[shard],self.own.at[a,shard]).wait()
            self.copy(Rc.at[shard],Rc.at[shard],self.core_s.at[a,shard],self.core_r.at[a,shard],p.other_core()).wait_recv()
            self.add(H.at[shard],[Rc.at[shard]])
    def to_pair(self,k,d):
        p=self.p; shard=d*p.Y+lax.rem(p.y+k,p.Y)
        if not self.x_first: return
        self.join_core(shard)
        for a in self.A:
            def make(a=a):
                shard=d*p.Y+lax.rem(p.y+k,p.Y)
                return None,self.copy(self.mine(a,shard,1-p.x),self.bufs[a][4].at[shard],self.x_s.at[a,shard],self.x_r.at[a,shard],p.other_x(1))
            self.send(make)
    def ready(self,shard):
        p=self.p
        if not self.x_first: self.join_core(shard); return
        for a in self.A:
            got=self.bufs[a][4].at[shard]
            self.copy(got,got,self.x_s.at[a,shard],self.x_r.at[a,shard],p.other_x(1)).wait_recv()
            self.add(self.mine(a,shard),[got])
    def to_y(self,d):
        p=self.p
        for k in range(1,p.Y):
            self.ready(d*p.Y+lax.rem(p.y+k,p.Y))
            for a in self.A:
                H,_,Ry=self.bufs[a][0:3]
                def make(a=a,H=H,Ry=Ry,k=k):
                    shard=d*p.Y+lax.rem(p.y+k,p.Y)
                    return None,self.copy(self.mine(a,shard),Ry.at[k-1,d],self.y_s.at[a,k,d],self.y_r.at[a,k,d],p.other_y(k))
                self.send(make)
    def own_y(self,d):
        self.ready(d*self.p.Y+self.p.y)
    def along(self,d,up,j):
        p=self.p
        if (j>=d) if up else (ROWS-1-j<=d): return
        here=p.z==(j if up else ROWS-1-j)
        shard=d*p.Y+p.y
        if j>0:
            def add_in():
                for a in self.A:
                    H,Rl=self.bufs[a][0],self.bufs[a][3]
                    self.copy(Rl.at[d],Rl.at[d],self.line_s.at[a,d],self.line_r.at[a,d],p.near_z(0)).wait_recv()
                    self.add(self.mine(a,shard),[Rl.at[d]])
            pl.when(here)(add_in)
        last=(j==d-1) if up else (ROWS-1-j==d+1)
        slot=ROWS if last and not up else d
        for a in self.A:
            def make(a=a):
                H,Rl=self.bufs[a][0],self.bufs[a][3]
                return p.z==(j if up else ROWS-1-j),self.copy(self.mine(a,d*p.Y+p.y),Rl.at[slot],self.line_s.at[a,slot],self.line_r.at[a,slot],p.near_z(1 if up else -1))
            self.send(make)
    def line(self,d):
        p=self.p; shard=d*p.Y+p.y
        for a in self.A:
            H,_,Ry=self.bufs[a][0:3]
            for k in range(1,p.Y):
                self.copy(Ry.at[k-1,d],Ry.at[k-1,d],self.y_s.at[a,k,d],self.y_r.at[a,k,d],p.other_y(k)).wait_recv()
            self.add(self.mine(a,shard),[Ry.at[k-1,d] for k in range(1,p.Y)])
        self.along(d,True,0); self.along(d,False,0)
    def relay(self,d,j):
        self.along(d,True,j); self.along(d,False,j)
    def to_x(self):
        p=self.p
        for slot,cond in ((p.z,p.z>0),(ROWS,p.z<ROWS-1)):
            def add_in(slot=slot):
                for a in self.A:
                    H,Rl=self.bufs[a][0],self.bufs[a][3]
                    self.copy(Rl.at[slot],Rl.at[slot],self.line_s.at[a,slot],self.line_r.at[a,slot],p.near_z(0)).wait_recv()
                    self.add(self.mine(a,p.s),[Rl.at[slot]])
            pl.when(cond)(add_in)
        for a in self.A:
            H,Rx=self.bufs[a][0],self.bufs[a][4]
            if self.x_first:
                self.send(lambda a=a,Rx=Rx: (None,self.copy(self.mine(a,p.s),Rx.at[p.S],self.x_s.at[a,p.S],self.x_r.at[a,p.S],p.other_x(1))))
                continue
            for k in range(1,p.X):
                self.send(lambda a=a,H=H,Rx=Rx,k=k: (None,self.copy(H.at[p.s],Rx.at[p.x],self.x_s.at[a,k],self.x_r.at[a,p.x],p.other_x(k))))
    def to_core(self):
        p=self.p
        for a in self.A:
            H,Rx,F=self.bufs[a][0],self.bufs[a][4],self.bufs[a][5]
            if self.x_first:
                got=Rx.at[p.S]; m=H.shape[1]//2
                self.copy(got,got,self.x_s.at[a,p.S],self.x_r.at[a,p.S],p.other_x(1)).wait_recv()
                for x in range(2):
                    own=H[p.s,x*m:(x+1)*m,:]
                    F[p.core,x*m:(x+1)*m,:]=jnp.where(p.x==x,own,Rx[p.S]).astype(f32)
                continue
            for k in range(1,p.X):
                src=lax.rem(p.x-k+p.X,p.X)
                self.copy(Rx.at[src],Rx.at[src],self.x_s.at[a,k],self.x_r.at[a,src],p.other_x(k)).wait_recv()
            rows=H.shape[1]; step=48 if rows%48==0 else 16
            def body(i,_):
                at=pl.ds(pl.multiple_of(i*step,16),step)
                own=H[p.s,at,:].astype(f32)
                value=jnp.zeros_like(own)
                for q in range(p.X):
                    value=value+jnp.where(p.x==q,own,Rx[q,at,:].astype(f32))
                F[p.core,at,:]=value
                return 0
            lax.fori_loop(0,rows//step,body,0)
        for a in self.A:
            F=self.bufs[a][5]
            self.send(lambda a=a,F=F: (None,self.copy(F.at[p.core],F.at[p.core],self.end_s.at[a],self.end_r.at[a],p.other_core())))
    def result(self,a,core):
        F=self.bufs[a][5]; n=F.shape[2]
        return pltpu.make_async_copy(F.at[core],self.outs[a].at[:,core*n:(core+1)*n],self.out_s.at[a,core])
    def finish(self):
        p=self.p
        for a in self.A:
            ref=self.bufs[a][5].at[1-p.core]
            self.copy(ref,ref,self.end_s.at[a],self.end_r.at[a],p.other_core()).wait_recv()
            for core in range(2): self.result(a,core).start()
        for make in self.sent:
            cond,desc=make()
            when(cond,desc.wait_send)
        for a in self.A:
            for core in range(2): self.result(a,core).wait()
def result_shapes(shapes):
    return [jax.ShapeDtypeStruct((r,c),f32) for r,c in shapes]

GATHER_PLAN = {
    0: (("u", "begin"), ("d", "begin")),
    2: (("u", "wave", 1),),
    3: (("d", "wave", 1), ("u", "across", 0)),
    4: (("u", "wave", 2), ("d", "across", 0)),
    6: (("d", "wave", 2),),
    7: (("u", "wave", 3), ("u", "across", 1)),
    8: (("d", "wave", 3), ("d", "across", 1), ("d", "over", 0)),
    10: (("u", "across", 2), ("u", "across", 3), ("d", "across", 2), ("d", "across", 3)),
    11: (("d", "over", 1),),
    100: (("d", "over", 2), ("d", "over", 3), ("u", "finish"), ("d", "finish")),
}


def each(name, what, *more):
    return tuple((name, what, d) + more for d in ORDER)


REDUCE_PLAN = {
    0: (("d", "begin"), ("u", "begin"), ("d", "begin", (0,)), ("u", "begin", (0,))),
    1: each("d", "to_y") + tuple(("u", "to_pair", 1, d) for d in ORDER),
    2: tuple(("u", "to_pair", 0, d) for d in ORDER) + each("d", "own_y") + (("d", "line", 3),),
    3: (("d", "line", 0), ("d", "relay", 3, 1)),
    4: (("g", "begin"), ("g", "begin", (0,)))
    + (("d", "line", 2), ("d", "relay", 0, 1), ("d", "relay", 3, 2))
    + each("u", "to_y"),
    5: (("d", "line", 1), ("d", "relay", 2, 1), ("d", "relay", 0, 2))
    + each("g", "to_y")
    + each("g", "own_y")
    + (("u", "own_y", 3), ("u", "own_y", 0)),
    6: (("d", "relay", 1, 1), ("u", "line", 3), ("u", "line", 0), ("u", "own_y", 2), ("u", "own_y", 1)),
    7: (("d", "to_x"), ("u", "relay", 3, 1), ("u", "relay", 0, 1), ("u", "line", 2), ("u", "line", 1)),
    8: (("d", "to_core"), ("u", "relay", 3, 2), ("u", "relay", 0, 2)) + each("g", "line"),
    9: (("u", "relay", 2, 1), ("u", "relay", 1, 1)) + each("g", "relay", 1),
    10: (("u", "to_x"),) + each("g", "relay", 2),
    11: (("g", "to_x"), ("u", "to_core")),
    100: (("g", "to_core"), ("d", "finish"), ("u", "finish"), ("g", "finish")),
}
LAST_PLAN = {
    0: (("a", "begin"), ("b", "begin"), ("a", "begin", (0,)), ("b", "begin", (0,))),
    1: each("a", "to_y"),
    2: tuple(("b", "to_pair", k, d) for k in (1, 0) for d in ORDER) + each("a", "own_y"),
    4: (("a", "line", 3), ("a", "line", 0)),
    5: (("a", "line", 2), ("a", "line", 1)) + each("b", "to_y"),
    6: each("b", "own_y") + each("a", "relay", 1),
    7: (("a", "relay", 3, 2), ("a", "relay", 0, 2)) + each("b", "line"),
    100: (("a", "to_x"),)
    + each("b", "relay", 1)
    + (("a", "to_core"),)
    + each("b", "relay", 2)
    + (("b", "to_x"), ("b", "to_core"), ("a", "finish"), ("b", "finish")),
}


def follow(plan, jobs, step, last, ready):
    def run(at):
        for name, what, *more in plan.get(at, ()):
            getattr(jobs[name], what)(*more)

    def first():
        ready()
        run(0)

    pl.when(step == 0)(first)
    for at in sorted(plan):
        if 0 < at < 100:
            pl.when(step == at)(partial(run, at))
    return lambda: pl.when(step == last)(partial(run, 100))


def low_lanes():
    return lax.broadcasted_iota(jnp.int32, (LEN, CLUSTER), 1) < DH


def table_of(order_row):
    held = jnp.broadcast_to(order_row.astype(jnp.int16), (LEN, LEN))
    positions = lax.broadcasted_iota(jnp.int16, (LEN, LEN), 0)
    return jnp.where(held == positions, jnp.ones((), bf), jnp.zeros((), bf))


def turned_table_of(order_row):
    held = jnp.transpose(jnp.broadcast_to(order_row, (128, LEN))).astype(jnp.int16)
    lanes = lax.broadcasted_iota(jnp.int16, (LEN, 128), 1)
    return jnp.concatenate(
        [
            jnp.where(held == lanes + jnp.int16(128 * b), jnp.ones((), bf), jnp.zeros((), bf))
            for b in range(LEN // 128)
        ],
        axis=1,
    )


def half_roll(source):
    return pltpu.roll(source, DH, 1)


def softmax_rows(scores):
    top = jnp.max(scores, axis=-1, keepdims=True)
    grown = jnp.exp(scores - top)
    return grown * (1.0 / jnp.sum(grown, axis=-1, keepdims=True))


def attention_forward_body(
    shards, reps, len_ref, h_ref, wq_ref, wk_ref, wv_ref, bq_ref, bk_ref, bv_ref, row_ref, *rest
):
    ins, (att_ref, proj_ref, x_ref), outs = rest[:3], rest[3:6], rest[6:9]
    tables, scores, mixed = rest[9:11], rest[11:13], rest[13:15]
    sems = rest[15:]
    step = pl.program_id(0) * PAIRS + pl.program_id(1)
    place = Place(shards, reps)
    jobs = {
        "u": Gather(place, ins[:1], outs[:1], sems[:9]),
        "d": Gather(place, ins[1:], outs[1:], sems[9:], True),
    }
    end = follow(
        GATHER_PLAN, jobs, step, pl.num_programs(0) * PAIRS - 1, lambda: meet(place, True)
    )

    @pl.when(pl.program_id(1) == 0)
    def _():
        x_ref[...] = h_ref[...].astype(bf)

    count = len_ref[pl.program_id(0)]
    weight = jnp.concatenate([wq_ref[...], wk_ref[...], wv_ref[...]], axis=1)
    bias = jnp.concatenate([bq_ref[...], bk_ref[...], bv_ref[...]], axis=1)
    proj = (dot_nn(x_ref[...], weight) + bias).astype(bf)
    low = low_lanes()
    query, key, value = proj[:, 0:128], proj[:, 128:256], proj[:, 256:384]
    pairs = [jnp.where(low, query, half_roll(key)), jnp.where(low, half_roll(query), key)]
    proj_ref[...] = jnp.concatenate([pairs[0], value, pairs[1]], axis=1)
    rows = [row_ref[0, pl.ds(2 * pl.program_id(1) + e, 1), :] for e in range(2)]
    for e in range(2):
        tables[e][...] = table_of(rows[e])
    picked = [
        dot_nn(turned_table_of(rows[e]), jnp.concatenate([pairs[e], value], axis=1)).astype(bf)
        for e in range(2)
    ]
    for e in range(2):
        qk = picked[e][:, 0:128]
        key_low = jnp.where(low, half_roll(qk), jnp.zeros((), bf))
        bias = jnp.where(rows[e] < count, 0.0, -30000.0)
        for sl in SLICES:
            scores[e][sl, :] = 0.125 * dot_nt(qk[sl], key_low[sl]) + bias[:, sl]
    for e in range(2):
        values = picked[e][:, 128:256]
        for sl in SLICES:
            probs = softmax_rows(scores[e][sl, :]).astype(bf)
            mixed[e][sl, :] = dot_nn(probs, values[sl]).astype(bf)
    placed = [dot_nn(tables[e][...], mixed[e][...]) for e in range(2)]
    att_ref[...] = jnp.where(low, placed[0], placed[1]).astype(bf)
    end()


def attention_forward(lengths, hidden, weight, bias, rows, arrays, shards, reps, collective_id):
    seqs = rows.shape[0]
    tokens = seqs * LEN
    column = lambda part: pl.BlockSpec((D, 128), lambda s, h, n: (0, part * PAIRS + h))
    column_b = lambda part: pl.BlockSpec((1, 128), lambda s, h, n: (0, part * PAIRS + h))
    return pl.pallas_call(
        partial(attention_forward_body, shards, reps),
        grid_spec=pltpu.PrefetchScalarGridSpec(
            num_scalar_prefetch=1,
            grid=(seqs, PAIRS),
            in_specs=[pl.BlockSpec((LEN, D), lambda s, h, n: (s, 0))]
            + [column(part) for part in range(3)]
            + [column_b(part) for part in range(3)]
            + [pl.BlockSpec((1, H, LEN), lambda s, h, n: (s, 0, 0))]
            + [pl.BlockSpec(memory_space=pl.ANY)] * 3,
            out_specs=[
                pl.BlockSpec((LEN, 128), lambda s, h, n: (s, h)),
                pl.BlockSpec((LEN, 384), lambda s, h, n: (s, h)),
                pl.BlockSpec((LEN, D), lambda s, h, n: (s, 0)),
            ]
            + [pl.BlockSpec(memory_space=pl.ANY)] * 3,
            scratch_shapes=[pltpu.VMEM((LEN, LEN), bf)] * 2
            + [pltpu.VMEM((LEN, 128), f32)] * 2
            + [pltpu.VMEM((LEN, 128), bf)] * 2
            + gather_semaphores(1, shards)
            + gather_semaphores(2, shards),
        ),
        out_shape=[
            jax.ShapeDtypeStruct((tokens, D), bf),
            jax.ShapeDtypeStruct((tokens, 3 * D), bf),
            jax.ShapeDtypeStruct((tokens, D), bf),
        ]
        + [jax.ShapeDtypeStruct((shards,) + a.shape, bf) for a in arrays],
        compiler_params=pltpu.CompilerParams(
            vmem_limit_bytes=63 << 20, collective_id=collective_id, has_side_effects=True
        ),
        name="attention_forward",
    )(lengths, hidden, weight, weight, weight, bias, bias, bias, rows, *arrays)


def attention_backward_body(shards, reps, shapes, *refs):
    len_ref, x_ref, proj_ref, datt_ref, row_ref = refs[:5]
    grads, refs = refs[5:8], refs[8:]
    (dq_ref, dk_ref, dv_ref, dw_ref, db_ref), sums, refs = refs[:5], refs[5:9], refs[9:]
    t0, t1, s0, s1, d0, d1, p0, p1, e0, e1, total, group = refs[:12]
    refs = refs[12:]
    turn = pl.program_id(0)
    step = turn * pl.num_programs(1) + pl.program_id(1)
    place = Place(shards, reps)
    sizes = [len(reduce_scratch(shapes[k], shards, reps, k == "u")) for k in "dug"]
    parts = [refs[sum(sizes[:k]) : sum(sizes[: k + 1])] for k in range(3)]
    jobs = {
        "d": Reduce(place, grads[:1], sums[:1], parts[0]),
        "u": Reduce(place, grads[1:], sums[1:3], parts[1], True),
        "g": Reduce(place, [group], sums[3:], parts[2]),
    }
    end = follow(
        REDUCE_PLAN,
        jobs,
        step,
        pl.num_programs(0) * pl.num_programs(1) - 1,
        lambda: meet(place, True),
    )
    seq = pl.program_id(1)
    count = len_ref[seq]
    low = low_lanes()
    zero = jnp.zeros((), bf)
    tables, scores, back_probs, probs_low, backs = (t0, t1), (s0, s1), (d0, d1), (p0, p1), (e0, e1)
    rows = [row_ref[0, pl.ds(2 * pair_at(turn) + e, 1), :] for e in range(2)]
    for e in range(2):
        tables[e][...] = table_of(rows[e])
    datt = datt_ref[...]
    swapped = half_roll(proj_ref[:, 128:256])
    middle = [jnp.where(low, datt, swapped), jnp.where(low, swapped, datt)]
    sources = [
        jnp.concatenate([proj_ref[:, 256 * e : 256 * e + 128], middle[e]], axis=1)
        for e in range(2)
    ]
    picked = [dot_nn(turned_table_of(rows[e]), sources[e]).astype(bf) for e in range(2)]
    for e in range(2):
        qk, dv = picked[e][:, 0:128], picked[e][:, 128:256]
        key_low = jnp.where(low, half_roll(qk), zero)
        turned = half_roll(dv)
        value_only = jnp.where(low, turned, zero) if e == 0 else jnp.where(low, zero, turned)
        bias = jnp.where(rows[e] < count, 0.0, -30000.0)
        for sl in SLICES:
            scores[e][sl, :] = 0.125 * dot_nt(qk[sl], key_low[sl]) + bias[:, sl]
            back_probs[e][sl, :] = dot_nt(dv[sl], value_only[sl])
    for e in range(2):
        for sl in SLICES:
            probs = softmax_rows(scores[e][sl, :])
            back = back_probs[e][sl, :]
            probs_low[e][sl, :] = probs.astype(bf)
            inner = jnp.sum(back * probs, axis=-1, keepdims=True)
            backs[e][sl, :] = (0.125 * (probs * (back - inner))).astype(bf)
    moved = []
    for e in range(2):
        qk, dv = picked[e][:, 0:128], picked[e][:, 128:256]
        queries, keys, values = [], [], []
        for sl in SLICES:
            back = backs[e][sl, :]
            queries.append(dot_nn(back, qk[sl]))
            keys.append(dot_tn(back, qk[sl]))
            values.append(dot_tn(probs_low[e][sl, :], dv[sl]))
        key_query = jnp.where(low, jnp.concatenate(keys, 0), jnp.concatenate(queries, 0))
        value = jnp.concatenate(values, 0)
        db_ref[0, 0, e : e + 1, :] = jnp.sum(key_query, axis=0, keepdims=True)
        db_ref[0, 0, 2 + e : 3 + e, :] = jnp.sum(value, axis=0, keepdims=True)
        moved.append(jnp.concatenate([key_query.astype(bf), value.astype(bf)], axis=1))
    placed = [dot_nn(tables[e][...], moved[e]) for e in range(2)]
    key_queries = [placed[e][:, 0:128] for e in range(2)]
    turned = [pltpu.roll(t, DH, 1) for t in key_queries]
    query = jnp.where(low, turned[0], key_queries[1]).astype(bf)
    key = jnp.where(low, key_queries[0], turned[1]).astype(bf)
    value = jnp.where(low, placed[0][:, 128:256], placed[1][:, 128:256]).astype(bf)
    dq_ref[...] = query
    dk_ref[...] = key
    dv_ref[...] = value
    out = jnp.concatenate([query, key, value], axis=1)
    part = dot_tn(x_ref[...], out)

    @pl.when(seq == 0)
    def _():
        total[...] = part

    @pl.when(seq != 0)
    def _():
        total[...] += part

    dw_ref[0] = total[...].astype(bf)

    @pl.when(turn < 2)
    def _():
        rows = D // shards
        columns = pl.ds(pl.multiple_of(turn * 384, 128), 384)
        for k in range(shards):
            group[k, :, columns] = total[k * rows : (k + 1) * rows, :].astype(bf)

    end()


def pair_at(i):
    return (i % 2) * (PAIRS // 2) + i // 2


def pair_at(i):
    return (i % 2) * (PAIRS // 2) + i // 2


def attention_backward(lengths, rounded, proj, datt, rows, grads, shards, reps, collective_id):
    seqs = rows.shape[0]
    tokens = seqs * LEN
    own = lambda width: pl.BlockSpec((LEN, width), lambda i, s, n: (s, pair_at(i)))
    part = (D // shards, D)
    shapes = {
        "d": [grads[0].shape[1:]],
        "u": [g.shape[1:] for g in grads[1:]],
        "g": [part],
    }
    every = shapes["d"] + shapes["u"] + shapes["g"]
    return pl.pallas_call(
        partial(attention_backward_body, shards, reps, shapes),
        grid_spec=pltpu.PrefetchScalarGridSpec(
            num_scalar_prefetch=1,
            grid=(PAIRS, seqs),
            in_specs=[
                pl.BlockSpec((LEN, D), lambda i, s, n: (s, 0)),
                own(384),
                own(128),
                pl.BlockSpec((1, H, LEN), lambda i, s, n: (s, 0, 0)),
            ]
            + [pl.BlockSpec(memory_space=pl.ANY)] * 3,
            out_specs=[own(128)] * 3
            + [
                pl.BlockSpec((1, D, 384), lambda i, s, n: (i // 2, 0, i % 2)),
                pl.BlockSpec((1, 1, 4, 128), lambda i, s, n: (s, pair_at(i), 0, 0)),
            ]
            + [pl.BlockSpec(memory_space=pl.ANY)] * 4,
            scratch_shapes=[pltpu.VMEM((LEN, LEN), bf)] * 2
            + [pltpu.VMEM((LEN, 128), f32)] * 4
            + [pltpu.VMEM((LEN, 128), bf)] * 4
            + [pltpu.VMEM((D, 384), f32), pltpu.VMEM((shards,) + part, bf)]
            + sum([reduce_scratch(shapes[k], shards, reps, k == "u") for k in "dug"], []),
        ),
        out_shape=[jax.ShapeDtypeStruct((tokens, D), bf)] * 3
        + [
            jax.ShapeDtypeStruct((PAIRS // 2, D, D), bf),
            jax.ShapeDtypeStruct((seqs, PAIRS, 4, 128), f32),
        ]
        + result_shapes(every),
        compiler_params=pltpu.CompilerParams(
            vmem_limit_bytes=62 << 20, collective_id=collective_id, has_side_effects=True
        ),
        name="attention_backward",
    )(lengths, rounded, proj, datt, rows, *grads)


def norm_stats(x):
    c=jnp.mean(x,axis=-1,keepdims=True)
    xc=x-c
    r=lax.rsqrt(jnp.mean(xc*xc,axis=-1,keepdims=True)+eps_norm)
    return xc*r,r

def norm_back(up,normed,r,gain):
    g=up*gain
    return r*(g-jnp.mean(g,axis=-1,keepdims=True)-normed*jnp.mean(g*normed,axis=-1,keepdims=True))

def colsum(x): return jnp.sum(x,axis=0,keepdims=True)

def gelu_parts(u):
    cdf=0.5+0.5*lax.erf(u*0.7071067811865476)
    pdf=jnp.exp(-0.5*u*u)*0.3989422804014327
    return u*cdf,cdf+u*pdf

def middle_body(len_ref,h_ref,a_ref,ct_ref,ow_ref,uw_ref,dw_ref,vec_ref,ub_ref,
               out_ref,bs_ref,ba_ref,act,pl_,low_ref,d2_ref,sl_ref,small_ref,ubg_ref,
               gp,n1_ref,*,T,sub_rows,chunk):
    i=pl.program_id(0)
    per=LEN//T
    count=len_ref[i//per]
    @pl.when(i==0)
    def _():
        small_ref[...]=jnp.zeros_like(small_ref); ubg_ref[...]=jnp.zeros_like(ubg_ref)
    out_b,g1,b1,down_b,g2,b2=[vec_ref[j:j+1,:] for j in range(6)]
    parts=[slice(k,k+sub_rows) for k in range(0,T,sub_rows)]
    r1s=[];sums=[]
    xs=[dot_nn(a_ref[p,:],ow_ref[...]) for p in parts]
    for p,x in zip(parts,xs):
        n1,r1=norm_stats(h_ref[p,:]+x+out_b)
        n1_ref[p,:]=n1; r1s.append(r1)
        low_ref[p,:]=(n1*g1+b1).astype(bf)
    for j in range(0,FF,chunk):
        sl=slice(j,j+chunk)
        for p in parts:
            u=dot_nn(low_ref[p,:],uw_ref[:,sl])+ub_ref[:,sl]
            a,g=gelu_parts(u)
            act[p,sl]=a.astype(bf); gp[p,sl]=g.astype(gp.dtype)
    ys=[dot_nn(act[p,:],dw_ref[...]) for p in parts]
    for p,y in zip(parts,ys):
        pos=lax.broadcasted_iota(jnp.int32,(sub_rows,1),0)+(i%per)*T+p.start
        valid=jnp.where(pos<count,1.0,0.0)
        second=n1_ref[p,:]*g1+b1+y+down_b
        n2,r2=norm_stats(second)
        out_ref[p,:]=valid*(n2*g2+b2)
        up=valid*ct_ref[p,:]
        b2nd=norm_back(up,n2,r2,g2)
        d2_ref[p,:]=b2nd.astype(bf)
        bs_ref[p,:]=b2nd
        sums.append(jnp.concatenate([colsum(b2nd),colsum(up*n2),colsum(up)],axis=0))
    small_ref[3:6,:]+=sum(sums[1:],sums[0])
    for j in range(0,FF,chunk):
        sl=slice(j,j+chunk)
        cs=[]
        for p in parts:
            bp=dot_nt(d2_ref[p,:],dw_ref[sl,:])*gp[p,sl].astype(f32)
            cs.append(colsum(bp))
            pl_[p,sl]=bp.astype(bf)
        ubg_ref[:,sl]+=sum(cs[1:],cs[0])
    zs=[dot_nt(pl_[p,:],uw_ref[...]) for p in parts]
    sums=[]
    for p,z,r1 in zip(parts,zs,r1s):
        bfirst=z+bs_ref[p,:]
        n1=n1_ref[p,:]
        bsum=norm_back(bfirst,n1,r1,g1)
        bs_ref[p,:]=bsum
        sl_ref[p,:]=bsum.astype(bf)
        sums.append(jnp.concatenate([colsum(bsum),colsum(bfirst*n1),colsum(bfirst)],axis=0))
    small_ref[0:3,:]+=sum(sums[1:],sums[0])
    for p in parts:
        ba_ref[p,:]=dot_nt(sl_ref[p,:],ow_ref[...]).astype(bf)

def middle(lengths,hidden,att,ct,ow,uw,dw,vec,ub,T=512,chunk=768,gpt=f32,sub_rows=256):
    tokens=hidden.shape[0]
    tile=lambda n=D: pl.BlockSpec((T,n),lambda i,l:(i,0))
    const=lambda shape: pl.BlockSpec(shape,lambda i,l:(0,0),pipeline_mode=pl.Buffered(1))
    whole=lambda shape: pl.BlockSpec(shape,lambda i,l:(0,0))
    sd=lambda n,dt: jax.ShapeDtypeStruct((tokens,n),dt)
    return pl.pallas_call(
        partial(middle_body,T=T,chunk=chunk,sub_rows=sub_rows),
        grid_spec=pltpu.PrefetchScalarGridSpec(num_scalar_prefetch=1,grid=(tokens//T,),
          in_specs=[tile(),tile(),tile(),const((D,D)),const((D,FF)),const((FF,D)),whole((8,D)),whole((1,FF))],
          out_specs=[tile(),tile(),tile(),tile(FF),tile(FF),tile(),tile(),tile(),whole((8,D)),whole((1,FF))],
          scratch_shapes=[pltpu.VMEM((T,FF),gpt),pltpu.VMEM((T,D),f32)]),
        out_shape=[sd(D,f32),sd(D,f32),sd(D,bf),sd(FF,bf),sd(FF,bf),sd(D,bf),sd(D,bf),sd(D,bf),jax.ShapeDtypeStruct((8,D),f32),jax.ShapeDtypeStruct((1,FF),f32)],
        compiler_params=pltpu.CompilerParams(vmem_limit_bytes=63<<20),
        name="middle")(lengths,hidden,att,ct,ow,uw,dw,vec,ub)


def weight_grads_body(act,d2,low,pre,att,sl,down_ref,up_ref,out_ref,left,right,left_sem,right_sem):
    i=pl.program_id(0)
    def block(ref,j):
        return ref if ref.shape[1]==D else ref.at[:,j*D:(j+1)*D]
    def fetch(ref,j,slot,to_left):
        return pltpu.make_async_copy(block(ref,j),(left if to_left else right).at[slot],(left_sem if to_left else right_sem).at[slot])
    loads={0:((act,0,0,True),(d2,0,0,False),(act,1,1,True)),1:((act,2,0,True),(pre,0,1,False)),2:((act,3,1,True),),
           3:((low,0,0,True),),4:((pre,1,0,False),(att,0,1,True)),5:((pre,2,1,False),),6:((pre,3,0,False),),7:((sl,0,1,False),)}
    needs={0:((act,0,0,True),(d2,0,0,False)),1:((act,1,1,True),),2:((act,2,0,True),),3:((act,3,1,True),),4:((low,0,0,True),(pre,0,1,False)),
           5:((pre,1,0,False),),6:((pre,2,1,False),),7:((pre,3,0,False),),8:((att,0,1,True),(sl,0,1,False))}
    for k in range(9):
        def move(k=k):
            for one in loads.get(k,()): fetch(*one).start()
            for one in needs[k]: fetch(*one).wait()
        pl.when(i==k)(move)
    l=jnp.where(i<4,lax.rem(i,2),jnp.where(i<8,0,1))
    r=jnp.where(i<4,0,jnp.where(i<8,lax.rem(i+1,2),1))
    grad=dot_tn(left[l],right[r]).astype(bf)
    @pl.when(i<4)
    def _(): down_ref[...]=grad
    @pl.when(jnp.logical_and(i>=4,i<8))
    def _(): up_ref[...]=grad
    @pl.when(i==8)
    def _(): out_ref[...]=grad
def weight_grads(act,d2,low,pre,att,sl):
    tokens=act.shape[0]
    return pl.pallas_call(weight_grads_body,grid=(9,),
        in_specs=[pl.BlockSpec(memory_space=pl.ANY)]*6,
        out_specs=[pl.BlockSpec((D,D),lambda i:(jnp.minimum(i,3),0)),pl.BlockSpec((D,D),lambda i:(0,jnp.clip(i-4,0,3))),pl.BlockSpec((D,D),lambda i:(0,0))],
        out_shape=[jax.ShapeDtypeStruct((FF,D),bf),jax.ShapeDtypeStruct((D,FF),bf),jax.ShapeDtypeStruct((D,D),bf)],
        scratch_shapes=[pltpu.VMEM((2,tokens,D),bf),pltpu.VMEM((2,tokens,D),bf),pltpu.SemaphoreType.DMA((2,)),pltpu.SemaphoreType.DMA((2,))],
        compiler_params=pltpu.CompilerParams(vmem_limit_bytes=60<<20),name="weight_grads")(act,d2,low,pre,att,sl)


def input_grad_body(shards,reps,shapes,bs_ref,dq_ref,dk_ref,dv_ref,w_ref,*refs):
    n=len(shapes)
    grads,out_ref,sums,scratch=refs[:n],refs[n],refs[n+1:2*n+1],refs[2*n+1:]
    weight,loaded=scratch[-2:]
    load=lambda: pltpu.make_async_copy(w_ref,weight,loaded.at[0])
    def ready():
        load().start()
        meet(place,True)
    place=Place(shards,reps); step=pl.program_id(0)
    size=len(reduce_scratch(shapes[1:],shards,reps))
    jobs={"a":Reduce(place,grads[1:],sums[1:],scratch[:size]),"b":Reduce(place,grads[:1],sums[:1],scratch[size:-2],True)}
    end=follow(LAST_PLAN,jobs,step,pl.num_programs(0)-1,ready)
    pl.when(step==0)(lambda: load().wait())
    out_ref[...]=bs_ref[...]+dot_nt(dq_ref[...],weight[:,0:D])+dot_nt(dk_ref[...],weight[:,D:2*D])+dot_nt(dv_ref[...],weight[:,2*D:3*D])
    end()
def input_grad(back_sum,dq,dk,dv,weight,grads,shards,reps,collective_id):
    rows=back_sum.shape[0]//8
    tile=pl.BlockSpec((rows,D),lambda i:(i,0))
    anywhere=[pl.BlockSpec(memory_space=pl.ANY)]*len(grads)
    shapes=[g.shape[1:] for g in grads]
    return pl.pallas_call(partial(input_grad_body,shards,reps,shapes),grid=(8,),
        in_specs=[tile]*4+[pl.BlockSpec(memory_space=pl.ANY)]+anywhere,
        out_specs=[tile]+anywhere,
        out_shape=[jax.ShapeDtypeStruct(back_sum.shape,f32)]+result_shapes(shapes),
        scratch_shapes=reduce_scratch(shapes[1:],shards,reps)+reduce_scratch(shapes[:1],shards,reps,True)+[pltpu.VMEM((D,3*D),bf),pltpu.SemaphoreType.DMA((1,))],
        compiler_params=pltpu.CompilerParams(vmem_limit_bytes=50<<20,collective_id=collective_id,has_side_effects=True),name="input_grad")(back_sum,dq,dk,dv,weight,*grads)


def as_rows(row):
    filled = -(-row.shape[-1] // 128)
    row = jnp.pad(row, ((0, 0), (0, filled * 128 - row.shape[-1])))
    return jnp.pad(row.reshape(-1, filled, 128), ((0, 0), (0, 0), (0, 128)))


def pack_body(*refs):
    *ins, out = refs
    rows = []
    for ref in ins:
        value = ref[...].astype(f32)
        for at in range(0, value.shape[0], 128):
            part = value[at : at + 128].reshape(1, -1)
            rows.append(jnp.pad(part, ((0, 0), (0, 256 - part.shape[1]))))
    rows.append(jnp.zeros((16 - len(rows), 256), f32))
    out[...] = jnp.concatenate(rows, axis=0).astype(bf)


def pack_shards(vectors):
    return pl.pallas_call(
        pack_body, out_shape=jax.ShapeDtypeStruct((16, 256), bf), name="pack_vectors"
    )(*vectors)


def pack_vectors(vectors):
    rows = jnp.concatenate([as_rows(v) for v in vectors], axis=1)
    return jnp.pad(rows, ((0, 0), (0, 16 - rows.shape[1]), (0, 0)))


def local(
    hidden,
    lengths,
    clusters,
    input_weight,
    query_bias,
    value_bias,
    out_weight,
    out_bias,
    norm1_gain,
    norm1_bias,
    up_weight,
    up_bias,
    down_weight,
    down_bias,
    norm2_gain,
    norm2_bias,
    cotangent,
    *,
    shards,
    reps,
):
    seqs = hidden.shape[0]
    tokens = seqs * LEN
    part = D // shards
    vectors = pack_shards(
        (
            query_bias,
            value_bias,
            out_bias,
            norm1_gain,
            norm1_bias,
            down_bias,
            norm2_gain,
            norm2_bias,
            up_bias,
        )
    )
    in_w, vectors = gather_now((input_weight, vectors), shards, reps, 1)
    in_w = in_w.reshape(D, 3 * D)
    vectors = vectors.astype(f32)
    table = vectors[:, :8, :part].transpose(1, 0, 2).reshape(8, D)
    bias_all = jnp.concatenate([table[0], jnp.zeros((D,), f32), table[1]])[None]
    norm_rows = jnp.concatenate([table[2:], table[:2]])
    up_b = vectors[:, 8:, :128].reshape(shards, -1)[:, : FF // shards].reshape(1, FF)

    flat = hidden.reshape(tokens, D)
    attended, proj, rounded, up_w, down_w, out_w = attention_forward(
        lengths,
        flat,
        in_w,
        bias_all,
        clusters,
        (up_weight, down_weight, out_weight),
        shards,
        reps,
        2,
    )
    out_w, up_w, down_w = [w.reshape(-1, w.shape[-1]) for w in (out_w, up_w, down_w)]
    (
        result,
        back_sum,
        back_attended,
        activated,
        pre_low,
        first_low,
        second_low,
        sum_low,
        norm_sums,
        up_b_sum,
    ) = middle(
        lengths,
        flat,
        attended,
        cotangent.reshape(tokens, D),
        out_w,
        up_w,
        down_w,
        norm_rows,
        up_b,
    )
    down_g, up_g, out_g = weight_grads(
        activated, second_low, first_low, pre_low, attended, sum_low
    )
    dq, dk, dv, in_g, bias_sums, down_s, up_s, out_s, in_first = attention_backward(
        lengths,
        rounded,
        proj,
        back_attended,
        clusters,
        [g.reshape(shards, -1, g.shape[-1]) for g in (down_g, up_g, out_g)],
        shards,
        reps,
        3,
    )
    bias_sums = jnp.sum(bias_sums, axis=0)
    query_sum = bias_sums[:, 0:2, DH:].reshape(D)
    value_sum = jnp.concatenate([bias_sums[:, 2, :DH], bias_sums[:, 3, DH:]], axis=1).reshape(D)
    table = jnp.concatenate([query_sum[None], value_sum[None], norm_sums[:6]])
    table = table.reshape(8, shards, part)
    small = pack_vectors(
        [table[i].astype(bf) for i in range(8)] + [up_b_sum.reshape(shards, -1).astype(bf)]
    )
    back_input, *in_s, small_s = input_grad(
        back_sum,
        dq,
        dk,
        dv,
        in_w,
        [in_g[2].reshape(shards, part, D), in_g[1].reshape(shards, part, D), small],
        shards,
        reps,
        4,
    )
    back_input = back_input.reshape(seqs, LEN, D)
    in_s = [in_first, in_s[1], in_s[0]]
    in_s = jnp.concatenate(
        [
            in_s[g][:, 384 * c + 128 * t : 384 * c + 128 * t + 128]
            for t in range(3)
            for c in range(2)
            for g in range(PAIRS // 2)
        ],
        axis=1,
    )

    small_s = small_s[:, :128]
    vec = [small_s[i, :part] for i in range(8)]
    return (
        result.reshape(seqs, LEN, D),
        back_input,
        in_s,
        vec[0],
        vec[1],
        out_s,
        vec[2],
        vec[3],
        vec[4],
        up_s,
        small_s[8:].reshape(-1)[: FF // shards],
        down_s,
        vec[5],
        vec[6],
        vec[7],
    )


def solution(mesh):
    tokens = P(("rep", "shard"), None, None)
    matrix, vector = P("shard", None), P("shard")
    params = (
        matrix,
        vector,
        vector,
        matrix,
        vector,
        vector,
        vector,
        matrix,
        vector,
        matrix,
        vector,
        vector,
        vector,
    )
    return jax.shard_map(
        partial(local, shards=mesh.shape["shard"], reps=mesh.shape["rep"]),
        mesh=mesh,
        in_specs=(tokens, P(("rep", "shard")), tokens) + params + (tokens,),
        out_specs=(tokens, tokens) + params,
        check_vma=False,
    )
```

```python
from functools import partial

import jax
import jax.numpy as jnp
from jax import lax
from jax.experimental import pallas as pl
from jax.experimental.pallas import tpu as pltpu
from jax.sharding import PartitionSpec as P

D = 768
H = 12
DH = 64
FF = 3072
CLUSTER = 128
LEN = 1024
PAIRS = H // 2
SLICES = [slice(c * CLUSTER, (c + 1) * CLUSTER) for c in range(LEN // CLUSTER)]
bf = jnp.bfloat16
f32 = jnp.float32
eps_norm = 1e-12


def dot_nn(left, right):
    return lax.dot_general(left, right, (((1,), (0,)), ((), ())), preferred_element_type=f32)


def dot_nt(left, right):
    return lax.dot_general(left, right, (((1,), (1,)), ((), ())), preferred_element_type=f32)


def dot_tn(left, right):
    return lax.dot_general(left, right, (((0,), (0,)), ((), ())), preferred_element_type=f32)


ROWS = 4
MESH=pl.DeviceIdType.MESH

def when(cond,do):
    if cond is None: do()
    else: pl.when(cond)(do)

class Place:
    def __init__(self,shards,reps):
        self.Y=shards//ROWS; self.S=shards; self.X=reps//2
        self.s=lax.axis_index("shard"); self.r=lax.axis_index("rep")
        self.z=self.s//self.Y; self.y=lax.rem(self.s,self.Y)
        self.core=lax.rem(self.r,2); self.x=self.r//2
    def near_z(self,step): return {"shard":self.s+step*self.Y}
    def other_y(self,k): return {"shard":self.z*self.Y+lax.rem(self.y+k,self.Y)}
    def other_core(self): return {"rep":self.r+1-2*self.core}
    def other_x(self,k): return {"rep":2*lax.rem(self.x+k,self.X)+self.core}

def meet(place,with_x):
    sem=pltpu.get_barrier_semaphore()
    def tell(dev): pl.semaphore_signal(sem,inc=1,device_id=dev,device_id_type=MESH)
    pl.when(place.z>0)(lambda: tell(place.near_z(-1)))
    pl.when(place.z<ROWS-1)(lambda: tell(place.near_z(1)))
    for k in range(1,place.Y): tell(place.other_y(k))
    tell(place.other_core())
    if with_x:
        for k in range(1,place.X): tell(place.other_x(k))
    others=place.Y+(place.X-1 if with_x else 0)
    inner=jnp.logical_and(place.z>0,place.z<ROWS-1)
    pl.when(inner)(lambda: pl.semaphore_wait(sem,others+2))
    pl.when(jnp.logical_not(inner))(lambda: pl.semaphore_wait(sem,others+1))

def gather_semaphores(count,shards):
    Y=shards//ROWS; dma=pltpu.SemaphoreType.DMA
    return [dma((count,2,ROWS)),dma((count,2,ROWS)),dma((count,ROWS,Y)),dma((count,ROWS,Y)),
            dma((count,2,shards)),dma((count,2,shards)),dma((count,shards)),dma((count,shards)),dma((count,))]

class Gather:
    def __init__(self,place,ins,outs,sems,share=False):
        self.p=place; self.ins=ins; self.outs=outs; self.share=share and place.X==2
        self.line_s,self.line_r,self.y_s,self.y_r,self.core_s,self.core_r,self.x_s,self.x_r,self.own=sems
        self.sent=[]
    def piece(self,ref,shard=None,core=None,x=None):
        p=self.p; n=ref.shape[-1]//2; r=ref.shape[-2]
        cols=pl.ds(pl.multiple_of((p.core if core is None else core)*n,128),n)
        rows=slice(None)
        if self.share:
            rows=pl.ds(pl.multiple_of((p.x if x is None else x)*(r//2),16),r//2)
        return ref.at[rows,cols] if shard is None else ref.at[shard,rows,cols]
    def send(self,make):
        cond,desc=make()
        when(cond,desc.start); self.sent.append(make)
    def copy(self,src,dst,ss,rs,dev):
        return pltpu.make_async_remote_copy(src_ref=src,dst_ref=dst,send_sem=ss,recv_sem=rs,device_id=dev,device_id_type=MESH)
    def at(self,places):
        zz=self.p.z+places
        if places==0: return None,zz
        return jnp.logical_and(zz>=0,zz<ROWS),jnp.clip(zz,0,ROWS-1)
    def shard_at(self,zz,k):
        p=self.p
        return zz*p.Y+(lax.rem(p.y-k+p.Y,p.Y) if k else p.y)
    def to_line(self,a,places,d):
        p=self.p; i,o=self.ins[a],self.outs[a]
        def make():
            cond,zz=self.at(places); shard=zz*p.Y+p.y
            edge=(p.z<ROWS-1) if d==0 else (p.z>0)
            src=self.piece(i) if places==0 else self.piece(o,shard)
            return (edge if cond is None else jnp.logical_and(cond,edge)),self.copy(src,self.piece(o,shard),self.line_s.at[a,d,zz],self.line_r.at[a,d,zz],p.near_z(1 if d==0 else -1))
        self.send(make)
    def to_y(self,a,places,k):
        p=self.p; i,o=self.ins[a],self.outs[a]
        def make():
            cond,zz=self.at(places); shard=zz*p.Y+p.y
            src=self.piece(i) if places==0 else self.piece(o,shard)
            return cond,self.copy(src,self.piece(o,shard),self.y_s.at[a,zz,k],self.y_r.at[a,zz,k],p.other_y(k))
        self.send(make)
    def to_core(self,a,places,k,other=False):
        p=self.p; o=self.outs[a]; slot=1 if other else 0
        def make():
            cond,zz=self.at(places); shard=self.shard_at(zz,k)
            ref=self.piece(o,shard,x=1-p.x if other else p.x)
            return cond,self.copy(ref,ref,self.core_s.at[a,slot,shard],self.core_r.at[a,slot,shard],p.other_core())
        self.send(make)
    def to_x(self,a,places,k):
        p=self.p; o=self.outs[a]
        if not self.share: return
        def make():
            cond,zz=self.at(places); shard=self.shard_at(zz,k)
            ref=self.piece(o,shard)
            return cond,self.copy(ref,ref,self.x_s.at[a,shard],self.x_r.at[a,shard],p.other_x(1))
        self.send(make)
    def begin(self):
        for a,(i,o) in enumerate(zip(self.ins,self.outs)):
            for d in (0,1): self.to_line(a,0,d)
            for k in range(1,self.p.Y): self.to_y(a,0,k)
            pltpu.make_async_copy(i,o.at[self.p.s],self.own.at[a]).start()
    def wave(self,w):
        p=self.p
        for d in (0,1):
            places=-w if d==0 else w
            for a,o in enumerate(self.outs):
                cond,zz=self.at(places); ref=self.piece(o,zz*p.Y+p.y)
                when(cond,self.copy(ref,ref,self.line_s.at[a,d,zz],self.line_r.at[a,d,zz],p.near_z(0)).wait_recv)
                self.to_line(a,places,d)
                for k in range(1,p.Y): self.to_y(a,places,k)
                self.to_x(a,places,0); self.to_core(a,places,0)
    def across(self,w):
        p=self.p
        for places in ((0,) if w==0 else (-w,w)):
            for k in range(1,p.Y):
                for a,o in enumerate(self.outs):
                    cond,zz=self.at(places); ref=self.piece(o,self.shard_at(zz,k))
                    when(cond,self.copy(ref,ref,self.y_s.at[a,zz,k],self.y_r.at[a,zz,k],p.other_y(k)).wait_recv)
                    self.to_x(a,places,k); self.to_core(a,places,k)
    def over(self,w):
        p=self.p
        if not self.share: return
        for places in ((0,) if w==0 else (-w,w)):
            for k in range(1 if w==0 else 0,p.Y):
                for a,o in enumerate(self.outs):
                    cond,zz=self.at(places); shard=self.shard_at(zz,k); ref=self.piece(o,shard,x=1-p.x)
                    when(cond,self.copy(ref,ref,self.x_s.at[a,shard],self.x_r.at[a,shard],p.other_x(1)).wait_recv)
                    self.to_core(a,places,k,True)
    def finish(self):
        p=self.p
        for a,(i,o) in enumerate(zip(self.ins,self.outs)):
            for k in range(1,p.S):
                shard=lax.rem(p.s+k,p.S)
                for slot in range(2 if self.share else 1):
                    ref=self.piece(o,shard,core=1-p.core,x=1-p.x if slot else p.x)
                    self.copy(ref,ref,self.core_s.at[a,slot,shard],self.core_r.at[a,slot,shard],p.other_core()).wait_recv()
            pltpu.make_async_copy(i,o.at[p.s],self.own.at[a]).wait()
        for make in self.sent:
            cond,desc=make()
            when(cond,desc.wait_send)
def gather_body(shards,reps,count,*refs):
    ins,outs,sems=refs[:count],refs[count:2*count],refs[2*count:]
    place=Place(shards,reps)
    meet(place,False)
    G=Gather(place,ins,outs,sems)
    G.begin(); G.wave(1); G.across(0); G.wave(2); G.across(1); G.wave(3); G.across(2); G.across(3); G.finish()

def gather_now(arrays,shards,reps,collective_id):
    count=len(arrays)
    return pl.pallas_call(partial(gather_body,shards,reps,count),
        in_specs=[pl.BlockSpec(memory_space=pltpu.VMEM)]*count,
        out_specs=[pl.BlockSpec(memory_space=pl.ANY)]*count,
        out_shape=[jax.ShapeDtypeStruct((shards,)+a.shape,a.dtype) for a in arrays],
        scratch_shapes=gather_semaphores(count,shards),
        compiler_params=pltpu.CompilerParams(collective_id=collective_id,has_side_effects=True,vmem_limit_bytes=16<<20),
        name="gather_weights")(*arrays)

ORDER=(3,0,2,1)
def reduce_scratch(shapes,shards,reps,x_first=False):
    x_first=x_first and reps==4
    S=shards; Y=S//ROWS; X=reps//2; A=len(shapes)
    out=[]
    for r,c in shapes:
        n=c//2; m=r//2 if x_first else r
        out+=[pltpu.VMEM((S,r,n),bf),pltpu.VMEM((S,r,n),bf),pltpu.VMEM((max(Y-1,1),ROWS,m,n),bf),
              pltpu.VMEM((ROWS+1,m,n),bf),pltpu.VMEM((S+1,m,n) if x_first else (X,r,n),bf),pltpu.VMEM((2,r,n),f32)]
    dma=pltpu.SemaphoreType.DMA
    return out+[dma((A,S)),dma((A,S)),dma((A,S)),dma((A,Y,ROWS)),dma((A,Y,ROWS)),dma((A,ROWS+1)),dma((A,ROWS+1)),dma((A,S+X)),dma((A,S+X)),dma((A,)),dma((A,)),dma((A,2))]
class Reduce:
    def __init__(self,place,ins,outs,scratch,x_first=False):
        self.p=place; self.ins=ins; self.outs=outs; A=len(ins); self.A=range(A)
        self.bufs=[scratch[6*a:6*a+6] for a in range(A)]
        (self.own,self.core_s,self.core_r,self.y_s,self.y_r,self.line_s,self.line_r,self.x_s,self.x_r,self.end_s,self.end_r,self.out_s)=scratch[6*A:]
        self.sent=[]; self.x_first=x_first and place.X==2
    def copy(self,src,dst,ss,rs,dev):
        return pltpu.make_async_remote_copy(src_ref=src,dst_ref=dst,send_sem=ss,recv_sem=rs,device_id=dev,device_id_type=MESH)
    def send(self,make):
        cond,desc=make()
        when(cond,desc.start); self.sent.append(make)
    def half(self,a,shard,core):
        n=self.ins[a].shape[-1]//2
        return self.ins[a].at[shard,:,pl.ds(pl.multiple_of(core*n,128),n)]
    def mine(self,a,shard,x=None):
        H=self.bufs[a][0]
        if not self.x_first: return H.at[shard]
        m=H.shape[1]//2
        return H.at[shard,pl.ds(pl.multiple_of((self.p.x if x is None else x)*m,16),m)]
    def add(self,dst,others):
        rows,n=dst.shape; step=next(s for s in (192,96,48,16) if rows%s==0 and (s==16 or s*n<=96*768))
        def block(at):
            value=dst[at,:]
            for o in others: value=value+o[at,:]
            dst[at,:]=value
        if rows==step: block(slice(0,rows)); return
        def body(i,_):
            block(pl.ds(pl.multiple_of(i*step,16),step))
            return 0
        lax.fori_loop(0,rows//step,body,0)
    def begin(self,ks=None):
        p=self.p
        for k in (list(range(1,p.Y)) if ks is None else ks):
            for d in ORDER:
                for a in self.A:
                    H,Rc=self.bufs[a][0:2]
                    def make(a=a,d=d,k=k,Rc=Rc):
                        shard=d*p.Y+lax.rem(p.y+k,p.Y)
                        return None,self.copy(self.half(a,shard,1-p.core),Rc.at[shard],self.core_s.at[a,shard],self.core_r.at[a,shard],p.other_core())
                    self.send(make)
                    shard=d*p.Y+lax.rem(p.y+k,p.Y)
                    pltpu.make_async_copy(self.half(a,shard,p.core),H.at[shard],self.own.at[a,shard]).start()
    def join_core(self,shard):
        p=self.p
        for a in self.A:
            H,Rc=self.bufs[a][0:2]
            pltpu.make_async_copy(self.half(a,shard,p.core),H.at[shard],self.own.at[a,shard]).wait()
            self.copy(Rc.at[shard],Rc.at[shard],self.core_s.at[a,shard],self.core_r.at[a,shard],p.other_core()).wait_recv()
            self.add(H.at[shard],[Rc.at[shard]])
    def to_pair(self,k,d):
        p=self.p; shard=d*p.Y+lax.rem(p.y+k,p.Y)
        if not self.x_first: return
        self.join_core(shard)
        for a in self.A:
            def make(a=a):
                shard=d*p.Y+lax.rem(p.y+k,p.Y)
                return None,self.copy(self.mine(a,shard,1-p.x),self.bufs[a][4].at[shard],self.x_s.at[a,shard],self.x_r.at[a,shard],p.other_x(1))
            self.send(make)
    def ready(self,shard):
        p=self.p
        if not self.x_first: self.join_core(shard); return
        for a in self.A:
            got=self.bufs[a][4].at[shard]
            self.copy(got,got,self.x_s.at[a,shard],self.x_r.at[a,shard],p.other_x(1)).wait_recv()
            self.add(self.mine(a,shard),[got])
    def to_y(self,d):
        p=self.p
        for k in range(1,p.Y):
            self.ready(d*p.Y+lax.rem(p.y+k,p.Y))
            for a in self.A:
                H,_,Ry=self.bufs[a][0:3]
                def make(a=a,H=H,Ry=Ry,k=k):
                    shard=d*p.Y+lax.rem(p.y+k,p.Y)
                    return None,self.copy(self.mine(a,shard),Ry.at[k-1,d],self.y_s.at[a,k,d],self.y_r.at[a,k,d],p.other_y(k))
                self.send(make)
    def own_y(self,d):
        self.ready(d*self.p.Y+self.p.y)
    def along(self,d,up,j):
        p=self.p
        if (j>=d) if up else (ROWS-1-j<=d): return
        here=p.z==(j if up else ROWS-1-j)
        shard=d*p.Y+p.y
        if j>0:
            def add_in():
                for a in self.A:
                    H,Rl=self.bufs[a][0],self.bufs[a][3]
                    self.copy(Rl.at[d],Rl.at[d],self.line_s.at[a,d],self.line_r.at[a,d],p.near_z(0)).wait_recv()
                    self.add(self.mine(a,shard),[Rl.at[d]])
            pl.when(here)(add_in)
        last=(j==d-1) if up else (ROWS-1-j==d+1)
        slot=ROWS if last and not up else d
        for a in self.A:
            def make(a=a):
                H,Rl=self.bufs[a][0],self.bufs[a][3]
                return p.z==(j if up else ROWS-1-j),self.copy(self.mine(a,d*p.Y+p.y),Rl.at[slot],self.line_s.at[a,slot],self.line_r.at[a,slot],p.near_z(1 if up else -1))
            self.send(make)
    def line(self,d):
        p=self.p; shard=d*p.Y+p.y
        for a in self.A:
            H,_,Ry=self.bufs[a][0:3]
            for k in range(1,p.Y):
                self.copy(Ry.at[k-1,d],Ry.at[k-1,d],self.y_s.at[a,k,d],self.y_r.at[a,k,d],p.other_y(k)).wait_recv()
            self.add(self.mine(a,shard),[Ry.at[k-1,d] for k in range(1,p.Y)])
        self.along(d,True,0); self.along(d,False,0)
    def relay(self,d,j):
        self.along(d,True,j); self.along(d,False,j)
    def to_x(self):
        p=self.p
        for slot,cond in ((p.z,p.z>0),(ROWS,p.z<ROWS-1)):
            def add_in(slot=slot):
                for a in self.A:
                    H,Rl=self.bufs[a][0],self.bufs[a][3]
                    self.copy(Rl.at[slot],Rl.at[slot],self.line_s.at[a,slot],self.line_r.at[a,slot],p.near_z(0)).wait_recv()
                    self.add(self.mine(a,p.s),[Rl.at[slot]])
            pl.when(cond)(add_in)
        for a in self.A:
            H,Rx=self.bufs[a][0],self.bufs[a][4]
            if self.x_first:
                self.send(lambda a=a,Rx=Rx: (None,self.copy(self.mine(a,p.s),Rx.at[p.S],self.x_s.at[a,p.S],self.x_r.at[a,p.S],p.other_x(1))))
                continue
            for k in range(1,p.X):
                self.send(lambda a=a,H=H,Rx=Rx,k=k: (None,self.copy(H.at[p.s],Rx.at[p.x],self.x_s.at[a,k],self.x_r.at[a,p.x],p.other_x(k))))
    def to_core(self):
        p=self.p
        for a in self.A:
            H,Rx,F=self.bufs[a][0],self.bufs[a][4],self.bufs[a][5]
            if self.x_first:
                got=Rx.at[p.S]; m=H.shape[1]//2
                self.copy(got,got,self.x_s.at[a,p.S],self.x_r.at[a,p.S],p.other_x(1)).wait_recv()
                for x in range(2):
                    own=H[p.s,x*m:(x+1)*m,:]
                    F[p.core,x*m:(x+1)*m,:]=jnp.where(p.x==x,own,Rx[p.S]).astype(f32)
                continue
            for k in range(1,p.X):
                src=lax.rem(p.x-k+p.X,p.X)
                self.copy(Rx.at[src],Rx.at[src],self.x_s.at[a,k],self.x_r.at[a,src],p.other_x(k)).wait_recv()
            rows=H.shape[1]; step=48 if rows%48==0 else 16
            def body(i,_):
                at=pl.ds(pl.multiple_of(i*step,16),step)
                own=H[p.s,at,:].astype(f32)
                value=jnp.zeros_like(own)
                for q in range(p.X):
                    value=value+jnp.where(p.x==q,own,Rx[q,at,:].astype(f32))
                F[p.core,at,:]=value
                return 0
            lax.fori_loop(0,rows//step,body,0)
        for a in self.A:
            F=self.bufs[a][5]
            self.send(lambda a=a,F=F: (None,self.copy(F.at[p.core],F.at[p.core],self.end_s.at[a],self.end_r.at[a],p.other_core())))
    def result(self,a,core):
        F=self.bufs[a][5]; n=F.shape[2]
        return pltpu.make_async_copy(F.at[core],self.outs[a].at[:,core*n:(core+1)*n],self.out_s.at[a,core])
    def finish(self):
        p=self.p
        for a in self.A:
            ref=self.bufs[a][5].at[1-p.core]
            self.copy(ref,ref,self.end_s.at[a],self.end_r.at[a],p.other_core()).wait_recv()
            for core in range(2): self.result(a,core).start()
        for make in self.sent:
            cond,desc=make()
            when(cond,desc.wait_send)
        for a in self.A:
            for core in range(2): self.result(a,core).wait()
def result_shapes(shapes):
    return [jax.ShapeDtypeStruct((r,c),f32) for r,c in shapes]

GATHER_PLAN = {
    0: (("u", "begin"), ("d", "begin")),
    2: (("u", "wave", 1),),
    3: (("d", "wave", 1), ("u", "across", 0)),
    4: (("u", "wave", 2), ("d", "across", 0)),
    6: (("d", "wave", 2),),
    7: (("u", "wave", 3), ("u", "across", 1)),
    8: (("d", "wave", 3), ("d", "across", 1), ("d", "over", 0)),
    10: (("u", "across", 2), ("u", "across", 3), ("d", "across", 2), ("d", "across", 3)),
    11: (("d", "over", 1),),
    100: (("d", "over", 2), ("d", "over", 3), ("u", "finish"), ("d", "finish")),
}


def each(name, what, *more):
    return tuple((name, what, d) + more for d in ORDER)


REDUCE_PLAN = {
    0: (("d", "begin"), ("u", "begin"), ("d", "begin", (0,)), ("u", "begin", (0,))),
    1: each("d", "to_y") + tuple(("u", "to_pair", 1, d) for d in ORDER),
    2: tuple(("u", "to_pair", 0, d) for d in ORDER) + each("d", "own_y") + (("d", "line", 3),),
    3: (("d", "line", 0), ("d", "relay", 3, 1)),
    4: (("g", "begin"), ("g", "begin", (0,)))
    + (("d", "line", 2), ("d", "relay", 0, 1), ("d", "relay", 3, 2))
    + each("u", "to_y"),
    5: (("d", "line", 1), ("d", "relay", 2, 1), ("d", "relay", 0, 2))
    + each("g", "to_y")
    + each("g", "own_y")
    + (("u", "own_y", 3), ("u", "own_y", 0)),
    6: (("d", "relay", 1, 1), ("u", "line", 3), ("u", "line", 0), ("u", "own_y", 2), ("u", "own_y", 1)),
    7: (("d", "to_x"), ("u", "relay", 3, 1), ("u", "relay", 0, 1), ("u", "line", 2), ("u", "line", 1)),
    8: (("d", "to_core"), ("u", "relay", 3, 2), ("u", "relay", 0, 2)) + each("g", "line"),
    9: (("u", "relay", 2, 1), ("u", "relay", 1, 1)) + each("g", "relay", 1),
    10: (("u", "to_x"),) + each("g", "relay", 2),
    11: (("g", "to_x"), ("u", "to_core")),
    100: (("g", "to_core"), ("d", "finish"), ("u", "finish"), ("g", "finish")),
}
LAST_PLAN = {
    0: (("a", "begin"), ("b", "begin"), ("a", "begin", (0,)), ("b", "begin", (0,))),
    1: each("a", "to_y"),
    2: tuple(("b", "to_pair", k, d) for k in (1, 0) for d in ORDER) + each("a", "own_y"),
    4: (("a", "line", 3), ("a", "line", 0)),
    5: (("a", "line", 2), ("a", "line", 1)) + each("b", "to_y"),
    6: each("b", "own_y") + each("a", "relay", 1),
    7: (("a", "relay", 3, 2), ("a", "relay", 0, 2)) + each("b", "line"),
    100: (("a", "to_x"),)
    + each("b", "relay", 1)
    + (("a", "to_core"),)
    + each("b", "relay", 2)
    + (("b", "to_x"), ("b", "to_core"), ("a", "finish"), ("b", "finish")),
}


def follow(plan, jobs, step, last, ready):
    def run(at):
        for name, what, *more in plan.get(at, ()):
            getattr(jobs[name], what)(*more)

    def first():
        ready()
        run(0)

    pl.when(step == 0)(first)
    for at in sorted(plan):
        if 0 < at < 100:
            pl.when(step == at)(partial(run, at))
    return lambda: pl.when(step == last)(partial(run, 100))


def low_lanes():
    return lax.broadcasted_iota(jnp.int32, (LEN, CLUSTER), 1) < DH


def table_of(order_row):
    held = jnp.broadcast_to(order_row.astype(jnp.int16), (LEN, LEN))
    positions = lax.broadcasted_iota(jnp.int16, (LEN, LEN), 0)
    return jnp.where(held == positions, jnp.ones((), bf), jnp.zeros((), bf))


def turned_table_of(order_row):
    held = jnp.transpose(jnp.broadcast_to(order_row, (128, LEN))).astype(jnp.int16)
    lanes = lax.broadcasted_iota(jnp.int16, (LEN, 128), 1)
    return jnp.concatenate(
        [
            jnp.where(held == lanes + jnp.int16(128 * b), jnp.ones((), bf), jnp.zeros((), bf))
            for b in range(LEN // 128)
        ],
        axis=1,
    )


def half_roll(source):
    return pltpu.roll(source, DH, 1)


def softmax_rows(scores):
    top = jnp.max(scores, axis=-1, keepdims=True)
    grown = jnp.exp(scores - top)
    return grown * (1.0 / jnp.sum(grown, axis=-1, keepdims=True))


def attention_forward_body(
    shards, reps, len_ref, h_ref, wq_ref, wk_ref, wv_ref, bq_ref, bk_ref, bv_ref, row_ref, *rest
):
    ins, (att_ref, proj_ref, x_ref), outs = rest[:3], rest[3:6], rest[6:9]
    tables, scores, mixed = rest[9:11], rest[11:13], rest[13:15]
    sems = rest[15:]
    step = pl.program_id(0) * PAIRS + pl.program_id(1)
    place = Place(shards, reps)
    jobs = {
        "u": Gather(place, ins[:1], outs[:1], sems[:9]),
        "d": Gather(place, ins[1:], outs[1:], sems[9:], True),
    }
    end = follow(
        GATHER_PLAN, jobs, step, pl.num_programs(0) * PAIRS - 1, lambda: meet(place, True)
    )

    @pl.when(pl.program_id(1) == 0)
    def _():
        x_ref[...] = h_ref[...].astype(bf)

    count = len_ref[pl.program_id(0)]
    weight = jnp.concatenate([wq_ref[...], wk_ref[...], wv_ref[...]], axis=1)
    bias = jnp.concatenate([bq_ref[...], bk_ref[...], bv_ref[...]], axis=1)
    proj = (dot_nn(x_ref[...], weight) + bias).astype(bf)
    low = low_lanes()
    query, key, value = proj[:, 0:128], proj[:, 128:256], proj[:, 256:384]
    pairs = [jnp.where(low, query, half_roll(key)), jnp.where(low, half_roll(query), key)]
    proj_ref[...] = jnp.concatenate([pairs[0], value, pairs[1]], axis=1)
    rows = [row_ref[0, pl.ds(2 * pl.program_id(1) + e, 1), :] for e in range(2)]
    for e in range(2):
        tables[e][...] = table_of(rows[e])
    picked = [
        dot_nn(turned_table_of(rows[e]), jnp.concatenate([pairs[e], value], axis=1)).astype(bf)
        for e in range(2)
    ]
    for e in range(2):
        qk = picked[e][:, 0:128]
        key_low = jnp.where(low, half_roll(qk), jnp.zeros((), bf))
        bias = jnp.where(rows[e] < count, 0.0, -30000.0)
        for sl in SLICES:
            scores[e][sl, :] = 0.125 * dot_nt(qk[sl], key_low[sl]) + bias[:, sl]
    for e in range(2):
        values = picked[e][:, 128:256]
        for sl in SLICES:
            probs = softmax_rows(scores[e][sl, :]).astype(bf)
            mixed[e][sl, :] = dot_nn(probs, values[sl]).astype(bf)
    placed = [dot_nn(tables[e][...], mixed[e][...]) for e in range(2)]
    att_ref[...] = jnp.where(low, placed[0], placed[1]).astype(bf)
    end()


def attention_forward(lengths, hidden, weight, bias, rows, arrays, shards, reps, collective_id):
    seqs = rows.shape[0]
    tokens = seqs * LEN
    column = lambda part: pl.BlockSpec((D, 128), lambda s, h, n: (0, part * PAIRS + h))
    column_b = lambda part: pl.BlockSpec((1, 128), lambda s, h, n: (0, part * PAIRS + h))
    return pl.pallas_call(
        partial(attention_forward_body, shards, reps),
        grid_spec=pltpu.PrefetchScalarGridSpec(
            num_scalar_prefetch=1,
            grid=(seqs, PAIRS),
            in_specs=[pl.BlockSpec((LEN, D), lambda s, h, n: (s, 0))]
            + [column(part) for part in range(3)]
            + [column_b(part) for part in range(3)]
            + [pl.BlockSpec((1, H, LEN), lambda s, h, n: (s, 0, 0))]
            + [pl.BlockSpec(memory_space=pl.ANY)] * 3,
            out_specs=[
                pl.BlockSpec((LEN, 128), lambda s, h, n: (s, h)),
                pl.BlockSpec((LEN, 384), lambda s, h, n: (s, h)),
                pl.BlockSpec((LEN, D), lambda s, h, n: (s, 0)),
            ]
            + [pl.BlockSpec(memory_space=pl.ANY)] * 3,
            scratch_shapes=[pltpu.VMEM((LEN, LEN), bf)] * 2
            + [pltpu.VMEM((LEN, 128), f32)] * 2
            + [pltpu.VMEM((LEN, 128), bf)] * 2
            + gather_semaphores(1, shards)
            + gather_semaphores(2, shards),
        ),
        out_shape=[
            jax.ShapeDtypeStruct((tokens, D), bf),
            jax.ShapeDtypeStruct((tokens, 3 * D), bf),
            jax.ShapeDtypeStruct((tokens, D), bf),
        ]
        + [jax.ShapeDtypeStruct((shards,) + a.shape, bf) for a in arrays],
        compiler_params=pltpu.CompilerParams(
            vmem_limit_bytes=63 << 20, collective_id=collective_id, has_side_effects=True
        ),
        name="attention_forward",
    )(lengths, hidden, weight, weight, weight, bias, bias, bias, rows, *arrays)


def attention_backward_body(shards, reps, shapes, *refs):
    len_ref, x_ref, proj_ref, datt_ref, row_ref = refs[:5]
    grads, refs = refs[5:8], refs[8:]
    (dq_ref, dk_ref, dv_ref, dw_ref, db_ref), sums, refs = refs[:5], refs[5:9], refs[9:]
    t0, t1, s0, s1, d0, d1, p0, p1, e0, e1, total, group = refs[:12]
    refs = refs[12:]
    turn = pl.program_id(0)
    step = turn * pl.num_programs(1) + pl.program_id(1)
    place = Place(shards, reps)
    sizes = [len(reduce_scratch(shapes[k], shards, reps, k == "u")) for k in "dug"]
    parts = [refs[sum(sizes[:k]) : sum(sizes[: k + 1])] for k in range(3)]
    jobs = {
        "d": Reduce(place, grads[:1], sums[:1], parts[0]),
        "u": Reduce(place, grads[1:], sums[1:3], parts[1], True),
        "g": Reduce(place, [group], sums[3:], parts[2]),
    }
    end = follow(
        REDUCE_PLAN,
        jobs,
        step,
        pl.num_programs(0) * pl.num_programs(1) - 1,
        lambda: meet(place, True),
    )
    seq = pl.program_id(1)
    count = len_ref[seq]
    low = low_lanes()
    zero = jnp.zeros((), bf)
    tables, scores, back_probs, probs_low, backs = (t0, t1), (s0, s1), (d0, d1), (p0, p1), (e0, e1)
    rows = [row_ref[0, pl.ds(2 * pair_at(turn) + e, 1), :] for e in range(2)]
    for e in range(2):
        tables[e][...] = table_of(rows[e])
    datt = datt_ref[...]
    swapped = half_roll(proj_ref[:, 128:256])
    middle = [jnp.where(low, datt, swapped), jnp.where(low, swapped, datt)]
    sources = [
        jnp.concatenate([proj_ref[:, 256 * e : 256 * e + 128], middle[e]], axis=1)
        for e in range(2)
    ]
    picked = [dot_nn(turned_table_of(rows[e]), sources[e]).astype(bf) for e in range(2)]
    for e in range(2):
        qk, dv = picked[e][:, 0:128], picked[e][:, 128:256]
        key_low = jnp.where(low, half_roll(qk), zero)
        turned = half_roll(dv)
        value_only = jnp.where(low, turned, zero) if e == 0 else jnp.where(low, zero, turned)
        bias = jnp.where(rows[e] < count, 0.0, -30000.0)
        for sl in SLICES:
            scores[e][sl, :] = 0.125 * dot_nt(qk[sl], key_low[sl]) + bias[:, sl]
            back_probs[e][sl, :] = dot_nt(dv[sl], value_only[sl])
    for e in range(2):
        for sl in SLICES:
            probs = softmax_rows(scores[e][sl, :])
            back = back_probs[e][sl, :]
            probs_low[e][sl, :] = probs.astype(bf)
            inner = jnp.sum(back * probs, axis=-1, keepdims=True)
            backs[e][sl, :] = (0.125 * (probs * (back - inner))).astype(bf)
    moved = []
    for e in range(2):
        qk, dv = picked[e][:, 0:128], picked[e][:, 128:256]
        queries, keys, values = [], [], []
        for sl in SLICES:
            back = backs[e][sl, :]
            queries.append(dot_nn(back, qk[sl]))
            keys.append(dot_tn(back, qk[sl]))
            values.append(dot_tn(probs_low[e][sl, :], dv[sl]))
        key_query = jnp.where(low, jnp.concatenate(keys, 0), jnp.concatenate(queries, 0))
        value = jnp.concatenate(values, 0)
        db_ref[0, 0, e : e + 1, :] = jnp.sum(key_query, axis=0, keepdims=True)
        db_ref[0, 0, 2 + e : 3 + e, :] = jnp.sum(value, axis=0, keepdims=True)
        moved.append(jnp.concatenate([key_query.astype(bf), value.astype(bf)], axis=1))
    placed = [dot_nn(tables[e][...], moved[e]) for e in range(2)]
    key_queries = [placed[e][:, 0:128] for e in range(2)]
    turned = [pltpu.roll(t, DH, 1) for t in key_queries]
    query = jnp.where(low, turned[0], key_queries[1]).astype(bf)
    key = jnp.where(low, key_queries[0], turned[1]).astype(bf)
    value = jnp.where(low, placed[0][:, 128:256], placed[1][:, 128:256]).astype(bf)
    dq_ref[...] = query
    dk_ref[...] = key
    dv_ref[...] = value
    out = jnp.concatenate([query, key, value], axis=1)
    part = dot_tn(x_ref[...], out)

    @pl.when(seq == 0)
    def _():
        total[...] = part

    @pl.when(seq != 0)
    def _():
        total[...] += part

    dw_ref[0] = total[...].astype(bf)

    @pl.when(turn < 2)
    def _():
        rows = D // shards
        columns = pl.ds(pl.multiple_of(turn * 384, 128), 384)
        for k in range(shards):
            group[k, :, columns] = total[k * rows : (k + 1) * rows, :].astype(bf)

    end()


def pair_at(i):
    return (i % 2) * (PAIRS // 2) + i // 2


def pair_at(i):
    return (i % 2) * (PAIRS // 2) + i // 2


def attention_backward(lengths, rounded, proj, datt, rows, grads, shards, reps, collective_id):
    seqs = rows.shape[0]
    tokens = seqs * LEN
    own = lambda width: pl.BlockSpec((LEN, width), lambda i, s, n: (s, pair_at(i)))
    part = (D // shards, D)
    shapes = {
        "d": [grads[0].shape[1:]],
        "u": [g.shape[1:] for g in grads[1:]],
        "g": [part],
    }
    every = shapes["d"] + shapes["u"] + shapes["g"]
    return pl.pallas_call(
        partial(attention_backward_body, shards, reps, shapes),
        grid_spec=pltpu.PrefetchScalarGridSpec(
            num_scalar_prefetch=1,
            grid=(PAIRS, seqs),
            in_specs=[
                pl.BlockSpec((LEN, D), lambda i, s, n: (s, 0)),
                own(384),
                own(128),
                pl.BlockSpec((1, H, LEN), lambda i, s, n: (s, 0, 0)),
            ]
            + [pl.BlockSpec(memory_space=pl.ANY)] * 3,
            out_specs=[own(128)] * 3
            + [
                pl.BlockSpec((1, D, 384), lambda i, s, n: (i // 2, 0, i % 2)),
                pl.BlockSpec((1, 1, 4, 128), lambda i, s, n: (s, pair_at(i), 0, 0)),
            ]
            + [pl.BlockSpec(memory_space=pl.ANY)] * 4,
            scratch_shapes=[pltpu.VMEM((LEN, LEN), bf)] * 2
            + [pltpu.VMEM((LEN, 128), f32)] * 4
            + [pltpu.VMEM((LEN, 128), bf)] * 4
            + [pltpu.VMEM((D, 384), f32), pltpu.VMEM((shards,) + part, bf)]
            + sum([reduce_scratch(shapes[k], shards, reps, k == "u") for k in "dug"], []),
        ),
        out_shape=[jax.ShapeDtypeStruct((tokens, D), bf)] * 3
        + [
            jax.ShapeDtypeStruct((PAIRS // 2, D, D), bf),
            jax.ShapeDtypeStruct((seqs, PAIRS, 4, 128), f32),
        ]
        + result_shapes(every),
        compiler_params=pltpu.CompilerParams(
            vmem_limit_bytes=62 << 20, collective_id=collective_id, has_side_effects=True
        ),
        name="attention_backward",
    )(lengths, rounded, proj, datt, rows, *grads)


def norm_stats(x):
    c=jnp.mean(x,axis=-1,keepdims=True)
    xc=x-c
    r=lax.rsqrt(jnp.mean(xc*xc,axis=-1,keepdims=True)+eps_norm)
    return xc*r,r

def norm_back(up,normed,r,gain):
    g=up*gain
    return r*(g-jnp.mean(g,axis=-1,keepdims=True)-normed*jnp.mean(g*normed,axis=-1,keepdims=True))

def colsum(x): return jnp.sum(x,axis=0,keepdims=True)

def gelu_parts(u):
    cdf=0.5+0.5*lax.erf(u*0.7071067811865476)
    pdf=jnp.exp(-0.5*u*u)*0.3989422804014327
    return u*cdf,cdf+u*pdf

def middle_body(len_ref,h_ref,a_ref,ct_ref,ow_ref,uw_ref,dw_ref,vec_ref,ub_ref,
               out_ref,bs_ref,ba_ref,act,pl_,low_ref,d2_ref,sl_ref,small_ref,ubg_ref,
               gp,n1_ref,*,T,sub_rows,chunk):
    i=pl.program_id(0)
    per=LEN//T
    count=len_ref[i//per]
    @pl.when(i==0)
    def _():
        small_ref[...]=jnp.zeros_like(small_ref); ubg_ref[...]=jnp.zeros_like(ubg_ref)
    out_b,g1,b1,down_b,g2,b2=[vec_ref[j:j+1,:] for j in range(6)]
    parts=[slice(k,k+sub_rows) for k in range(0,T,sub_rows)]
    r1s=[];sums=[]
    xs=[dot_nn(a_ref[p,:],ow_ref[...]) for p in parts]
    for p,x in zip(parts,xs):
        n1,r1=norm_stats(h_ref[p,:]+x+out_b)
        n1_ref[p,:]=n1; r1s.append(r1)
        low_ref[p,:]=(n1*g1+b1).astype(bf)
    for j in range(0,FF,chunk):
        sl=slice(j,j+chunk)
        for p in parts:
            u=dot_nn(low_ref[p,:],uw_ref[:,sl])+ub_ref[:,sl]
            a,g=gelu_parts(u)
            act[p,sl]=a.astype(bf); gp[p,sl]=g.astype(gp.dtype)
    ys=[dot_nn(act[p,:],dw_ref[...]) for p in parts]
    for p,y in zip(parts,ys):
        pos=lax.broadcasted_iota(jnp.int32,(sub_rows,1),0)+(i%per)*T+p.start
        valid=jnp.where(pos<count,1.0,0.0)
        second=n1_ref[p,:]*g1+b1+y+down_b
        n2,r2=norm_stats(second)
        out_ref[p,:]=valid*(n2*g2+b2)
        up=valid*ct_ref[p,:]
        b2nd=norm_back(up,n2,r2,g2)
        d2_ref[p,:]=b2nd.astype(bf)
        bs_ref[p,:]=b2nd
        sums.append(jnp.concatenate([colsum(b2nd),colsum(up*n2),colsum(up)],axis=0))
    small_ref[3:6,:]+=sum(sums[1:],sums[0])
    for j in range(0,FF,chunk):
        sl=slice(j,j+chunk)
        cs=[]
        for p in parts:
            bp=dot_nt(d2_ref[p,:],dw_ref[sl,:])*gp[p,sl].astype(f32)
            cs.append(colsum(bp))
            pl_[p,sl]=bp.astype(bf)
        ubg_ref[:,sl]+=sum(cs[1:],cs[0])
    zs=[dot_nt(pl_[p,:],uw_ref[...]) for p in parts]
    sums=[]
    for p,z,r1 in zip(parts,zs,r1s):
        bfirst=z+bs_ref[p,:]
        n1=n1_ref[p,:]
        bsum=norm_back(bfirst,n1,r1,g1)
        bs_ref[p,:]=bsum
        sl_ref[p,:]=bsum.astype(bf)
        sums.append(jnp.concatenate([colsum(bsum),colsum(bfirst*n1),colsum(bfirst)],axis=0))
    small_ref[0:3,:]+=sum(sums[1:],sums[0])
    for p in parts:
        ba_ref[p,:]=dot_nt(sl_ref[p,:],ow_ref[...]).astype(bf)

def middle(lengths,hidden,att,ct,ow,uw,dw,vec,ub,T=512,chunk=768,gpt=f32,sub_rows=256):
    tokens=hidden.shape[0]
    tile=lambda n=D: pl.BlockSpec((T,n),lambda i,l:(i,0))
    const=lambda shape: pl.BlockSpec(shape,lambda i,l:(0,0),pipeline_mode=pl.Buffered(1))
    whole=lambda shape: pl.BlockSpec(shape,lambda i,l:(0,0))
    sd=lambda n,dt: jax.ShapeDtypeStruct((tokens,n),dt)
    return pl.pallas_call(
        partial(middle_body,T=T,chunk=chunk,sub_rows=sub_rows),
        grid_spec=pltpu.PrefetchScalarGridSpec(num_scalar_prefetch=1,grid=(tokens//T,),
          in_specs=[tile(),tile(),tile(),const((D,D)),const((D,FF)),const((FF,D)),whole((8,D)),whole((1,FF))],
          out_specs=[tile(),tile(),tile(),tile(FF),tile(FF),tile(),tile(),tile(),whole((8,D)),whole((1,FF))],
          scratch_shapes=[pltpu.VMEM((T,FF),gpt),pltpu.VMEM((T,D),f32)]),
        out_shape=[sd(D,f32),sd(D,f32),sd(D,bf),sd(FF,bf),sd(FF,bf),sd(D,bf),sd(D,bf),sd(D,bf),jax.ShapeDtypeStruct((8,D),f32),jax.ShapeDtypeStruct((1,FF),f32)],
        compiler_params=pltpu.CompilerParams(vmem_limit_bytes=63<<20),
        name="middle")(lengths,hidden,att,ct,ow,uw,dw,vec,ub)


def weight_grads_body(act,d2,low,pre,att,sl,down_ref,up_ref,out_ref,left,right,left_sem,right_sem):
    i=pl.program_id(0)
    def block(ref,j):
        return ref if ref.shape[1]==D else ref.at[:,j*D:(j+1)*D]
    def fetch(ref,j,slot,to_left):
        return pltpu.make_async_copy(block(ref,j),(left if to_left else right).at[slot],(left_sem if to_left else right_sem).at[slot])
    loads={0:((act,0,0,True),(d2,0,0,False)),1:((act,2,0,True),(pre,0,1,False)),2:((act,3,1,True),),
           3:((low,0,0,True),),4:((pre,1,0,False),(att,0,1,True)),5:((pre,2,1,False),),6:((pre,3,0,False),),7:((sl,0,1,False),)}
    needs={0:((act,0,0,True),(d2,0,0,False)),1:((act,1,1,True),),2:((act,2,0,True),),3:((act,3,1,True),),4:((low,0,0,True),(pre,0,1,False)),
           5:((pre,1,0,False),),6:((pre,2,1,False),),7:((pre,3,0,False),),8:((att,0,1,True),(sl,0,1,False))}
    for k in range(9):
        def move(k=k):
            for one in loads.get(k,()): fetch(*one).start()
            for one in needs[k]: fetch(*one).wait()
            if k==0: fetch(act,1,1,True).start()
        pl.when(i==k)(move)
    l=jnp.where(i<4,lax.rem(i,2),jnp.where(i<8,0,1))
    r=jnp.where(i<4,0,jnp.where(i<8,lax.rem(i+1,2),1))
    grad=dot_tn(left[l],right[r]).astype(bf)
    @pl.when(i<4)
    def _(): down_ref[...]=grad
    @pl.when(jnp.logical_and(i>=4,i<8))
    def _(): up_ref[...]=grad
    @pl.when(i==8)
    def _(): out_ref[...]=grad
def weight_grads(act,d2,low,pre,att,sl):
    tokens=act.shape[0]
    return pl.pallas_call(weight_grads_body,grid=(9,),
        in_specs=[pl.BlockSpec(memory_space=pl.ANY)]*6,
        out_specs=[pl.BlockSpec((D,D),lambda i:(jnp.minimum(i,3),0)),pl.BlockSpec((D,D),lambda i:(0,jnp.clip(i-4,0,3))),pl.BlockSpec((D,D),lambda i:(0,0))],
        out_shape=[jax.ShapeDtypeStruct((FF,D),bf),jax.ShapeDtypeStruct((D,FF),bf),jax.ShapeDtypeStruct((D,D),bf)],
        scratch_shapes=[pltpu.VMEM((2,tokens,D),bf),pltpu.VMEM((2,tokens,D),bf),pltpu.SemaphoreType.DMA((2,)),pltpu.SemaphoreType.DMA((2,))],
        compiler_params=pltpu.CompilerParams(vmem_limit_bytes=60<<20),name="weight_grads")(act,d2,low,pre,att,sl)


def input_grad_body(shards,reps,shapes,bs_ref,dq_ref,dk_ref,dv_ref,w_ref,*refs):
    n=len(shapes)
    grads,out_ref,sums,scratch=refs[:n],refs[n],refs[n+1:2*n+1],refs[2*n+1:]
    weight,loaded=scratch[-2:]
    load=lambda: pltpu.make_async_copy(w_ref,weight,loaded.at[0])
    def ready():
        load().start()
        meet(place,True)
    place=Place(shards,reps); step=pl.program_id(0)
    size=len(reduce_scratch(shapes[1:],shards,reps))
    jobs={"a":Reduce(place,grads[1:],sums[1:],scratch[:size]),"b":Reduce(place,grads[:1],sums[:1],scratch[size:-2],True)}
    end=follow(LAST_PLAN,jobs,step,pl.num_programs(0)-1,ready)
    pl.when(step==0)(lambda: load().wait())
    out_ref[...]=bs_ref[...]+dot_nt(dq_ref[...],weight[:,0:D])+dot_nt(dk_ref[...],weight[:,D:2*D])+dot_nt(dv_ref[...],weight[:,2*D:3*D])
    end()
def input_grad(back_sum,dq,dk,dv,weight,grads,shards,reps,collective_id):
    rows=back_sum.shape[0]//8
    tile=pl.BlockSpec((rows,D),lambda i:(i,0))
    anywhere=[pl.BlockSpec(memory_space=pl.ANY)]*len(grads)
    shapes=[g.shape[1:] for g in grads]
    return pl.pallas_call(partial(input_grad_body,shards,reps,shapes),grid=(8,),
        in_specs=[tile]*4+[pl.BlockSpec(memory_space=pl.ANY)]+anywhere,
        out_specs=[tile]+anywhere,
        out_shape=[jax.ShapeDtypeStruct(back_sum.shape,f32)]+result_shapes(shapes),
        scratch_shapes=reduce_scratch(shapes[1:],shards,reps)+reduce_scratch(shapes[:1],shards,reps,True)+[pltpu.VMEM((D,3*D),bf),pltpu.SemaphoreType.DMA((1,))],
        compiler_params=pltpu.CompilerParams(vmem_limit_bytes=50<<20,collective_id=collective_id,has_side_effects=True),name="input_grad")(back_sum,dq,dk,dv,weight,*grads)


def as_rows(row):
    filled = -(-row.shape[-1] // 128)
    row = jnp.pad(row, ((0, 0), (0, filled * 128 - row.shape[-1])))
    return jnp.pad(row.reshape(-1, filled, 128), ((0, 0), (0, 0), (0, 128)))


def pack_body(*refs):
    *ins, out = refs
    rows = []
    for ref in ins:
        value = ref[...].astype(f32)
        for at in range(0, value.shape[0], 128):
            part = value[at : at + 128].reshape(1, -1)
            rows.append(jnp.pad(part, ((0, 0), (0, 256 - part.shape[1]))))
    rows.append(jnp.zeros((16 - len(rows), 256), f32))
    out[...] = jnp.concatenate(rows, axis=0).astype(bf)


def pack_shards(vectors):
    return pl.pallas_call(
        pack_body, out_shape=jax.ShapeDtypeStruct((16, 256), bf), name="pack_vectors"
    )(*vectors)


def pack_vectors(vectors):
    rows = jnp.concatenate([as_rows(v) for v in vectors], axis=1)
    return jnp.pad(rows, ((0, 0), (0, 16 - rows.shape[1]), (0, 0)))


def local(
    hidden,
    lengths,
    clusters,
    input_weight,
    query_bias,
    value_bias,
    out_weight,
    out_bias,
    norm1_gain,
    norm1_bias,
    up_weight,
    up_bias,
    down_weight,
    down_bias,
    norm2_gain,
    norm2_bias,
    cotangent,
    *,
    shards,
    reps,
):
    seqs = hidden.shape[0]
    tokens = seqs * LEN
    part = D // shards
    vectors = pack_shards(
        (
            query_bias,
            value_bias,
            out_bias,
            norm1_gain,
            norm1_bias,
            down_bias,
            norm2_gain,
            norm2_bias,
            up_bias,
        )
    )
    in_w, vectors = gather_now((input_weight, vectors), shards, reps, 1)
    in_w = in_w.reshape(D, 3 * D)
    vectors = vectors.astype(f32)
    table = vectors[:, :8, :part].transpose(1, 0, 2).reshape(8, D)
    bias_all = jnp.concatenate([table[0], jnp.zeros((D,), f32), table[1]])[None]
    norm_rows = jnp.concatenate([table[2:], table[:2]])
    up_b = vectors[:, 8:, :128].reshape(shards, -1)[:, : FF // shards].reshape(1, FF)

    flat = hidden.reshape(tokens, D)
    attended, proj, rounded, up_w, down_w, out_w = attention_forward(
        lengths,
        flat,
        in_w,
        bias_all,
        clusters,
        (up_weight, down_weight, out_weight),
        shards,
        reps,
        2,
    )
    out_w, up_w, down_w = [w.reshape(-1, w.shape[-1]) for w in (out_w, up_w, down_w)]
    (
        result,
        back_sum,
        back_attended,
        activated,
        pre_low,
        first_low,
        second_low,
        sum_low,
        norm_sums,
        up_b_sum,
    ) = middle(
        lengths,
        flat,
        attended,
        cotangent.reshape(tokens, D),
        out_w,
        up_w,
        down_w,
        norm_rows,
        up_b,
    )
    down_g, up_g, out_g = weight_grads(
        activated, second_low, first_low, pre_low, attended, sum_low
    )
    dq, dk, dv, in_g, bias_sums, down_s, up_s, out_s, in_first = attention_backward(
        lengths,
        rounded,
        proj,
        back_attended,
        clusters,
        [g.reshape(shards, -1, g.shape[-1]) for g in (down_g, up_g, out_g)],
        shards,
        reps,
        3,
    )
    bias_sums = jnp.sum(bias_sums, axis=0)
    query_sum = bias_sums[:, 0:2, DH:].reshape(D)
    value_sum = jnp.concatenate([bias_sums[:, 2, :DH], bias_sums[:, 3, DH:]], axis=1).reshape(D)
    table = jnp.concatenate([query_sum[None], value_sum[None], norm_sums[:6]])
    table = table.reshape(8, shards, part)
    small = pack_vectors(
        [table[i].astype(bf) for i in range(8)] + [up_b_sum.reshape(shards, -1).astype(bf)]
    )
    back_input, *in_s, small_s = input_grad(
        back_sum,
        dq,
        dk,
        dv,
        in_w,
        [in_g[2].reshape(shards, part, D), in_g[1].reshape(shards, part, D), small],
        shards,
        reps,
        4,
    )
    back_input = back_input.reshape(seqs, LEN, D)
    in_s = [in_first, in_s[1], in_s[0]]
    in_s = jnp.concatenate(
        [
            in_s[g][:, 384 * c + 128 * t : 384 * c + 128 * t + 128]
            for t in range(3)
            for c in range(2)
            for g in range(PAIRS // 2)
        ],
        axis=1,
    )

    small_s = small_s[:, :128]
    vec = [small_s[i, :part] for i in range(8)]
    return (
        result.reshape(seqs, LEN, D),
        back_input,
        in_s,
        vec[0],
        vec[1],
        out_s,
        vec[2],
        vec[3],
        vec[4],
        up_s,
        small_s[8:].reshape(-1)[: FF // shards],
        down_s,
        vec[5],
        vec[6],
        vec[7],
    )


def solution(mesh):
    tokens = P(("rep", "shard"), None, None)
    matrix, vector = P("shard", None), P("shard")
    params = (
        matrix,
        vector,
        vector,
        matrix,
        vector,
        vector,
        vector,
        matrix,
        vector,
        matrix,
        vector,
        vector,
        vector,
    )
    return jax.shard_map(
        partial(local, shards=mesh.shape["shard"], reps=mesh.shape["rep"]),
        mesh=mesh,
        in_specs=(tokens, P(("rep", "shard")), tokens) + params + (tokens,),
        out_specs=(tokens, tokens) + params,
        check_vma=False,
    )
```
